32 devices in a mesh: dp: 4 (over x, core), seq: 8 (over z, y).
Axes of the slice: x: 2, y: 2, z: 4, core: 2. Of those that a mesh axis runs over, the one named last changes fastest.
Arguments:
- hidden_in: bfloat16 [4, 1024, 2048], P('dp', 'seq'), may hold values from -6 to 6
- segment_ids: int32 [4, 1024], P('dp'), may hold values from 0 to 3, never falling along the last dimension, each value on 1 to 512 neighbouring positions
- routes: int32 [4, 1024, 8], P('dp', 'seq'), may hold values from 0 to 15, all different within a row; in each aligned block of 128 rows (0 to 127, 128 to 255, ..., all dimensions but the last counted through in order) at most 96 rows name the same one
- w_query: bfloat16 [2048, 2048], P(('dp', 'seq')), may hold values from -0.125 to 0.125
- w_key: bfloat16 [2048, 2048], P(('dp', 'seq')), may hold values from -0.125 to 0.125
- w_value: bfloat16 [2048, 2048], P(('dp', 'seq')), may hold values from -0.125 to 0.125
- w_out: bfloat16 [2048, 2048], P(('dp', 'seq')), may hold values from -0.5 to 0.5
- gain_attn: bfloat16 [2048], P(('dp', 'seq')), may hold values from 0.099609375 to 1.8984375
- gain_query: bfloat16 [2048], P(('dp', 'seq')), may hold values from 0.796875 to 2
- gain_key: bfloat16 [2048], P(('dp', 'seq')), may hold values from 0.796875 to 2
- gain_ffn: bfloat16 [2048], P(('dp', 'seq')), may hold values from 0.099609375 to 1.8984375
- w_router: bfloat16 [2048, 16], P(('dp', 'seq')), may hold values from -0.0625 to 0.0625
- w_gate: bfloat16 [16, 2048, 1024], P('seq', 'dp'), may hold values from -0.125 to 0.125
- w_up: bfloat16 [16, 2048, 1024], P('seq', 'dp'), may hold values from -0.125 to 0.125
- w_down: bfloat16 [16, 1024, 2048], P('seq', None, 'dp'), may hold values from -6 to 6
- cotangent: bfloat16 [4, 1024, 2048], P('dp', 'seq'), may hold values from -6 to 6
Outputs:
- block_out: bfloat16 [4, 1024, 2048], P('dp', 'seq')
- grad_hidden: float32 [4, 1024, 2048], P('dp', 'seq')
- grad_query: float32 [2048, 2048], P(('dp', 'seq'))
- grad_key: float32 [2048, 2048], P(('dp', 'seq'))
- grad_value: float32 [2048, 2048], P(('dp', 'seq'))
- grad_out_proj: float32 [2048, 2048], P(('dp', 'seq'))
- grad_gain_attn: float32 [2048], P(('dp', 'seq'))
- grad_gain_query: float32 [2048], P(('dp', 'seq'))
- grad_gain_key: float32 [2048], P(('dp', 'seq'))
- grad_gain_ffn: float32 [2048], P(('dp', 'seq'))
- grad_router: float32 [2048, 16], P(('dp', 'seq'))
- grad_gate: float32 [16, 2048, 1024], P('seq', 'dp')
- grad_up: float32 [16, 2048, 1024], P('seq', 'dp')
- grad_down: float32 [16, 1024, 2048], P('seq', None, 'dp')
The draws below stay inside these ranges and needn't reach their ends.
Inputs may be any that keep to these rules, and one draw needn't show every extreme that they name: `routes`: within the rows of one device (aligned blocks of 128 tokens of the flattened rows), each expert is named by at most 96 token choices; a token's 8 experts are distinct. `segment_ids`: file numbers never fall along a row; each file is a run of 1 to 512 positions.
All inputs are finite; a program needn't handle non-finite values.
Results may differ from the reference program's by a relative error of at most 0.02.
Values may be sent and summed in bfloat16 or wider, within the bound.
No kernel may reach another device: no remote copies, remote signals or barrier semaphores. Data moves between devices by JAX's collectives and lax.ppermute only.
A program may use at most 448 MiB of HBM per device.

```python
import math
import jax
import jax.numpy as jnp
import numpy as np
from jax import lax

D = 2048
HEAD = 128
FF = 1024
TOPK = 8
T_DEV = 128
BATCH = 4
SEQLEN = 1024
EXPERTS = 16
CAP = 96
SEGS = 4
SEG_MOST = 512


def strengthened(values, stream_key, source, target, shards_of, factor):
    def block_of(position):
        return (jnp.arange(values.shape[position]) // (values.shape[position] // shards_of)).reshape((-1,) + (1,) * (values.ndim - 1 - position))

    near = jax.random.permutation(stream_key, shards_of)[block_of(target)]
    other_side = (block_of(target) + shards_of // 2) % shards_of
    return jnp.where((block_of(source) == near) | (block_of(source) == other_side), factor * values, values)


def shard_levels(key, dims, cuts, low, top_value):
    level = 1.0
    for position, parts in cuts:
        draws = jax.random.uniform(jax.random.fold_in(jax.random.fold_in(key, 6), position), (parts,), jnp.float32, low / len(cuts), top_value / len(cuts))
        level = level * jnp.repeat(jnp.exp(draws), dims[position] // parts).reshape((-1,) + (1,) * (len(dims) - 1 - position))
    return level


def split_up(number_of, total, limit, lean):
    weights = [(1 << 20) // math.isqrt(rank ** lean) + 1 for rank in range(2, number_of + 1)]
    surplus, holding = total - limit - (number_of - 1), [1] * (number_of - 1)
    while surplus > 0:
        free = [i for i in range(number_of - 1) if holding[i] < limit]
        mass, budget = sum([weights[i] for i in free]), surplus
        for i in free:
            addition = min(limit - holding[i], max(1, budget * weights[i] // mass), surplus)
            holding[i] = holding[i] + addition
            surplus = surplus - addition
    return np.array([limit] + holding)


def ragged(rng, number_of, total, bound, skew):
    if number_of == 2:
        one = jax.random.randint(rng, (), max(1, total - bound), min(bound, total - 1) + 1)
        return jnp.stack([one, total - one])
    lengths = jnp.asarray(split_up(number_of, total, bound, skew), jnp.int32)
    twos = (number_of - 1) // 2
    giver, sink = lengths[1:1 + 2 * twos:2], lengths[2:2 + 2 * twos:2]
    margin = jnp.minimum(giver - 1, bound - sink)
    passed = jax.random.randint(jax.random.fold_in(rng, 1), (twos,), 0, 1 << 20) % (margin + 1)
    lengths = lengths.at[1:1 + 2 * twos:2].set(giver - passed).at[2:2 + 2 * twos:2].set(sink + passed)
    return lengths[jax.random.permutation(jax.random.fold_in(rng, 2), number_of)]


def shared_out(key, own, number, rows, amount, top, most, slope):
    ranking = jax.random.permutation(key, amount)
    crowded, usual = portions_of(amount, rows * top, most, slope, True), portions_of(amount, rows * top, most, slope, False)
    places = jnp.arange(amount)

    def named(tallies, turn):
        used = int((tallies > 0).sum())
        fixed = max(1, used // 4)
        shifted = fixed + (places - fixed + turn * (used - fixed)) % max(1, amount - fixed)
        return jnp.zeros((amount,), jnp.int32).at[ranking[jnp.where(places < fixed, places, shifted)]].set(jnp.asarray(tallies, jnp.int32))

    tallies = jnp.where(number % 4 == 0, named(crowded, number // 4), named(usual, number - number // 4 - 1))
    mixed = jax.random.permutation(jax.random.fold_in(own, 3), amount)
    giver, sink = mixed[0:amount // 2 * 2:2], mixed[1:amount // 2 * 2:2]
    room = jnp.minimum(tallies[giver] - 1, most - tallies[sink]) // 2
    room = jnp.where((giver == ranking[0]) | (sink == ranking[0]) | (tallies[sink] == 0), 0, jnp.maximum(room, 0))
    shifted = jax.random.randint(jax.random.fold_in(own, 4), (amount // 2,), 0, 1 << 20) % (room + 1)
    tallies = tallies.at[giver].add(-shifted).at[sink].add(shifted)
    items = jnp.searchsorted(jnp.cumsum(tallies), jnp.arange(rows * top), side="right").astype(jnp.int32)
    listing = items.reshape(top, rows).T
    listing = listing[jax.random.permutation(jax.random.fold_in(own, 1), rows)]
    turn = jax.random.randint(jax.random.fold_in(own, 2), (rows, 1), 0, top)
    return jnp.take_along_axis(listing, (jnp.arange(top)[None, :] + turn) % top, axis=1)


def portions_of(count, total, bound, slope, full):
    portions = [(1 << 20) // math.isqrt(rank ** slope) + 1 for rank in range(1, count + 1)]
    largest = bound if full else min(bound, max(-(-total // count), total * portions[0] // sum(portions)))
    least = 1 if total - largest >= count - 1 else 0
    holding, rest = [largest] + [least] * (count - 1), total - largest - least * (count - 1)
    while rest > 0:
        free = [i for i in range(1, count) if holding[i] < largest] or [i for i in range(1, count) if holding[i] < bound]
        mass, left = sum([portions[i] for i in free]), rest
        for i in free:
            extra = min(bound - holding[i], max(1, left * portions[i] // mass), rest)
            holding[i] = holding[i] + extra
            rest = rest - extra
    return np.array(holding)


def scatter_about(key, shape, scale, reach, split=(), held_as=jnp.bfloat16):
    entries = jax.random.normal(key, shape, jnp.float32) * scale
    if len(split) > 0:
        entries = shard_levels(key, shape, split, -0.22, 0.18) * entries
    return jnp.clip(entries, min=-reach, max=reach).astype(held_as)


def bell_draw_with(key, dims, width, reach, cuts, heavy, kind=jnp.bfloat16):
    array = width * jax.random.normal(key, dims, jnp.float32)
    if cuts:
        array = array * shard_levels(key, dims, cuts, -0.22, 0.18)
    return jnp.clip(strengthened(array, jax.random.fold_in(key, 3), *heavy), -reach, reach).astype(kind)


def setup_inputs(seed: int = 0) -> dict:
    arg_keys = jax.random.split(jax.random.key(seed), 17)
    hidden_in = bell_draw_with(arg_keys[0], (BATCH, SEQLEN, D), 1.0, 6.0, ((0, 4), (1, 8)), (1, 2, 8, 2.0))
    segment_ids = jax.vmap(lambda own: jnp.searchsorted(jnp.cumsum(ragged(own, SEGS, SEQLEN, SEG_MOST, 2)), jnp.arange(SEQLEN), side="right"))(jax.random.split(arg_keys[1], BATCH)).reshape((BATCH, SEQLEN)).astype(jnp.int32)
    routes_keys = jax.random.split(jax.random.fold_in(arg_keys[2], 1), BATCH * SEQLEN // T_DEV)
    routes_turns = jax.random.permutation(jax.random.fold_in(arg_keys[2], 3), BATCH * SEQLEN // T_DEV)
    routes = jax.vmap(lambda own, number: shared_out(jax.random.fold_in(arg_keys[2], 2), own, number, T_DEV, EXPERTS, TOPK, CAP, 1))(routes_keys, routes_turns).reshape((BATCH, SEQLEN, TOPK))
    w_query = scatter_about(arg_keys[3], (D, D), D ** -0.5, 0.125, ((0, 32),))
    w_key = scatter_about(arg_keys[4], (D, D), D ** -0.5, 0.125, ((0, 32),))
    w_value = scatter_about(arg_keys[5], (D, D), D ** -0.5, 0.125, ((0, 32),))
    w_out = scatter_about(arg_keys[6], (D, D), (D // 16) ** -0.5, 0.5, ((0, 32),))
    gain_attn = jnp.clip(1.0 + 0.18 * jax.random.normal(arg_keys[7], (D,), jnp.float32), 0.099609375, 1.8984375).astype(jnp.bfloat16)
    gain_query = jnp.clip(jnp.exp(math.log(2.0) - 0.92020463 * jax.random.uniform(arg_keys[8], (D,), jnp.float32) ** shard_levels(arg_keys[8], (D,), ((0, 32),), -0.2, 0.2)), 0.796875, 2.0).astype(jnp.bfloat16)
    gain_key = jnp.clip(jnp.exp(math.log(2.0) - 0.92020463 * jax.random.uniform(arg_keys[9], (D,), jnp.float32) ** shard_levels(arg_keys[9], (D,), ((0, 32),), -0.2, 0.2)), 0.796875, 2.0).astype(jnp.bfloat16)
    gain_ffn = jnp.clip(1.0 + 0.18 * jax.random.normal(arg_keys[10], (D,), jnp.float32), 0.099609375, 1.8984375).astype(jnp.bfloat16)
    w_router = scatter_about(arg_keys[11], (D, EXPERTS), (4 * D) ** -0.5, 0.0625, ((0, 32),))
    w_gate = scatter_about(arg_keys[12], (EXPERTS, D, FF), D ** -0.5, 0.125, ((0, 8), (1, 4)))
    w_up = scatter_about(arg_keys[13], (EXPERTS, D, FF), D ** -0.5, 0.125, ((0, 8), (1, 4)))
    w_down = scatter_about(arg_keys[14], (EXPERTS, FF, D), 1.0, 6.0, ((0, 8), (2, 4)))
    cotangent = scatter_about(arg_keys[15], (BATCH, SEQLEN, D), 1.0, 6.0, ((0, 4), (1, 8)))
    return dict(hidden_in=hidden_in, segment_ids=segment_ids, routes=routes, w_query=w_query, w_key=w_key, w_value=w_value, w_out=w_out, gain_attn=gain_attn, gain_query=gain_query, gain_key=gain_key, gain_ffn=gain_ffn, w_router=w_router, w_gate=w_gate, w_up=w_up, w_down=w_down, cotangent=cotangent)


highest = lax.Precision.HIGHEST
epsilon = 1e-05
masked_score = -1e+30
rope_base = 10000.0

@jax.custom_vjp
def low(v):
    return lax.optimization_barrier(v.astype(jnp.bfloat16)).astype(jnp.float32)

@jax.custom_vjp
def low_back(v):
    return v

def low_keep(v):
    return (low(v), None)

def low_pass(kept, grad):
    return (grad,)

def back_keep(v):
    return (v, None)

def back_low(kept, grad):
    return (low(grad),)
low.defvjp(low_keep, low_pass)
low_back.defvjp(back_keep, back_low)

def normalize(values, gain_vec):
    return values * lax.rsqrt(lax.optimization_barrier(jnp.mean(values * values, axis=-1, keepdims=True)) + epsilon) * gain_vec

def rotary(values, positions):
    half_dim = values.shape[-1] // 2
    frequency = jnp.exp(jnp.arange(half_dim, dtype=jnp.float32) * (-2.0 * math.log(rope_base) / values.shape[-1]))
    angles = positions.astype(jnp.float32)[:, None] * frequency[None, :]
    cosine = jnp.cos(angles)[:, None, :]
    sine_table = jnp.sin(angles)[:, None, :]
    first_half = values[..., :half_dim]
    second = values[..., half_dim:]
    return jnp.concatenate([first_half * cosine - second * sine_table, second * cosine + first_half * sine_table], axis=-1)

def softmax_rows(values):
    peak_value = lax.optimization_barrier(jnp.max(values, axis=-1, keepdims=True))
    raised = jnp.exp(values - peak_value)
    return raised / lax.optimization_barrier(jnp.sum(raised, axis=-1, keepdims=True))

def attend_row(row_item):
    query_rot, key_rot, value_in, segments = row_item
    length = query_rot.shape[0]
    span = min(512, length)
    scaling = query_rot.shape[-1] ** (-0.5)
    positions = jnp.arange(length, dtype=jnp.int32)

    def one_block(block_item):
        queries, query_pos, query_seg = block_item
        raw_scores = low_back(jnp.einsum('qhd,khd->hqk', queries, key_rot, precision=highest))
        allowed = (query_pos[:, None] >= positions[None, :]) & (query_seg[:, None] == segments[None, :])
        scores = jnp.where(allowed[None], raw_scores * scaling, masked_score)
        peak_value = lax.optimization_barrier(jnp.max(scores, axis=-1, keepdims=True))
        log_total = peak_value + jnp.log(lax.optimization_barrier(jnp.sum(jnp.exp(scores - peak_value), axis=-1, keepdims=True)))
        weights = low(jnp.exp(scores - log_total))
        return jnp.einsum('hqk,khd->qhd', weights, value_in, precision=highest)
    block_count = length // span
    items = (query_rot.reshape((block_count, span) + query_rot.shape[1:]), positions.reshape(block_count, span), segments.reshape(block_count, span))
    result = lax.map(jax.checkpoint(one_block), items)
    return result.reshape(query_rot.shape)

def run_expert(expert_item):
    inputs, gate_weight, up_weight, down_weight = expert_item
    gate_pre = low_back(jnp.dot(inputs, gate_weight, precision=highest))
    up_pre = low_back(jnp.dot(inputs, up_weight, precision=highest))
    activated = low(gate_pre * lax.logistic(gate_pre) * up_pre)
    return low(low_back(jnp.dot(activated, down_weight, precision=highest)))

def forward(params, segment_ids, routes):
    hidden, w_query, w_key, w_value, w_out, gain_attn, gain_query, gain_key, gain_ffn, w_router, w_gate, w_up, w_down = params
    batch_rows, length, model_width = hidden.shape
    head_count = model_width // HEAD
    positions = jnp.arange(length, dtype=jnp.int32)
    head_shape = (batch_rows, length, head_count, HEAD)
    normed = low(normalize(hidden, gain_attn))
    query = low_back(jnp.einsum('bsd,de->bse', normed, w_query, precision=highest))
    key_proj = low_back(jnp.einsum('bsd,de->bse', normed, w_key, precision=highest))
    value_proj = low(low_back(jnp.einsum('bsd,de->bse', normed, w_value, precision=highest)))
    query_rot = low(rotary(normalize(query, gain_query).reshape(head_shape), positions))
    key_rot = low(rotary(normalize(key_proj, gain_key).reshape(head_shape), positions))
    attention = lax.map(attend_row, (query_rot, key_rot, value_proj.reshape(head_shape), segment_ids))
    attended = low(low_back(attention.reshape(batch_rows, length, model_width)))
    hidden_mid = hidden + low_back(jnp.einsum('bsd,de->bse', attended, w_out, precision=highest))
    normed_ffn = low(normalize(hidden_mid, gain_ffn))
    logits = low_back(jnp.einsum('bsd,de->bse', normed_ffn, w_router, precision=highest))
    chances = softmax_rows(logits)
    picks = routes[..., None] == jnp.arange(EXPERTS, dtype=jnp.int32)
    gate_values = lax.optimization_barrier(jnp.sum(jnp.where(picks, chances[:, :, None, :], 0.0), axis=-1))
    flat_routes = routes.reshape(-1).astype(jnp.int32)
    pair_count = flat_routes.shape[0]
    device_blocks = batch_rows * length // T_DEV
    pair_hits = (flat_routes[:, None] == jnp.arange(EXPERTS, dtype=jnp.int32)[None, :]).astype(jnp.int32)
    pair_hits = pair_hits.reshape(device_blocks, T_DEV * TOPK, EXPERTS)
    earlier = jnp.cumsum(pair_hits, axis=1) - pair_hits
    slot_index = lax.optimization_barrier(jnp.sum(earlier * pair_hits, axis=-1)).reshape(-1).astype(jnp.int32)
    pair_ids = jnp.arange(pair_count, dtype=jnp.int32)
    block_of = pair_ids // (T_DEV * TOPK)
    token_of = pair_ids // TOPK
    row_inputs = normed_ffn.reshape(-1, model_width)[token_of]
    buffer = jnp.zeros((EXPERTS, device_blocks, CAP, model_width), jnp.float32)
    buffer = low_back(buffer.at[flat_routes, block_of, slot_index].set(row_inputs))
    expert_rows = buffer.reshape(EXPERTS, device_blocks * CAP, model_width)
    results = lax.map(jax.checkpoint(run_expert), (expert_rows, w_gate, w_up, w_down))
    results = results.reshape(EXPERTS, device_blocks, CAP, model_width)
    picked = results[flat_routes, block_of, slot_index].reshape(batch_rows, length, TOPK, model_width)
    mixture = low_back(lax.optimization_barrier(jnp.sum(gate_values[..., None] * picked, axis=2)))
    return hidden_mid + mixture

def reference(hidden_in, segment_ids, routes, w_query, w_key, w_value, w_out, gain_attn, gain_query, gain_key, gain_ffn, w_router, w_gate, w_up, w_down, cotangent):
    floats = (hidden_in, w_query, w_key, w_value, w_out, gain_attn, gain_query, gain_key, gain_ffn, w_router, w_gate, w_up, w_down)
    params = tuple((array_in.astype(jnp.float32) for array_in in floats))

    def run_forward(*values):
        return forward(values, segment_ids, routes)
    block_out, pullback = jax.vjp(run_forward, *params)
    gradients = pullback(cotangent.astype(jnp.float32))
    return (block_out.astype(jnp.bfloat16), gradients[0], gradients[1], gradients[2], gradients[3], gradients[4], gradients[5], gradients[6], gradients[7], gradients[8], gradients[9], gradients[10], gradients[11], gradients[12])
```

```python
import math

import jax
import jax.numpy as jnp
from jax import lax
from jax.sharding import PartitionSpec as P

HEAD = 128


epsilon = 1e-05
masked_score = -1e30
rope_base = 10000.0


def normalize(values, gain_vec):
    return (
        values * lax.rsqrt(jnp.mean(values * values, axis=-1, keepdims=True) + epsilon) * gain_vec
    )


def rotary(values, positions):
    half_dim = values.shape[-1] // 2
    frequency = jnp.exp(
        jnp.arange(half_dim, dtype=jnp.float32) * (-2.0 * math.log(rope_base) / values.shape[-1])
    )
    angles = positions.astype(jnp.float32)[:, None] * frequency[None, :]
    cosine = jnp.cos(angles)[:, None, :]
    sine_table = jnp.sin(angles)[:, None, :]
    first_half = values[..., :half_dim]
    second = values[..., half_dim:]
    return jnp.concatenate(
        [first_half * cosine - second * sine_table, second * cosine + first_half * sine_table],
        axis=-1,
    )


def softmax_rows(values):
    peak_value = jnp.max(values, axis=-1, keepdims=True)
    raised = jnp.exp(values - peak_value)
    return raised / jnp.sum(raised, axis=-1, keepdims=True)


def rotate_normed(projection, gain_vec, positions):
    tokens, model_width = projection.shape
    return rotary(
        normalize(projection, gain_vec).reshape(tokens, model_width // HEAD, HEAD), positions
    )


def masked_scores(queries, key_block, query_pos, query_seg, key_pos, key_seg, scaling):
    raw_scores = jnp.einsum("qhd,khd->hqk", queries, key_block, preferred_element_type=jnp.float32)
    allowed = (query_pos[:, None] >= key_pos[None, :]) & (query_seg[:, None] == key_seg[None, :])
    return jnp.where(allowed[None], raw_scores * scaling, masked_score)


def key_window(keys_all, values_all, row_seg, begin_at, span):
    key_block = lax.dynamic_slice_in_dim(keys_all, begin_at, span)
    value_block = lax.dynamic_slice_in_dim(values_all, begin_at, span)
    key_pos = begin_at + lax.iota(jnp.int32, span)
    key_seg = lax.dynamic_slice_in_dim(row_seg, begin_at, span)
    return (key_block, value_block, key_pos, key_seg)


def project_front(hidden, layer_full, positions):
    tokens, model_width = hidden.shape
    normed = normalize(hidden, layer_full[5].astype(jnp.float32)).astype(jnp.bfloat16)
    query = jnp.dot(normed, layer_full[0], preferred_element_type=jnp.float32)
    key_proj = jnp.dot(normed, layer_full[1], preferred_element_type=jnp.float32)
    value_proj = jnp.dot(normed, layer_full[2], preferred_element_type=jnp.float32)
    query_rot = rotate_normed(query, layer_full[6].astype(jnp.float32), positions).astype(
        jnp.bfloat16
    )
    key_rot = rotate_normed(key_proj, layer_full[7].astype(jnp.float32), positions).astype(
        jnp.bfloat16
    )
    value_in = value_proj.astype(jnp.bfloat16).reshape(tokens, model_width // HEAD, HEAD)
    return (normed, query, key_proj, query_rot, key_rot, value_in)


def attend_local(query_rot, keys_all, values_all, row_seg, offset, span):
    tokens, head_count, head_dim = query_rot.shape
    scaling = head_dim ** (-0.5)
    query_pos = offset + lax.iota(jnp.int32, tokens)
    query_seg = lax.dynamic_slice_in_dim(row_seg, offset, tokens)
    reach_blocks = (offset + tokens + span - 1) // span

    def block_scores(block_index):
        begin_at = block_index * span
        key_block, value_block, key_pos, key_seg = key_window(
            keys_all, values_all, row_seg, begin_at, span
        )
        return (
            masked_scores(query_rot, key_block, query_pos, query_seg, key_pos, key_seg, scaling),
            value_block,
        )

    def first_pass(block_index, state_pair):
        peak_value, denominator = state_pair
        scores, unused_values = block_scores(block_index)
        new_peak = jnp.maximum(peak_value, jnp.max(scores, axis=-1))
        denominator = denominator * jnp.exp(peak_value - new_peak) + jnp.sum(
            jnp.exp(scores - new_peak[..., None]), axis=-1
        )
        return (new_peak, denominator)

    start_state = (
        jnp.full((head_count, tokens), masked_score, jnp.float32),
        jnp.zeros((head_count, tokens), jnp.float32),
    )
    peak_value, denominator = lax.fori_loop(0, reach_blocks, first_pass, start_state)
    log_total = peak_value + jnp.log(denominator)

    def second_pass(block_index, running):
        scores, value_block = block_scores(block_index)
        weights = jnp.exp(scores - log_total[..., None]).astype(jnp.bfloat16)
        return running + jnp.einsum(
            "hqk,khd->qhd", weights, value_block, preferred_element_type=jnp.float32
        )

    attention = lax.fori_loop(
        0, reach_blocks, second_pass, jnp.zeros((tokens, head_count, head_dim), jnp.float32)
    )
    return (attention, log_total)


def query_grads(query_rot, keys_all, values_all, row_seg, offset, span, log_total, grad_attended):
    tokens, head_count, head_dim = query_rot.shape
    scaling = head_dim ** (-0.5)
    query_pos = offset + lax.iota(jnp.int32, tokens)
    query_seg = lax.dynamic_slice_in_dim(row_seg, offset, tokens)
    reach_blocks = (offset + tokens + span - 1) // span

    def block_terms(block_index):
        begin_at = block_index * span
        key_block, value_block, key_pos, key_seg = key_window(
            keys_all, values_all, row_seg, begin_at, span
        )
        scores = masked_scores(
            query_rot, key_block, query_pos, query_seg, key_pos, key_seg, scaling
        )
        weights = jnp.exp(scores - log_total[..., None])
        grad_weights = jnp.einsum(
            "qhd,khd->hqk", grad_attended, value_block, preferred_element_type=jnp.float32
        )
        return (key_block, weights, grad_weights)

    def delta_pass(block_index, running):
        unused_keys, weights, grad_weights = block_terms(block_index)
        return running + jnp.sum(weights * grad_weights, axis=-1)

    delta = lax.fori_loop(0, reach_blocks, delta_pass, jnp.zeros((head_count, tokens), jnp.float32))

    def query_pass(block_index, running):
        key_block, weights, grad_weights = block_terms(block_index)
        grad_scores = (weights * (grad_weights - delta[..., None]) * scaling).astype(jnp.bfloat16)
        return running + jnp.einsum(
            "hqk,khd->qhd", grad_scores, key_block, preferred_element_type=jnp.float32
        )

    grad_query_rot = lax.fori_loop(
        0, reach_blocks, query_pass, jnp.zeros((tokens, head_count, head_dim), jnp.float32)
    )
    return (delta, grad_query_rot)


def route_tokens(hidden_mid, layer_full, choice_rows):
    tokens, pick_count = choice_rows.shape
    normed_ffn = normalize(hidden_mid, layer_full[8].astype(jnp.float32)).astype(jnp.bfloat16)
    logits = jnp.dot(normed_ffn, layer_full[4], preferred_element_type=jnp.float32)
    expert_count = logits.shape[1]
    capacity = 3 * tokens * pick_count // (2 * expert_count)
    chances = softmax_rows(logits)
    picks = choice_rows[:, :, None] == lax.iota(jnp.int32, expert_count)[None, None, :]
    gate_values = jnp.sum(jnp.where(picks, chances[:, None, :], 0.0), axis=-1)
    flat_hits = picks.reshape(tokens * pick_count, expert_count).astype(jnp.int32)
    earlier = jnp.cumsum(flat_hits, axis=0) - flat_hits
    slot_ids = choice_rows.reshape(-1) * capacity + jnp.sum(earlier * flat_hits, axis=1)
    pair_table = lax.iota(jnp.int32, expert_count * capacity)[:, None] == slot_ids[None, :]
    spread = jnp.sum(
        pair_table.reshape(expert_count * capacity, tokens, pick_count).astype(jnp.int32), axis=2
    ).astype(jnp.bfloat16)
    send_rows = jnp.dot(spread, normed_ffn, preferred_element_type=jnp.float32).astype(jnp.bfloat16)
    send_rows = send_rows.reshape(expert_count, capacity, hidden_mid.shape[1])
    return (normed_ffn, chances, picks, gate_values, slot_ids, pair_table, spread, send_rows)


def group_rows(row_block, held_experts):
    sources = row_block.shape[0] // held_experts
    grouped = row_block.reshape(
        sources, held_experts, row_block.shape[1], row_block.shape[2]
    ).transpose(1, 0, 2, 3)
    return grouped.reshape(held_experts, sources * row_block.shape[1], row_block.shape[2])


def ungroup_rows(grouped, whole_shape):
    held_experts = grouped.shape[0]
    sources = whole_shape[0] // held_experts
    spread_out = grouped.reshape(held_experts, sources, whole_shape[1], whole_shape[2]).transpose(
        1, 0, 2, 3
    )
    return spread_out.reshape(whole_shape)


def expert_forward(row_block, gate_full, up_full, down_full):
    inputs = group_rows(row_block, gate_full.shape[0])
    gate_pre = jnp.einsum("erd,edf->erf", inputs, gate_full, preferred_element_type=jnp.float32)
    up_pre = jnp.einsum("erd,edf->erf", inputs, up_full, preferred_element_type=jnp.float32)
    activated = (gate_pre * lax.logistic(gate_pre) * up_pre).astype(jnp.bfloat16)
    result = jnp.einsum(
        "erf,efd->erd", activated, down_full, preferred_element_type=jnp.float32
    ).astype(jnp.bfloat16)
    return ungroup_rows(result, row_block.shape)


def expert_backward(row_block, grad_block, gate_full, up_full, down_full):
    inputs = group_rows(row_block, gate_full.shape[0])
    grad_outputs = group_rows(grad_block, gate_full.shape[0])
    gate_pre = jnp.einsum("erd,edf->erf", inputs, gate_full, preferred_element_type=jnp.float32)
    up_pre = jnp.einsum("erd,edf->erf", inputs, up_full, preferred_element_type=jnp.float32)
    sigmoid_gate = lax.logistic(gate_pre)
    activated = (gate_pre * sigmoid_gate * up_pre).astype(jnp.bfloat16)
    grad_act = jnp.einsum(
        "erd,efd->erf", grad_outputs, down_full, preferred_element_type=jnp.float32
    )
    grad_down = jnp.einsum(
        "erf,erd->efd", activated, grad_outputs, preferred_element_type=jnp.float32
    )
    grad_gate_pre = (
        grad_act * up_pre * sigmoid_gate * (1.0 + gate_pre * (1.0 - sigmoid_gate))
    ).astype(jnp.bfloat16)
    grad_up_pre = (grad_act * gate_pre * sigmoid_gate).astype(jnp.bfloat16)
    grad_gate_w = jnp.einsum(
        "erd,erf->edf", inputs, grad_gate_pre, preferred_element_type=jnp.float32
    )
    grad_up_w = jnp.einsum("erd,erf->edf", inputs, grad_up_pre, preferred_element_type=jnp.float32)
    grad_inputs = jnp.einsum(
        "erf,edf->erd", grad_gate_pre, gate_full, preferred_element_type=jnp.float32
    )
    grad_inputs = grad_inputs + jnp.einsum(
        "erf,edf->erd", grad_up_pre, up_full, preferred_element_type=jnp.float32
    )
    return (
        ungroup_rows(grad_inputs.astype(jnp.bfloat16), row_block.shape),
        grad_gate_w,
        grad_up_w,
        grad_down,
    )


def contract_rows(left, right):
    return lax.dot_general(
        left, right, (((0,), (0,)), ((), ())), preferred_element_type=jnp.float32
    )


def contract_cols(left, right):
    return lax.dot_general(
        left, right, (((1,), (1,)), ((), ())), preferred_element_type=jnp.float32
    )


def on_device(
    hidden_in,
    segment_ids,
    routes,
    w_query,
    w_key,
    w_value,
    w_out,
    gain_attn,
    gain_query,
    gain_key,
    gain_ffn,
    w_router,
    w_gate,
    w_up,
    w_down,
    cotangent,
):
    hidden = hidden_in[0].astype(jnp.float32)
    tokens, model_width = hidden.shape
    head_count = model_width // HEAD
    row_seg = segment_ids[0]
    choice_rows = routes[0]
    offset = lax.axis_index("seq") * tokens
    positions = offset + lax.iota(jnp.int32, tokens)
    span = min(512, row_seg.shape[0])
    layer_full = (
        lax.all_gather(w_query, ("dp", "seq"), axis=0, tiled=True),
        lax.all_gather(w_key, ("dp", "seq"), axis=0, tiled=True),
        lax.all_gather(w_value, ("dp", "seq"), axis=0, tiled=True),
        lax.all_gather(w_out, ("dp", "seq"), axis=0, tiled=True),
        lax.all_gather(w_router, ("dp", "seq"), axis=0, tiled=True),
        lax.all_gather(gain_attn, ("dp", "seq"), axis=0, tiled=True),
        lax.all_gather(gain_query, ("dp", "seq"), axis=0, tiled=True),
        lax.all_gather(gain_key, ("dp", "seq"), axis=0, tiled=True),
        lax.all_gather(gain_ffn, ("dp", "seq"), axis=0, tiled=True),
    )
    expert_full = (
        lax.all_gather(w_gate, "dp", axis=1, tiled=True),
        lax.all_gather(w_up, "dp", axis=1, tiled=True),
        lax.all_gather(w_down, "dp", axis=2, tiled=True),
    )
    projected = project_front(hidden, layer_full, positions)
    keys_all, values_all = (
        lax.all_gather(projected[4], "seq", axis=0, tiled=True),
        lax.all_gather(projected[5], "seq", axis=0, tiled=True),
    )
    attention, log_total = attend_local(projected[3], keys_all, values_all, row_seg, offset, span)
    attended = attention.reshape(tokens, model_width).astype(jnp.bfloat16)
    hidden_mid = hidden + jnp.dot(attended, layer_full[3], preferred_element_type=jnp.float32)
    routing = route_tokens(hidden_mid, layer_full, choice_rows)
    expert_count, capacity = (routing[7].shape[0], routing[7].shape[1])
    expert_out = expert_forward(
        lax.all_to_all(routing[7], "seq", split_axis=0, concat_axis=0, tiled=True),
        expert_full[0],
        expert_full[1],
        expert_full[2],
    )
    returned = lax.all_to_all(expert_out, "seq", split_axis=0, concat_axis=0, tiled=True)
    picked = jnp.take(returned.reshape(expert_count * capacity, model_width), routing[4], axis=0)
    picked = picked.reshape(tokens, choice_rows.shape[1], model_width)
    mixture = jnp.sum(routing[3][:, :, None] * picked.astype(jnp.float32), axis=1)
    block_out = (hidden_mid + mixture).astype(jnp.bfloat16)
    layer_full = (
        lax.all_gather(w_query, ("dp", "seq"), axis=0, tiled=True),
        lax.all_gather(w_key, ("dp", "seq"), axis=0, tiled=True),
        lax.all_gather(w_value, ("dp", "seq"), axis=0, tiled=True),
        lax.all_gather(w_out, ("dp", "seq"), axis=0, tiled=True),
        lax.all_gather(w_router, ("dp", "seq"), axis=0, tiled=True),
        lax.all_gather(gain_attn, ("dp", "seq"), axis=0, tiled=True),
        lax.all_gather(gain_query, ("dp", "seq"), axis=0, tiled=True),
        lax.all_gather(gain_key, ("dp", "seq"), axis=0, tiled=True),
        lax.all_gather(gain_ffn, ("dp", "seq"), axis=0, tiled=True),
    )
    expert_full = (
        lax.all_gather(w_gate, "dp", axis=1, tiled=True),
        lax.all_gather(w_up, "dp", axis=1, tiled=True),
        lax.all_gather(w_down, "dp", axis=2, tiled=True),
    )
    projected = project_front(hidden, layer_full, positions)
    keys_all, values_all = (
        lax.all_gather(projected[4], "seq", axis=0, tiled=True),
        lax.all_gather(projected[5], "seq", axis=0, tiled=True),
    )
    attention, log_total = attend_local(projected[3], keys_all, values_all, row_seg, offset, span)
    attended = attention.reshape(tokens, model_width).astype(jnp.bfloat16)
    hidden_mid = hidden + jnp.dot(attended, layer_full[3], preferred_element_type=jnp.float32)
    routing = route_tokens(hidden_mid, layer_full, choice_rows)
    normed_ffn, chances, picks, gate_values, slot_ids, pair_table, spread, send_rows = routing
    grad_out = cotangent[0].astype(jnp.float32)
    grad_gates = jnp.sum(grad_out[:, None, :] * picked.astype(jnp.float32), axis=-1)
    slot_gates = jnp.sum(jnp.where(pair_table, gate_values.reshape(-1)[None, :], 0.0), axis=1)
    grad_rows_in = jnp.dot(spread, cotangent[0], preferred_element_type=jnp.float32)
    grad_slots = (
        (slot_gates[:, None] * grad_rows_in)
        .astype(jnp.bfloat16)
        .reshape(expert_count, capacity, model_width)
    )
    arrived_rows, arrived_grads = (
        lax.all_to_all(send_rows, "seq", split_axis=0, concat_axis=0, tiled=True),
        lax.all_to_all(grad_slots, "seq", split_axis=0, concat_axis=0, tiled=True),
    )
    grad_inputs, grad_gate_w, grad_up_w, grad_down_w = expert_backward(
        arrived_rows, arrived_grads, expert_full[0], expert_full[1], expert_full[2]
    )
    grad_back = lax.all_to_all(grad_inputs, "seq", split_axis=0, concat_axis=0, tiled=True)
    grad_normed_ffn = contract_rows(spread, grad_back.reshape(expert_count * capacity, model_width))
    grad_chances = jnp.sum(jnp.where(picks, grad_gates[:, :, None], 0.0), axis=1)
    grad_logits = (
        chances * (grad_chances - jnp.sum(chances * grad_chances, axis=-1, keepdims=True))
    ).astype(jnp.bfloat16)
    grad_router_w = contract_rows(normed_ffn, grad_logits)
    grad_normed_ffn = grad_normed_ffn + contract_cols(grad_logits, layer_full[4])
    unused_ffn, pull_ffn = jax.vjp(normalize, hidden_mid, layer_full[8].astype(jnp.float32))
    grad_mid_norm, grad_gain_ffn_w = pull_ffn(grad_normed_ffn)
    grad_mid = grad_out + grad_mid_norm
    grad_mid_low = grad_mid.astype(jnp.bfloat16)
    grad_w_out = contract_rows(attended, grad_mid_low)
    grad_attended = (
        contract_cols(grad_mid_low, layer_full[3])
        .astype(jnp.bfloat16)
        .reshape(tokens, head_count, HEAD)
    )
    query_rot = projected[3]
    delta, grad_query_rot = query_grads(
        query_rot, keys_all, values_all, row_seg, offset, span, log_total, grad_attended
    )
    scaling = HEAD ** (-0.5)
    query_seg = lax.dynamic_slice_in_dim(row_seg, offset, tokens)
    row_count = lax.axis_size("seq") * tokens
    step_rows = math.gcd(row_count, 512)

    def one_window(window_index, running):
        window_start = window_index * step_rows
        key_block, value_block, key_pos, key_seg = key_window(
            keys_all, values_all, row_seg, window_start, step_rows
        )
        scores = masked_scores(
            query_rot, key_block, positions, query_seg, key_pos, key_seg, scaling
        )
        weights = jnp.exp(scores - log_total[..., None])
        grad_weights = jnp.einsum(
            "qhd,khd->hqk", grad_attended, value_block, preferred_element_type=jnp.float32
        )
        grad_scores = (weights * (grad_weights - delta[..., None]) * scaling).astype(jnp.bfloat16)
        grad_key_part = jnp.einsum(
            "hqk,qhd->khd", grad_scores, query_rot, preferred_element_type=jnp.float32
        )
        grad_value_part = jnp.einsum(
            "hqk,qhd->khd",
            weights.astype(jnp.bfloat16),
            grad_attended,
            preferred_element_type=jnp.float32,
        )
        term = jnp.concatenate(
            [
                grad_key_part.reshape(step_rows, model_width),
                grad_value_part.reshape(step_rows, model_width),
            ],
            axis=1,
        )
        return lax.dynamic_update_slice_in_dim(running, term, window_index * step_rows, 0)

    key_sums = lax.psum_scatter(
        lax.fori_loop(
            0,
            row_count // step_rows,
            one_window,
            jnp.zeros((row_count, 2 * model_width), jnp.float32),
        ).astype(jnp.bfloat16),
        "seq",
        scatter_dimension=0,
        tiled=True,
    ).astype(jnp.float32)
    grad_key_rot = key_sums[:, :model_width].reshape(tokens, head_count, HEAD)
    grad_v_low = key_sums[:, model_width:].astype(jnp.bfloat16)

    def query_chain(projection, gain_vec):
        return rotate_normed(projection, gain_vec, positions)

    unused_query, pull_query = jax.vjp(query_chain, projected[1], layer_full[6].astype(jnp.float32))
    grad_query_pre, grad_gain_query_w = pull_query(grad_query_rot)
    unused_key, pull_key = jax.vjp(query_chain, projected[2], layer_full[7].astype(jnp.float32))
    grad_key_pre, grad_gain_key_w = pull_key(grad_key_rot)
    grad_q_low = grad_query_pre.astype(jnp.bfloat16)
    grad_k_low = grad_key_pre.astype(jnp.bfloat16)
    normed = projected[0]
    grad_w_query = contract_rows(normed, grad_q_low)
    grad_w_key = contract_rows(normed, grad_k_low)
    grad_w_value = contract_rows(normed, grad_v_low)
    grad_normed = (
        contract_cols(grad_q_low, layer_full[0])
        + contract_cols(grad_k_low, layer_full[1])
        + contract_cols(grad_v_low, layer_full[2])
    )
    unused_attn, pull_attn = jax.vjp(normalize, hidden, layer_full[5].astype(jnp.float32))
    grad_hidden_norm, grad_gain_attn_w = pull_attn(grad_normed)
    grad_hidden = grad_mid + grad_hidden_norm
    shares = (
        lax.psum_scatter(grad_w_query, ("dp", "seq"), scatter_dimension=0, tiled=True),
        lax.psum_scatter(grad_w_key, ("dp", "seq"), scatter_dimension=0, tiled=True),
        lax.psum_scatter(grad_w_value, ("dp", "seq"), scatter_dimension=0, tiled=True),
        lax.psum_scatter(grad_w_out, ("dp", "seq"), scatter_dimension=0, tiled=True),
        lax.psum_scatter(grad_router_w, ("dp", "seq"), scatter_dimension=0, tiled=True),
        lax.psum_scatter(grad_gain_attn_w, ("dp", "seq"), scatter_dimension=0, tiled=True),
        lax.psum_scatter(grad_gain_query_w, ("dp", "seq"), scatter_dimension=0, tiled=True),
        lax.psum_scatter(grad_gain_key_w, ("dp", "seq"), scatter_dimension=0, tiled=True),
        lax.psum_scatter(grad_gain_ffn_w, ("dp", "seq"), scatter_dimension=0, tiled=True),
    )
    expert_shares = (
        lax.psum_scatter(
            grad_gate_w.astype(jnp.bfloat16), "dp", scatter_dimension=1, tiled=True
        ).astype(jnp.float32),
        lax.psum_scatter(
            grad_up_w.astype(jnp.bfloat16), "dp", scatter_dimension=1, tiled=True
        ).astype(jnp.float32),
        lax.psum_scatter(
            grad_down_w.astype(jnp.bfloat16), "dp", scatter_dimension=2, tiled=True
        ).astype(jnp.float32),
    )
    return (
        block_out[None],
        grad_hidden[None],
        shares[0],
        shares[1],
        shares[2],
        shares[3],
        shares[5],
        shares[6],
        shares[7],
        shares[8],
        shares[4],
        expert_shares[0],
        expert_shares[1],
        expert_shares[2],
    )


def rope_tables(row_count, head_dim):
    half_dim = head_dim // 2
    frequency = jnp.exp(
        jnp.arange(half_dim, dtype=jnp.float32) * (-2.0 * math.log(rope_base) / head_dim)
    )
    angles = jnp.arange(row_count, dtype=jnp.float32)[:, None] * frequency[None, :]
    return (jnp.cos(angles), jnp.sin(angles))


def rotate(values, cosine, sine):
    half_dim = values.shape[-1] // 2
    first, second = (values[:, :half_dim], values[:, half_dim:])
    return jnp.concatenate(
        [first * cosine - second * sine, second * cosine + first * sine], axis=-1
    )


def mm(left, right, dims):
    return lax.dot_general(left, right, (dims, ((), ())), preferred_element_type=jnp.float32)


def swap(values, bits, size):
    return lax.ppermute(values, "dp", [(i, i ^ bits) for i in range(size)])


def gather_pieces(shard):
    across = swap(shard, 2, 4)
    return (shard, swap(shard, 1, 4), across, swap(across, 1, 4))


def sum_pieces(pieces):
    arrived_own, arrived_across = (swap(pieces[1], 1, 4), swap(pieces[3], 1, 4))
    kept = pieces[0].astype(jnp.float32) + arrived_own.astype(jnp.float32)
    passed = (pieces[2].astype(jnp.float32) + arrived_across.astype(jnp.float32)).astype(
        jnp.bfloat16
    )
    return kept + swap(passed, 2, 4).astype(jnp.float32)


def reorder(values, dp_index, pieces):
    width = values.shape[1] // pieces
    return jnp.concatenate(
        [
            lax.dynamic_slice_in_dim(values, (dp_index ^ k) * width, width, axis=1)
            for k in range(pieces)
        ],
        axis=1,
    )


def on_device_heads(
    hidden_in,
    segment_ids,
    routes,
    w_query,
    w_key,
    w_value,
    w_out,
    gain_attn,
    gain_query,
    gain_key,
    gain_ffn,
    w_router,
    w_gate,
    w_up,
    w_down,
    cotangent,
):
    low, full = (jnp.bfloat16, jnp.float32)
    both = ("dp", "seq")
    shards, parts = (lax.axis_size("seq"), lax.axis_size("dp"))
    seq_index, dp_index = (lax.axis_index("seq"), lax.axis_index("dp"))
    tokens, width = hidden_in.shape[1:]
    rows = shards * tokens
    cols = width // shards
    heads = cols // HEAD
    held = w_gate.shape[0]
    ff = w_gate.shape[2]
    expert_count = held * shards
    block_rows = w_query.shape[0]
    row_seg = segment_ids[0]
    first_col = seq_index * cols
    first_row = seq_index * tokens

    def own_cols(values, count=cols):
        return lax.dynamic_slice_in_dim(values, seq_index * count, count, axis=values.ndim - 1)

    x_row = lax.all_gather(hidden_in[0], "seq", axis=0, tiled=True)
    small = lax.all_gather(
        jnp.concatenate(
            [
                w_router,
                gain_attn[:, None],
                gain_query[:, None],
                gain_key[:, None],
                gain_ffn[:, None],
            ],
            axis=1,
        ).T,
        both,
        axis=1,
        tiled=True,
    )
    router_t = small[:expert_count]
    gains = small[expert_count:].astype(full)
    qkv_blocks = jnp.stack([w_query, w_key, w_value], axis=1)
    qkv_blocks = qkv_blocks.reshape(block_rows, 3, shards, cols).transpose(2, 0, 1, 3)
    w_qkv = lax.all_to_all(qkv_blocks, "seq", 0, 0, tiled=True)
    w_qkv = lax.all_gather(
        w_qkv.reshape(shards * block_rows, 3 * cols), "dp", axis=0, tiled=True
    )
    out_full = lax.all_gather(w_out, both, axis=0, tiled=True)
    dy_shard = reorder(cotangent[0], dp_index, parts)
    routes_low = jnp.pad(routes[0].astype(low), ((0, 0), (0, 128 - routes.shape[2])))
    dy_ext = lax.all_gather(
        jnp.concatenate([dy_shard, routes_low], axis=1), "seq", axis=0, tiled=True
    )
    dy_row = dy_ext[:, :width]
    routes_row = dy_ext[:, width : width + routes.shape[2]].astype(jnp.int32)
    gate_full = jnp.concatenate(gather_pieces(w_gate), axis=1)
    up_full = jnp.concatenate(gather_pieces(w_up), axis=1)
    down_full = jnp.concatenate(gather_pieces(w_down), axis=2)

    x_wide = x_row.astype(full)
    r_attn = lax.rsqrt(jnp.mean(x_wide * x_wide, axis=-1, keepdims=True) + epsilon)
    normed = (x_wide * r_attn * gains[0]).astype(low)
    qkv = mm(normed, w_qkv, ((1,), (0,)))
    query, key_proj = (qkv[:, :cols], qkv[:, cols : 2 * cols])
    value_in = qkv[:, 2 * cols :].astype(low)
    sums = lax.psum(
        jnp.stack([jnp.sum(query * query, axis=-1), jnp.sum(key_proj * key_proj, axis=-1)]), "seq"
    )
    r_query, r_key = (
        lax.rsqrt(sums[i] / width + epsilon)[:, None] for i in range(2)
    )
    g_query, g_key = (own_cols(gains[1]), own_cols(gains[2]))
    cosine, sine = rope_tables(rows, HEAD)
    q_normed, k_normed = (query * r_query * g_query, key_proj * r_key * g_key)
    position = lax.iota(jnp.int32, rows)
    allowed = (position[:, None] >= position[None, :]) & (row_seg[:, None] == row_seg[None, :])
    scaling = HEAD ** (-0.5)

    def head(values, h):
        return values[:, h * HEAD : (h + 1) * HEAD]

    q_rot, k_rot, log_total, attended = ([], [], [], [])
    for h in range(heads):
        q_rot.append(rotate(head(q_normed, h), cosine, sine).astype(low))
        k_rot.append(rotate(head(k_normed, h), cosine, sine).astype(low))
        scores = jnp.where(
            allowed, mm(q_rot[h], k_rot[h], ((1,), (1,))) * scaling, masked_score
        )
        peak = jnp.max(scores, axis=-1, keepdims=True)
        log_total.append(peak + jnp.log(jnp.sum(jnp.exp(scores - peak), axis=-1, keepdims=True)))
        weights = jnp.exp(scores - log_total[h]).astype(low)
        attended.append(mm(weights, head(value_in, h), ((1,), (0,))).astype(low))
    attended = jnp.concatenate(attended, axis=1)
    attended_row = lax.all_gather(attended, "seq", axis=0)
    hidden_mid = x_wide + jnp.einsum(
        "src,scn->rn",
        attended_row,
        out_full.reshape(shards, cols, width),
        preferred_element_type=full,
    )

    r_ffn = lax.rsqrt(jnp.mean(hidden_mid * hidden_mid, axis=-1, keepdims=True) + epsilon)
    normed_ffn = (hidden_mid * r_ffn * gains[3]).astype(low)
    chances = softmax_rows(mm(normed_ffn, router_t, ((1,), (1,))))
    expert_ids = lax.iota(jnp.int32, expert_count)
    chosen = jnp.any(routes_row[:, :, None] == expert_ids[None, None, :], axis=1)
    mine = own_cols(jnp.where(chosen, chances, 0.0), held)
    mine_chosen = own_cols(chosen, held)
    nf_parts = reorder(normed_ffn, dp_index, parts)
    scaled, gate_grads, up_grads, gate_sums = ([], [], [], [])
    for e in range(held):
        gate_pre = mm(nf_parts, gate_full[e], ((1,), (0,)))
        up_pre = mm(nf_parts, up_full[e], ((1,), (0,)))
        grad_act = mm(dy_row, down_full[e], ((1,), (1,)))
        weight = mine[:, e : e + 1]
        sig = lax.logistic(gate_pre)
        act = gate_pre * sig * up_pre
        gate_sums.append(jnp.sum(act * grad_act, axis=-1))
        scaled.append((weight * act).astype(low))
        grad_act = weight * grad_act
        gate_grads.append(
            (grad_act * up_pre * sig * (1.0 + gate_pre * (1.0 - sig))).astype(low)
        )
        up_grads.append((grad_act * gate_pre * sig).astype(low))
    mixture = sum(mm(scaled[e], down_full[e], ((1,), (0,))) for e in range(held)).astype(low)
    mixture_own = lax.psum_scatter(mixture, "seq", scatter_dimension=0, tiled=True)
    nf_grad = sum(
        mm(gate_grads[e], gate_full[e], ((1,), (1,))) + mm(up_grads[e], up_full[e], ((1,), (1,)))
        for e in range(held)
    )

    my_gates = jnp.where(mine_chosen, jnp.stack(gate_sums, axis=1), 0.0)
    my_chances = own_cols(chances, held)
    placed = lax.dynamic_update_slice_in_dim(
        jnp.zeros_like(chances), my_gates, seq_index * held, axis=1
    )
    grad_logits = (
        chances * (placed - jnp.sum(my_gates * my_chances, axis=1, keepdims=True))
    ).astype(low)
    router_grad = mm(grad_logits, normed_ffn, ((0,), (0,)))
    nf_grad = nf_grad + mm(grad_logits, reorder(router_t, dp_index, parts), ((1,), (0,)))
    nf_grad = lax.psum_scatter(nf_grad.astype(low), "seq", scatter_dimension=0, tiled=True)

    mid_own = lax.dynamic_slice_in_dim(hidden_mid, first_row, tokens)
    block_out = (mid_own + reorder(mixture_own, dp_index, parts).astype(full)).astype(low)
    nf_own = reorder(nf_grad, dp_index, parts).astype(full)
    r_own = lax.dynamic_slice_in_dim(r_ffn, first_row, tokens)
    gain_ffn_grad = jnp.sum(nf_own * mid_own * r_own, axis=0)
    scaled_grad = nf_own * gains[3]
    grad_mid = (
        cotangent[0].astype(full)
        + r_own * scaled_grad
        - mid_own * (r_own**3) * jnp.mean(scaled_grad * mid_own, axis=-1, keepdims=True)
    )
    mid_row = lax.all_gather(grad_mid.astype(low), "seq", axis=0, tiled=True)

    def expert_grad(left, right):
        return [mm(left[e], right[e], ((0,), (0,))).astype(low) for e in range(held)]

    down_grad = jnp.stack(expert_grad(scaled, [dy_row] * held))
    gate_grad = jnp.stack(expert_grad([nf_parts] * held, gate_grads))
    up_grad = jnp.stack(expert_grad([nf_parts] * held, up_grads))
    grad_w_down = sum_pieces(jnp.split(down_grad, parts, axis=2))
    grad_w_gate = sum_pieces(jnp.split(gate_grad, parts, axis=1))
    grad_w_up = sum_pieces(jnp.split(up_grad, parts, axis=1))

    out_rows = lax.dynamic_slice_in_dim(out_full, first_col, cols)
    grad_attended = mm(mid_row, out_rows, ((1,), (1,))).astype(low)
    q_grads, k_grads, v_grads = ([], [], [])
    for h in range(heads):
        scores = jnp.where(
            allowed, mm(q_rot[h], k_rot[h], ((1,), (1,))) * scaling, masked_score
        )
        p = jnp.exp(scores - log_total[h])
        grad_h = head(grad_attended, h)
        grad_weights = mm(grad_h, head(value_in, h), ((1,), (1,)))
        delta = jnp.sum(p * grad_weights, axis=-1, keepdims=True)
        grad_scores = (scaling * p * (grad_weights - delta)).astype(low)
        q_grads.append(rotate(mm(grad_scores, k_rot[h], ((1,), (0,))), cosine, -sine))
        k_grads.append(rotate(mm(grad_scores, q_rot[h], ((0,), (0,))), cosine, -sine))
        v_grads.append(mm(p.astype(low), grad_h, ((0,), (0,))))
    q_grad, k_grad = (jnp.concatenate(q_grads, axis=1), jnp.concatenate(k_grads, axis=1))
    gain_query_grad = jnp.sum(q_grad * query * r_query, axis=0)
    gain_key_grad = jnp.sum(k_grad * key_proj * r_key, axis=0)
    q_grad, k_grad = (q_grad * g_query, k_grad * g_key)
    means = lax.psum(
        jnp.stack([jnp.sum(q_grad * query, axis=-1), jnp.sum(k_grad * key_proj, axis=-1)]), "seq"
    )
    means = means / width
    q_low = (r_query * q_grad - query * (r_query**3) * means[0][:, None]).astype(low)
    k_low = (r_key * k_grad - key_proj * (r_key**3) * means[1][:, None]).astype(low)
    v_low = jnp.concatenate(v_grads, axis=1).astype(low)
    qkv_low = jnp.concatenate([q_low, k_low, v_low], axis=1)
    normed_grad = mm(qkv_low, w_qkv, ((1,), (1,)))
    gain_attn_grad = jnp.sum(normed_grad * x_wide * r_attn, axis=0)
    normed_grad = lax.psum_scatter(
        normed_grad.astype(low), "seq", scatter_dimension=0, tiled=True
    ).astype(full)

    out_grad = jnp.einsum(
        "src,rn->scn", attended_row, own_cols(mid_row), preferred_element_type=full
    ).reshape(width, cols)
    proj_grad = jnp.concatenate([mm(normed, qkv_low, ((0,), (0,))), out_grad], axis=1).astype(low)
    proj_grad = lax.psum_scatter(proj_grad, "dp", scatter_dimension=0, tiled=True)
    proj_grad = lax.all_to_all(
        proj_grad.reshape(shards, block_rows, 4, cols), "seq", 0, 0, tiled=True
    )
    proj_grad = proj_grad.transpose(2, 1, 0, 3).reshape(4, block_rows, width).astype(full)

    x_own = hidden_in[0].astype(full)
    r_here = lax.rsqrt(jnp.mean(x_own * x_own, axis=-1, keepdims=True) + epsilon)
    scaled_grad = normed_grad * gains[0]
    grad_hidden = (
        grad_mid
        + r_here * scaled_grad
        - x_own * (r_here**3) * jnp.mean(scaled_grad * x_own, axis=-1, keepdims=True)
    )

    def place(values):
        return lax.dynamic_update_slice_in_dim(jnp.zeros((width,), full), values, first_col, 0)

    vectors = jnp.concatenate(
        [
            router_grad,
            gain_attn_grad[None],
            place(gain_query_grad)[None],
            place(gain_key_grad)[None],
            gain_ffn_grad[None],
        ]
    )
    count = vectors.shape[0]
    vectors = vectors.reshape(count, parts * shards, block_rows).transpose(1, 0, 2)
    vectors = lax.psum_scatter(
        vectors.reshape(parts * shards, count * block_rows), both, scatter_dimension=0, tiled=True
    ).reshape(count, block_rows)
    return (
        block_out[None],
        grad_hidden[None],
        proj_grad[0],
        proj_grad[1],
        proj_grad[2],
        proj_grad[3],
        vectors[expert_count],
        vectors[expert_count + 1],
        vectors[expert_count + 2],
        vectors[expert_count + 3],
        vectors[:expert_count].T,
        grad_w_gate,
        grad_w_up,
        grad_w_down,
    )


def solution(mesh):
    def layer(*arrays):
        whole_heads = (arrays[0].shape[2] // HEAD) % mesh.shape["seq"] == 0
        if whole_heads and mesh.shape["dp"] == 4:
            return on_device_heads(*arrays)
        return on_device(*arrays)

    return jax.shard_map(
        layer,
        mesh=mesh,
        in_specs=(
            P("dp", "seq", None),
            P("dp", None),
            P("dp", "seq", None),
            P(("dp", "seq"), None),
            P(("dp", "seq"), None),
            P(("dp", "seq"), None),
            P(("dp", "seq"), None),
            P(("dp", "seq")),
            P(("dp", "seq")),
            P(("dp", "seq")),
            P(("dp", "seq")),
            P(("dp", "seq"), None),
            P("seq", "dp", None),
            P("seq", "dp", None),
            P("seq", None, "dp"),
            P("dp", "seq", None),
        ),
        out_specs=(
            P("dp", "seq", None),
            P("dp", "seq", None),
            P(("dp", "seq"), None),
            P(("dp", "seq"), None),
            P(("dp", "seq"), None),
            P(("dp", "seq"), None),
            P(("dp", "seq")),
            P(("dp", "seq")),
            P(("dp", "seq")),
            P(("dp", "seq")),
            P(("dp", "seq"), None),
            P("seq", "dp", None),
            P("seq", "dp", None),
            P("seq", None, "dp"),
        ),
        check_vma=False,
    )
```

```python
import math

import jax
import jax.numpy as jnp
from jax import lax
from jax.experimental import pallas as pl
from jax.experimental.pallas import tpu as pltpu
from jax.sharding import PartitionSpec as P

HEAD = 128


epsilon = 1e-05
masked_score = -1e30
rope_base = 10000.0


def normalize(values, gain_vec):
    return (
        values * lax.rsqrt(jnp.mean(values * values, axis=-1, keepdims=True) + epsilon) * gain_vec
    )


def rotary(values, positions):
    half_dim = values.shape[-1] // 2
    frequency = jnp.exp(
        jnp.arange(half_dim, dtype=jnp.float32) * (-2.0 * math.log(rope_base) / values.shape[-1])
    )
    angles = positions.astype(jnp.float32)[:, None] * frequency[None, :]
    cosine = jnp.cos(angles)[:, None, :]
    sine_table = jnp.sin(angles)[:, None, :]
    first_half = values[..., :half_dim]
    second = values[..., half_dim:]
    return jnp.concatenate(
        [first_half * cosine - second * sine_table, second * cosine + first_half * sine_table],
        axis=-1,
    )


def softmax_rows(values):
    peak_value = jnp.max(values, axis=-1, keepdims=True)
    raised = jnp.exp(values - peak_value)
    return raised / jnp.sum(raised, axis=-1, keepdims=True)


def rotate_normed(projection, gain_vec, positions):
    tokens, model_width = projection.shape
    return rotary(
        normalize(projection, gain_vec).reshape(tokens, model_width // HEAD, HEAD), positions
    )


def masked_scores(queries, key_block, query_pos, query_seg, key_pos, key_seg, scaling):
    raw_scores = jnp.einsum("qhd,khd->hqk", queries, key_block, preferred_element_type=jnp.float32)
    allowed = (query_pos[:, None] >= key_pos[None, :]) & (query_seg[:, None] == key_seg[None, :])
    return jnp.where(allowed[None], raw_scores * scaling, masked_score)


def key_window(keys_all, values_all, row_seg, begin_at, span):
    key_block = lax.dynamic_slice_in_dim(keys_all, begin_at, span)
    value_block = lax.dynamic_slice_in_dim(values_all, begin_at, span)
    key_pos = begin_at + lax.iota(jnp.int32, span)
    key_seg = lax.dynamic_slice_in_dim(row_seg, begin_at, span)
    return (key_block, value_block, key_pos, key_seg)


def project_front(hidden, layer_full, positions):
    tokens, model_width = hidden.shape
    normed = normalize(hidden, layer_full[5].astype(jnp.float32)).astype(jnp.bfloat16)
    query = jnp.dot(normed, layer_full[0], preferred_element_type=jnp.float32)
    key_proj = jnp.dot(normed, layer_full[1], preferred_element_type=jnp.float32)
    value_proj = jnp.dot(normed, layer_full[2], preferred_element_type=jnp.float32)
    query_rot = rotate_normed(query, layer_full[6].astype(jnp.float32), positions).astype(
        jnp.bfloat16
    )
    key_rot = rotate_normed(key_proj, layer_full[7].astype(jnp.float32), positions).astype(
        jnp.bfloat16
    )
    value_in = value_proj.astype(jnp.bfloat16).reshape(tokens, model_width // HEAD, HEAD)
    return (normed, query, key_proj, query_rot, key_rot, value_in)


def attend_local(query_rot, keys_all, values_all, row_seg, offset, span):
    tokens, head_count, head_dim = query_rot.shape
    scaling = head_dim ** (-0.5)
    query_pos = offset + lax.iota(jnp.int32, tokens)
    query_seg = lax.dynamic_slice_in_dim(row_seg, offset, tokens)
    reach_blocks = (offset + tokens + span - 1) // span

    def block_scores(block_index):
        begin_at = block_index * span
        key_block, value_block, key_pos, key_seg = key_window(
            keys_all, values_all, row_seg, begin_at, span
        )
        return (
            masked_scores(query_rot, key_block, query_pos, query_seg, key_pos, key_seg, scaling),
            value_block,
        )

    def first_pass(block_index, state_pair):
        peak_value, denominator = state_pair
        scores, unused_values = block_scores(block_index)
        new_peak = jnp.maximum(peak_value, jnp.max(scores, axis=-1))
        denominator = denominator * jnp.exp(peak_value - new_peak) + jnp.sum(
            jnp.exp(scores - new_peak[..., None]), axis=-1
        )
        return (new_peak, denominator)

    start_state = (
        jnp.full((head_count, tokens), masked_score, jnp.float32),
        jnp.zeros((head_count, tokens), jnp.float32),
    )
    peak_value, denominator = lax.fori_loop(0, reach_blocks, first_pass, start_state)
    log_total = peak_value + jnp.log(denominator)

    def second_pass(block_index, running):
        scores, value_block = block_scores(block_index)
        weights = jnp.exp(scores - log_total[..., None]).astype(jnp.bfloat16)
        return running + jnp.einsum(
            "hqk,khd->qhd", weights, value_block, preferred_element_type=jnp.float32
        )

    attention = lax.fori_loop(
        0, reach_blocks, second_pass, jnp.zeros((tokens, head_count, head_dim), jnp.float32)
    )
    return (attention, log_total)


def query_grads(query_rot, keys_all, values_all, row_seg, offset, span, log_total, grad_attended):
    tokens, head_count, head_dim = query_rot.shape
    scaling = head_dim ** (-0.5)
    query_pos = offset + lax.iota(jnp.int32, tokens)
    query_seg = lax.dynamic_slice_in_dim(row_seg, offset, tokens)
    reach_blocks = (offset + tokens + span - 1) // span

    def block_terms(block_index):
        begin_at = block_index * span
        key_block, value_block, key_pos, key_seg = key_window(
            keys_all, values_all, row_seg, begin_at, span
        )
        scores = masked_scores(
            query_rot, key_block, query_pos, query_seg, key_pos, key_seg, scaling
        )
        weights = jnp.exp(scores - log_total[..., None])
        grad_weights = jnp.einsum(
            "qhd,khd->hqk", grad_attended, value_block, preferred_element_type=jnp.float32
        )
        return (key_block, weights, grad_weights)

    def delta_pass(block_index, running):
        unused_keys, weights, grad_weights = block_terms(block_index)
        return running + jnp.sum(weights * grad_weights, axis=-1)

    delta = lax.fori_loop(0, reach_blocks, delta_pass, jnp.zeros((head_count, tokens), jnp.float32))

    def query_pass(block_index, running):
        key_block, weights, grad_weights = block_terms(block_index)
        grad_scores = (weights * (grad_weights - delta[..., None]) * scaling).astype(jnp.bfloat16)
        return running + jnp.einsum(
            "hqk,khd->qhd", grad_scores, key_block, preferred_element_type=jnp.float32
        )

    grad_query_rot = lax.fori_loop(
        0, reach_blocks, query_pass, jnp.zeros((tokens, head_count, head_dim), jnp.float32)
    )
    return (delta, grad_query_rot)


def route_tokens(hidden_mid, layer_full, choice_rows):
    tokens, pick_count = choice_rows.shape
    normed_ffn = normalize(hidden_mid, layer_full[8].astype(jnp.float32)).astype(jnp.bfloat16)
    logits = jnp.dot(normed_ffn, layer_full[4], preferred_element_type=jnp.float32)
    expert_count = logits.shape[1]
    capacity = 3 * tokens * pick_count // (2 * expert_count)
    chances = softmax_rows(logits)
    picks = choice_rows[:, :, None] == lax.iota(jnp.int32, expert_count)[None, None, :]
    gate_values = jnp.sum(jnp.where(picks, chances[:, None, :], 0.0), axis=-1)
    flat_hits = picks.reshape(tokens * pick_count, expert_count).astype(jnp.int32)
    earlier = jnp.cumsum(flat_hits, axis=0) - flat_hits
    slot_ids = choice_rows.reshape(-1) * capacity + jnp.sum(earlier * flat_hits, axis=1)
    pair_table = lax.iota(jnp.int32, expert_count * capacity)[:, None] == slot_ids[None, :]
    spread = jnp.sum(
        pair_table.reshape(expert_count * capacity, tokens, pick_count).astype(jnp.int32), axis=2
    ).astype(jnp.bfloat16)
    send_rows = jnp.dot(spread, normed_ffn, preferred_element_type=jnp.float32).astype(jnp.bfloat16)
    send_rows = send_rows.reshape(expert_count, capacity, hidden_mid.shape[1])
    return (normed_ffn, chances, picks, gate_values, slot_ids, pair_table, spread, send_rows)


def group_rows(row_block, held_experts):
    sources = row_block.shape[0] // held_experts
    grouped = row_block.reshape(
        sources, held_experts, row_block.shape[1], row_block.shape[2]
    ).transpose(1, 0, 2, 3)
    return grouped.reshape(held_experts, sources * row_block.shape[1], row_block.shape[2])


def ungroup_rows(grouped, whole_shape):
    held_experts = grouped.shape[0]
    sources = whole_shape[0] // held_experts
    spread_out = grouped.reshape(held_experts, sources, whole_shape[1], whole_shape[2]).transpose(
        1, 0, 2, 3
    )
    return spread_out.reshape(whole_shape)


def expert_forward(row_block, gate_full, up_full, down_full):
    inputs = group_rows(row_block, gate_full.shape[0])
    gate_pre = jnp.einsum("erd,edf->erf", inputs, gate_full, preferred_element_type=jnp.float32)
    up_pre = jnp.einsum("erd,edf->erf", inputs, up_full, preferred_element_type=jnp.float32)
    activated = (gate_pre * lax.logistic(gate_pre) * up_pre).astype(jnp.bfloat16)
    result = jnp.einsum(
        "erf,efd->erd", activated, down_full, preferred_element_type=jnp.float32
    ).astype(jnp.bfloat16)
    return ungroup_rows(result, row_block.shape)


def expert_backward(row_block, grad_block, gate_full, up_full, down_full):
    inputs = group_rows(row_block, gate_full.shape[0])
    grad_outputs = group_rows(grad_block, gate_full.shape[0])
    gate_pre = jnp.einsum("erd,edf->erf", inputs, gate_full, preferred_element_type=jnp.float32)
    up_pre = jnp.einsum("erd,edf->erf", inputs, up_full, preferred_element_type=jnp.float32)
    sigmoid_gate = lax.logistic(gate_pre)
    activated = (gate_pre * sigmoid_gate * up_pre).astype(jnp.bfloat16)
    grad_act = jnp.einsum(
        "erd,efd->erf", grad_outputs, down_full, preferred_element_type=jnp.float32
    )
    grad_down = jnp.einsum(
        "erf,erd->efd", activated, grad_outputs, preferred_element_type=jnp.float32
    )
    grad_gate_pre = (
        grad_act * up_pre * sigmoid_gate * (1.0 + gate_pre * (1.0 - sigmoid_gate))
    ).astype(jnp.bfloat16)
    grad_up_pre = (grad_act * gate_pre * sigmoid_gate).astype(jnp.bfloat16)
    grad_gate_w = jnp.einsum(
        "erd,erf->edf", inputs, grad_gate_pre, preferred_element_type=jnp.float32
    )
    grad_up_w = jnp.einsum("erd,erf->edf", inputs, grad_up_pre, preferred_element_type=jnp.float32)
    grad_inputs = jnp.einsum(
        "erf,edf->erd", grad_gate_pre, gate_full, preferred_element_type=jnp.float32
    )
    grad_inputs = grad_inputs + jnp.einsum(
        "erf,edf->erd", grad_up_pre, up_full, preferred_element_type=jnp.float32
    )
    return (
        ungroup_rows(grad_inputs.astype(jnp.bfloat16), row_block.shape),
        grad_gate_w,
        grad_up_w,
        grad_down,
    )


def contract_rows(left, right):
    return lax.dot_general(
        left, right, (((0,), (0,)), ((), ())), preferred_element_type=jnp.float32
    )


def contract_cols(left, right):
    return lax.dot_general(
        left, right, (((1,), (1,)), ((), ())), preferred_element_type=jnp.float32
    )


def on_device(
    hidden_in,
    segment_ids,
    routes,
    w_query,
    w_key,
    w_value,
    w_out,
    gain_attn,
    gain_query,
    gain_key,
    gain_ffn,
    w_router,
    w_gate,
    w_up,
    w_down,
    cotangent,
):
    hidden = hidden_in[0].astype(jnp.float32)
    tokens, model_width = hidden.shape
    head_count = model_width // HEAD
    row_seg = segment_ids[0]
    choice_rows = routes[0]
    offset = lax.axis_index("seq") * tokens
    positions = offset + lax.iota(jnp.int32, tokens)
    span = min(512, row_seg.shape[0])
    layer_full = (
        lax.all_gather(w_query, ("dp", "seq"), axis=0, tiled=True),
        lax.all_gather(w_key, ("dp", "seq"), axis=0, tiled=True),
        lax.all_gather(w_value, ("dp", "seq"), axis=0, tiled=True),
        lax.all_gather(w_out, ("dp", "seq"), axis=0, tiled=True),
        lax.all_gather(w_router, ("dp", "seq"), axis=0, tiled=True),
        lax.all_gather(gain_attn, ("dp", "seq"), axis=0, tiled=True),
        lax.all_gather(gain_query, ("dp", "seq"), axis=0, tiled=True),
        lax.all_gather(gain_key, ("dp", "seq"), axis=0, tiled=True),
        lax.all_gather(gain_ffn, ("dp", "seq"), axis=0, tiled=True),
    )
    expert_full = (
        lax.all_gather(w_gate, "dp", axis=1, tiled=True),
        lax.all_gather(w_up, "dp", axis=1, tiled=True),
        lax.all_gather(w_down, "dp", axis=2, tiled=True),
    )
    projected = project_front(hidden, layer_full, positions)
    keys_all, values_all = (
        lax.all_gather(projected[4], "seq", axis=0, tiled=True),
        lax.all_gather(projected[5], "seq", axis=0, tiled=True),
    )
    attention, log_total = attend_local(projected[3], keys_all, values_all, row_seg, offset, span)
    attended = attention.reshape(tokens, model_width).astype(jnp.bfloat16)
    hidden_mid = hidden + jnp.dot(attended, layer_full[3], preferred_element_type=jnp.float32)
    routing = route_tokens(hidden_mid, layer_full, choice_rows)
    expert_count, capacity = (routing[7].shape[0], routing[7].shape[1])
    expert_out = expert_forward(
        lax.all_to_all(routing[7], "seq", split_axis=0, concat_axis=0, tiled=True),
        expert_full[0],
        expert_full[1],
        expert_full[2],
    )
    returned = lax.all_to_all(expert_out, "seq", split_axis=0, concat_axis=0, tiled=True)
    picked = jnp.take(returned.reshape(expert_count * capacity, model_width), routing[4], axis=0)
    picked = picked.reshape(tokens, choice_rows.shape[1], model_width)
    mixture = jnp.sum(routing[3][:, :, None] * picked.astype(jnp.float32), axis=1)
    block_out = (hidden_mid + mixture).astype(jnp.bfloat16)
    layer_full = (
        lax.all_gather(w_query, ("dp", "seq"), axis=0, tiled=True),
        lax.all_gather(w_key, ("dp", "seq"), axis=0, tiled=True),
        lax.all_gather(w_value, ("dp", "seq"), axis=0, tiled=True),
        lax.all_gather(w_out, ("dp", "seq"), axis=0, tiled=True),
        lax.all_gather(w_router, ("dp", "seq"), axis=0, tiled=True),
        lax.all_gather(gain_attn, ("dp", "seq"), axis=0, tiled=True),
        lax.all_gather(gain_query, ("dp", "seq"), axis=0, tiled=True),
        lax.all_gather(gain_key, ("dp", "seq"), axis=0, tiled=True),
        lax.all_gather(gain_ffn, ("dp", "seq"), axis=0, tiled=True),
    )
    expert_full = (
        lax.all_gather(w_gate, "dp", axis=1, tiled=True),
        lax.all_gather(w_up, "dp", axis=1, tiled=True),
        lax.all_gather(w_down, "dp", axis=2, tiled=True),
    )
    projected = project_front(hidden, layer_full, positions)
    keys_all, values_all = (
        lax.all_gather(projected[4], "seq", axis=0, tiled=True),
        lax.all_gather(projected[5], "seq", axis=0, tiled=True),
    )
    attention, log_total = attend_local(projected[3], keys_all, values_all, row_seg, offset, span)
    attended = attention.reshape(tokens, model_width).astype(jnp.bfloat16)
    hidden_mid = hidden + jnp.dot(attended, layer_full[3], preferred_element_type=jnp.float32)
    routing = route_tokens(hidden_mid, layer_full, choice_rows)
    normed_ffn, chances, picks, gate_values, slot_ids, pair_table, spread, send_rows = routing
    grad_out = cotangent[0].astype(jnp.float32)
    grad_gates = jnp.sum(grad_out[:, None, :] * picked.astype(jnp.float32), axis=-1)
    slot_gates = jnp.sum(jnp.where(pair_table, gate_values.reshape(-1)[None, :], 0.0), axis=1)
    grad_rows_in = jnp.dot(spread, cotangent[0], preferred_element_type=jnp.float32)
    grad_slots = (
        (slot_gates[:, None] * grad_rows_in)
        .astype(jnp.bfloat16)
        .reshape(expert_count, capacity, model_width)
    )
    arrived_rows, arrived_grads = (
        lax.all_to_all(send_rows, "seq", split_axis=0, concat_axis=0, tiled=True),
        lax.all_to_all(grad_slots, "seq", split_axis=0, concat_axis=0, tiled=True),
    )
    grad_inputs, grad_gate_w, grad_up_w, grad_down_w = expert_backward(
        arrived_rows, arrived_grads, expert_full[0], expert_full[1], expert_full[2]
    )
    grad_back = lax.all_to_all(grad_inputs, "seq", split_axis=0, concat_axis=0, tiled=True)
    grad_normed_ffn = contract_rows(spread, grad_back.reshape(expert_count * capacity, model_width))
    grad_chances = jnp.sum(jnp.where(picks, grad_gates[:, :, None], 0.0), axis=1)
    grad_logits = (
        chances * (grad_chances - jnp.sum(chances * grad_chances, axis=-1, keepdims=True))
    ).astype(jnp.bfloat16)
    grad_router_w = contract_rows(normed_ffn, grad_logits)
    grad_normed_ffn = grad_normed_ffn + contract_cols(grad_logits, layer_full[4])
    unused_ffn, pull_ffn = jax.vjp(normalize, hidden_mid, layer_full[8].astype(jnp.float32))
    grad_mid_norm, grad_gain_ffn_w = pull_ffn(grad_normed_ffn)
    grad_mid = grad_out + grad_mid_norm
    grad_mid_low = grad_mid.astype(jnp.bfloat16)
    grad_w_out = contract_rows(attended, grad_mid_low)
    grad_attended = (
        contract_cols(grad_mid_low, layer_full[3])
        .astype(jnp.bfloat16)
        .reshape(tokens, head_count, HEAD)
    )
    query_rot = projected[3]
    delta, grad_query_rot = query_grads(
        query_rot, keys_all, values_all, row_seg, offset, span, log_total, grad_attended
    )
    scaling = HEAD ** (-0.5)
    query_seg = lax.dynamic_slice_in_dim(row_seg, offset, tokens)
    row_count = lax.axis_size("seq") * tokens
    step_rows = math.gcd(row_count, 512)

    def one_window(window_index, running):
        window_start = window_index * step_rows
        key_block, value_block, key_pos, key_seg = key_window(
            keys_all, values_all, row_seg, window_start, step_rows
        )
        scores = masked_scores(
            query_rot, key_block, positions, query_seg, key_pos, key_seg, scaling
        )
        weights = jnp.exp(scores - log_total[..., None])
        grad_weights = jnp.einsum(
            "qhd,khd->hqk", grad_attended, value_block, preferred_element_type=jnp.float32
        )
        grad_scores = (weights * (grad_weights - delta[..., None]) * scaling).astype(jnp.bfloat16)
        grad_key_part = jnp.einsum(
            "hqk,qhd->khd", grad_scores, query_rot, preferred_element_type=jnp.float32
        )
        grad_value_part = jnp.einsum(
            "hqk,qhd->khd",
            weights.astype(jnp.bfloat16),
            grad_attended,
            preferred_element_type=jnp.float32,
        )
        term = jnp.concatenate(
            [
                grad_key_part.reshape(step_rows, model_width),
                grad_value_part.reshape(step_rows, model_width),
            ],
            axis=1,
        )
        return lax.dynamic_update_slice_in_dim(running, term, window_index * step_rows, 0)

    key_sums = lax.psum_scatter(
        lax.fori_loop(
            0,
            row_count // step_rows,
            one_window,
            jnp.zeros((row_count, 2 * model_width), jnp.float32),
        ).astype(jnp.bfloat16),
        "seq",
        scatter_dimension=0,
        tiled=True,
    ).astype(jnp.float32)
    grad_key_rot = key_sums[:, :model_width].reshape(tokens, head_count, HEAD)
    grad_v_low = key_sums[:, model_width:].astype(jnp.bfloat16)

    def query_chain(projection, gain_vec):
        return rotate_normed(projection, gain_vec, positions)

    unused_query, pull_query = jax.vjp(query_chain, projected[1], layer_full[6].astype(jnp.float32))
    grad_query_pre, grad_gain_query_w = pull_query(grad_query_rot)
    unused_key, pull_key = jax.vjp(query_chain, projected[2], layer_full[7].astype(jnp.float32))
    grad_key_pre, grad_gain_key_w = pull_key(grad_key_rot)
    grad_q_low = grad_query_pre.astype(jnp.bfloat16)
    grad_k_low = grad_key_pre.astype(jnp.bfloat16)
    normed = projected[0]
    grad_w_query = contract_rows(normed, grad_q_low)
    grad_w_key = contract_rows(normed, grad_k_low)
    grad_w_value = contract_rows(normed, grad_v_low)
    grad_normed = (
        contract_cols(grad_q_low, layer_full[0])
        + contract_cols(grad_k_low, layer_full[1])
        + contract_cols(grad_v_low, layer_full[2])
    )
    unused_attn, pull_attn = jax.vjp(normalize, hidden, layer_full[5].astype(jnp.float32))
    grad_hidden_norm, grad_gain_attn_w = pull_attn(grad_normed)
    grad_hidden = grad_mid + grad_hidden_norm
    shares = (
        lax.psum_scatter(grad_w_query, ("dp", "seq"), scatter_dimension=0, tiled=True),
        lax.psum_scatter(grad_w_key, ("dp", "seq"), scatter_dimension=0, tiled=True),
        lax.psum_scatter(grad_w_value, ("dp", "seq"), scatter_dimension=0, tiled=True),
        lax.psum_scatter(grad_w_out, ("dp", "seq"), scatter_dimension=0, tiled=True),
        lax.psum_scatter(grad_router_w, ("dp", "seq"), scatter_dimension=0, tiled=True),
        lax.psum_scatter(grad_gain_attn_w, ("dp", "seq"), scatter_dimension=0, tiled=True),
        lax.psum_scatter(grad_gain_query_w, ("dp", "seq"), scatter_dimension=0, tiled=True),
        lax.psum_scatter(grad_gain_key_w, ("dp", "seq"), scatter_dimension=0, tiled=True),
        lax.psum_scatter(grad_gain_ffn_w, ("dp", "seq"), scatter_dimension=0, tiled=True),
    )
    expert_shares = (
        lax.psum_scatter(
            grad_gate_w.astype(jnp.bfloat16), "dp", scatter_dimension=1, tiled=True
        ).astype(jnp.float32),
        lax.psum_scatter(
            grad_up_w.astype(jnp.bfloat16), "dp", scatter_dimension=1, tiled=True
        ).astype(jnp.float32),
        lax.psum_scatter(
            grad_down_w.astype(jnp.bfloat16), "dp", scatter_dimension=2, tiled=True
        ).astype(jnp.float32),
    )
    return (
        block_out[None],
        grad_hidden[None],
        shares[0],
        shares[1],
        shares[2],
        shares[3],
        shares[5],
        shares[6],
        shares[7],
        shares[8],
        shares[4],
        expert_shares[0],
        expert_shares[1],
        expert_shares[2],
    )


VMEM_GRANT = 56 * 1024 * 1024


def mm(left, right, dims):
    return lax.dot_general(left, right, (dims, ((), ())), preferred_element_type=jnp.float32)


def cost(flops, transcendentals, *arrays):
    moved = sum(math.prod(a.shape) * a.dtype.itemsize for a in arrays)
    return pl.CostEstimate(flops=flops, transcendentals=transcendentals, bytes_accessed=moved)


def grid_call(body, grid, in_specs, out_specs, outs, flops, transcendentals, *args):
    return pl.pallas_call(
        body,
        grid=grid,
        in_specs=in_specs,
        out_specs=out_specs,
        out_shape=outs,
        compiler_params=pltpu.CompilerParams(vmem_limit_bytes=VMEM_GRANT),
        cost_estimate=cost(flops, transcendentals, *args, *jax.tree.leaves(outs)),
    )(*args)


def row_tiles(rows):
    return math.gcd(rows, 512)


def finish_attention(order, attended, out_pieces, x_row, gain, router, chosen, own, expert_count):
    shards, rows, cols = attended.shape
    width = x_row.shape[1]
    held = own.shape[0]
    chunk = width // 4
    per_chunk = chunk // cols
    tm = math.gcd(rows, 256)

    def body(order_ref, att_ref, p0, p1, p2, p3, x_ref, gain_ref, router_ref, chosen_ref, own_ref, *outs):
        mid_ref, normed_ref, r_ref, chance_ref, gate_ref, att_all = outs
        for h in range(shards):
            source = order_ref[h // per_chunk] * per_chunk + h % per_chunk
            att_all[:, h * cols : (h + 1) * cols] = att_ref[source]
        squares = jnp.zeros((tm, 1), jnp.float32)
        for n in range(4):
            at = slice(n * chunk, (n + 1) * chunk)
            total = x_ref[:, at].astype(jnp.float32)
            for j, piece in enumerate((p0, p1, p2, p3)):
                k = n ^ j
                total = total + mm(
                    att_all[:, j * chunk : (j + 1) * chunk],
                    piece[:, k * chunk : (k + 1) * chunk],
                    ((1,), (0,)),
                )
            mid_ref[:, at] = total
            squares = squares + jnp.sum(total * total, axis=-1, keepdims=True)
        r = lax.rsqrt(squares / width + epsilon)
        r_ref[...] = r
        logits = jnp.zeros((tm, 128), jnp.float32)
        for n in range(4):
            at = slice(n * chunk, (n + 1) * chunk)
            normed = (mid_ref[:, at] * r * gain_ref[:, at]).astype(jnp.bfloat16)
            normed_ref[:, at] = normed
            logits = logits + mm(normed, router_ref[at, :], ((1,), (0,)))
        lane = lax.broadcasted_iota(jnp.int32, (tm, 128), 1)
        logits = jnp.where(lane < expert_count, logits, masked_score)
        raised = jnp.exp(logits - jnp.max(logits, axis=-1, keepdims=True))
        chances = raised / jnp.sum(raised, axis=-1, keepdims=True)
        chance_ref[...] = chances
        taken = chances * chosen_ref[...]
        for e in range(held):
            gate_ref[e] = jnp.sum(taken * own_ref[e : e + 1, :], axis=-1, keepdims=True)

    full = jnp.float32
    piece_spec = pl.BlockSpec((chunk, width), lambda i, o: (0, 0))
    wide = pl.BlockSpec((tm, width), lambda i, o: (i, 0))
    lanes = pl.BlockSpec((tm, 128), lambda i, o: (i, 0))
    outs = [
        jax.ShapeDtypeStruct((rows, width), full),
        jax.ShapeDtypeStruct((rows, width), jnp.bfloat16),
        jax.ShapeDtypeStruct((rows, 1), full),
        jax.ShapeDtypeStruct((rows, 128), full),
        jax.ShapeDtypeStruct((held, rows, 1), full),
    ]
    return pl.pallas_call(
        body,
        grid_spec=pltpu.PrefetchScalarGridSpec(
            num_scalar_prefetch=1,
            grid=(rows // tm,),
            in_specs=[
                pl.BlockSpec((shards, tm, cols), lambda i, o: (0, i, 0)),
                piece_spec,
                piece_spec,
                piece_spec,
                piece_spec,
                wide,
                pl.BlockSpec((1, width), lambda i, o: (0, 0)),
                pl.BlockSpec((width, 128), lambda i, o: (0, 0)),
                lanes,
                pl.BlockSpec((held, 128), lambda i, o: (0, 0)),
            ],
            out_specs=[
                wide,
                wide,
                pl.BlockSpec((tm, 1), lambda i, o: (i, 0)),
                lanes,
                pl.BlockSpec((held, tm, 1), lambda i, o: (0, i, 0)),
            ],
            scratch_shapes=[pltpu.VMEM((tm, width), jnp.bfloat16)],
        ),
        out_shape=outs,
        compiler_params=pltpu.CompilerParams(vmem_limit_bytes=VMEM_GRANT),
        cost_estimate=cost(2 * rows * width * width, rows * 128, attended, *out_pieces, *outs),
    )(order, attended, *out_pieces, x_row, gain, router, chosen, own)


def expert_activations(normed, gate, up):
    held, width, ff = gate.shape
    rows = normed.shape[0]
    tile, tm = (math.gcd(ff, 512), row_tiles(rows))

    def body(x_ref, gate_ref, up_ref, act_ref, dgate_ref, dup_ref):
        @pl.loop(0, rows // tm)
        def _(i):
            at = pl.ds(pl.multiple_of(i * tm, tm), tm)
            gate_pre = mm(x_ref[at, :], gate_ref[0], ((1,), (0,)))
            up_pre = mm(x_ref[at, :], up_ref[0], ((1,), (0,)))
            sig = lax.logistic(gate_pre)
            silu = gate_pre * sig
            act_ref[0, at, :] = (silu * up_pre).astype(jnp.bfloat16)
            dgate_ref[0, at, :] = (up_pre * (sig + silu * (1.0 - sig))).astype(jnp.bfloat16)
            dup_ref[0, at, :] = silu.astype(jnp.bfloat16)

    tiled = pl.BlockSpec((1, rows, tile), lambda e, f: (e, 0, f))
    low = jax.ShapeDtypeStruct((held, rows, ff), jnp.bfloat16)
    return grid_call(
        body,
        (held, ff // tile),
        [
            pl.BlockSpec((rows, width), lambda e, f: (0, 0)),
            pl.BlockSpec((1, width, tile), lambda e, f: (e, 0, f)),
            pl.BlockSpec((1, width, tile), lambda e, f: (e, 0, f)),
        ],
        [tiled, tiled, tiled],
        [low, low, low],
        4 * held * rows * ff * width,
        held * rows * ff,
        normed,
        gate,
        up,
    )


def expert_gradients(dy, down, act, dgate_factor, dup_factor, weight):
    held, ff, width = down.shape
    rows = dy.shape[0]
    tile, tm = (math.gcd(ff, 512), row_tiles(rows))

    def body(dy_ref, down_ref, act_ref, a_ref, b_ref, weight_ref, out_ref, dgate_ref, dup_ref, sum_ref):
        first = pl.program_id(1) == 0

        @pl.loop(0, rows // tm)
        def _(i):
            at = pl.ds(pl.multiple_of(i * tm, tm), tm)
            grad = mm(dy_ref[at, :], down_ref[0], ((1,), (1,)))
            scale = weight_ref[0, at, :]
            act = act_ref[0, at, :].astype(jnp.float32)
            product = act * grad
            partial = product[:, :128]
            for j in range(1, tile // 128):
                partial = partial + product[:, j * 128 : (j + 1) * 128]

            @pl.when(first)
            def _():
                sum_ref[0, at, :] = partial

            @pl.when(jnp.logical_not(first))
            def _():
                sum_ref[0, at, :] = sum_ref[0, at, :] + partial

            out_ref[0, at, :] = (scale * act).astype(jnp.bfloat16)
            grad = scale * grad
            dgate_ref[0, at, :] = (grad * a_ref[0, at, :].astype(jnp.float32)).astype(jnp.bfloat16)
            dup_ref[0, at, :] = (grad * b_ref[0, at, :].astype(jnp.float32)).astype(jnp.bfloat16)

    tiled = pl.BlockSpec((1, rows, tile), lambda e, f: (e, 0, f))
    low = jax.ShapeDtypeStruct((held, rows, ff), jnp.bfloat16)
    return grid_call(
        body,
        (held, ff // tile),
        [
            pl.BlockSpec((rows, width), lambda e, f: (0, 0)),
            pl.BlockSpec((1, tile, width), lambda e, f: (e, f, 0)),
            tiled,
            tiled,
            tiled,
            pl.BlockSpec((1, rows, 1), lambda e, f: (e, 0, 0)),
        ],
        [tiled, tiled, tiled, pl.BlockSpec((1, rows, 128), lambda e, f: (e, 0, 0))],
        [low, low, low, jax.ShapeDtypeStruct((held, rows, 128), jnp.float32)],
        2 * held * rows * ff * width,
        0,
        dy,
        down,
        act,
        dgate_factor,
        dup_factor,
        weight,
    )


def input_gradient(dgate, dup, gate, up, gate_sums, chances, chosen, own, router):
    held, width, ff = gate.shape
    rows = dgate.shape[1]
    tile, tm = (math.gcd(width, 512), row_tiles(rows))

    def body(dgate_ref, dup_ref, gate_ref, up_ref, sum_ref, chance_ref, chosen_ref, own_ref, router_ref, out_ref, logits_ref):
        @pl.loop(0, rows // tm)
        def _(i):
            at = pl.ds(pl.multiple_of(i * tm, tm), tm)
            chances = chance_ref[at, :]
            placed = jnp.zeros((tm, 128), jnp.float32)
            for e in range(held):
                got = jnp.sum(sum_ref[e, at, :], axis=-1, keepdims=True)
                placed = placed + own_ref[e : e + 1, :] * got
            placed = placed * chosen_ref[at, :]
            inner = jnp.sum(chances * placed, axis=-1, keepdims=True)
            logits = (chances * (placed - inner)).astype(jnp.bfloat16)
            logits_ref[at, :] = logits
            total = mm(logits, router_ref[...], ((1,), (1,)))
            for e in range(held):
                total = total + mm(dgate_ref[e, at, :], gate_ref[e], ((1,), (1,)))
                total = total + mm(dup_ref[e, at, :], up_ref[e], ((1,), (1,)))
            out_ref[at, :] = total.astype(jnp.bfloat16)

    whole = pl.BlockSpec((held, rows, ff), lambda n: (0, 0, 0))
    weights = pl.BlockSpec((held, tile, ff), lambda n: (0, n, 0))
    lanes = pl.BlockSpec((rows, 128), lambda n: (0, 0))
    return grid_call(
        body,
        (width // tile,),
        [
            whole,
            whole,
            weights,
            weights,
            pl.BlockSpec((held, rows, 128), lambda n: (0, 0, 0)),
            lanes,
            lanes,
            pl.BlockSpec((held, 128), lambda n: (0, 0)),
            pl.BlockSpec((tile, 128), lambda n: (n, 0)),
        ],
        [pl.BlockSpec((rows, tile), lambda n: (0, n)), lanes],
        [jax.ShapeDtypeStruct((rows, width), jnp.bfloat16), jax.ShapeDtypeStruct((rows, 128), jnp.bfloat16)],
        4 * held * rows * ff * width,
        0,
        dgate,
        dup,
        gate,
        up,
        gate_sums,
        chances,
        chosen,
        own,
        router,
    )


def combine_experts(act, down, weight):
    held, ff, width = down.shape
    rows = act.shape[1]
    tile, tm = (math.gcd(width, 512), row_tiles(rows))

    def body(act_ref, down_ref, weight_ref, out_ref):
        @pl.loop(0, rows // tm)
        def _(i):
            at = pl.ds(pl.multiple_of(i * tm, tm), tm)
            total = weight_ref[0, at, :] * mm(act_ref[0, at, :], down_ref[0], ((1,), (0,)))
            for e in range(1, held):
                term = mm(act_ref[e, at, :], down_ref[e], ((1,), (0,)))
                total = total + weight_ref[e, at, :] * term
            out_ref[at, :] = total.astype(jnp.bfloat16)

    return grid_call(
        body,
        (width // tile,),
        [
            pl.BlockSpec((held, rows, ff), lambda n: (0, 0, 0)),
            pl.BlockSpec((held, ff, tile), lambda n: (0, 0, n)),
            pl.BlockSpec((held, rows, 1), lambda n: (0, 0, 0)),
        ],
        pl.BlockSpec((rows, tile), lambda n: (0, n)),
        jax.ShapeDtypeStruct((rows, width), jnp.bfloat16),
        2 * held * rows * ff * width,
        0,
        act,
        down,
        weight,
    )


def weight_pieces(left, right, parts, split_left):
    flat, stacked = (left, right) if split_left else (right, left)
    held, rows, ff = stacked.shape
    piece = flat.shape[1] // parts
    shape = (held, piece, ff) if split_left else (held, ff, piece)
    tm = math.gcd(shape[1], 512)

    def body(flat_ref, stacked_ref, *outs):
        step = pl.program_id(0)
        for j in range(parts):

            @pl.when(step == j)
            def _(j=j):
                @pl.loop(0, shape[1] // tm)
                def _(i):
                    at = pl.ds(pl.multiple_of(i * tm, tm), tm)
                    if split_left:
                        value = mm(flat_ref[:, at], stacked_ref[0], ((0,), (0,)))
                    else:
                        value = mm(stacked_ref[0, :, at], flat_ref[...], ((0,), (0,)))
                    outs[j][0, at, :] = value.astype(jnp.bfloat16)

    def place(j):
        return lambda k, e: (jnp.where(k < j, 0, jnp.where(k > j, held - 1, e)), 0, 0)

    return grid_call(
        body,
        (parts, held),
        [
            pl.BlockSpec((rows, piece), lambda k, e: (0, k)),
            pl.BlockSpec((1, rows, ff), lambda k, e: (e, 0, 0)),
        ],
        [pl.BlockSpec((1,) + shape[1:], place(j)) for j in range(parts)],
        [jax.ShapeDtypeStruct(shape, jnp.bfloat16)] * parts,
        2 * held * rows * ff * flat.shape[1],
        0,
        flat,
        stacked,
    )


def rope_tables(row_count, head_dim):
    half_dim = head_dim // 2
    frequency = jnp.exp(
        jnp.arange(half_dim, dtype=jnp.float32) * (-2.0 * math.log(rope_base) / head_dim)
    )
    angles = jnp.arange(row_count, dtype=jnp.float32)[:, None] * frequency[None, :]
    return (jnp.cos(angles), jnp.sin(angles))


def rotate(values, cosine, sine):
    half_dim = values.shape[-1] // 2
    first, second = (values[:, :half_dim], values[:, half_dim:])
    return jnp.concatenate(
        [first * cosine - second * sine, second * cosine + first * sine], axis=-1
    )


def swap(values, bits):
    return lax.ppermute(values, "dp", [(i, i ^ bits) for i in range(4)])


def sum_in_chip(pieces, sent):
    wide = jnp.float32
    kept = pieces[0].astype(wide) + swap(pieces[1], 1).astype(wide)
    return (kept.astype(sent), (pieces[2].astype(wide) + swap(pieces[3], 1).astype(wide)).astype(sent))


def sum_pieces(pieces, sent):
    kept, passed = sum_in_chip(pieces, sent)
    return kept.astype(jnp.float32) + swap(passed, 2).astype(jnp.float32)


def reorder(values, dp_index, axis):
    size = values.shape[axis] // 4
    return jnp.concatenate(
        [
            lax.dynamic_slice_in_dim(values, (dp_index ^ k) * size, size, axis=axis)
            for k in range(4)
        ],
        axis=axis,
    )


def sum_over_seq(values, shards):
    spread = jnp.broadcast_to(values[None], (shards,) + values.shape)
    return jnp.sum(lax.all_to_all(spread, "seq", 0, 0, tiled=True), axis=0)


def on_device_heads(
    hidden_in,
    segment_ids,
    routes,
    w_query,
    w_key,
    w_value,
    w_out,
    gain_attn,
    gain_query,
    gain_key,
    gain_ffn,
    w_router,
    w_gate,
    w_up,
    w_down,
    cotangent,
):
    low, full = (jnp.bfloat16, jnp.float32)
    shards = lax.axis_size("seq")
    seq_index, dp_index = (lax.axis_index("seq"), lax.axis_index("dp"))
    tokens, width = hidden_in.shape[1:]
    rows = shards * tokens
    cols = width // shards
    heads = cols // HEAD
    held = w_gate.shape[0]
    expert_count = held * shards
    block_rows = w_query.shape[0]
    chunk = shards * block_rows
    row_seg = segment_ids[0]
    first_row = seq_index * tokens
    barrier = lax.optimization_barrier

    def own_cols(values, count):
        return lax.dynamic_slice_in_dim(values, seq_index * count, count, axis=values.ndim - 1)

    x_shard = reorder(hidden_in[0], dp_index, 1)
    x_row = lax.all_gather(x_shard, "seq", axis=0, tiled=True)
    blocks = jnp.stack(
        [w.reshape(block_rows, shards, cols).transpose(1, 0, 2) for w in (w_query, w_key, w_value)],
        axis=1,
    )
    blocks = blocks.reshape(shards, 3 * block_rows, cols)
    place_at = (dp_index * shards + seq_index) * block_rows
    gain_rows = lax.dynamic_update_slice(
        jnp.zeros((shards, 16, cols), low),
        jnp.stack([gain_query, gain_key])[None],
        (place_at // cols, 0, place_at % cols),
    )
    gain_rows = lax.dynamic_update_slice(
        gain_rows, jnp.broadcast_to(gain_attn[None, None], (shards, 1, block_rows)), (0, 2, 0)
    )
    blocks = lax.all_to_all(jnp.concatenate([blocks, gain_rows], axis=1), "seq", 0, 0, tiled=True)
    across = swap(blocks, 2)
    qkv_pieces = (blocks, swap(blocks, 1), across, swap(across, 1))
    gate_across = swap(w_gate, 2)
    x_row, qkv_pieces, gate_across = barrier((x_row, qkv_pieces, gate_across))

    w_qkv = jnp.concatenate(
        [
            p[:, : 3 * block_rows]
            .reshape(shards, 3, block_rows, cols)
            .transpose(0, 2, 1, 3)
            .reshape(chunk, 3 * cols)
            for p in qkv_pieces
        ],
        axis=0,
    )
    gain_pair = sum(
        jnp.sum(p[:, 3 * block_rows : 3 * block_rows + 2].astype(full), axis=0) for p in qkv_pieces
    )
    g_query, g_key = (gain_pair[0], gain_pair[1])
    g_attn = jnp.concatenate(
        [p[:, 3 * block_rows + 2, :block_rows].reshape(1, chunk) for p in qkv_pieces], axis=1
    ).astype(full)

    picks = routes.shape[2]
    packed = tokens // block_rows
    extra = jnp.concatenate(
        [routes[0].astype(low).reshape(block_rows, packed * picks), w_router, gain_ffn[:, None]],
        axis=1,
    )
    extra = jnp.pad(extra, ((0, 0), (0, 128 - extra.shape[1])))
    out_own = lax.all_gather(
        jnp.concatenate([reorder(w_out, dp_index, 1), extra], axis=1), "seq", axis=0, tiled=True
    )
    up_across = swap(w_up, 2)

    x_wide = x_row.astype(full)
    r_attn = lax.rsqrt(jnp.mean(x_wide * x_wide, axis=-1, keepdims=True) + epsilon)
    normed = (x_wide * r_attn * g_attn).astype(low)
    qkv = mm(normed, w_qkv, ((1,), (0,)))
    query, key_proj = (qkv[:, :cols], qkv[:, cols : 2 * cols])
    value_in = qkv[:, 2 * cols :].astype(low)
    sums = sum_over_seq(
        jnp.stack([jnp.sum(query * query, axis=-1), jnp.sum(key_proj * key_proj, axis=-1)]), shards
    )
    r_query, r_key = (lax.rsqrt(sums[i] / width + epsilon)[:, None] for i in range(2))
    cosine, sine = rope_tables(rows, HEAD)
    q_normed, k_normed = (query * r_query * g_query, key_proj * r_key * g_key)
    position = lax.iota(jnp.int32, rows)
    allowed = (position[:, None] >= position[None, :]) & (row_seg[:, None] == row_seg[None, :])
    scaling = HEAD ** (-0.5)

    def head(values, h):
        return values[:, h * HEAD : (h + 1) * HEAD]

    q_rot, k_rot, log_total, attended = ([], [], [], [])
    for h in range(heads):
        q_rot.append(rotate(head(q_normed, h), cosine, sine).astype(low))
        k_rot.append(rotate(head(k_normed, h), cosine, sine).astype(low))
        scores = jnp.where(
            allowed, mm(q_rot[h], k_rot[h], ((1,), (1,))) * scaling, masked_score
        )
        peak = jnp.max(scores, axis=-1, keepdims=True)
        log_total.append(peak + jnp.log(jnp.sum(jnp.exp(scores - peak), axis=-1, keepdims=True)))
        weights = jnp.exp(scores - log_total[h]).astype(low)
        attended.append(mm(weights, head(value_in, h), ((1,), (0,))).astype(low))
    attended = jnp.concatenate(attended, axis=1)
    attended, out_own, up_across = barrier((attended, out_own, up_across))

    attended_row = lax.all_gather(attended, "seq", axis=0)
    out_across = swap(out_own, 2)
    out_pieces = (out_own, swap(out_own, 1), out_across, swap(out_across, 1))
    extras = [p[:, width:] for p in out_pieces]
    routes_row = extras[0][:, : packed * picks].reshape(rows, picks).astype(jnp.int32)
    extras = jnp.concatenate([p[:, packed * picks :] for p in extras], axis=0)
    router = jnp.pad(extras[:, :expert_count], ((0, 0), (0, 128 - expert_count)))
    g_ffn = extras[:, expert_count].astype(full)[None]
    lane_ids = lax.iota(jnp.int32, 128)
    chosen = jnp.any(routes_row[:, :, None] == lane_ids[None, None, :], axis=1).astype(full)
    own = (
        lane_ids[None, :] == seq_index * held + lax.iota(jnp.int32, held)[:, None]
    ).astype(full)
    gate_full = jnp.concatenate([w_gate, swap(w_gate, 1), gate_across, swap(gate_across, 1)], axis=1)
    up_full = jnp.concatenate([w_up, swap(w_up, 1), up_across, swap(up_across, 1)], axis=1)
    attended_row, out_pieces, gate_full, up_full, router, g_ffn, chosen = barrier(
        (attended_row, out_pieces, gate_full, up_full, router, g_ffn, chosen)
    )

    dy_shard, attended_row = barrier((reorder(cotangent[0], dp_index, 1), attended_row))
    dy_row = lax.all_gather(dy_shard, "seq", axis=0, tiled=True)
    down_across = swap(w_down, 2)
    down_full = jnp.concatenate([w_down, swap(w_down, 1), down_across, swap(down_across, 1)], axis=2)
    order = jnp.stack([dp_index ^ k for k in range(4)]).astype(jnp.int32)
    hidden_mid, normed_ffn, r_ffn, chances, gates = finish_attention(
        order, attended_row, out_pieces, x_row, g_ffn, router, chosen, own, expert_count
    )
    act, dgate_factor, dup_factor = expert_activations(normed_ffn, gate_full, up_full)
    mixture = combine_experts(act, down_full, gates)
    dy_row, mixture, act = barrier((dy_row, mixture, act))

    scaled, dgate, dup, gate_sums = expert_gradients(
        dy_row, down_full, act, dgate_factor, dup_factor, gates
    )
    nf_grad, grad_logits = input_gradient(
        dgate, dup, gate_full, up_full, gate_sums, chances, chosen, own, router
    )
    nf_sum = lax.psum_scatter(nf_grad, "seq", scatter_dimension=0, tiled=True)

    down_kept, down_passed = sum_in_chip(weight_pieces(scaled, dy_row, 4, False), low)
    gate_kept, gate_passed = sum_in_chip(weight_pieces(normed_ffn, dgate, 4, True), low)
    up_kept, up_passed = sum_in_chip(weight_pieces(normed_ffn, dup, 4, True), low)
    down_arrived = swap(down_passed, 2)
    router_grad = mm(grad_logits[:, :expert_count], normed_ffn, ((0,), (0,)))
    nf_sum, mixture, down_arrived, gate_passed, up_passed, router_grad = barrier(
        (nf_sum, mixture, down_arrived, gate_passed, up_passed, router_grad)
    )
    mixture_own = lax.psum_scatter(mixture, "seq", scatter_dimension=0, tiled=True)
    gate_arrived, up_arrived = (swap(gate_passed, 2), swap(up_passed, 2))
    grad_w_down = down_kept.astype(full) + down_arrived.astype(full)

    mid_own = lax.dynamic_slice_in_dim(hidden_mid, first_row, tokens)
    nf_own = nf_sum.astype(full)
    r_own = lax.dynamic_slice_in_dim(r_ffn, first_row, tokens)
    gain_ffn_grad = jnp.sum(nf_own * mid_own * r_own, axis=0)
    scaled_grad = nf_own * g_ffn
    grad_mid = (
        dy_shard.astype(full)
        + r_own * scaled_grad
        - mid_own * (r_own**3) * jnp.mean(scaled_grad * mid_own, axis=-1, keepdims=True)
    )
    mid_low = grad_mid.astype(low)

    def to_columns(values):
        return lax.all_to_all(
            values.reshape(tokens, shards, cols).transpose(1, 0, 2), "seq", 0, 0, tiled=True
        ).reshape(rows, cols)

    def out_transposed(j):
        mixed = jnp.concatenate(
            [mid_low[:, (k ^ j) * chunk : ((k ^ j) + 1) * chunk] for k in range(4)], axis=1
        )
        return mm(mixed, out_pieces[j][:, :width], ((1,), (1,))).astype(low)

    grad_attended = jnp.concatenate([out_transposed(j) for j in range(4)], axis=1)
    grad_attended = to_columns(reorder(grad_attended, dp_index, 1))
    mid_cols = to_columns(reorder(mid_low, dp_index, 1))
    out_grad = jnp.einsum(
        "src,rn->scn", attended_row, mid_cols, preferred_element_type=full
    ).reshape(width, cols)
    out_grad = reorder(out_grad.astype(low), dp_index, 0)

    q_grads, k_grads, v_grads = ([], [], [])
    for h in range(heads):
        scores = jnp.where(
            allowed, mm(q_rot[h], k_rot[h], ((1,), (1,))) * scaling, masked_score
        )
        p = jnp.exp(scores - log_total[h])
        grad_h = head(grad_attended, h)
        grad_weights = mm(grad_h, head(value_in, h), ((1,), (1,)))
        delta = jnp.sum(p * grad_weights, axis=-1, keepdims=True)
        grad_scores = (scaling * p * (grad_weights - delta)).astype(low)
        q_grads.append(rotate(mm(grad_scores, k_rot[h], ((1,), (0,))), cosine, -sine))
        k_grads.append(rotate(mm(grad_scores, q_rot[h], ((0,), (0,))), cosine, -sine))
        v_grads.append(mm(p.astype(low), grad_h, ((0,), (0,))))
    q_grad, k_grad = (jnp.concatenate(q_grads, axis=1), jnp.concatenate(k_grads, axis=1))
    gain_query_grad = jnp.sum(q_grad * query * r_query, axis=0)
    gain_key_grad = jnp.sum(k_grad * key_proj * r_key, axis=0)
    q_grad, k_grad = (q_grad * g_query, k_grad * g_key)
    means = sum_over_seq(
        jnp.stack([jnp.sum(q_grad * query, axis=-1), jnp.sum(k_grad * key_proj, axis=-1)]), shards
    )
    means = means / width
    q_low = (r_query * q_grad - query * (r_query**3) * means[0][:, None]).astype(low)
    k_low = (r_key * k_grad - key_proj * (r_key**3) * means[1][:, None]).astype(low)
    v_low = jnp.concatenate(v_grads, axis=1).astype(low)
    qkv_low = jnp.concatenate([q_low, k_low, v_low], axis=1)
    normed_grad = mm(qkv_low, w_qkv, ((1,), (1,)))
    gain_attn_grad = jnp.sum(normed_grad * x_row.astype(full) * r_attn, axis=0)
    normed_grad, mixture_own, gate_arrived, up_arrived = barrier(
        (normed_grad.astype(low), mixture_own, gate_arrived, up_arrived)
    )
    grad_w_gate = gate_kept.astype(full) + gate_arrived.astype(full)
    grad_w_up = up_kept.astype(full) + up_arrived.astype(full)
    normed_sum = lax.psum_scatter(normed_grad, "seq", scatter_dimension=0, tiled=True).astype(full)

    proj_grad = jnp.concatenate(
        [mm(normed, qkv_low, ((0,), (0,))).astype(low), out_grad], axis=1
    )
    proj_grad = sum_pieces([proj_grad[k * chunk : (k + 1) * chunk] for k in range(4)], low)
    proj_grad = lax.all_to_all(
        proj_grad.astype(low).reshape(shards, block_rows, 4 * cols), "seq", 0, 0, tiled=True
    )
    proj_grad = proj_grad.reshape(shards, block_rows, 4, cols).transpose(2, 1, 0, 3)
    proj_grad = proj_grad.reshape(4, block_rows, width).astype(full)

    x_own = x_shard.astype(full)
    r_here = lax.rsqrt(jnp.mean(x_own * x_own, axis=-1, keepdims=True) + epsilon)
    scaled_grad = normed_sum * g_attn
    grad_hidden = (
        grad_mid
        + r_here * scaled_grad
        - x_own * (r_here**3) * jnp.mean(scaled_grad * x_own, axis=-1, keepdims=True)
    )
    block_out = (mid_own + mixture_own.astype(full)).astype(low)

    def place(values):
        whole = lax.dynamic_update_slice_in_dim(
            jnp.zeros((1, width), full), values[None], seq_index * cols, 1
        )
        return reorder(whole, dp_index, 1)

    vectors = jnp.concatenate(
        [
            router_grad,
            gain_attn_grad[None],
            place(gain_query_grad),
            place(gain_key_grad),
            gain_ffn_grad[None],
        ]
    )
    count = vectors.shape[0]
    vectors = sum_pieces([vectors[:, k * chunk : (k + 1) * chunk] for k in range(4)], full)
    vectors = vectors.reshape(count, shards, block_rows).transpose(1, 0, 2)
    vectors = jnp.sum(lax.all_to_all(vectors, "seq", 0, 0, tiled=True), axis=0)
    return (
        reorder(block_out, dp_index, 1)[None],
        reorder(grad_hidden, dp_index, 1)[None],
        proj_grad[0],
        proj_grad[1],
        proj_grad[2],
        proj_grad[3],
        vectors[expert_count],
        vectors[expert_count + 1],
        vectors[expert_count + 2],
        vectors[expert_count + 3],
        vectors[:expert_count].T,
        grad_w_gate,
        grad_w_up,
        grad_w_down,
    )


def solution(mesh):
    def layer(*arrays):
        whole_heads = (arrays[0].shape[2] // HEAD) % mesh.shape["seq"] == 0
        if whole_heads and mesh.shape["dp"] == 4:
            return on_device_heads(*arrays)
        return on_device(*arrays)

    return jax.shard_map(
        layer,
        mesh=mesh,
        in_specs=(
            P("dp", "seq", None),
            P("dp", None),
            P("dp", "seq", None),
            P(("dp", "seq"), None),
            P(("dp", "seq"), None),
            P(("dp", "seq"), None),
            P(("dp", "seq"), None),
            P(("dp", "seq")),
            P(("dp", "seq")),
            P(("dp", "seq")),
            P(("dp", "seq")),
            P(("dp", "seq"), None),
            P("seq", "dp", None),
            P("seq", "dp", None),
            P("seq", None, "dp"),
            P("dp", "seq", None),
        ),
        out_specs=(
            P("dp", "seq", None),
            P("dp", "seq", None),
            P(("dp", "seq"), None),
            P(("dp", "seq"), None),
            P(("dp", "seq"), None),
            P(("dp", "seq"), None),
            P(("dp", "seq")),
            P(("dp", "seq")),
            P(("dp", "seq")),
            P(("dp", "seq")),
            P(("dp", "seq"), None),
            P("seq", "dp", None),
            P("seq", "dp", None),
            P("seq", None, "dp"),
        ),
        check_vma=False,
    )
```

```python
import math

import jax
import jax.numpy as jnp
from jax import lax
from jax.experimental import pallas as pl
from jax.experimental.pallas import tpu as pltpu
from jax.sharding import PartitionSpec as P

HEAD = 128


epsilon = 1e-05
masked_score = -1e30
rope_base = 10000.0


def normalize(values, gain_vec):
    return (
        values * lax.rsqrt(jnp.mean(values * values, axis=-1, keepdims=True) + epsilon) * gain_vec
    )


def rotary(values, positions):
    half_dim = values.shape[-1] // 2
    frequency = jnp.exp(
        jnp.arange(half_dim, dtype=jnp.float32) * (-2.0 * math.log(rope_base) / values.shape[-1])
    )
    angles = positions.astype(jnp.float32)[:, None] * frequency[None, :]
    cosine = jnp.cos(angles)[:, None, :]
    sine_table = jnp.sin(angles)[:, None, :]
    first_half = values[..., :half_dim]
    second = values[..., half_dim:]
    return jnp.concatenate(
        [first_half * cosine - second * sine_table, second * cosine + first_half * sine_table],
        axis=-1,
    )


def softmax_rows(values):
    peak_value = jnp.max(values, axis=-1, keepdims=True)
    raised = jnp.exp(values - peak_value)
    return raised / jnp.sum(raised, axis=-1, keepdims=True)


def rotate_normed(projection, gain_vec, positions):
    tokens, model_width = projection.shape
    return rotary(
        normalize(projection, gain_vec).reshape(tokens, model_width // HEAD, HEAD), positions
    )


def masked_scores(queries, key_block, query_pos, query_seg, key_pos, key_seg, scaling):
    raw_scores = jnp.einsum("qhd,khd->hqk", queries, key_block, preferred_element_type=jnp.float32)
    allowed = (query_pos[:, None] >= key_pos[None, :]) & (query_seg[:, None] == key_seg[None, :])
    return jnp.where(allowed[None], raw_scores * scaling, masked_score)


def key_window(keys_all, values_all, row_seg, begin_at, span):
    key_block = lax.dynamic_slice_in_dim(keys_all, begin_at, span)
    value_block = lax.dynamic_slice_in_dim(values_all, begin_at, span)
    key_pos = begin_at + lax.iota(jnp.int32, span)
    key_seg = lax.dynamic_slice_in_dim(row_seg, begin_at, span)
    return (key_block, value_block, key_pos, key_seg)


def project_front(hidden, layer_full, positions):
    tokens, model_width = hidden.shape
    normed = normalize(hidden, layer_full[5].astype(jnp.float32)).astype(jnp.bfloat16)
    query = jnp.dot(normed, layer_full[0], preferred_element_type=jnp.float32)
    key_proj = jnp.dot(normed, layer_full[1], preferred_element_type=jnp.float32)
    value_proj = jnp.dot(normed, layer_full[2], preferred_element_type=jnp.float32)
    query_rot = rotate_normed(query, layer_full[6].astype(jnp.float32), positions).astype(
        jnp.bfloat16
    )
    key_rot = rotate_normed(key_proj, layer_full[7].astype(jnp.float32), positions).astype(
        jnp.bfloat16
    )
    value_in = value_proj.astype(jnp.bfloat16).reshape(tokens, model_width // HEAD, HEAD)
    return (normed, query, key_proj, query_rot, key_rot, value_in)


def attend_local(query_rot, keys_all, values_all, row_seg, offset, span):
    tokens, head_count, head_dim = query_rot.shape
    scaling = head_dim ** (-0.5)
    query_pos = offset + lax.iota(jnp.int32, tokens)
    query_seg = lax.dynamic_slice_in_dim(row_seg, offset, tokens)
    reach_blocks = (offset + tokens + span - 1) // span

    def block_scores(block_index):
        begin_at = block_index * span
        key_block, value_block, key_pos, key_seg = key_window(
            keys_all, values_all, row_seg, begin_at, span
        )
        return (
            masked_scores(query_rot, key_block, query_pos, query_seg, key_pos, key_seg, scaling),
            value_block,
        )

    def first_pass(block_index, state_pair):
        peak_value, denominator = state_pair
        scores, unused_values = block_scores(block_index)
        new_peak = jnp.maximum(peak_value, jnp.max(scores, axis=-1))
        denominator = denominator * jnp.exp(peak_value - new_peak) + jnp.sum(
            jnp.exp(scores - new_peak[..., None]), axis=-1
        )
        return (new_peak, denominator)

    start_state = (
        jnp.full((head_count, tokens), masked_score, jnp.float32),
        jnp.zeros((head_count, tokens), jnp.float32),
    )
    peak_value, denominator = lax.fori_loop(0, reach_blocks, first_pass, start_state)
    log_total = peak_value + jnp.log(denominator)

    def second_pass(block_index, running):
        scores, value_block = block_scores(block_index)
        weights = jnp.exp(scores - log_total[..., None]).astype(jnp.bfloat16)
        return running + jnp.einsum(
            "hqk,khd->qhd", weights, value_block, preferred_element_type=jnp.float32
        )

    attention = lax.fori_loop(
        0, reach_blocks, second_pass, jnp.zeros((tokens, head_count, head_dim), jnp.float32)
    )
    return (attention, log_total)


def query_grads(query_rot, keys_all, values_all, row_seg, offset, span, log_total, grad_attended):
    tokens, head_count, head_dim = query_rot.shape
    scaling = head_dim ** (-0.5)
    query_pos = offset + lax.iota(jnp.int32, tokens)
    query_seg = lax.dynamic_slice_in_dim(row_seg, offset, tokens)
    reach_blocks = (offset + tokens + span - 1) // span

    def block_terms(block_index):
        begin_at = block_index * span
        key_block, value_block, key_pos, key_seg = key_window(
            keys_all, values_all, row_seg, begin_at, span
        )
        scores = masked_scores(
            query_rot, key_block, query_pos, query_seg, key_pos, key_seg, scaling
        )
        weights = jnp.exp(scores - log_total[..., None])
        grad_weights = jnp.einsum(
            "qhd,khd->hqk", grad_attended, value_block, preferred_element_type=jnp.float32
        )
        return (key_block, weights, grad_weights)

    def delta_pass(block_index, running):
        unused_keys, weights, grad_weights = block_terms(block_index)
        return running + jnp.sum(weights * grad_weights, axis=-1)

    delta = lax.fori_loop(0, reach_blocks, delta_pass, jnp.zeros((head_count, tokens), jnp.float32))

    def query_pass(block_index, running):
        key_block, weights, grad_weights = block_terms(block_index)
        grad_scores = (weights * (grad_weights - delta[..., None]) * scaling).astype(jnp.bfloat16)
        return running + jnp.einsum(
            "hqk,khd->qhd", grad_scores, key_block, preferred_element_type=jnp.float32
        )

    grad_query_rot = lax.fori_loop(
        0, reach_blocks, query_pass, jnp.zeros((tokens, head_count, head_dim), jnp.float32)
    )
    return (delta, grad_query_rot)


def route_tokens(hidden_mid, layer_full, choice_rows):
    tokens, pick_count = choice_rows.shape
    normed_ffn = normalize(hidden_mid, layer_full[8].astype(jnp.float32)).astype(jnp.bfloat16)
    logits = jnp.dot(normed_ffn, layer_full[4], preferred_element_type=jnp.float32)
    expert_count = logits.shape[1]
    capacity = 3 * tokens * pick_count // (2 * expert_count)
    chances = softmax_rows(logits)
    picks = choice_rows[:, :, None] == lax.iota(jnp.int32, expert_count)[None, None, :]
    gate_values = jnp.sum(jnp.where(picks, chances[:, None, :], 0.0), axis=-1)
    flat_hits = picks.reshape(tokens * pick_count, expert_count).astype(jnp.int32)
    earlier = jnp.cumsum(flat_hits, axis=0) - flat_hits
    slot_ids = choice_rows.reshape(-1) * capacity + jnp.sum(earlier * flat_hits, axis=1)
    pair_table = lax.iota(jnp.int32, expert_count * capacity)[:, None] == slot_ids[None, :]
    spread = jnp.sum(
        pair_table.reshape(expert_count * capacity, tokens, pick_count).astype(jnp.int32), axis=2
    ).astype(jnp.bfloat16)
    send_rows = jnp.dot(spread, normed_ffn, preferred_element_type=jnp.float32).astype(jnp.bfloat16)
    send_rows = send_rows.reshape(expert_count, capacity, hidden_mid.shape[1])
    return (normed_ffn, chances, picks, gate_values, slot_ids, pair_table, spread, send_rows)


def group_rows(row_block, held_experts):
    sources = row_block.shape[0] // held_experts
    grouped = row_block.reshape(
        sources, held_experts, row_block.shape[1], row_block.shape[2]
    ).transpose(1, 0, 2, 3)
    return grouped.reshape(held_experts, sources * row_block.shape[1], row_block.shape[2])


def ungroup_rows(grouped, whole_shape):
    held_experts = grouped.shape[0]
    sources = whole_shape[0] // held_experts
    spread_out = grouped.reshape(held_experts, sources, whole_shape[1], whole_shape[2]).transpose(
        1, 0, 2, 3
    )
    return spread_out.reshape(whole_shape)


def expert_forward(row_block, gate_full, up_full, down_full):
    inputs = group_rows(row_block, gate_full.shape[0])
    gate_pre = jnp.einsum("erd,edf->erf", inputs, gate_full, preferred_element_type=jnp.float32)
    up_pre = jnp.einsum("erd,edf->erf", inputs, up_full, preferred_element_type=jnp.float32)
    activated = (gate_pre * lax.logistic(gate_pre) * up_pre).astype(jnp.bfloat16)
    result = jnp.einsum(
        "erf,efd->erd", activated, down_full, preferred_element_type=jnp.float32
    ).astype(jnp.bfloat16)
    return ungroup_rows(result, row_block.shape)


def expert_backward(row_block, grad_block, gate_full, up_full, down_full):
    inputs = group_rows(row_block, gate_full.shape[0])
    grad_outputs = group_rows(grad_block, gate_full.shape[0])
    gate_pre = jnp.einsum("erd,edf->erf", inputs, gate_full, preferred_element_type=jnp.float32)
    up_pre = jnp.einsum("erd,edf->erf", inputs, up_full, preferred_element_type=jnp.float32)
    sigmoid_gate = lax.logistic(gate_pre)
    activated = (gate_pre * sigmoid_gate * up_pre).astype(jnp.bfloat16)
    grad_act = jnp.einsum(
        "erd,efd->erf", grad_outputs, down_full, preferred_element_type=jnp.float32
    )
    grad_down = jnp.einsum(
        "erf,erd->efd", activated, grad_outputs, preferred_element_type=jnp.float32
    )
    grad_gate_pre = (
        grad_act * up_pre * sigmoid_gate * (1.0 + gate_pre * (1.0 - sigmoid_gate))
    ).astype(jnp.bfloat16)
    grad_up_pre = (grad_act * gate_pre * sigmoid_gate).astype(jnp.bfloat16)
    grad_gate_w = jnp.einsum(
        "erd,erf->edf", inputs, grad_gate_pre, preferred_element_type=jnp.float32
    )
    grad_up_w = jnp.einsum("erd,erf->edf", inputs, grad_up_pre, preferred_element_type=jnp.float32)
    grad_inputs = jnp.einsum(
        "erf,edf->erd", grad_gate_pre, gate_full, preferred_element_type=jnp.float32
    )
    grad_inputs = grad_inputs + jnp.einsum(
        "erf,edf->erd", grad_up_pre, up_full, preferred_element_type=jnp.float32
    )
    return (
        ungroup_rows(grad_inputs.astype(jnp.bfloat16), row_block.shape),
        grad_gate_w,
        grad_up_w,
        grad_down,
    )


def contract_rows(left, right):
    return lax.dot_general(
        left, right, (((0,), (0,)), ((), ())), preferred_element_type=jnp.float32
    )


def contract_cols(left, right):
    return lax.dot_general(
        left, right, (((1,), (1,)), ((), ())), preferred_element_type=jnp.float32
    )


def on_device(
    hidden_in,
    segment_ids,
    routes,
    w_query,
    w_key,
    w_value,
    w_out,
    gain_attn,
    gain_query,
    gain_key,
    gain_ffn,
    w_router,
    w_gate,
    w_up,
    w_down,
    cotangent,
):
    hidden = hidden_in[0].astype(jnp.float32)
    tokens, model_width = hidden.shape
    head_count = model_width // HEAD
    row_seg = segment_ids[0]
    choice_rows = routes[0]
    offset = lax.axis_index("seq") * tokens
    positions = offset + lax.iota(jnp.int32, tokens)
    span = min(512, row_seg.shape[0])
    layer_full = (
        lax.all_gather(w_query, ("dp", "seq"), axis=0, tiled=True),
        lax.all_gather(w_key, ("dp", "seq"), axis=0, tiled=True),
        lax.all_gather(w_value, ("dp", "seq"), axis=0, tiled=True),
        lax.all_gather(w_out, ("dp", "seq"), axis=0, tiled=True),
        lax.all_gather(w_router, ("dp", "seq"), axis=0, tiled=True),
        lax.all_gather(gain_attn, ("dp", "seq"), axis=0, tiled=True),
        lax.all_gather(gain_query, ("dp", "seq"), axis=0, tiled=True),
        lax.all_gather(gain_key, ("dp", "seq"), axis=0, tiled=True),
        lax.all_gather(gain_ffn, ("dp", "seq"), axis=0, tiled=True),
    )
    expert_full = (
        lax.all_gather(w_gate, "dp", axis=1, tiled=True),
        lax.all_gather(w_up, "dp", axis=1, tiled=True),
        lax.all_gather(w_down, "dp", axis=2, tiled=True),
    )
    projected = project_front(hidden, layer_full, positions)
    keys_all, values_all = (
        lax.all_gather(projected[4], "seq", axis=0, tiled=True),
        lax.all_gather(projected[5], "seq", axis=0, tiled=True),
    )
    attention, log_total = attend_local(projected[3], keys_all, values_all, row_seg, offset, span)
    attended = attention.reshape(tokens, model_width).astype(jnp.bfloat16)
    hidden_mid = hidden + jnp.dot(attended, layer_full[3], preferred_element_type=jnp.float32)
    routing = route_tokens(hidden_mid, layer_full, choice_rows)
    expert_count, capacity = (routing[7].shape[0], routing[7].shape[1])
    expert_out = expert_forward(
        lax.all_to_all(routing[7], "seq", split_axis=0, concat_axis=0, tiled=True),
        expert_full[0],
        expert_full[1],
        expert_full[2],
    )
    returned = lax.all_to_all(expert_out, "seq", split_axis=0, concat_axis=0, tiled=True)
    picked = jnp.take(returned.reshape(expert_count * capacity, model_width), routing[4], axis=0)
    picked = picked.reshape(tokens, choice_rows.shape[1], model_width)
    mixture = jnp.sum(routing[3][:, :, None] * picked.astype(jnp.float32), axis=1)
    block_out = (hidden_mid + mixture).astype(jnp.bfloat16)
    layer_full = (
        lax.all_gather(w_query, ("dp", "seq"), axis=0, tiled=True),
        lax.all_gather(w_key, ("dp", "seq"), axis=0, tiled=True),
        lax.all_gather(w_value, ("dp", "seq"), axis=0, tiled=True),
        lax.all_gather(w_out, ("dp", "seq"), axis=0, tiled=True),
        lax.all_gather(w_router, ("dp", "seq"), axis=0, tiled=True),
        lax.all_gather(gain_attn, ("dp", "seq"), axis=0, tiled=True),
        lax.all_gather(gain_query, ("dp", "seq"), axis=0, tiled=True),
        lax.all_gather(gain_key, ("dp", "seq"), axis=0, tiled=True),
        lax.all_gather(gain_ffn, ("dp", "seq"), axis=0, tiled=True),
    )
    expert_full = (
        lax.all_gather(w_gate, "dp", axis=1, tiled=True),
        lax.all_gather(w_up, "dp", axis=1, tiled=True),
        lax.all_gather(w_down, "dp", axis=2, tiled=True),
    )
    projected = project_front(hidden, layer_full, positions)
    keys_all, values_all = (
        lax.all_gather(projected[4], "seq", axis=0, tiled=True),
        lax.all_gather(projected[5], "seq", axis=0, tiled=True),
    )
    attention, log_total = attend_local(projected[3], keys_all, values_all, row_seg, offset, span)
    attended = attention.reshape(tokens, model_width).astype(jnp.bfloat16)
    hidden_mid = hidden + jnp.dot(attended, layer_full[3], preferred_element_type=jnp.float32)
    routing = route_tokens(hidden_mid, layer_full, choice_rows)
    normed_ffn, chances, picks, gate_values, slot_ids, pair_table, spread, send_rows = routing
    grad_out = cotangent[0].astype(jnp.float32)
    grad_gates = jnp.sum(grad_out[:, None, :] * picked.astype(jnp.float32), axis=-1)
    slot_gates = jnp.sum(jnp.where(pair_table, gate_values.reshape(-1)[None, :], 0.0), axis=1)
    grad_rows_in = jnp.dot(spread, cotangent[0], preferred_element_type=jnp.float32)
    grad_slots = (
        (slot_gates[:, None] * grad_rows_in)
        .astype(jnp.bfloat16)
        .reshape(expert_count, capacity, model_width)
    )
    arrived_rows, arrived_grads = (
        lax.all_to_all(send_rows, "seq", split_axis=0, concat_axis=0, tiled=True),
        lax.all_to_all(grad_slots, "seq", split_axis=0, concat_axis=0, tiled=True),
    )
    grad_inputs, grad_gate_w, grad_up_w, grad_down_w = expert_backward(
        arrived_rows, arrived_grads, expert_full[0], expert_full[1], expert_full[2]
    )
    grad_back = lax.all_to_all(grad_inputs, "seq", split_axis=0, concat_axis=0, tiled=True)
    grad_normed_ffn = contract_rows(spread, grad_back.reshape(expert_count * capacity, model_width))
    grad_chances = jnp.sum(jnp.where(picks, grad_gates[:, :, None], 0.0), axis=1)
    grad_logits = (
        chances * (grad_chances - jnp.sum(chances * grad_chances, axis=-1, keepdims=True))
    ).astype(jnp.bfloat16)
    grad_router_w = contract_rows(normed_ffn, grad_logits)
    grad_normed_ffn = grad_normed_ffn + contract_cols(grad_logits, layer_full[4])
    unused_ffn, pull_ffn = jax.vjp(normalize, hidden_mid, layer_full[8].astype(jnp.float32))
    grad_mid_norm, grad_gain_ffn_w = pull_ffn(grad_normed_ffn)
    grad_mid = grad_out + grad_mid_norm
    grad_mid_low = grad_mid.astype(jnp.bfloat16)
    grad_w_out = contract_rows(attended, grad_mid_low)
    grad_attended = (
        contract_cols(grad_mid_low, layer_full[3])
        .astype(jnp.bfloat16)
        .reshape(tokens, head_count, HEAD)
    )
    query_rot = projected[3]
    delta, grad_query_rot = query_grads(
        query_rot, keys_all, values_all, row_seg, offset, span, log_total, grad_attended
    )
    scaling = HEAD ** (-0.5)
    query_seg = lax.dynamic_slice_in_dim(row_seg, offset, tokens)
    row_count = lax.axis_size("seq") * tokens
    step_rows = math.gcd(row_count, 512)

    def one_window(window_index, running):
        window_start = window_index * step_rows
        key_block, value_block, key_pos, key_seg = key_window(
            keys_all, values_all, row_seg, window_start, step_rows
        )
        scores = masked_scores(
            query_rot, key_block, positions, query_seg, key_pos, key_seg, scaling
        )
        weights = jnp.exp(scores - log_total[..., None])
        grad_weights = jnp.einsum(
            "qhd,khd->hqk", grad_attended, value_block, preferred_element_type=jnp.float32
        )
        grad_scores = (weights * (grad_weights - delta[..., None]) * scaling).astype(jnp.bfloat16)
        grad_key_part = jnp.einsum(
            "hqk,qhd->khd", grad_scores, query_rot, preferred_element_type=jnp.float32
        )
        grad_value_part = jnp.einsum(
            "hqk,qhd->khd",
            weights.astype(jnp.bfloat16),
            grad_attended,
            preferred_element_type=jnp.float32,
        )
        term = jnp.concatenate(
            [
                grad_key_part.reshape(step_rows, model_width),
                grad_value_part.reshape(step_rows, model_width),
            ],
            axis=1,
        )
        return lax.dynamic_update_slice_in_dim(running, term, window_index * step_rows, 0)

    key_sums = lax.psum_scatter(
        lax.fori_loop(
            0,
            row_count // step_rows,
            one_window,
            jnp.zeros((row_count, 2 * model_width), jnp.float32),
        ).astype(jnp.bfloat16),
        "seq",
        scatter_dimension=0,
        tiled=True,
    ).astype(jnp.float32)
    grad_key_rot = key_sums[:, :model_width].reshape(tokens, head_count, HEAD)
    grad_v_low = key_sums[:, model_width:].astype(jnp.bfloat16)

    def query_chain(projection, gain_vec):
        return rotate_normed(projection, gain_vec, positions)

    unused_query, pull_query = jax.vjp(query_chain, projected[1], layer_full[6].astype(jnp.float32))
    grad_query_pre, grad_gain_query_w = pull_query(grad_query_rot)
    unused_key, pull_key = jax.vjp(query_chain, projected[2], layer_full[7].astype(jnp.float32))
    grad_key_pre, grad_gain_key_w = pull_key(grad_key_rot)
    grad_q_low = grad_query_pre.astype(jnp.bfloat16)
    grad_k_low = grad_key_pre.astype(jnp.bfloat16)
    normed = projected[0]
    grad_w_query = contract_rows(normed, grad_q_low)
    grad_w_key = contract_rows(normed, grad_k_low)
    grad_w_value = contract_rows(normed, grad_v_low)
    grad_normed = (
        contract_cols(grad_q_low, layer_full[0])
        + contract_cols(grad_k_low, layer_full[1])
        + contract_cols(grad_v_low, layer_full[2])
    )
    unused_attn, pull_attn = jax.vjp(normalize, hidden, layer_full[5].astype(jnp.float32))
    grad_hidden_norm, grad_gain_attn_w = pull_attn(grad_normed)
    grad_hidden = grad_mid + grad_hidden_norm
    shares = (
        lax.psum_scatter(grad_w_query, ("dp", "seq"), scatter_dimension=0, tiled=True),
        lax.psum_scatter(grad_w_key, ("dp", "seq"), scatter_dimension=0, tiled=True),
        lax.psum_scatter(grad_w_value, ("dp", "seq"), scatter_dimension=0, tiled=True),
        lax.psum_scatter(grad_w_out, ("dp", "seq"), scatter_dimension=0, tiled=True),
        lax.psum_scatter(grad_router_w, ("dp", "seq"), scatter_dimension=0, tiled=True),
        lax.psum_scatter(grad_gain_attn_w, ("dp", "seq"), scatter_dimension=0, tiled=True),
        lax.psum_scatter(grad_gain_query_w, ("dp", "seq"), scatter_dimension=0, tiled=True),
        lax.psum_scatter(grad_gain_key_w, ("dp", "seq"), scatter_dimension=0, tiled=True),
        lax.psum_scatter(grad_gain_ffn_w, ("dp", "seq"), scatter_dimension=0, tiled=True),
    )
    expert_shares = (
        lax.psum_scatter(
            grad_gate_w.astype(jnp.bfloat16), "dp", scatter_dimension=1, tiled=True
        ).astype(jnp.float32),
        lax.psum_scatter(
            grad_up_w.astype(jnp.bfloat16), "dp", scatter_dimension=1, tiled=True
        ).astype(jnp.float32),
        lax.psum_scatter(
            grad_down_w.astype(jnp.bfloat16), "dp", scatter_dimension=2, tiled=True
        ).astype(jnp.float32),
    )
    return (
        block_out[None],
        grad_hidden[None],
        shares[0],
        shares[1],
        shares[2],
        shares[3],
        shares[5],
        shares[6],
        shares[7],
        shares[8],
        shares[4],
        expert_shares[0],
        expert_shares[1],
        expert_shares[2],
    )


VMEM_GRANT = 56 * 1024 * 1024


def mm(left, right, dims):
    return lax.dot_general(left, right, (dims, ((), ())), preferred_element_type=jnp.float32)


def cost(flops, transcendentals, *arrays):
    moved = sum(math.prod(a.shape) * a.dtype.itemsize for a in arrays)
    return pl.CostEstimate(
        flops=flops // 4, transcendentals=transcendentals // 4, bytes_accessed=moved // 4
    )


def grid_call(body, grid, in_specs, out_specs, outs, flops, transcendentals, *args):
    return pl.pallas_call(
        body,
        grid=grid,
        in_specs=in_specs,
        out_specs=out_specs,
        out_shape=outs,
        compiler_params=pltpu.CompilerParams(vmem_limit_bytes=VMEM_GRANT),
        cost_estimate=cost(flops, transcendentals, *args, *jax.tree.leaves(outs)),
    )(*args)


def row_tiles(rows):
    return math.gcd(rows, 512)


def finish_attention(order, attended, out_pieces, x_row, gain, router, chosen, own, expert_count):
    shards, rows, cols = attended.shape
    width = x_row.shape[1]
    held = own.shape[0]
    chunk = width // 4
    per_chunk = chunk // cols
    tm = math.gcd(rows, 256)

    def body(order_ref, att_ref, p0, p1, p2, p3, x_ref, gain_ref, router_ref, chosen_ref, own_ref, *outs):
        mid_ref, normed_ref, r_ref, chance_ref, gate_ref, att_all = outs
        for h in range(shards):
            source = order_ref[h // per_chunk] * per_chunk + h % per_chunk
            att_all[:, h * cols : (h + 1) * cols] = att_ref[source]
        squares = jnp.zeros((tm, 1), jnp.float32)
        for n in range(4):
            at = slice(n * chunk, (n + 1) * chunk)
            total = x_ref[:, at].astype(jnp.float32)
            for j, piece in enumerate((p0, p1, p2, p3)):
                k = n ^ j
                total = total + mm(
                    att_all[:, j * chunk : (j + 1) * chunk],
                    piece[:, k * chunk : (k + 1) * chunk],
                    ((1,), (0,)),
                )
            mid_ref[:, at] = total
            squares = squares + jnp.sum(total * total, axis=-1, keepdims=True)
        r = lax.rsqrt(squares / width + epsilon)
        r_ref[...] = r
        logits = jnp.zeros((tm, 128), jnp.float32)
        for n in range(4):
            at = slice(n * chunk, (n + 1) * chunk)
            normed = (mid_ref[:, at] * r * gain_ref[:, at]).astype(jnp.bfloat16)
            normed_ref[:, at] = normed
            logits = logits + mm(normed, router_ref[at, :], ((1,), (0,)))
        lane = lax.broadcasted_iota(jnp.int32, (tm, 128), 1)
        logits = jnp.where(lane < expert_count, logits, masked_score)
        raised = jnp.exp(logits - jnp.max(logits, axis=-1, keepdims=True))
        chances = raised / jnp.sum(raised, axis=-1, keepdims=True)
        chance_ref[...] = chances
        taken = chances * chosen_ref[...]
        for e in range(held):
            gate_ref[e] = jnp.sum(taken * own_ref[e : e + 1, :], axis=-1, keepdims=True)

    full = jnp.float32
    piece_spec = pl.BlockSpec((chunk, width), lambda i, o: (0, 0))
    wide = pl.BlockSpec((tm, width), lambda i, o: (i, 0))
    lanes = pl.BlockSpec((tm, 128), lambda i, o: (i, 0))
    outs = [
        jax.ShapeDtypeStruct((rows, width), full),
        jax.ShapeDtypeStruct((rows, width), jnp.bfloat16),
        jax.ShapeDtypeStruct((rows, 1), full),
        jax.ShapeDtypeStruct((rows, 128), full),
        jax.ShapeDtypeStruct((held, rows, 1), full),
    ]
    return pl.pallas_call(
        body,
        grid_spec=pltpu.PrefetchScalarGridSpec(
            num_scalar_prefetch=1,
            grid=(rows // tm,),
            in_specs=[
                pl.BlockSpec((shards, tm, cols), lambda i, o: (0, i, 0)),
                piece_spec,
                piece_spec,
                piece_spec,
                piece_spec,
                wide,
                pl.BlockSpec((1, width), lambda i, o: (0, 0)),
                pl.BlockSpec((width, 128), lambda i, o: (0, 0)),
                lanes,
                pl.BlockSpec((held, 128), lambda i, o: (0, 0)),
            ],
            out_specs=[
                wide,
                wide,
                pl.BlockSpec((tm, 1), lambda i, o: (i, 0)),
                lanes,
                pl.BlockSpec((held, tm, 1), lambda i, o: (0, i, 0)),
            ],
            scratch_shapes=[pltpu.VMEM((tm, width), jnp.bfloat16)],
        ),
        out_shape=outs,
        compiler_params=pltpu.CompilerParams(vmem_limit_bytes=VMEM_GRANT),
        cost_estimate=cost(2 * rows * width * width, rows * 128, attended, *out_pieces, *outs),
    )(order, attended, *out_pieces, x_row, gain, router, chosen, own)


def expert_activations(normed, gate, up):
    held, width, ff = gate.shape
    rows = normed.shape[0]
    tile, tm = (math.gcd(ff, 512), row_tiles(rows))

    def body(x_ref, gate_ref, up_ref, act_ref, dgate_ref, dup_ref):
        @pl.loop(0, rows // tm)
        def _(i):
            at = pl.ds(pl.multiple_of(i * tm, tm), tm)
            gate_pre = mm(x_ref[at, :], gate_ref[0], ((1,), (0,)))
            up_pre = mm(x_ref[at, :], up_ref[0], ((1,), (0,)))
            sig = lax.logistic(gate_pre)
            silu = gate_pre * sig
            act_ref[0, at, :] = (silu * up_pre).astype(jnp.bfloat16)
            dgate_ref[0, at, :] = (up_pre * (sig + silu * (1.0 - sig))).astype(jnp.bfloat16)
            dup_ref[0, at, :] = silu.astype(jnp.bfloat16)

    tiled = pl.BlockSpec((1, rows, tile), lambda e, f: (e, 0, f))
    low = jax.ShapeDtypeStruct((held, rows, ff), jnp.bfloat16)
    return grid_call(
        body,
        (held, ff // tile),
        [
            pl.BlockSpec((rows, width), lambda e, f: (0, 0)),
            pl.BlockSpec((1, width, tile), lambda e, f: (e, 0, f)),
            pl.BlockSpec((1, width, tile), lambda e, f: (e, 0, f)),
        ],
        [tiled, tiled, tiled],
        [low, low, low],
        4 * held * rows * ff * width,
        held * rows * ff,
        normed,
        gate,
        up,
    )


def expert_gradients(dy, down, act, dgate_factor, dup_factor, weight):
    held, ff, width = down.shape
    rows = dy.shape[0]
    tile, tm = (math.gcd(ff, 512), row_tiles(rows))

    def body(dy_ref, down_ref, act_ref, a_ref, b_ref, weight_ref, out_ref, dgate_ref, dup_ref, sum_ref):
        first = pl.program_id(1) == 0

        @pl.loop(0, rows // tm)
        def _(i):
            at = pl.ds(pl.multiple_of(i * tm, tm), tm)
            grad = mm(dy_ref[at, :], down_ref[0], ((1,), (1,)))
            scale = weight_ref[0, at, :]
            act = act_ref[0, at, :].astype(jnp.float32)
            product = act * grad
            partial = product[:, :128]
            for j in range(1, tile // 128):
                partial = partial + product[:, j * 128 : (j + 1) * 128]

            @pl.when(first)
            def _():
                sum_ref[0, at, :] = partial

            @pl.when(jnp.logical_not(first))
            def _():
                sum_ref[0, at, :] = sum_ref[0, at, :] + partial

            out_ref[0, at, :] = (scale * act).astype(jnp.bfloat16)
            grad = scale * grad
            dgate_ref[0, at, :] = (grad * a_ref[0, at, :].astype(jnp.float32)).astype(jnp.bfloat16)
            dup_ref[0, at, :] = (grad * b_ref[0, at, :].astype(jnp.float32)).astype(jnp.bfloat16)

    tiled = pl.BlockSpec((1, rows, tile), lambda e, f: (e, 0, f))
    low = jax.ShapeDtypeStruct((held, rows, ff), jnp.bfloat16)
    return grid_call(
        body,
        (held, ff // tile),
        [
            pl.BlockSpec((rows, width), lambda e, f: (0, 0)),
            pl.BlockSpec((1, tile, width), lambda e, f: (e, f, 0)),
            tiled,
            tiled,
            tiled,
            pl.BlockSpec((1, rows, 1), lambda e, f: (e, 0, 0)),
        ],
        [tiled, tiled, tiled, pl.BlockSpec((1, rows, 128), lambda e, f: (e, 0, 0))],
        [low, low, low, jax.ShapeDtypeStruct((held, rows, 128), jnp.float32)],
        2 * held * rows * ff * width,
        0,
        dy,
        down,
        act,
        dgate_factor,
        dup_factor,
        weight,
    )


def input_gradient(dgate, dup, gate, up, gate_sums, chances, chosen, own, router):
    held, width, ff = gate.shape
    rows = dgate.shape[1]
    tile, tm = (math.gcd(width, 512), row_tiles(rows))

    def body(dgate_ref, dup_ref, gate_ref, up_ref, sum_ref, chance_ref, chosen_ref, own_ref, router_ref, out_ref, logits_ref):
        @pl.loop(0, rows // tm)
        def _(i):
            at = pl.ds(pl.multiple_of(i * tm, tm), tm)
            chances = chance_ref[at, :]
            placed = jnp.zeros((tm, 128), jnp.float32)
            for e in range(held):
                got = jnp.sum(sum_ref[e, at, :], axis=-1, keepdims=True)
                placed = placed + own_ref[e : e + 1, :] * got
            placed = placed * chosen_ref[at, :]
            inner = jnp.sum(chances * placed, axis=-1, keepdims=True)
            logits = (chances * (placed - inner)).astype(jnp.bfloat16)
            logits_ref[at, :] = logits
            total = mm(logits, router_ref[...], ((1,), (1,)))
            for e in range(held):
                total = total + mm(dgate_ref[e, at, :], gate_ref[e], ((1,), (1,)))
                total = total + mm(dup_ref[e, at, :], up_ref[e], ((1,), (1,)))
            out_ref[at, :] = total.astype(jnp.bfloat16)

    whole = pl.BlockSpec((held, rows, ff), lambda n: (0, 0, 0))
    weights = pl.BlockSpec((held, tile, ff), lambda n: (0, n, 0))
    lanes = pl.BlockSpec((rows, 128), lambda n: (0, 0))
    return grid_call(
        body,
        (width // tile,),
        [
            whole,
            whole,
            weights,
            weights,
            pl.BlockSpec((held, rows, 128), lambda n: (0, 0, 0)),
            lanes,
            lanes,
            pl.BlockSpec((held, 128), lambda n: (0, 0)),
            pl.BlockSpec((tile, 128), lambda n: (n, 0)),
        ],
        [pl.BlockSpec((rows, tile), lambda n: (0, n)), lanes],
        [jax.ShapeDtypeStruct((rows, width), jnp.bfloat16), jax.ShapeDtypeStruct((rows, 128), jnp.bfloat16)],
        4 * held * rows * ff * width,
        0,
        dgate,
        dup,
        gate,
        up,
        gate_sums,
        chances,
        chosen,
        own,
        router,
    )


def combine_experts(act, down, weight):
    held, ff, width = down.shape
    rows = act.shape[1]
    tile, tm = (math.gcd(width, 512), row_tiles(rows))

    def body(act_ref, down_ref, weight_ref, out_ref):
        @pl.loop(0, rows // tm)
        def _(i):
            at = pl.ds(pl.multiple_of(i * tm, tm), tm)
            total = weight_ref[0, at, :] * mm(act_ref[0, at, :], down_ref[0], ((1,), (0,)))
            for e in range(1, held):
                term = mm(act_ref[e, at, :], down_ref[e], ((1,), (0,)))
                total = total + weight_ref[e, at, :] * term
            out_ref[at, :] = total.astype(jnp.bfloat16)

    return grid_call(
        body,
        (width // tile,),
        [
            pl.BlockSpec((held, rows, ff), lambda n: (0, 0, 0)),
            pl.BlockSpec((held, ff, tile), lambda n: (0, 0, n)),
            pl.BlockSpec((held, rows, 1), lambda n: (0, 0, 0)),
        ],
        pl.BlockSpec((rows, tile), lambda n: (0, n)),
        jax.ShapeDtypeStruct((rows, width), jnp.bfloat16),
        2 * held * rows * ff * width,
        0,
        act,
        down,
        weight,
    )


def weight_pieces(left, right, parts, split_left):
    flat, stacked = (left, right) if split_left else (right, left)
    held, rows, ff = stacked.shape
    piece = flat.shape[1] // parts
    shape = (held, piece, ff) if split_left else (held, ff, piece)
    tm = math.gcd(shape[1], 512)

    def body(flat_ref, stacked_ref, *outs):
        step = pl.program_id(0)
        for j in range(parts):

            @pl.when(step == j)
            def _(j=j):
                @pl.loop(0, shape[1] // tm)
                def _(i):
                    at = pl.ds(pl.multiple_of(i * tm, tm), tm)
                    if split_left:
                        value = mm(flat_ref[:, at], stacked_ref[0], ((0,), (0,)))
                    else:
                        value = mm(stacked_ref[0, :, at], flat_ref[...], ((0,), (0,)))
                    outs[j][0, at, :] = value.astype(jnp.bfloat16)

    def place(j):
        return lambda k, e: (jnp.where(k < j, 0, jnp.where(k > j, held - 1, e)), 0, 0)

    return grid_call(
        body,
        (parts, held),
        [
            pl.BlockSpec((rows, piece), lambda k, e: (0, k)),
            pl.BlockSpec((1, rows, ff), lambda k, e: (e, 0, 0)),
        ],
        [pl.BlockSpec((1,) + shape[1:], place(j)) for j in range(parts)],
        [jax.ShapeDtypeStruct(shape, jnp.bfloat16)] * parts,
        2 * held * rows * ff * flat.shape[1],
        0,
        flat,
        stacked,
    )


def rope_tables(row_count, head_dim):
    half_dim = head_dim // 2
    frequency = jnp.exp(
        jnp.arange(half_dim, dtype=jnp.float32) * (-2.0 * math.log(rope_base) / head_dim)
    )
    angles = jnp.arange(row_count, dtype=jnp.float32)[:, None] * frequency[None, :]
    cosine, sine = (jnp.cos(angles), jnp.sin(angles))
    return (
        jnp.concatenate([cosine, cosine], axis=1),
        jnp.concatenate([-sine, sine], axis=1),
    )


def seen(first, count, keys, seg_col, seg_row):
    position = first + lax.broadcasted_iota(jnp.int32, (count, keys), 0)
    other = lax.broadcasted_iota(jnp.int32, (count, keys), 1)
    return (position >= other) & (seg_col == seg_row)


def pair_rows(first, second):
    lane = lax.broadcasted_iota(jnp.int32, (first.shape[0], 128), 1)
    both = jnp.where(lane == 0, first, jnp.where(lane == 1, second, 0.0))
    return both.T[:8]


def pair_columns(sums):
    total = sum(sums[1:], sums[0])
    total = jnp.concatenate([total] * 16, axis=0).T
    return (total[:, 0:1], total[:, 1:2])


def project(x_row, gain, w_qkv):
    rows, width = x_row.shape
    held_cols = w_qkv.shape[1]
    cols = held_cols // 3
    tm = math.gcd(rows, 256)

    def body(x_ref, gain_ref, w_ref, normed_ref, qkv_ref, r_ref, stat_ref):
        x = x_ref[...].astype(jnp.float32)
        r = lax.rsqrt(jnp.mean(x * x, axis=-1, keepdims=True) + epsilon)
        r_ref[...] = r
        normed = (x * r * gain_ref[...]).astype(jnp.bfloat16)
        normed_ref[...] = normed
        qkv = mm(normed, w_ref[...], ((1,), (0,)))
        qkv_ref[...] = qkv
        squares = qkv[:, : 2 * cols] * qkv[:, : 2 * cols]
        stat_ref[...] = pair_rows(
            jnp.sum(squares[:, :cols], axis=-1, keepdims=True),
            jnp.sum(squares[:, cols:], axis=-1, keepdims=True),
        )

    full = jnp.float32
    return grid_call(
        body,
        (rows // tm,),
        [
            pl.BlockSpec((tm, width), lambda i: (i, 0)),
            pl.BlockSpec((1, width), lambda i: (0, 0)),
            pl.BlockSpec((width, held_cols), lambda i: (0, 0)),
        ],
        [
            pl.BlockSpec((tm, width), lambda i: (i, 0)),
            pl.BlockSpec((tm, held_cols), lambda i: (i, 0)),
            pl.BlockSpec((tm, 1), lambda i: (i, 0)),
            pl.BlockSpec((8, tm), lambda i: (0, i)),
        ],
        [
            jax.ShapeDtypeStruct((rows, width), jnp.bfloat16),
            jax.ShapeDtypeStruct((rows, held_cols), full),
            jax.ShapeDtypeStruct((rows, 1), full),
            jax.ShapeDtypeStruct((8, rows), full),
        ],
        2 * rows * width * held_cols,
        0,
        x_row,
        gain,
        w_qkv,
    )


def attend(qkv, sums, width, g_query, g_key, cosine, sine, seg_col, seg_row):
    rows, held_cols = qkv.shape
    cols = held_cols // 3
    heads = cols // HEAD
    tq = math.gcd(rows, 256)
    scaling = HEAD ** (-0.5)
    shards = sums.shape[0]

    def body(q, k, v, sums_ref, gq, gk, cos, sin, sc, sr, q_out, k_out, v_out, att_out, log_out, rq, rk):
        @pl.when(pl.program_id(0) == 0)
        def _():
            for i in range(rows // tq):
                at = slice(i * tq, (i + 1) * tq)
                first, second = pair_columns([sums_ref[d, :, at] for d in range(shards)])
                rq[at, :] = lax.rsqrt(first / width + epsilon)
                rk[at, :] = lax.rsqrt(second / width + epsilon)

        def rotated(ref, r, g):
            values = ref[...] * r[...] * g[...]
            swapped = pltpu.roll(values, HEAD // 2, 1)
            return (values * cos[...] + swapped * sin[...]).astype(jnp.bfloat16)

        q_out[...] = rotated(q, rq, gq)
        k_out[...] = rotated(k, rk, gk)
        v_out[...] = v[...].astype(jnp.bfloat16)
        for i in range(rows // tq):
            at, keys = (slice(i * tq, (i + 1) * tq), (i + 1) * tq)
            scores = mm(q_out[at, :], k_out[:keys, :], ((1,), (1,))) * scaling
            allowed = seen(i * tq, tq, keys, sc[at, :], sr[:, :keys])
            scores = jnp.where(allowed, scores, masked_score)
            peak = jnp.max(scores, axis=-1, keepdims=True)
            raised = jnp.exp(scores - peak)
            total = jnp.sum(raised, axis=-1, keepdims=True)
            log_out[0, at, :] = peak + jnp.log(total)
            weights = (raised * (1.0 / total)).astype(jnp.bfloat16)
            att_out[at, :] = mm(weights, v_out[:keys, :], ((1,), (0,))).astype(jnp.bfloat16)

    def col(offset):
        return pl.BlockSpec((rows, HEAD), lambda h: (0, offset + h))

    row = pl.BlockSpec((1, HEAD), lambda h: (0, h))
    one = pl.BlockSpec((rows, 1), lambda h: (0, 0))
    table = pl.BlockSpec((rows, HEAD), lambda h: (0, 0))
    low = jax.ShapeDtypeStruct((rows, cols), jnp.bfloat16)
    column = jax.ShapeDtypeStruct((rows, 1), jnp.float32)
    return grid_call(
        body,
        (heads,),
        [
            col(0),
            col(heads),
            col(2 * heads),
            pl.BlockSpec((shards, 8, rows), lambda h: (0, 0, 0)),
            row,
            row,
            table,
            table,
            one,
            pl.BlockSpec((1, rows), lambda h: (0, 0)),
        ],
        [col(0)] * 4 + [pl.BlockSpec((1, rows, 1), lambda h: (h, 0, 0)), one, one],
        [low] * 4 + [jax.ShapeDtypeStruct((heads, rows, 1), jnp.float32), column, column],
        4 * heads * rows * rows * HEAD,
        heads * rows * rows,
        qkv,
        qkv,
        qkv,
        sums,
        g_query,
        g_key,
        cosine,
        sine,
        seg_col,
        seg_row,
    )


def attend_back(qkv, q_rot, k_rot, value_in, grad, log_total, r_query, r_key, g_query, g_key, cosine, sine, seg_col, seg_row):
    rows, cols = q_rot.shape
    heads = cols // HEAD
    tq = math.gcd(rows, 256)
    scaling = HEAD ** (-0.5)

    def body(q, k, qr, kr, v, ga, lt, rq, rk, gq, gk, cos, sin, sc, sr, q_out, k_out, v_out, stat_out, gq_out, gk_out, q_sum, k_sum, v_sum, stats):
        k_sum[...] = jnp.zeros_like(k_sum)
        v_sum[...] = jnp.zeros_like(v_sum)
        for i in range(rows // tq):
            at, keys = (slice(i * tq, (i + 1) * tq), (i + 1) * tq)
            scores = mm(qr[at, :], kr[:keys, :], ((1,), (1,))) * scaling
            allowed = seen(i * tq, tq, keys, sc[at, :], sr[:, :keys])
            p = jnp.exp(jnp.where(allowed, scores, masked_score) - lt[0, at, :])
            grad_weights = mm(ga[at, :], v[:keys, :], ((1,), (1,)))
            delta = jnp.sum(p * grad_weights, axis=-1, keepdims=True)
            grad_scores = (scaling * p * (grad_weights - delta)).astype(jnp.bfloat16)
            q_sum[at, :] = mm(grad_scores, kr[:keys, :], ((1,), (0,)))
            k_sum[:keys, :] += mm(grad_scores, qr[at, :], ((0,), (0,)))
            v_sum[:keys, :] += mm(p.astype(jnp.bfloat16), ga[at, :], ((0,), (0,)))

        first = pl.program_id(0) == 0

        def back(total, ref, r, g, out, place, gain):
            values = total[...]
            values = values * cos[...] - pltpu.roll(values, HEAD // 2, 1) * sin[...]
            gain[...] = jnp.sum(values * ref[...] * r[...], axis=0, keepdims=True)
            values = values * g[...]
            stat = jnp.sum(values * ref[...], axis=-1, keepdims=True)
            stats[place] += stat
            out[...] = values

        @pl.when(first)
        def _():
            stats[...] = jnp.zeros_like(stats)

        back(q_sum, q, rq, gq, q_out, 0, gq_out)
        back(k_sum, k, rk, gk, k_out, 1, gk_out)

        @pl.when(pl.program_id(0) == heads - 1)
        def _():
            for i in range(rows // tq):
                at = slice(i * tq, (i + 1) * tq)
                stat_out[:, at] = pair_rows(stats[0, at, :], stats[1, at, :])

        v_out[...] = v_sum[...].astype(jnp.bfloat16)

    def col(offset):
        return pl.BlockSpec((rows, HEAD), lambda h: (0, offset + h))

    row = pl.BlockSpec((1, HEAD), lambda h: (0, h))
    one = pl.BlockSpec((rows, 1), lambda h: (0, 0))
    stat = pl.BlockSpec((1, rows, 1), lambda h: (h, 0, 0))
    table = pl.BlockSpec((rows, HEAD), lambda h: (0, 0))
    full = jnp.float32
    outs = (
        [jax.ShapeDtypeStruct((rows, cols), full)] * 2
        + [jax.ShapeDtypeStruct((rows, cols), jnp.bfloat16)]
        + [jax.ShapeDtypeStruct((8, rows), full)]
        + [jax.ShapeDtypeStruct((1, cols), full)] * 2
    )
    args = (qkv, qkv, q_rot, k_rot, value_in, grad, log_total, r_query, r_key, g_query, g_key, cosine, sine, seg_col, seg_row)
    return pl.pallas_call(
        body,
        grid=(heads,),
        in_specs=[col(0), col(heads), col(0), col(0), col(0), col(0), stat, one, one, row, row, table, table, one,
                  pl.BlockSpec((1, rows), lambda h: (0, 0))],
        out_specs=[col(0), col(0), col(0), pl.BlockSpec((8, rows), lambda h: (0, 0)), row, row],
        out_shape=outs,
        scratch_shapes=[pltpu.VMEM((rows, HEAD), full)] * 3 + [pltpu.VMEM((2, rows, 1), full)],
        compiler_params=pltpu.CompilerParams(vmem_limit_bytes=VMEM_GRANT),
        cost_estimate=cost(10 * heads * rows * rows * HEAD, heads * rows * rows, *args, *outs),
    )(*args)


def normed_gradient(q_grad, k_grad, v_low, qkv, sums, r_query, r_key, w_qkv, x_row, r_attn):
    rows, cols = q_grad.shape
    width = x_row.shape[1]
    shards = sums.shape[0]
    tm = math.gcd(rows, 256)

    def body(qg, kg, v, q, k, sums_ref, rq, rk, w, x, ra, low_ref, out_ref, gain_ref):
        means = pair_columns([sums_ref[d] for d in range(shards)])
        parts = []
        for grad, ref, r_ref, mean in ((qg, q, rq, means[0]), (kg, k, rk, means[1])):
            r = r_ref[...]
            part = r * grad[...] - ref[...] * (r * r * r) * (mean / width)
            parts.append(part.astype(jnp.bfloat16))
        parts.append(v[...])
        for i in range(3):
            low_ref[:, i * cols : (i + 1) * cols] = parts[i]
        total = mm(low_ref[...], w[...], ((1,), (1,)))
        out_ref[...] = total.astype(jnp.bfloat16)
        gain = jnp.sum(total * x[...].astype(jnp.float32) * ra[...], axis=0, keepdims=True)
        first = pl.program_id(0) == 0

        @pl.when(first)
        def _():
            gain_ref[...] = gain

        @pl.when(jnp.logical_not(first))
        def _():
            gain_ref[...] += gain

    def tiled(count, at=0):
        return pl.BlockSpec((tm, count), lambda i: (i, at))

    return grid_call(
        body,
        (rows // tm,),
        [
            tiled(cols),
            tiled(cols),
            tiled(cols),
            tiled(cols),
            tiled(cols, 1),
            pl.BlockSpec((shards, 8, tm), lambda i: (0, 0, i)),
            tiled(1),
            tiled(1),
            pl.BlockSpec((width, 3 * cols), lambda i: (0, 0)),
            tiled(width),
            tiled(1),
        ],
        [tiled(3 * cols), tiled(width), pl.BlockSpec((1, width), lambda i: (0, 0))],
        [
            jax.ShapeDtypeStruct((rows, 3 * cols), jnp.bfloat16),
            jax.ShapeDtypeStruct((rows, width), jnp.bfloat16),
            jax.ShapeDtypeStruct((1, width), jnp.float32),
        ],
        6 * rows * width * cols,
        0,
        q_grad,
        k_grad,
        v_low,
        qkv,
        qkv,
        sums,
        r_query,
        r_key,
        w_qkv,
        x_row,
        r_attn,
    )


def middle(order, nf_own, mid, r_ffn, gain, dy, out_pieces):
    tokens, width = nf_own.shape
    chunk = width // 4

    def body(order_ref, nf, mid_ref, r_ref, gain_ref, dy_ref, p0, p1, p2, p3, grad_ref, low_ref, att_ref, gain_out):
        r = r_ref[...]
        own = mid_ref[...]
        grad = nf[...].astype(jnp.float32)
        gain_out[...] = jnp.sum(grad * own * r, axis=0, keepdims=True)
        grad = grad * gain_ref[...]
        mean = jnp.mean(grad * own, axis=-1, keepdims=True)
        total = dy_ref[...].astype(jnp.float32) + r * grad - own * (r * r * r) * mean
        grad_ref[...] = total
        low_ref[...] = total.astype(jnp.bfloat16)
        for j, piece in enumerate((p0, p1, p2, p3)):
            back = jnp.zeros((tokens, chunk), jnp.float32)
            for k in range(4):
                n = k ^ j
                back = back + mm(
                    low_ref[:, n * chunk : (n + 1) * chunk],
                    piece[:, k * chunk : (k + 1) * chunk],
                    ((1,), (1,)),
                )
            att_ref[order_ref[j]] = back.astype(jnp.bfloat16)

    def whole(*shape):
        return pl.BlockSpec(shape, lambda i, o: (0,) * len(shape))

    outs = [
        jax.ShapeDtypeStruct((tokens, width), jnp.float32),
        jax.ShapeDtypeStruct((tokens, width), jnp.bfloat16),
        jax.ShapeDtypeStruct((4, tokens, chunk), jnp.bfloat16),
        jax.ShapeDtypeStruct((1, width), jnp.float32),
    ]
    return pl.pallas_call(
        body,
        grid_spec=pltpu.PrefetchScalarGridSpec(
            num_scalar_prefetch=1,
            grid=(1,),
            in_specs=[
                whole(tokens, width),
                pl.BlockSpec((tokens, width), lambda i, o: (o[4], 0)),
                pl.BlockSpec((tokens, 1), lambda i, o: (o[4], 0)),
                whole(1, width),
                whole(tokens, width),
                *[whole(chunk, width)] * 4,
            ],
            out_specs=[whole(*o.shape) for o in outs],
        ),
        out_shape=outs,
        compiler_params=pltpu.CompilerParams(vmem_limit_bytes=VMEM_GRANT),
        cost_estimate=cost(2 * tokens * width * width, 0, *out_pieces, *outs),
    )(order, nf_own, mid, r_ffn, gain, dy, *out_pieces)


def out_grad_pieces(order, attended, columns):
    shards, rows, cols = attended.shape
    per_chunk = shards // 4
    count = columns.shape[1]
    tm = math.gcd(cols, 256)

    def body(order_ref, att_ref, col_ref, *outs):
        step = pl.program_id(0)
        for j in range(4):

            @pl.when(step == j)
            def _(j=j):
                outs[j][...] = mm(att_ref[0], col_ref[...], ((0,), (0,))).astype(jnp.bfloat16)

    def place(j):
        return lambda k, i, o: (jnp.where(k < j, 0, jnp.where(k > j, per_chunk - 1, i)), 0)

    outs = [jax.ShapeDtypeStruct((per_chunk * cols, count), jnp.bfloat16)] * 4
    return pl.pallas_call(
        body,
        grid_spec=pltpu.PrefetchScalarGridSpec(
            num_scalar_prefetch=1,
            grid=(4, per_chunk),
            in_specs=[
                pl.BlockSpec((1, rows, cols), lambda k, i, o: (o[k] * per_chunk + i, 0, 0)),
                pl.BlockSpec((rows, count), lambda k, i, o: (0, 0)),
            ],
            out_specs=[pl.BlockSpec((cols, count), place(j)) for j in range(4)],
        ),
        out_shape=outs,
        compiler_params=pltpu.CompilerParams(vmem_limit_bytes=VMEM_GRANT),
        cost_estimate=cost(2 * rows * shards * cols * count, 0, attended, columns, *outs),
    )(order, attended, columns)


def swap(values, bits):
    return lax.ppermute(values, "dp", [(i, i ^ bits) for i in range(4)])


def sum_in_chip(pieces, sent):
    wide = jnp.float32
    kept = pieces[0].astype(wide) + swap(pieces[1], 1).astype(wide)
    return (kept.astype(sent), (pieces[2].astype(wide) + swap(pieces[3], 1).astype(wide)).astype(sent))


def across_by_expert(passed):
    return [swap(passed[e], 2) for e in range(passed.shape[0])]


def add_arrived(kept, arrived):
    return jnp.stack(
        [kept[e].astype(jnp.float32) + a.astype(jnp.float32) for e, a in enumerate(arrived)]
    )


def sum_pieces(pieces, sent):
    kept, passed = sum_in_chip(pieces, sent)
    return kept.astype(jnp.float32) + swap(passed, 2).astype(jnp.float32)


def reorder(values, dp_index, axis):
    size = values.shape[axis] // 4
    return jnp.concatenate(
        [
            lax.dynamic_slice_in_dim(values, (dp_index ^ k) * size, size, axis=axis)
            for k in range(4)
        ],
        axis=axis,
    )


def on_device_heads(
    hidden_in,
    segment_ids,
    routes,
    w_query,
    w_key,
    w_value,
    w_out,
    gain_attn,
    gain_query,
    gain_key,
    gain_ffn,
    w_router,
    w_gate,
    w_up,
    w_down,
    cotangent,
):
    low, full = (jnp.bfloat16, jnp.float32)
    shards = lax.axis_size("seq")
    seq_index, dp_index = (lax.axis_index("seq"), lax.axis_index("dp"))
    tokens, width = hidden_in.shape[1:]
    rows = shards * tokens
    cols = width // shards
    heads = cols // HEAD
    held = w_gate.shape[0]
    expert_count = held * shards
    block_rows = w_query.shape[0]
    chunk = shards * block_rows
    row_seg = segment_ids[0]
    first_row = seq_index * tokens
    barrier = lax.optimization_barrier

    def own_cols(values, count):
        return lax.dynamic_slice_in_dim(values, seq_index * count, count, axis=values.ndim - 1)

    cosine, sine = rope_tables(rows, HEAD)
    seg_col, seg_row = (row_seg[:, None], row_seg[None, :])

    x_shard = reorder(hidden_in[0], dp_index, 1)
    x_row = lax.all_gather(x_shard, "seq", axis=0, tiled=True)
    blocks = jnp.stack(
        [w.reshape(block_rows, shards, cols).transpose(1, 0, 2) for w in (w_query, w_key, w_value)],
        axis=1,
    )
    blocks = blocks.reshape(shards, 3 * block_rows, cols)
    place_at = (dp_index * shards + seq_index) * block_rows
    gain_rows = lax.dynamic_update_slice(
        jnp.zeros((shards, 16, cols), low),
        jnp.stack([gain_query, gain_key])[None],
        (place_at // cols, 0, place_at % cols),
    )
    gain_rows = lax.dynamic_update_slice(
        gain_rows, jnp.broadcast_to(gain_attn[None, None], (shards, 1, block_rows)), (0, 2, 0)
    )
    blocks = lax.all_to_all(jnp.concatenate([blocks, gain_rows], axis=1), "seq", 0, 0, tiled=True)
    across = swap(blocks, 2)
    qkv_pieces = (blocks, swap(blocks, 1), across, swap(across, 1))
    gate_across = swap(w_gate, 2)
    gate_full = jnp.concatenate([w_gate, swap(w_gate, 1), gate_across, swap(gate_across, 1)], axis=1)
    x_row, qkv_pieces, gate_full = barrier((x_row, qkv_pieces, gate_full))

    w_qkv = jnp.concatenate(
        [
            p[:, : 3 * block_rows]
            .reshape(shards, 3, block_rows, cols)
            .transpose(0, 2, 1, 3)
            .reshape(chunk, 3 * cols)
            for p in qkv_pieces
        ],
        axis=0,
    )
    gain_pair = sum(
        jnp.sum(p[:, 3 * block_rows : 3 * block_rows + 2].astype(full), axis=0) for p in qkv_pieces
    )
    g_query, g_key = (gain_pair[0:1], gain_pair[1:2])
    g_attn = jnp.concatenate(
        [p[:, 3 * block_rows + 2, :block_rows].reshape(1, chunk) for p in qkv_pieces], axis=1
    ).astype(full)

    picks = routes.shape[2]
    packed = tokens // block_rows
    extra = jnp.concatenate(
        [routes[0].astype(low).reshape(block_rows, packed * picks), w_router, gain_ffn[:, None]],
        axis=1,
    )
    extra = jnp.pad(extra, ((0, 0), (0, 128 - extra.shape[1])))
    out_own = lax.all_gather(
        jnp.concatenate([reorder(w_out, dp_index, 1), extra], axis=1), "seq", axis=0, tiled=True
    )
    up_across = swap(w_up, 2)

    def share(sums):
        spread = jnp.broadcast_to(sums[None], (shards,) + sums.shape)
        return lax.all_to_all(spread, "seq", 0, 0, tiled=True)

    normed, qkv, r_attn, sums = project(x_row, g_attn, w_qkv)
    q_rot, k_rot, value_in, attended, log_total, r_query, r_key = attend(
        qkv, share(sums), width, g_query, g_key, cosine, sine, seg_col, seg_row
    )
    attended, out_own, up_across = barrier((attended, out_own, up_across))

    attended_row = lax.all_gather(attended, "seq", axis=0)
    out_across = swap(out_own, 2)
    out_pieces = (out_own, swap(out_own, 1), out_across, swap(out_across, 1))
    extras = [p[:, width:] for p in out_pieces]
    routes_row = extras[0][:, : packed * picks].reshape(rows, picks).astype(jnp.int32)
    extras = jnp.concatenate([p[:, packed * picks :] for p in extras], axis=0)
    router = jnp.pad(extras[:, :expert_count], ((0, 0), (0, 128 - expert_count)))
    g_ffn = extras[:, expert_count].astype(full)[None]
    lane_ids = lax.iota(jnp.int32, 128)
    chosen = jnp.any(routes_row[:, :, None] == lane_ids[None, None, :], axis=1).astype(full)
    own = (
        lane_ids[None, :] == seq_index * held + lax.iota(jnp.int32, held)[:, None]
    ).astype(full)
    up_full = jnp.concatenate([w_up, swap(w_up, 1), up_across, swap(up_across, 1)], axis=1)
    attended_row, out_pieces, up_full, router, g_ffn, chosen = barrier(
        (attended_row, out_pieces, up_full, router, g_ffn, chosen)
    )

    dy_shard, attended_row = barrier((reorder(cotangent[0], dp_index, 1), attended_row))
    dy_row = lax.all_gather(dy_shard, "seq", axis=0, tiled=True)
    order = jnp.stack([dp_index ^ k for k in range(4)] + [seq_index]).astype(jnp.int32)
    hidden_mid, normed_ffn, r_ffn, chances, gates = finish_attention(
        order, attended_row, out_pieces, x_row, g_ffn, router, chosen, own, expert_count
    )
    act, dgate_factor, dup_factor = expert_activations(normed_ffn, gate_full, up_full)
    act, down_across = barrier((act, swap(w_down, 2)))
    down_full = jnp.concatenate([w_down, swap(w_down, 1), down_across, swap(down_across, 1)], axis=2)
    mixture = combine_experts(act, down_full, gates)
    dy_row, mixture, act = barrier((dy_row, mixture, act))

    scaled, dgate, dup, gate_sums = expert_gradients(
        dy_row, down_full, act, dgate_factor, dup_factor, gates
    )
    nf_grad, grad_logits = input_gradient(
        dgate, dup, gate_full, up_full, gate_sums, chances, chosen, own, router
    )
    nf_sum = lax.psum_scatter(nf_grad, "seq", scatter_dimension=0, tiled=True)

    down_kept, down_passed = sum_in_chip(weight_pieces(scaled, dy_row, 4, False), low)
    gate_pieces = weight_pieces(normed_ffn, dgate, 4, True)
    dup, down_passed = barrier((dup, down_passed))
    down_arrived = across_by_expert(down_passed)
    gate_kept, gate_passed = sum_in_chip(gate_pieces, low)
    up_pieces = weight_pieces(normed_ffn, dup, 4, True)
    nf_sum, mixture, up_pieces, down_arrived[0], gate_passed = barrier(
        (nf_sum, mixture, up_pieces, down_arrived[0], gate_passed)
    )
    mixture_own = lax.psum_scatter(mixture, "seq", scatter_dimension=0, tiled=True)
    up_kept, up_passed = sum_in_chip(up_pieces, low)
    router_grad = mm(grad_logits[:, :expert_count], normed_ffn, ((0,), (0,)))
    nf_sum, down_arrived[1], up_passed, router_grad = barrier(
        (nf_sum, down_arrived[1], up_passed, router_grad)
    )
    gate_arrived, up_arrived = (across_by_expert(gate_passed), across_by_expert(up_passed))

    grad_mid, mid_low, grad_attended, gain_ffn_grad = middle(
        order, nf_sum, hidden_mid, r_ffn, g_ffn, dy_shard, out_pieces
    )
    grad_attended, gate_arrived[0] = barrier((grad_attended, gate_arrived[0]))

    def to_columns(values):
        return lax.all_to_all(values, "seq", 0, 0, tiled=True).reshape(rows, cols)

    grad_attended = grad_attended.reshape(4, tokens, shards // 4, cols).transpose(0, 2, 1, 3)
    grad_attended = to_columns(grad_attended.reshape(shards, tokens, cols))
    grad_attended, gate_arrived[1] = barrier((grad_attended, gate_arrived[1]))
    mid_cols = to_columns(
        reorder(mid_low, dp_index, 1).reshape(tokens, shards, cols).transpose(1, 0, 2)
    )
    q_grad, k_grad, v_low, sums, gain_query_grad, gain_key_grad = attend_back(
        qkv, q_rot, k_rot, value_in, grad_attended, log_total,
        r_query, r_key, g_query, g_key, cosine, sine, seg_col, seg_row,
    )
    sums, up_arrived[0] = barrier((sums, up_arrived[0]))
    sums, mid_cols = barrier((share(sums), mid_cols))
    qkv_low, normed_grad, gain_attn_grad = normed_gradient(
        q_grad, k_grad, v_low, qkv, sums, r_query, r_key, w_qkv, x_row, r_attn
    )
    normed_grad, up_arrived[1], mixture_own = barrier((normed_grad, up_arrived[1], mixture_own))
    normed_sum = lax.psum_scatter(normed_grad, "seq", scatter_dimension=0, tiled=True).astype(full)

    def to_owners(kept, passed, count):
        total = kept.astype(full) + swap(passed, 2).astype(full)
        total = lax.all_to_all(
            total.astype(low).reshape(shards, block_rows, count * cols), "seq", 0, 0, tiled=True
        )
        total = total.reshape(shards, block_rows, count, cols).transpose(2, 1, 0, 3)
        return total.reshape(count, block_rows, width).astype(full)

    out_kept, out_passed = sum_in_chip(out_grad_pieces(order, attended_row, mid_cols), low)
    out_grad = to_owners(out_kept, out_passed, 1)
    qkv_kept, qkv_passed = sum_in_chip(
        [p[0] for p in weight_pieces(normed, qkv_low[None], 4, True)], low
    )
    proj_grad = to_owners(qkv_kept, qkv_passed, 3)
    grad_w_down = add_arrived(down_kept, down_arrived)
    grad_w_gate = add_arrived(gate_kept, gate_arrived)
    grad_w_up = add_arrived(up_kept, up_arrived)
    mid_own = lax.dynamic_slice_in_dim(hidden_mid, first_row, tokens)
    block_out = (mid_own + mixture_own.astype(full)).astype(low)
    normed_sum, grad_w_down, grad_w_gate, grad_w_up, out_grad, block_out = barrier(
        (normed_sum, grad_w_down, grad_w_gate, grad_w_up, out_grad, block_out)
    )

    x_own = x_shard.astype(full)
    r_here = lax.rsqrt(jnp.mean(x_own * x_own, axis=-1, keepdims=True) + epsilon)
    scaled_grad = normed_sum * g_attn
    grad_hidden = (
        grad_mid
        + r_here * scaled_grad
        - x_own * (r_here**3) * jnp.mean(scaled_grad * x_own, axis=-1, keepdims=True)
    )

    def place(values):
        whole = lax.dynamic_update_slice_in_dim(
            jnp.zeros((1, width), full), values[None], seq_index * cols, 1
        )
        return reorder(whole, dp_index, 1)

    vectors = jnp.concatenate(
        [
            router_grad,
            gain_attn_grad,
            place(gain_query_grad[0]),
            place(gain_key_grad[0]),
            gain_ffn_grad,
        ]
    )
    count = vectors.shape[0]
    vectors = sum_pieces([vectors[:, k * chunk : (k + 1) * chunk] for k in range(4)], full)
    vectors = vectors.reshape(count, shards, block_rows).transpose(1, 0, 2)
    vectors = jnp.sum(lax.all_to_all(vectors, "seq", 0, 0, tiled=True), axis=0)
    return (
        reorder(block_out, dp_index, 1)[None],
        reorder(grad_hidden, dp_index, 1)[None],
        proj_grad[0],
        proj_grad[1],
        proj_grad[2],
        out_grad[0],
        vectors[expert_count],
        vectors[expert_count + 1],
        vectors[expert_count + 2],
        vectors[expert_count + 3],
        vectors[:expert_count].T,
        grad_w_gate,
        grad_w_up,
        grad_w_down,
    )


def solution(mesh):
    def layer(*arrays):
        whole_heads = (arrays[0].shape[2] // HEAD) % mesh.shape["seq"] == 0
        if whole_heads and mesh.shape["dp"] == 4:
            return on_device_heads(*arrays)
        return on_device(*arrays)

    return jax.shard_map(
        layer,
        mesh=mesh,
        in_specs=(
            P("dp", "seq", None),
            P("dp", None),
            P("dp", "seq", None),
            P(("dp", "seq"), None),
            P(("dp", "seq"), None),
            P(("dp", "seq"), None),
            P(("dp", "seq"), None),
            P(("dp", "seq")),
            P(("dp", "seq")),
            P(("dp", "seq")),
            P(("dp", "seq")),
            P(("dp", "seq"), None),
            P("seq", "dp", None),
            P("seq", "dp", None),
            P("seq", None, "dp"),
            P("dp", "seq", None),
        ),
        out_specs=(
            P("dp", "seq", None),
            P("dp", "seq", None),
            P(("dp", "seq"), None),
            P(("dp", "seq"), None),
            P(("dp", "seq"), None),
            P(("dp", "seq"), None),
            P(("dp", "seq")),
            P(("dp", "seq")),
            P(("dp", "seq")),
            P(("dp", "seq")),
            P(("dp", "seq"), None),
            P("seq", "dp", None),
            P("seq", "dp", None),
            P("seq", None, "dp"),
        ),
        check_vma=False,
    )
```

```python
import math

import jax
import jax.numpy as jnp
from jax import lax
from jax.experimental import pallas as pl
from jax.experimental.pallas import tpu as pltpu
from jax.sharding import PartitionSpec as P

HEAD = 128


epsilon = 1e-05
masked_score = -1e30
rope_base = 10000.0


def normalize(values, gain_vec):
    return (
        values * lax.rsqrt(jnp.mean(values * values, axis=-1, keepdims=True) + epsilon) * gain_vec
    )


def rotary(values, positions):
    half_dim = values.shape[-1] // 2
    frequency = jnp.exp(
        jnp.arange(half_dim, dtype=jnp.float32) * (-2.0 * math.log(rope_base) / values.shape[-1])
    )
    angles = positions.astype(jnp.float32)[:, None] * frequency[None, :]
    cosine = jnp.cos(angles)[:, None, :]
    sine_table = jnp.sin(angles)[:, None, :]
    first_half = values[..., :half_dim]
    second = values[..., half_dim:]
    return jnp.concatenate(
        [first_half * cosine - second * sine_table, second * cosine + first_half * sine_table],
        axis=-1,
    )


def softmax_rows(values):
    peak_value = jnp.max(values, axis=-1, keepdims=True)
    raised = jnp.exp(values - peak_value)
    return raised / jnp.sum(raised, axis=-1, keepdims=True)


def rotate_normed(projection, gain_vec, positions):
    tokens, model_width = projection.shape
    return rotary(
        normalize(projection, gain_vec).reshape(tokens, model_width // HEAD, HEAD), positions
    )


def masked_scores(queries, key_block, query_pos, query_seg, key_pos, key_seg, scaling):
    raw_scores = jnp.einsum("qhd,khd->hqk", queries, key_block, preferred_element_type=jnp.float32)
    allowed = (query_pos[:, None] >= key_pos[None, :]) & (query_seg[:, None] == key_seg[None, :])
    return jnp.where(allowed[None], raw_scores * scaling, masked_score)


def key_window(keys_all, values_all, row_seg, begin_at, span):
    key_block = lax.dynamic_slice_in_dim(keys_all, begin_at, span)
    value_block = lax.dynamic_slice_in_dim(values_all, begin_at, span)
    key_pos = begin_at + lax.iota(jnp.int32, span)
    key_seg = lax.dynamic_slice_in_dim(row_seg, begin_at, span)
    return (key_block, value_block, key_pos, key_seg)


def project_front(hidden, layer_full, positions):
    tokens, model_width = hidden.shape
    normed = normalize(hidden, layer_full[5].astype(jnp.float32)).astype(jnp.bfloat16)
    query = jnp.dot(normed, layer_full[0], preferred_element_type=jnp.float32)
    key_proj = jnp.dot(normed, layer_full[1], preferred_element_type=jnp.float32)
    value_proj = jnp.dot(normed, layer_full[2], preferred_element_type=jnp.float32)
    query_rot = rotate_normed(query, layer_full[6].astype(jnp.float32), positions).astype(
        jnp.bfloat16
    )
    key_rot = rotate_normed(key_proj, layer_full[7].astype(jnp.float32), positions).astype(
        jnp.bfloat16
    )
    value_in = value_proj.astype(jnp.bfloat16).reshape(tokens, model_width // HEAD, HEAD)
    return (normed, query, key_proj, query_rot, key_rot, value_in)


def attend_local(query_rot, keys_all, values_all, row_seg, offset, span):
    tokens, head_count, head_dim = query_rot.shape
    scaling = head_dim ** (-0.5)
    query_pos = offset + lax.iota(jnp.int32, tokens)
    query_seg = lax.dynamic_slice_in_dim(row_seg, offset, tokens)
    reach_blocks = (offset + tokens + span - 1) // span

    def block_scores(block_index):
        begin_at = block_index * span
        key_block, value_block, key_pos, key_seg = key_window(
            keys_all, values_all, row_seg, begin_at, span
        )
        return (
            masked_scores(query_rot, key_block, query_pos, query_seg, key_pos, key_seg, scaling),
            value_block,
        )

    def first_pass(block_index, state_pair):
        peak_value, denominator = state_pair
        scores, unused_values = block_scores(block_index)
        new_peak = jnp.maximum(peak_value, jnp.max(scores, axis=-1))
        denominator = denominator * jnp.exp(peak_value - new_peak) + jnp.sum(
            jnp.exp(scores - new_peak[..., None]), axis=-1
        )
        return (new_peak, denominator)

    start_state = (
        jnp.full((head_count, tokens), masked_score, jnp.float32),
        jnp.zeros((head_count, tokens), jnp.float32),
    )
    peak_value, denominator = lax.fori_loop(0, reach_blocks, first_pass, start_state)
    log_total = peak_value + jnp.log(denominator)

    def second_pass(block_index, running):
        scores, value_block = block_scores(block_index)
        weights = jnp.exp(scores - log_total[..., None]).astype(jnp.bfloat16)
        return running + jnp.einsum(
            "hqk,khd->qhd", weights, value_block, preferred_element_type=jnp.float32
        )

    attention = lax.fori_loop(
        0, reach_blocks, second_pass, jnp.zeros((tokens, head_count, head_dim), jnp.float32)
    )
    return (attention, log_total)


def query_grads(query_rot, keys_all, values_all, row_seg, offset, span, log_total, grad_attended):
    tokens, head_count, head_dim = query_rot.shape
    scaling = head_dim ** (-0.5)
    query_pos = offset + lax.iota(jnp.int32, tokens)
    query_seg = lax.dynamic_slice_in_dim(row_seg, offset, tokens)
    reach_blocks = (offset + tokens + span - 1) // span

    def block_terms(block_index):
        begin_at = block_index * span
        key_block, value_block, key_pos, key_seg = key_window(
            keys_all, values_all, row_seg, begin_at, span
        )
        scores = masked_scores(
            query_rot, key_block, query_pos, query_seg, key_pos, key_seg, scaling
        )
        weights = jnp.exp(scores - log_total[..., None])
        grad_weights = jnp.einsum(
            "qhd,khd->hqk", grad_attended, value_block, preferred_element_type=jnp.float32
        )
        return (key_block, weights, grad_weights)

    def delta_pass(block_index, running):
        unused_keys, weights, grad_weights = block_terms(block_index)
        return running + jnp.sum(weights * grad_weights, axis=-1)

    delta = lax.fori_loop(0, reach_blocks, delta_pass, jnp.zeros((head_count, tokens), jnp.float32))

    def query_pass(block_index, running):
        key_block, weights, grad_weights = block_terms(block_index)
        grad_scores = (weights * (grad_weights - delta[..., None]) * scaling).astype(jnp.bfloat16)
        return running + jnp.einsum(
            "hqk,khd->qhd", grad_scores, key_block, preferred_element_type=jnp.float32
        )

    grad_query_rot = lax.fori_loop(
        0, reach_blocks, query_pass, jnp.zeros((tokens, head_count, head_dim), jnp.float32)
    )
    return (delta, grad_query_rot)


def route_tokens(hidden_mid, layer_full, choice_rows):
    tokens, pick_count = choice_rows.shape
    normed_ffn = normalize(hidden_mid, layer_full[8].astype(jnp.float32)).astype(jnp.bfloat16)
    logits = jnp.dot(normed_ffn, layer_full[4], preferred_element_type=jnp.float32)
    expert_count = logits.shape[1]
    capacity = 3 * tokens * pick_count // (2 * expert_count)
    chances = softmax_rows(logits)
    picks = choice_rows[:, :, None] == lax.iota(jnp.int32, expert_count)[None, None, :]
    gate_values = jnp.sum(jnp.where(picks, chances[:, None, :], 0.0), axis=-1)
    flat_hits = picks.reshape(tokens * pick_count, expert_count).astype(jnp.int32)
    earlier = jnp.cumsum(flat_hits, axis=0) - flat_hits
    slot_ids = choice_rows.reshape(-1) * capacity + jnp.sum(earlier * flat_hits, axis=1)
    pair_table = lax.iota(jnp.int32, expert_count * capacity)[:, None] == slot_ids[None, :]
    spread = jnp.sum(
        pair_table.reshape(expert_count * capacity, tokens, pick_count).astype(jnp.int32), axis=2
    ).astype(jnp.bfloat16)
    send_rows = jnp.dot(spread, normed_ffn, preferred_element_type=jnp.float32).astype(jnp.bfloat16)
    send_rows = send_rows.reshape(expert_count, capacity, hidden_mid.shape[1])
    return (normed_ffn, chances, picks, gate_values, slot_ids, pair_table, spread, send_rows)


def group_rows(row_block, held_experts):
    sources = row_block.shape[0] // held_experts
    grouped = row_block.reshape(
        sources, held_experts, row_block.shape[1], row_block.shape[2]
    ).transpose(1, 0, 2, 3)
    return grouped.reshape(held_experts, sources * row_block.shape[1], row_block.shape[2])


def ungroup_rows(grouped, whole_shape):
    held_experts = grouped.shape[0]
    sources = whole_shape[0] // held_experts
    spread_out = grouped.reshape(held_experts, sources, whole_shape[1], whole_shape[2]).transpose(
        1, 0, 2, 3
    )
    return spread_out.reshape(whole_shape)


def expert_forward(row_block, gate_full, up_full, down_full):
    inputs = group_rows(row_block, gate_full.shape[0])
    gate_pre = jnp.einsum("erd,edf->erf", inputs, gate_full, preferred_element_type=jnp.float32)
    up_pre = jnp.einsum("erd,edf->erf", inputs, up_full, preferred_element_type=jnp.float32)
    activated = (gate_pre * lax.logistic(gate_pre) * up_pre).astype(jnp.bfloat16)
    result = jnp.einsum(
        "erf,efd->erd", activated, down_full, preferred_element_type=jnp.float32
    ).astype(jnp.bfloat16)
    return ungroup_rows(result, row_block.shape)


def expert_backward(row_block, grad_block, gate_full, up_full, down_full):
    inputs = group_rows(row_block, gate_full.shape[0])
    grad_outputs = group_rows(grad_block, gate_full.shape[0])
    gate_pre = jnp.einsum("erd,edf->erf", inputs, gate_full, preferred_element_type=jnp.float32)
    up_pre = jnp.einsum("erd,edf->erf", inputs, up_full, preferred_element_type=jnp.float32)
    sigmoid_gate = lax.logistic(gate_pre)
    activated = (gate_pre * sigmoid_gate * up_pre).astype(jnp.bfloat16)
    grad_act = jnp.einsum(
        "erd,efd->erf", grad_outputs, down_full, preferred_element_type=jnp.float32
    )
    grad_down = jnp.einsum(
        "erf,erd->efd", activated, grad_outputs, preferred_element_type=jnp.float32
    )
    grad_gate_pre = (
        grad_act * up_pre * sigmoid_gate * (1.0 + gate_pre * (1.0 - sigmoid_gate))
    ).astype(jnp.bfloat16)
    grad_up_pre = (grad_act * gate_pre * sigmoid_gate).astype(jnp.bfloat16)
    grad_gate_w = jnp.einsum(
        "erd,erf->edf", inputs, grad_gate_pre, preferred_element_type=jnp.float32
    )
    grad_up_w = jnp.einsum("erd,erf->edf", inputs, grad_up_pre, preferred_element_type=jnp.float32)
    grad_inputs = jnp.einsum(
        "erf,edf->erd", grad_gate_pre, gate_full, preferred_element_type=jnp.float32
    )
    grad_inputs = grad_inputs + jnp.einsum(
        "erf,edf->erd", grad_up_pre, up_full, preferred_element_type=jnp.float32
    )
    return (
        ungroup_rows(grad_inputs.astype(jnp.bfloat16), row_block.shape),
        grad_gate_w,
        grad_up_w,
        grad_down,
    )


def contract_rows(left, right):
    return lax.dot_general(
        left, right, (((0,), (0,)), ((), ())), preferred_element_type=jnp.float32
    )


def contract_cols(left, right):
    return lax.dot_general(
        left, right, (((1,), (1,)), ((), ())), preferred_element_type=jnp.float32
    )


def on_device(
    hidden_in,
    segment_ids,
    routes,
    w_query,
    w_key,
    w_value,
    w_out,
    gain_attn,
    gain_query,
    gain_key,
    gain_ffn,
    w_router,
    w_gate,
    w_up,
    w_down,
    cotangent,
):
    hidden = hidden_in[0].astype(jnp.float32)
    tokens, model_width = hidden.shape
    head_count = model_width // HEAD
    row_seg = segment_ids[0]
    choice_rows = routes[0]
    offset = lax.axis_index("seq") * tokens
    positions = offset + lax.iota(jnp.int32, tokens)
    span = min(512, row_seg.shape[0])
    layer_full = (
        lax.all_gather(w_query, ("dp", "seq"), axis=0, tiled=True),
        lax.all_gather(w_key, ("dp", "seq"), axis=0, tiled=True),
        lax.all_gather(w_value, ("dp", "seq"), axis=0, tiled=True),
        lax.all_gather(w_out, ("dp", "seq"), axis=0, tiled=True),
        lax.all_gather(w_router, ("dp", "seq"), axis=0, tiled=True),
        lax.all_gather(gain_attn, ("dp", "seq"), axis=0, tiled=True),
        lax.all_gather(gain_query, ("dp", "seq"), axis=0, tiled=True),
        lax.all_gather(gain_key, ("dp", "seq"), axis=0, tiled=True),
        lax.all_gather(gain_ffn, ("dp", "seq"), axis=0, tiled=True),
    )
    expert_full = (
        lax.all_gather(w_gate, "dp", axis=1, tiled=True),
        lax.all_gather(w_up, "dp", axis=1, tiled=True),
        lax.all_gather(w_down, "dp", axis=2, tiled=True),
    )
    projected = project_front(hidden, layer_full, positions)
    keys_all, values_all = (
        lax.all_gather(projected[4], "seq", axis=0, tiled=True),
        lax.all_gather(projected[5], "seq", axis=0, tiled=True),
    )
    attention, log_total = attend_local(projected[3], keys_all, values_all, row_seg, offset, span)
    attended = attention.reshape(tokens, model_width).astype(jnp.bfloat16)
    hidden_mid = hidden + jnp.dot(attended, layer_full[3], preferred_element_type=jnp.float32)
    routing = route_tokens(hidden_mid, layer_full, choice_rows)
    expert_count, capacity = (routing[7].shape[0], routing[7].shape[1])
    expert_out = expert_forward(
        lax.all_to_all(routing[7], "seq", split_axis=0, concat_axis=0, tiled=True),
        expert_full[0],
        expert_full[1],
        expert_full[2],
    )
    returned = lax.all_to_all(expert_out, "seq", split_axis=0, concat_axis=0, tiled=True)
    picked = jnp.take(returned.reshape(expert_count * capacity, model_width), routing[4], axis=0)
    picked = picked.reshape(tokens, choice_rows.shape[1], model_width)
    mixture = jnp.sum(routing[3][:, :, None] * picked.astype(jnp.float32), axis=1)
    block_out = (hidden_mid + mixture).astype(jnp.bfloat16)
    layer_full = (
        lax.all_gather(w_query, ("dp", "seq"), axis=0, tiled=True),
        lax.all_gather(w_key, ("dp", "seq"), axis=0, tiled=True),
        lax.all_gather(w_value, ("dp", "seq"), axis=0, tiled=True),
        lax.all_gather(w_out, ("dp", "seq"), axis=0, tiled=True),
        lax.all_gather(w_router, ("dp", "seq"), axis=0, tiled=True),
        lax.all_gather(gain_attn, ("dp", "seq"), axis=0, tiled=True),
        lax.all_gather(gain_query, ("dp", "seq"), axis=0, tiled=True),
        lax.all_gather(gain_key, ("dp", "seq"), axis=0, tiled=True),
        lax.all_gather(gain_ffn, ("dp", "seq"), axis=0, tiled=True),
    )
    expert_full = (
        lax.all_gather(w_gate, "dp", axis=1, tiled=True),
        lax.all_gather(w_up, "dp", axis=1, tiled=True),
        lax.all_gather(w_down, "dp", axis=2, tiled=True),
    )
    projected = project_front(hidden, layer_full, positions)
    keys_all, values_all = (
        lax.all_gather(projected[4], "seq", axis=0, tiled=True),
        lax.all_gather(projected[5], "seq", axis=0, tiled=True),
    )
    attention, log_total = attend_local(projected[3], keys_all, values_all, row_seg, offset, span)
    attended = attention.reshape(tokens, model_width).astype(jnp.bfloat16)
    hidden_mid = hidden + jnp.dot(attended, layer_full[3], preferred_element_type=jnp.float32)
    routing = route_tokens(hidden_mid, layer_full, choice_rows)
    normed_ffn, chances, picks, gate_values, slot_ids, pair_table, spread, send_rows = routing
    grad_out = cotangent[0].astype(jnp.float32)
    grad_gates = jnp.sum(grad_out[:, None, :] * picked.astype(jnp.float32), axis=-1)
    slot_gates = jnp.sum(jnp.where(pair_table, gate_values.reshape(-1)[None, :], 0.0), axis=1)
    grad_rows_in = jnp.dot(spread, cotangent[0], preferred_element_type=jnp.float32)
    grad_slots = (
        (slot_gates[:, None] * grad_rows_in)
        .astype(jnp.bfloat16)
        .reshape(expert_count, capacity, model_width)
    )
    arrived_rows, arrived_grads = (
        lax.all_to_all(send_rows, "seq", split_axis=0, concat_axis=0, tiled=True),
        lax.all_to_all(grad_slots, "seq", split_axis=0, concat_axis=0, tiled=True),
    )
    grad_inputs, grad_gate_w, grad_up_w, grad_down_w = expert_backward(
        arrived_rows, arrived_grads, expert_full[0], expert_full[1], expert_full[2]
    )
    grad_back = lax.all_to_all(grad_inputs, "seq", split_axis=0, concat_axis=0, tiled=True)
    grad_normed_ffn = contract_rows(spread, grad_back.reshape(expert_count * capacity, model_width))
    grad_chances = jnp.sum(jnp.where(picks, grad_gates[:, :, None], 0.0), axis=1)
    grad_logits = (
        chances * (grad_chances - jnp.sum(chances * grad_chances, axis=-1, keepdims=True))
    ).astype(jnp.bfloat16)
    grad_router_w = contract_rows(normed_ffn, grad_logits)
    grad_normed_ffn = grad_normed_ffn + contract_cols(grad_logits, layer_full[4])
    unused_ffn, pull_ffn = jax.vjp(normalize, hidden_mid, layer_full[8].astype(jnp.float32))
    grad_mid_norm, grad_gain_ffn_w = pull_ffn(grad_normed_ffn)
    grad_mid = grad_out + grad_mid_norm
    grad_mid_low = grad_mid.astype(jnp.bfloat16)
    grad_w_out = contract_rows(attended, grad_mid_low)
    grad_attended = (
        contract_cols(grad_mid_low, layer_full[3])
        .astype(jnp.bfloat16)
        .reshape(tokens, head_count, HEAD)
    )
    query_rot = projected[3]
    delta, grad_query_rot = query_grads(
        query_rot, keys_all, values_all, row_seg, offset, span, log_total, grad_attended
    )
    scaling = HEAD ** (-0.5)
    query_seg = lax.dynamic_slice_in_dim(row_seg, offset, tokens)
    row_count = lax.axis_size("seq") * tokens
    step_rows = math.gcd(row_count, 512)

    def one_window(window_index, running):
        window_start = window_index * step_rows
        key_block, value_block, key_pos, key_seg = key_window(
            keys_all, values_all, row_seg, window_start, step_rows
        )
        scores = masked_scores(
            query_rot, key_block, positions, query_seg, key_pos, key_seg, scaling
        )
        weights = jnp.exp(scores - log_total[..., None])
        grad_weights = jnp.einsum(
            "qhd,khd->hqk", grad_attended, value_block, preferred_element_type=jnp.float32
        )
        grad_scores = (weights * (grad_weights - delta[..., None]) * scaling).astype(jnp.bfloat16)
        grad_key_part = jnp.einsum(
            "hqk,qhd->khd", grad_scores, query_rot, preferred_element_type=jnp.float32
        )
        grad_value_part = jnp.einsum(
            "hqk,qhd->khd",
            weights.astype(jnp.bfloat16),
            grad_attended,
            preferred_element_type=jnp.float32,
        )
        term = jnp.concatenate(
            [
                grad_key_part.reshape(step_rows, model_width),
                grad_value_part.reshape(step_rows, model_width),
            ],
            axis=1,
        )
        return lax.dynamic_update_slice_in_dim(running, term, window_index * step_rows, 0)

    key_sums = lax.psum_scatter(
        lax.fori_loop(
            0,
            row_count // step_rows,
            one_window,
            jnp.zeros((row_count, 2 * model_width), jnp.float32),
        ).astype(jnp.bfloat16),
        "seq",
        scatter_dimension=0,
        tiled=True,
    ).astype(jnp.float32)
    grad_key_rot = key_sums[:, :model_width].reshape(tokens, head_count, HEAD)
    grad_v_low = key_sums[:, model_width:].astype(jnp.bfloat16)

    def query_chain(projection, gain_vec):
        return rotate_normed(projection, gain_vec, positions)

    unused_query, pull_query = jax.vjp(query_chain, projected[1], layer_full[6].astype(jnp.float32))
    grad_query_pre, grad_gain_query_w = pull_query(grad_query_rot)
    unused_key, pull_key = jax.vjp(query_chain, projected[2], layer_full[7].astype(jnp.float32))
    grad_key_pre, grad_gain_key_w = pull_key(grad_key_rot)
    grad_q_low = grad_query_pre.astype(jnp.bfloat16)
    grad_k_low = grad_key_pre.astype(jnp.bfloat16)
    normed = projected[0]
    grad_w_query = contract_rows(normed, grad_q_low)
    grad_w_key = contract_rows(normed, grad_k_low)
    grad_w_value = contract_rows(normed, grad_v_low)
    grad_normed = (
        contract_cols(grad_q_low, layer_full[0])
        + contract_cols(grad_k_low, layer_full[1])
        + contract_cols(grad_v_low, layer_full[2])
    )
    unused_attn, pull_attn = jax.vjp(normalize, hidden, layer_full[5].astype(jnp.float32))
    grad_hidden_norm, grad_gain_attn_w = pull_attn(grad_normed)
    grad_hidden = grad_mid + grad_hidden_norm
    shares = (
        lax.psum_scatter(grad_w_query, ("dp", "seq"), scatter_dimension=0, tiled=True),
        lax.psum_scatter(grad_w_key, ("dp", "seq"), scatter_dimension=0, tiled=True),
        lax.psum_scatter(grad_w_value, ("dp", "seq"), scatter_dimension=0, tiled=True),
        lax.psum_scatter(grad_w_out, ("dp", "seq"), scatter_dimension=0, tiled=True),
        lax.psum_scatter(grad_router_w, ("dp", "seq"), scatter_dimension=0, tiled=True),
        lax.psum_scatter(grad_gain_attn_w, ("dp", "seq"), scatter_dimension=0, tiled=True),
        lax.psum_scatter(grad_gain_query_w, ("dp", "seq"), scatter_dimension=0, tiled=True),
        lax.psum_scatter(grad_gain_key_w, ("dp", "seq"), scatter_dimension=0, tiled=True),
        lax.psum_scatter(grad_gain_ffn_w, ("dp", "seq"), scatter_dimension=0, tiled=True),
    )
    expert_shares = (
        lax.psum_scatter(
            grad_gate_w.astype(jnp.bfloat16), "dp", scatter_dimension=1, tiled=True
        ).astype(jnp.float32),
        lax.psum_scatter(
            grad_up_w.astype(jnp.bfloat16), "dp", scatter_dimension=1, tiled=True
        ).astype(jnp.float32),
        lax.psum_scatter(
            grad_down_w.astype(jnp.bfloat16), "dp", scatter_dimension=2, tiled=True
        ).astype(jnp.float32),
    )
    return (
        block_out[None],
        grad_hidden[None],
        shares[0],
        shares[1],
        shares[2],
        shares[3],
        shares[5],
        shares[6],
        shares[7],
        shares[8],
        shares[4],
        expert_shares[0],
        expert_shares[1],
        expert_shares[2],
    )


VMEM_GRANT = 56 * 1024 * 1024


def mm(left, right, dims):
    return lax.dot_general(left, right, (dims, ((), ())), preferred_element_type=jnp.float32)


def cost(flops, transcendentals, *arrays):
    moved = sum(math.prod(a.shape) * a.dtype.itemsize for a in arrays)
    return pl.CostEstimate(
        flops=flops // 4, transcendentals=transcendentals // 4, bytes_accessed=moved // 4
    )


def grid_call(body, grid, in_specs, out_specs, outs, flops, transcendentals, *args):
    return pl.pallas_call(
        body,
        grid=grid,
        in_specs=in_specs,
        out_specs=out_specs,
        out_shape=outs,
        compiler_params=pltpu.CompilerParams(vmem_limit_bytes=VMEM_GRANT),
        cost_estimate=cost(flops, transcendentals, *args, *jax.tree.leaves(outs)),
    )(*args)


def row_tiles(rows):
    return math.gcd(rows, 512)


def finish_attention(order, attended, out_pieces, x_row, gain, router, chosen, own, expert_count):
    shards, rows, cols = attended.shape
    width = x_row.shape[1]
    held = own.shape[0]
    chunk = width // 4
    per_chunk = chunk // cols
    tm = math.gcd(rows, 256)

    def body(order_ref, att_ref, p0, p1, p2, p3, x_ref, gain_ref, router_ref, chosen_ref, own_ref, *outs):
        mid_ref, normed_ref, r_ref, chance_ref, gate_ref, att_all = outs
        for h in range(shards):
            source = order_ref[h // per_chunk] * per_chunk + h % per_chunk
            att_all[:, h * cols : (h + 1) * cols] = att_ref[source]
        squares = jnp.zeros((tm, 1), jnp.float32)
        for n in range(4):
            at = slice(n * chunk, (n + 1) * chunk)
            total = x_ref[:, at].astype(jnp.float32)
            for j, piece in enumerate((p0, p1, p2, p3)):
                k = n ^ j
                total = total + mm(
                    att_all[:, j * chunk : (j + 1) * chunk],
                    piece[:, k * chunk : (k + 1) * chunk],
                    ((1,), (0,)),
                )
            mid_ref[:, at] = total
            squares = squares + jnp.sum(total * total, axis=-1, keepdims=True)
        r = lax.rsqrt(squares / width + epsilon)
        r_ref[...] = r
        logits = jnp.zeros((tm, 128), jnp.float32)
        for n in range(4):
            at = slice(n * chunk, (n + 1) * chunk)
            normed = (mid_ref[:, at] * r * gain_ref[:, at]).astype(jnp.bfloat16)
            normed_ref[:, at] = normed
            logits = logits + mm(normed, router_ref[at, :], ((1,), (0,)))
        lane = lax.broadcasted_iota(jnp.int32, (tm, 128), 1)
        logits = jnp.where(lane < expert_count, logits, masked_score)
        raised = jnp.exp(logits - jnp.max(logits, axis=-1, keepdims=True))
        chances = raised / jnp.sum(raised, axis=-1, keepdims=True)
        chance_ref[...] = chances
        taken = chances * chosen_ref[...]
        for e in range(held):
            gate_ref[e] = jnp.sum(taken * own_ref[e : e + 1, :], axis=-1, keepdims=True)

    full = jnp.float32
    piece_spec = pl.BlockSpec((chunk, width), lambda i, o: (0, 0))
    wide = pl.BlockSpec((tm, width), lambda i, o: (i, 0))
    lanes = pl.BlockSpec((tm, 128), lambda i, o: (i, 0))
    outs = [
        jax.ShapeDtypeStruct((rows, width), full),
        jax.ShapeDtypeStruct((rows, width), jnp.bfloat16),
        jax.ShapeDtypeStruct((rows, 1), full),
        jax.ShapeDtypeStruct((rows, 128), full),
        jax.ShapeDtypeStruct((held, rows, 1), full),
    ]
    return pl.pallas_call(
        body,
        grid_spec=pltpu.PrefetchScalarGridSpec(
            num_scalar_prefetch=1,
            grid=(rows // tm,),
            in_specs=[
                pl.BlockSpec((shards, tm, cols), lambda i, o: (0, i, 0)),
                piece_spec,
                piece_spec,
                piece_spec,
                piece_spec,
                wide,
                pl.BlockSpec((1, width), lambda i, o: (0, 0)),
                pl.BlockSpec((width, 128), lambda i, o: (0, 0)),
                lanes,
                pl.BlockSpec((held, 128), lambda i, o: (0, 0)),
            ],
            out_specs=[
                wide,
                wide,
                pl.BlockSpec((tm, 1), lambda i, o: (i, 0)),
                lanes,
                pl.BlockSpec((held, tm, 1), lambda i, o: (0, i, 0)),
            ],
            scratch_shapes=[pltpu.VMEM((tm, width), jnp.bfloat16)],
        ),
        out_shape=outs,
        compiler_params=pltpu.CompilerParams(vmem_limit_bytes=VMEM_GRANT),
        cost_estimate=cost(2 * rows * width * width, rows * 128, attended, *out_pieces, *outs),
    )(order, attended, *out_pieces, x_row, gain, router, chosen, own)


def expert_activations(normed, gate, up):
    held, width, ff = gate.shape
    rows = normed.shape[0]
    tile, tm = (math.gcd(ff, 512), row_tiles(rows))

    def body(x_ref, gate_ref, up_ref, act_ref, dgate_ref, dup_ref):
        @pl.loop(0, rows // tm)
        def _(i):
            at = pl.ds(pl.multiple_of(i * tm, tm), tm)
            gate_pre = mm(x_ref[at, :], gate_ref[0], ((1,), (0,)))
            up_pre = mm(x_ref[at, :], up_ref[0], ((1,), (0,)))
            sig = lax.logistic(gate_pre)
            silu = gate_pre * sig
            act_ref[0, at, :] = (silu * up_pre).astype(jnp.bfloat16)
            dgate_ref[0, at, :] = (up_pre * (sig + silu * (1.0 - sig))).astype(jnp.bfloat16)
            dup_ref[0, at, :] = silu.astype(jnp.bfloat16)

    tiled = pl.BlockSpec((1, rows, tile), lambda e, f: (e, 0, f))
    low = jax.ShapeDtypeStruct((held, rows, ff), jnp.bfloat16)
    return grid_call(
        body,
        (held, ff // tile),
        [
            pl.BlockSpec((rows, width), lambda e, f: (0, 0)),
            pl.BlockSpec((1, width, tile), lambda e, f: (e, 0, f)),
            pl.BlockSpec((1, width, tile), lambda e, f: (e, 0, f)),
        ],
        [tiled, tiled, tiled],
        [low, low, low],
        4 * held * rows * ff * width,
        held * rows * ff,
        normed,
        gate,
        up,
    )


def expert_gradients(dy, down, act, dgate_factor, dup_factor, weight):
    held, ff, width = down.shape
    rows = dy.shape[0]
    tile, tm = (math.gcd(ff, 512), row_tiles(rows))

    def body(dy_ref, down_ref, act_ref, a_ref, b_ref, weight_ref, out_ref, dgate_ref, dup_ref, sum_ref):
        first = pl.program_id(1) == 0

        @pl.loop(0, rows // tm)
        def _(i):
            at = pl.ds(pl.multiple_of(i * tm, tm), tm)
            grad = mm(dy_ref[at, :], down_ref[0], ((1,), (1,)))
            scale = weight_ref[0, at, :]
            act = act_ref[0, at, :].astype(jnp.float32)
            product = act * grad
            partial = product[:, :128]
            for j in range(1, tile // 128):
                partial = partial + product[:, j * 128 : (j + 1) * 128]

            @pl.when(first)
            def _():
                sum_ref[0, at, :] = partial

            @pl.when(jnp.logical_not(first))
            def _():
                sum_ref[0, at, :] = sum_ref[0, at, :] + partial

            out_ref[0, at, :] = (scale * act).astype(jnp.bfloat16)
            grad = scale * grad
            dgate_ref[0, at, :] = (grad * a_ref[0, at, :].astype(jnp.float32)).astype(jnp.bfloat16)
            dup_ref[0, at, :] = (grad * b_ref[0, at, :].astype(jnp.float32)).astype(jnp.bfloat16)

    tiled = pl.BlockSpec((1, rows, tile), lambda e, f: (e, 0, f))
    low = jax.ShapeDtypeStruct((held, rows, ff), jnp.bfloat16)
    return grid_call(
        body,
        (held, ff // tile),
        [
            pl.BlockSpec((rows, width), lambda e, f: (0, 0)),
            pl.BlockSpec((1, tile, width), lambda e, f: (e, f, 0)),
            tiled,
            tiled,
            tiled,
            pl.BlockSpec((1, rows, 1), lambda e, f: (e, 0, 0)),
        ],
        [tiled, tiled, tiled, pl.BlockSpec((1, rows, 128), lambda e, f: (e, 0, 0))],
        [low, low, low, jax.ShapeDtypeStruct((held, rows, 128), jnp.float32)],
        2 * held * rows * ff * width,
        0,
        dy,
        down,
        act,
        dgate_factor,
        dup_factor,
        weight,
    )


def input_gradient(dgate, dup, gate, up, gate_sums, chances, chosen, own, router):
    held, width, ff = gate.shape
    rows = dgate.shape[1]
    tile, tm = (math.gcd(width, 512), row_tiles(rows))

    def body(dgate_ref, dup_ref, gate_ref, up_ref, sum_ref, chance_ref, chosen_ref, own_ref, router_ref, out_ref, logits_ref):
        @pl.loop(0, rows // tm)
        def _(i):
            at = pl.ds(pl.multiple_of(i * tm, tm), tm)
            chances = chance_ref[at, :]
            placed = jnp.zeros((tm, 128), jnp.float32)
            for e in range(held):
                got = jnp.sum(sum_ref[e, at, :], axis=-1, keepdims=True)
                placed = placed + own_ref[e : e + 1, :] * got
            placed = placed * chosen_ref[at, :]
            inner = jnp.sum(chances * placed, axis=-1, keepdims=True)
            logits = (chances * (placed - inner)).astype(jnp.bfloat16)
            logits_ref[at, :] = logits
            total = mm(logits, router_ref[...], ((1,), (1,)))
            for e in range(held):
                total = total + mm(dgate_ref[e, at, :], gate_ref[e], ((1,), (1,)))
                total = total + mm(dup_ref[e, at, :], up_ref[e], ((1,), (1,)))
            out_ref[at, :] = total.astype(jnp.bfloat16)

    whole = pl.BlockSpec((held, rows, ff), lambda n: (0, 0, 0))
    weights = pl.BlockSpec((held, tile, ff), lambda n: (0, n, 0))
    lanes = pl.BlockSpec((rows, 128), lambda n: (0, 0))
    return grid_call(
        body,
        (width // tile,),
        [
            whole,
            whole,
            weights,
            weights,
            pl.BlockSpec((held, rows, 128), lambda n: (0, 0, 0)),
            lanes,
            lanes,
            pl.BlockSpec((held, 128), lambda n: (0, 0)),
            pl.BlockSpec((tile, 128), lambda n: (n, 0)),
        ],
        [pl.BlockSpec((rows, tile), lambda n: (0, n)), lanes],
        [jax.ShapeDtypeStruct((rows, width), jnp.bfloat16), jax.ShapeDtypeStruct((rows, 128), jnp.bfloat16)],
        4 * held * rows * ff * width,
        0,
        dgate,
        dup,
        gate,
        up,
        gate_sums,
        chances,
        chosen,
        own,
        router,
    )


def combine_experts(y_at, act, down, weight):
    held, ff, width = down.shape
    rows = act.shape[1]
    block = rows // 8
    tile, tm = (math.gcd(width, 512), 4 * block)

    def body(y_ref, act_ref, down_ref, weight_ref, near_ref, far_ref):
        for i in range(2):
            at = slice(i * tm, (i + 1) * tm)
            total = weight_ref[0, at, :] * mm(act_ref[0, at, :], down_ref[0], ((1,), (0,)))
            for e in range(1, held):
                term = mm(act_ref[e, at, :], down_ref[e], ((1,), (0,)))
                total = total + weight_ref[e, at, :] * term
            total = total.astype(jnp.bfloat16)
            for y, outs in ((0, (near_ref, far_ref)), (1, (far_ref, near_ref))):

                @pl.when(y_ref[0] == y)
                def _(outs=outs):
                    for j in range(4):
                        to = (2 * i + j // 2) * block
                        outs[j % 2][to : to + block, :] = total[j * block : (j + 1) * block]

    half = jax.ShapeDtypeStruct((rows // 2, width), jnp.bfloat16)
    tiled = pl.BlockSpec((rows // 2, tile), lambda n, y: (0, n))
    return pl.pallas_call(
        body,
        grid_spec=pltpu.PrefetchScalarGridSpec(
            num_scalar_prefetch=1,
            grid=(width // tile,),
            in_specs=[
                pl.BlockSpec((held, rows, ff), lambda n, y: (0, 0, 0)),
                pl.BlockSpec((held, ff, tile), lambda n, y: (0, 0, n)),
                pl.BlockSpec((held, rows, 1), lambda n, y: (0, 0, 0)),
            ],
            out_specs=[tiled, tiled],
        ),
        out_shape=[half, half],
        compiler_params=pltpu.CompilerParams(vmem_limit_bytes=VMEM_GRANT),
        cost_estimate=cost(2 * held * rows * ff * width, 0, act, down, half, half),
    )(y_at, act, down, weight)


def weight_pieces(left, right, parts, split_left):
    flat, stacked = (left, right) if split_left else (right, left)
    held, rows, ff = stacked.shape
    piece = flat.shape[1] // parts
    shape = (held, piece, ff) if split_left else (held, ff, piece)
    tm = math.gcd(shape[1], 512)

    def body(flat_ref, stacked_ref, *outs):
        step = pl.program_id(0)
        for j in range(parts):

            @pl.when(step == j)
            def _(j=j):
                @pl.loop(0, shape[1] // tm)
                def _(i):
                    at = pl.ds(pl.multiple_of(i * tm, tm), tm)
                    if split_left:
                        value = mm(flat_ref[:, at], stacked_ref[0], ((0,), (0,)))
                    else:
                        value = mm(stacked_ref[0, :, at], flat_ref[...], ((0,), (0,)))
                    outs[j][0, at, :] = value.astype(jnp.bfloat16)

    def place(j):
        return lambda k, e: (jnp.where(k < j, 0, jnp.where(k > j, held - 1, e)), 0, 0)

    return grid_call(
        body,
        (parts, held),
        [
            pl.BlockSpec((rows, piece), lambda k, e: (0, k)),
            pl.BlockSpec((1, rows, ff), lambda k, e: (e, 0, 0)),
        ],
        [pl.BlockSpec((1,) + shape[1:], place(j)) for j in range(parts)],
        [jax.ShapeDtypeStruct(shape, jnp.bfloat16)] * parts,
        2 * held * rows * ff * flat.shape[1],
        0,
        flat,
        stacked,
    )


def rope_tables(row_count, head_dim):
    half_dim = head_dim // 2
    frequency = jnp.exp(
        jnp.arange(half_dim, dtype=jnp.float32) * (-2.0 * math.log(rope_base) / head_dim)
    )
    angles = jnp.arange(row_count, dtype=jnp.float32)[:, None] * frequency[None, :]
    cosine, sine = (jnp.cos(angles), jnp.sin(angles))
    return (
        jnp.concatenate([cosine, cosine], axis=1),
        jnp.concatenate([-sine, sine], axis=1),
    )


def seen(first, count, keys, seg_col, seg_row):
    position = first + lax.broadcasted_iota(jnp.int32, (count, keys), 0)
    other = lax.broadcasted_iota(jnp.int32, (count, keys), 1)
    return (position >= other) & (seg_col == seg_row)


def pair_rows(first, second):
    lane = lax.broadcasted_iota(jnp.int32, (first.shape[0], 128), 1)
    both = jnp.where(lane == 0, first, jnp.where(lane == 1, second, 0.0))
    return both.T[:8]


def pair_columns(sums):
    total = sum(sums[1:], sums[0])
    total = jnp.concatenate([total] * 16, axis=0).T
    return (total[:, 0:1], total[:, 1:2])


def project(x_row, gain, w_qkv):
    rows, width = x_row.shape
    held_cols = w_qkv.shape[1]
    cols = held_cols // 3
    tm = math.gcd(rows, 256)

    def body(x_ref, gain_ref, w_ref, normed_ref, qkv_ref, r_ref, stat_ref):
        x = x_ref[...].astype(jnp.float32)
        r = lax.rsqrt(jnp.mean(x * x, axis=-1, keepdims=True) + epsilon)
        r_ref[...] = r
        normed = (x * r * gain_ref[...]).astype(jnp.bfloat16)
        normed_ref[...] = normed
        qkv = mm(normed, w_ref[...], ((1,), (0,)))
        qkv_ref[...] = qkv
        squares = qkv[:, : 2 * cols] * qkv[:, : 2 * cols]
        stat_ref[...] = pair_rows(
            jnp.sum(squares[:, :cols], axis=-1, keepdims=True),
            jnp.sum(squares[:, cols:], axis=-1, keepdims=True),
        )

    full = jnp.float32
    return grid_call(
        body,
        (rows // tm,),
        [
            pl.BlockSpec((tm, width), lambda i: (i, 0)),
            pl.BlockSpec((1, width), lambda i: (0, 0)),
            pl.BlockSpec((width, held_cols), lambda i: (0, 0)),
        ],
        [
            pl.BlockSpec((tm, width), lambda i: (i, 0)),
            pl.BlockSpec((tm, held_cols), lambda i: (i, 0)),
            pl.BlockSpec((tm, 1), lambda i: (i, 0)),
            pl.BlockSpec((8, tm), lambda i: (0, i)),
        ],
        [
            jax.ShapeDtypeStruct((rows, width), jnp.bfloat16),
            jax.ShapeDtypeStruct((rows, held_cols), full),
            jax.ShapeDtypeStruct((rows, 1), full),
            jax.ShapeDtypeStruct((8, rows), full),
        ],
        2 * rows * width * held_cols,
        0,
        x_row,
        gain,
        w_qkv,
    )


def attend(qkv, sums, width, g_query, g_key, cosine, sine, seg_col, seg_row):
    rows, held_cols = qkv.shape
    cols = held_cols // 3
    heads = cols // HEAD
    tq = math.gcd(rows, 256)
    scaling = HEAD ** (-0.5)
    shards = sums.shape[0]

    def body(q, k, v, sums_ref, gq, gk, cos, sin, sc, sr, q_out, k_out, v_out, att_out, log_out, rq, rk):
        @pl.when(pl.program_id(0) == 0)
        def _():
            for i in range(rows // tq):
                at = slice(i * tq, (i + 1) * tq)
                first, second = pair_columns([sums_ref[d, :, at] for d in range(shards)])
                rq[at, :] = lax.rsqrt(first / width + epsilon)
                rk[at, :] = lax.rsqrt(second / width + epsilon)

        def rotated(ref, r, g):
            values = ref[...] * r[...] * g[...]
            swapped = pltpu.roll(values, HEAD // 2, 1)
            return (values * cos[...] + swapped * sin[...]).astype(jnp.bfloat16)

        q_out[...] = rotated(q, rq, gq)
        k_out[...] = rotated(k, rk, gk)
        v_out[...] = v[...].astype(jnp.bfloat16)
        for i in range(rows // tq):
            at, keys = (slice(i * tq, (i + 1) * tq), (i + 1) * tq)
            scores = mm(q_out[at, :], k_out[:keys, :], ((1,), (1,))) * scaling
            allowed = seen(i * tq, tq, keys, sc[at, :], sr[:, :keys])
            scores = jnp.where(allowed, scores, masked_score)
            peak = jnp.max(scores, axis=-1, keepdims=True)
            raised = jnp.exp(scores - peak)
            total = jnp.sum(raised, axis=-1, keepdims=True)
            log_out[0, at, :] = peak + jnp.log(total)
            weights = (raised * (1.0 / total)).astype(jnp.bfloat16)
            att_out[at, :] = mm(weights, v_out[:keys, :], ((1,), (0,))).astype(jnp.bfloat16)

    def col(offset):
        return pl.BlockSpec((rows, HEAD), lambda h: (0, offset + h))

    row = pl.BlockSpec((1, HEAD), lambda h: (0, h))
    one = pl.BlockSpec((rows, 1), lambda h: (0, 0))
    table = pl.BlockSpec((rows, HEAD), lambda h: (0, 0))
    low = jax.ShapeDtypeStruct((rows, cols), jnp.bfloat16)
    column = jax.ShapeDtypeStruct((rows, 1), jnp.float32)
    return grid_call(
        body,
        (heads,),
        [
            col(0),
            col(heads),
            col(2 * heads),
            pl.BlockSpec((shards, 8, rows), lambda h: (0, 0, 0)),
            row,
            row,
            table,
            table,
            one,
            pl.BlockSpec((1, rows), lambda h: (0, 0)),
        ],
        [col(0)] * 4 + [pl.BlockSpec((1, rows, 1), lambda h: (h, 0, 0)), one, one],
        [low] * 4 + [jax.ShapeDtypeStruct((heads, rows, 1), jnp.float32), column, column],
        4 * heads * rows * rows * HEAD,
        heads * rows * rows,
        qkv,
        qkv,
        qkv,
        sums,
        g_query,
        g_key,
        cosine,
        sine,
        seg_col,
        seg_row,
    )


def attend_back(qkv, q_rot, k_rot, value_in, grad, log_total, r_query, r_key, g_query, g_key, cosine, sine, seg_col, seg_row):
    rows, cols = q_rot.shape
    heads = cols // HEAD
    tq = math.gcd(rows, 256)
    scaling = HEAD ** (-0.5)

    def body(q, k, qr, kr, v, ga, lt, rq, rk, gq, gk, cos, sin, sc, sr, q_out, k_out, v_out, stat_out, gq_out, gk_out, q_sum, k_sum, v_sum, stats):
        k_sum[...] = jnp.zeros_like(k_sum)
        v_sum[...] = jnp.zeros_like(v_sum)
        for i in range(rows // tq):
            at, keys = (slice(i * tq, (i + 1) * tq), (i + 1) * tq)
            scores = mm(qr[at, :], kr[:keys, :], ((1,), (1,))) * scaling
            allowed = seen(i * tq, tq, keys, sc[at, :], sr[:, :keys])
            p = jnp.exp(jnp.where(allowed, scores, masked_score) - lt[0, at, :])
            grad_weights = mm(ga[at, :], v[:keys, :], ((1,), (1,)))
            delta = jnp.sum(p * grad_weights, axis=-1, keepdims=True)
            grad_scores = (scaling * p * (grad_weights - delta)).astype(jnp.bfloat16)
            q_sum[at, :] = mm(grad_scores, kr[:keys, :], ((1,), (0,)))
            k_sum[:keys, :] += mm(grad_scores, qr[at, :], ((0,), (0,)))
            v_sum[:keys, :] += mm(p.astype(jnp.bfloat16), ga[at, :], ((0,), (0,)))

        first = pl.program_id(0) == 0

        def back(total, ref, r, g, out, place, gain):
            values = total[...]
            values = values * cos[...] - pltpu.roll(values, HEAD // 2, 1) * sin[...]
            gain[...] = jnp.sum(values * ref[...] * r[...], axis=0, keepdims=True)
            values = values * g[...]
            stat = jnp.sum(values * ref[...], axis=-1, keepdims=True)
            stats[place] += stat
            out[...] = values

        @pl.when(first)
        def _():
            stats[...] = jnp.zeros_like(stats)

        back(q_sum, q, rq, gq, q_out, 0, gq_out)
        back(k_sum, k, rk, gk, k_out, 1, gk_out)

        @pl.when(pl.program_id(0) == heads - 1)
        def _():
            for i in range(rows // tq):
                at = slice(i * tq, (i + 1) * tq)
                stat_out[:, at] = pair_rows(stats[0, at, :], stats[1, at, :])

        v_out[...] = v_sum[...].astype(jnp.bfloat16)

    def col(offset):
        return pl.BlockSpec((rows, HEAD), lambda h: (0, offset + h))

    row = pl.BlockSpec((1, HEAD), lambda h: (0, h))
    one = pl.BlockSpec((rows, 1), lambda h: (0, 0))
    stat = pl.BlockSpec((1, rows, 1), lambda h: (h, 0, 0))
    table = pl.BlockSpec((rows, HEAD), lambda h: (0, 0))
    full = jnp.float32
    outs = (
        [jax.ShapeDtypeStruct((rows, cols), full)] * 2
        + [jax.ShapeDtypeStruct((rows, cols), jnp.bfloat16)]
        + [jax.ShapeDtypeStruct((8, rows), full)]
        + [jax.ShapeDtypeStruct((1, cols), full)] * 2
    )
    args = (qkv, qkv, q_rot, k_rot, value_in, grad, log_total, r_query, r_key, g_query, g_key, cosine, sine, seg_col, seg_row)
    return pl.pallas_call(
        body,
        grid=(heads,),
        in_specs=[col(0), col(heads), col(0), col(0), col(0), col(0), stat, one, one, row, row, table, table, one,
                  pl.BlockSpec((1, rows), lambda h: (0, 0))],
        out_specs=[col(0), col(0), col(0), pl.BlockSpec((8, rows), lambda h: (0, 0)), row, row],
        out_shape=outs,
        scratch_shapes=[pltpu.VMEM((rows, HEAD), full)] * 3 + [pltpu.VMEM((2, rows, 1), full)],
        compiler_params=pltpu.CompilerParams(vmem_limit_bytes=VMEM_GRANT),
        cost_estimate=cost(10 * heads * rows * rows * HEAD, heads * rows * rows, *args, *outs),
    )(*args)


def normed_gradient(q_grad, k_grad, v_low, qkv, sums, r_query, r_key, w_qkv, x_row, r_attn):
    rows, cols = q_grad.shape
    width = x_row.shape[1]
    shards = sums.shape[0]
    tm = math.gcd(rows, 256)

    def body(qg, kg, v, q, k, sums_ref, rq, rk, w, x, ra, low_ref, out_ref, gain_ref):
        means = pair_columns([sums_ref[d] for d in range(shards)])
        parts = []
        for grad, ref, r_ref, mean in ((qg, q, rq, means[0]), (kg, k, rk, means[1])):
            r = r_ref[...]
            part = r * grad[...] - ref[...] * (r * r * r) * (mean / width)
            parts.append(part.astype(jnp.bfloat16))
        parts.append(v[...])
        for i in range(3):
            low_ref[:, i * cols : (i + 1) * cols] = parts[i]
        total = mm(low_ref[...], w[...], ((1,), (1,)))
        out_ref[...] = total.astype(jnp.bfloat16)
        gain = jnp.sum(total * x[...].astype(jnp.float32) * ra[...], axis=0, keepdims=True)
        first = pl.program_id(0) == 0

        @pl.when(first)
        def _():
            gain_ref[...] = gain

        @pl.when(jnp.logical_not(first))
        def _():
            gain_ref[...] += gain

    def tiled(count, at=0):
        return pl.BlockSpec((tm, count), lambda i: (i, at))

    return grid_call(
        body,
        (rows // tm,),
        [
            tiled(cols),
            tiled(cols),
            tiled(cols),
            tiled(cols),
            tiled(cols, 1),
            pl.BlockSpec((shards, 8, tm), lambda i: (0, 0, i)),
            tiled(1),
            tiled(1),
            pl.BlockSpec((width, 3 * cols), lambda i: (0, 0)),
            tiled(width),
            tiled(1),
        ],
        [tiled(3 * cols), tiled(width), pl.BlockSpec((1, width), lambda i: (0, 0))],
        [
            jax.ShapeDtypeStruct((rows, 3 * cols), jnp.bfloat16),
            jax.ShapeDtypeStruct((rows, width), jnp.bfloat16),
            jax.ShapeDtypeStruct((1, width), jnp.float32),
        ],
        6 * rows * width * cols,
        0,
        q_grad,
        k_grad,
        v_low,
        qkv,
        qkv,
        sums,
        r_query,
        r_key,
        w_qkv,
        x_row,
        r_attn,
    )


def middle(order, nf_own, mid, r_ffn, gain, dy, out_pieces):
    tokens, width = nf_own.shape
    chunk = width // 4

    def body(order_ref, nf, mid_ref, r_ref, gain_ref, dy_ref, p0, p1, p2, p3, grad_ref, low_ref, att_ref, gain_out):
        r = r_ref[...]
        own = mid_ref[...]
        grad = nf[...].astype(jnp.float32)
        gain_out[...] = jnp.sum(grad * own * r, axis=0, keepdims=True)
        grad = grad * gain_ref[...]
        mean = jnp.mean(grad * own, axis=-1, keepdims=True)
        total = dy_ref[...].astype(jnp.float32) + r * grad - own * (r * r * r) * mean
        grad_ref[...] = total
        low_ref[...] = total.astype(jnp.bfloat16)
        for j, piece in enumerate((p0, p1, p2, p3)):
            back = jnp.zeros((tokens, chunk), jnp.float32)
            for k in range(4):
                n = k ^ j
                back = back + mm(
                    low_ref[:, n * chunk : (n + 1) * chunk],
                    piece[:, k * chunk : (k + 1) * chunk],
                    ((1,), (1,)),
                )
            att_ref[order_ref[j]] = back.astype(jnp.bfloat16)

    def whole(*shape):
        return pl.BlockSpec(shape, lambda i, o: (0,) * len(shape))

    outs = [
        jax.ShapeDtypeStruct((tokens, width), jnp.float32),
        jax.ShapeDtypeStruct((tokens, width), jnp.bfloat16),
        jax.ShapeDtypeStruct((4, tokens, chunk), jnp.bfloat16),
        jax.ShapeDtypeStruct((1, width), jnp.float32),
    ]
    return pl.pallas_call(
        body,
        grid_spec=pltpu.PrefetchScalarGridSpec(
            num_scalar_prefetch=1,
            grid=(1,),
            in_specs=[
                whole(tokens, width),
                pl.BlockSpec((tokens, width), lambda i, o: (o[4], 0)),
                pl.BlockSpec((tokens, 1), lambda i, o: (o[4], 0)),
                whole(1, width),
                whole(tokens, width),
                *[whole(chunk, width)] * 4,
            ],
            out_specs=[whole(*o.shape) for o in outs],
        ),
        out_shape=outs,
        compiler_params=pltpu.CompilerParams(vmem_limit_bytes=VMEM_GRANT),
        cost_estimate=cost(2 * tokens * width * width, 0, *out_pieces, *outs),
    )(order, nf_own, mid, r_ffn, gain, dy, *out_pieces)


def out_grad_pieces(order, attended, columns):
    shards, rows, cols = attended.shape
    per_chunk = shards // 4
    count = columns.shape[1]
    tm = math.gcd(cols, 256)

    def body(order_ref, att_ref, col_ref, *outs):
        step = pl.program_id(0)
        for j in range(4):

            @pl.when(step == j)
            def _(j=j):
                outs[j][...] = mm(att_ref[0], col_ref[...], ((0,), (0,))).astype(jnp.bfloat16)

    def place(j):
        return lambda k, i, o: (jnp.where(k < j, 0, jnp.where(k > j, per_chunk - 1, i)), 0)

    outs = [jax.ShapeDtypeStruct((per_chunk * cols, count), jnp.bfloat16)] * 4
    return pl.pallas_call(
        body,
        grid_spec=pltpu.PrefetchScalarGridSpec(
            num_scalar_prefetch=1,
            grid=(4, per_chunk),
            in_specs=[
                pl.BlockSpec((1, rows, cols), lambda k, i, o: (o[k] * per_chunk + i, 0, 0)),
                pl.BlockSpec((rows, count), lambda k, i, o: (0, 0)),
            ],
            out_specs=[pl.BlockSpec((cols, count), place(j)) for j in range(4)],
        ),
        out_shape=outs,
        compiler_params=pltpu.CompilerParams(vmem_limit_bytes=VMEM_GRANT),
        cost_estimate=cost(2 * rows * shards * cols * count, 0, attended, columns, *outs),
    )(order, attended, columns)


def over_y(values):
    return lax.ppermute(values, "seq", [(i, i ^ 1) for i in range(8)])


def sum_along_z(values):
    lines = [[0, 2, 4, 6], [1, 3, 5, 7]]
    return lax.psum_scatter(
        values, "seq", scatter_dimension=0, tiled=True, axis_index_groups=lines
    )


def swap(values, bits):
    return lax.ppermute(values, "dp", [(i, i ^ bits) for i in range(4)])


def sum_in_chip(pieces, sent):
    wide = jnp.float32
    kept = pieces[0].astype(wide) + swap(pieces[1], 1).astype(wide)
    return (kept.astype(sent), (pieces[2].astype(wide) + swap(pieces[3], 1).astype(wide)).astype(sent))


def across_by_expert(passed):
    return [swap(passed[e], 2) for e in range(passed.shape[0])]


def add_arrived(kept, arrived):
    return jnp.stack(
        [kept[e].astype(jnp.float32) + a.astype(jnp.float32) for e, a in enumerate(arrived)]
    )


def sum_pieces(pieces, sent):
    kept, passed = sum_in_chip(pieces, sent)
    return kept.astype(jnp.float32) + swap(passed, 2).astype(jnp.float32)


def reorder(values, dp_index, axis):
    size = values.shape[axis] // 4
    return jnp.concatenate(
        [
            lax.dynamic_slice_in_dim(values, (dp_index ^ k) * size, size, axis=axis)
            for k in range(4)
        ],
        axis=axis,
    )


def on_device_heads(
    hidden_in,
    segment_ids,
    routes,
    w_query,
    w_key,
    w_value,
    w_out,
    gain_attn,
    gain_query,
    gain_key,
    gain_ffn,
    w_router,
    w_gate,
    w_up,
    w_down,
    cotangent,
):
    low, full = (jnp.bfloat16, jnp.float32)
    shards = lax.axis_size("seq")
    seq_index, dp_index = (lax.axis_index("seq"), lax.axis_index("dp"))
    tokens, width = hidden_in.shape[1:]
    rows = shards * tokens
    cols = width // shards
    heads = cols // HEAD
    held = w_gate.shape[0]
    expert_count = held * shards
    block_rows = w_query.shape[0]
    chunk = shards * block_rows
    row_seg = segment_ids[0]
    first_row = seq_index * tokens
    barrier = lax.optimization_barrier

    def own_cols(values, count):
        return lax.dynamic_slice_in_dim(values, seq_index * count, count, axis=values.ndim - 1)

    cosine, sine = rope_tables(rows, HEAD)
    seg_col, seg_row = (row_seg[:, None], row_seg[None, :])

    x_shard = reorder(hidden_in[0], dp_index, 1)
    x_row = lax.all_gather(x_shard, "seq", axis=0, tiled=True)
    blocks = jnp.stack(
        [w.reshape(block_rows, shards, cols).transpose(1, 0, 2) for w in (w_query, w_key, w_value)],
        axis=1,
    )
    blocks = blocks.reshape(shards, 3 * block_rows, cols)
    place_at = (dp_index * shards + seq_index) * block_rows
    gain_rows = lax.dynamic_update_slice(
        jnp.zeros((shards, 16, cols), low),
        jnp.stack([gain_query, gain_key])[None],
        (place_at // cols, 0, place_at % cols),
    )
    gain_rows = lax.dynamic_update_slice(
        gain_rows, jnp.broadcast_to(gain_attn[None, None], (shards, 1, block_rows)), (0, 2, 0)
    )
    blocks = lax.all_to_all(jnp.concatenate([blocks, gain_rows], axis=1), "seq", 0, 0, tiled=True)
    across = swap(blocks, 2)
    qkv_pieces = (blocks, swap(blocks, 1), across, swap(across, 1))
    gate_across = swap(w_gate, 2)
    gate_full = jnp.concatenate([w_gate, swap(w_gate, 1), gate_across, swap(gate_across, 1)], axis=1)
    w_qkv = jnp.concatenate(
        [
            p[:, : 3 * block_rows]
            .reshape(shards, 3, block_rows, cols)
            .transpose(0, 2, 1, 3)
            .reshape(chunk, 3 * cols)
            for p in qkv_pieces
        ],
        axis=0,
    )
    gain_pair = sum(
        jnp.sum(p[:, 3 * block_rows : 3 * block_rows + 2].astype(full), axis=0) for p in qkv_pieces
    )
    g_query, g_key = (gain_pair[0:1], gain_pair[1:2])
    g_attn = jnp.concatenate(
        [p[:, 3 * block_rows + 2, :block_rows].reshape(1, chunk) for p in qkv_pieces], axis=1
    ).astype(full)
    x_row, w_qkv, g_query, g_key, g_attn, gate_full = barrier(
        (x_row, w_qkv, g_query, g_key, g_attn, gate_full)
    )

    picks = routes.shape[2]
    packed = tokens // block_rows
    extra = jnp.concatenate(
        [routes[0].astype(low).reshape(block_rows, packed * picks), w_router, gain_ffn[:, None]],
        axis=1,
    )
    extra = jnp.pad(extra, ((0, 0), (0, 128 - extra.shape[1])))
    out_own = lax.all_gather(
        jnp.concatenate([reorder(w_out, dp_index, 1), extra], axis=1), "seq", axis=0, tiled=True
    )
    up_across = swap(w_up, 2)

    def share(sums):
        spread = jnp.broadcast_to(sums[None], (shards,) + sums.shape)
        return lax.all_to_all(spread, "seq", 0, 0, tiled=True)

    normed, qkv, r_attn, sums = project(x_row, g_attn, w_qkv)
    q_rot, k_rot, value_in, attended, log_total, r_query, r_key = attend(
        qkv, share(sums), width, g_query, g_key, cosine, sine, seg_col, seg_row
    )
    attended, out_own, up_across = barrier((attended, out_own, up_across))

    attended_row = lax.all_gather(attended, "seq", axis=0)
    out_across = swap(out_own, 2)
    out_pieces = (out_own, swap(out_own, 1), out_across, swap(out_across, 1))
    extras = [p[:, width:] for p in out_pieces]
    routes_row = extras[0][:, : packed * picks].reshape(rows, picks).astype(jnp.int32)
    extras = jnp.concatenate([p[:, packed * picks :] for p in extras], axis=0)
    router = jnp.pad(extras[:, :expert_count], ((0, 0), (0, 128 - expert_count)))
    g_ffn = extras[:, expert_count].astype(full)[None]
    lane_ids = lax.iota(jnp.int32, 128)
    chosen = jnp.any(routes_row[:, :, None] == lane_ids[None, None, :], axis=1).astype(full)
    own = (
        lane_ids[None, :] == seq_index * held + lax.iota(jnp.int32, held)[:, None]
    ).astype(full)
    up_full = jnp.concatenate([w_up, swap(w_up, 1), up_across, swap(up_across, 1)], axis=1)
    attended_row, out_pieces, up_full, router, g_ffn, chosen = barrier(
        (attended_row, out_pieces, up_full, router, g_ffn, chosen)
    )

    dy_shard, attended_row = barrier((reorder(cotangent[0], dp_index, 1), attended_row))
    dy_row = lax.all_gather(dy_shard, "seq", axis=0, tiled=True)
    order = jnp.stack([dp_index ^ k for k in range(4)] + [seq_index]).astype(jnp.int32)
    hidden_mid, normed_ffn, r_ffn, chances, gates = finish_attention(
        order, attended_row, out_pieces, x_row, g_ffn, router, chosen, own, expert_count
    )
    act, dgate_factor, dup_factor = expert_activations(normed_ffn, gate_full, up_full)
    act, down_across = barrier((act, swap(w_down, 2)))
    down_full = jnp.concatenate([w_down, swap(w_down, 1), down_across, swap(down_across, 1)], axis=2)
    y_at = (seq_index % 2).astype(jnp.int32)[None]
    mixture, mixture_far = combine_experts(y_at, act, down_full, gates)
    dy_row, mixture_far, act = barrier((dy_row, mixture_far, act))
    mixture_far = over_y(mixture_far)

    scaled, dgate, dup, gate_sums = expert_gradients(
        dy_row, down_full, act, dgate_factor, dup_factor, gates
    )
    nf_grad, grad_logits = input_gradient(
        dgate, dup, gate_full, up_full, gate_sums, chances, chosen, own, router
    )
    nf_grad, mixture_far = barrier((nf_grad, mixture_far))
    nf_sum = lax.psum_scatter(nf_grad, "seq", scatter_dimension=0, tiled=True)
    mixture = (mixture.astype(full) + mixture_far.astype(full)).astype(low)

    down_kept, down_passed = sum_in_chip(weight_pieces(scaled, dy_row, 4, False), low)
    gate_pieces = weight_pieces(normed_ffn, dgate, 4, True)
    dup, down_passed = barrier((dup, down_passed))
    down_arrived = across_by_expert(down_passed)
    gate_kept, gate_passed = sum_in_chip(gate_pieces, low)
    up_pieces = weight_pieces(normed_ffn, dup, 4, True)
    up_pieces, down_arrived[0] = barrier((up_pieces, down_arrived[0]))
    up_kept, up_passed = sum_in_chip(up_pieces, low)
    router_grad = mm(grad_logits[:, :expert_count], normed_ffn, ((0,), (0,)))
    nf_sum, mixture, down_arrived[1], gate_passed, up_passed, router_grad, down_kept, gate_kept, up_kept = barrier(
        (nf_sum, mixture, down_arrived[1], gate_passed, up_passed, router_grad, down_kept, gate_kept, up_kept)
    )
    gate_arrived, up_arrived = (across_by_expert(gate_passed), [swap(up_passed[0], 2)])

    grad_mid, mid_low, grad_attended, gain_ffn_grad = middle(
        order, nf_sum, hidden_mid, r_ffn, g_ffn, dy_shard, out_pieces
    )
    def to_columns(values):
        return lax.all_to_all(values, "seq", 0, 0, tiled=True).reshape(rows, cols)

    grad_attended = grad_attended.reshape(4, tokens, shards // 4, cols).transpose(0, 2, 1, 3)
    grad_attended = to_columns(grad_attended.reshape(shards, tokens, cols))
    grad_attended, gate_arrived[0], mixture = barrier((grad_attended, gate_arrived[0], mixture))
    mixture_own = sum_along_z(mixture)
    mid_cols = to_columns(
        reorder(mid_low, dp_index, 1).reshape(tokens, shards, cols).transpose(1, 0, 2)
    )
    q_grad, k_grad, v_low, sums, gain_query_grad, gain_key_grad = attend_back(
        qkv, q_rot, k_rot, value_in, grad_attended, log_total,
        r_query, r_key, g_query, g_key, cosine, sine, seg_col, seg_row,
    )
    sums, gate_arrived[1] = barrier((sums, gate_arrived[1]))
    sums, mid_cols = barrier((share(sums), mid_cols))
    qkv_low, normed_grad, gain_attn_grad = normed_gradient(
        q_grad, k_grad, v_low, qkv, sums, r_query, r_key, w_qkv, x_row, r_attn
    )
    normed_grad, up_arrived[0], mixture_own = barrier((normed_grad, up_arrived[0], mixture_own))
    normed_sum = lax.psum_scatter(normed_grad, "seq", scatter_dimension=0, tiled=True).astype(full)

    def to_owners(kept, passed, count):
        total = kept.astype(full) + swap(passed, 2).astype(full)
        total = lax.all_to_all(
            total.astype(low).reshape(shards, block_rows, count * cols), "seq", 0, 0, tiled=True
        )
        total = total.reshape(shards, block_rows, count, cols).transpose(2, 1, 0, 3)
        return total.reshape(count, block_rows, width).astype(full)

    qkv_parts = [p[0] for p in weight_pieces(normed, qkv_low[None], 4, True)]
    qkv_parts, mid_cols, gain_attn_grad, gain_ffn_grad = barrier(
        (qkv_parts, mid_cols, gain_attn_grad, gain_ffn_grad)
    )
    qkv_kept, qkv_passed = sum_in_chip(qkv_parts, low)
    out_parts = out_grad_pieces(order, attended_row, mid_cols)
    out_kept, out_passed = sum_in_chip(out_parts, low)
    qkv_passed, out_passed, up_last = barrier((qkv_passed, out_passed, up_passed[1]))
    proj_grad = to_owners(qkv_kept, qkv_passed, 3)
    out_grad = to_owners(out_kept, out_passed, 1)
    up_arrived.append(swap(up_last, 2))
    grad_w_down = add_arrived(down_kept, down_arrived)
    grad_w_gate = add_arrived(gate_kept, gate_arrived)
    grad_w_up = add_arrived(up_kept, up_arrived)
    mid_own = lax.dynamic_slice_in_dim(hidden_mid, first_row, tokens)
    block_out = (mid_own + mixture_own.astype(full)).astype(low)
    normed_sum, grad_w_down, grad_w_gate, grad_w_up, out_grad, block_out = barrier(
        (normed_sum, grad_w_down, grad_w_gate, grad_w_up, out_grad, block_out)
    )

    x_own = x_shard.astype(full)
    r_here = lax.rsqrt(jnp.mean(x_own * x_own, axis=-1, keepdims=True) + epsilon)
    scaled_grad = normed_sum * g_attn
    grad_hidden = (
        grad_mid
        + r_here * scaled_grad
        - x_own * (r_here**3) * jnp.mean(scaled_grad * x_own, axis=-1, keepdims=True)
    )

    def place(values):
        whole = lax.dynamic_update_slice_in_dim(
            jnp.zeros((1, width), full), values[None], seq_index * cols, 1
        )
        return reorder(whole, dp_index, 1)

    vectors = jnp.concatenate(
        [
            router_grad,
            gain_attn_grad,
            place(gain_query_grad[0]),
            place(gain_key_grad[0]),
            gain_ffn_grad,
        ]
    )
    count = vectors.shape[0]
    vectors = sum_pieces([vectors[:, k * chunk : (k + 1) * chunk] for k in range(4)], full)
    vectors = vectors.reshape(count, shards, block_rows).transpose(1, 0, 2)
    vectors = jnp.sum(lax.all_to_all(vectors, "seq", 0, 0, tiled=True), axis=0)
    return (
        reorder(block_out, dp_index, 1)[None],
        reorder(grad_hidden, dp_index, 1)[None],
        proj_grad[0],
        proj_grad[1],
        proj_grad[2],
        out_grad[0],
        vectors[expert_count],
        vectors[expert_count + 1],
        vectors[expert_count + 2],
        vectors[expert_count + 3],
        vectors[:expert_count].T,
        grad_w_gate,
        grad_w_up,
        grad_w_down,
    )


def solution(mesh):
    def layer(*arrays):
        whole_heads = (arrays[0].shape[2] // HEAD) % mesh.shape["seq"] == 0
        if whole_heads and mesh.shape["dp"] == 4 and mesh.shape["seq"] == 8:
            return on_device_heads(*arrays)
        return on_device(*arrays)

    return jax.shard_map(
        layer,
        mesh=mesh,
        in_specs=(
            P("dp", "seq", None),
            P("dp", None),
            P("dp", "seq", None),
            P(("dp", "seq"), None),
            P(("dp", "seq"), None),
            P(("dp", "seq"), None),
            P(("dp", "seq"), None),
            P(("dp", "seq")),
            P(("dp", "seq")),
            P(("dp", "seq")),
            P(("dp", "seq")),
            P(("dp", "seq"), None),
            P("seq", "dp", None),
            P("seq", "dp", None),
            P("seq", None, "dp"),
            P("dp", "seq", None),
        ),
        out_specs=(
            P("dp", "seq", None),
            P("dp", "seq", None),
            P(("dp", "seq"), None),
            P(("dp", "seq"), None),
            P(("dp", "seq"), None),
            P(("dp", "seq"), None),
            P(("dp", "seq")),
            P(("dp", "seq")),
            P(("dp", "seq")),
            P(("dp", "seq")),
            P(("dp", "seq"), None),
            P("seq", "dp", None),
            P("seq", "dp", None),
            P("seq", None, "dp"),
        ),
        check_vma=False,
    )
```

```python
import math

import jax
import jax.numpy as jnp
from jax import lax
from jax.experimental import pallas as pl
from jax.experimental.pallas import tpu as pltpu
from jax.sharding import PartitionSpec as P

HEAD = 128


epsilon = 1e-05
masked_score = -1e30
rope_base = 10000.0


def normalize(values, gain_vec):
    return (
        values * lax.rsqrt(jnp.mean(values * values, axis=-1, keepdims=True) + epsilon) * gain_vec
    )


def rotary(values, positions):
    half_dim = values.shape[-1] // 2
    frequency = jnp.exp(
        jnp.arange(half_dim, dtype=jnp.float32) * (-2.0 * math.log(rope_base) / values.shape[-1])
    )
    angles = positions.astype(jnp.float32)[:, None] * frequency[None, :]
    cosine = jnp.cos(angles)[:, None, :]
    sine_table = jnp.sin(angles)[:, None, :]
    first_half = values[..., :half_dim]
    second = values[..., half_dim:]
    return jnp.concatenate(
        [first_half * cosine - second * sine_table, second * cosine + first_half * sine_table],
        axis=-1,
    )


def softmax_rows(values):
    peak_value = jnp.max(values, axis=-1, keepdims=True)
    raised = jnp.exp(values - peak_value)
    return raised / jnp.sum(raised, axis=-1, keepdims=True)


def rotate_normed(projection, gain_vec, positions):
    tokens, model_width = projection.shape
    return rotary(
        normalize(projection, gain_vec).reshape(tokens, model_width // HEAD, HEAD), positions
    )


def masked_scores(queries, key_block, query_pos, query_seg, key_pos, key_seg, scaling):
    raw_scores = jnp.einsum("qhd,khd->hqk", queries, key_block, preferred_element_type=jnp.float32)
    allowed = (query_pos[:, None] >= key_pos[None, :]) & (query_seg[:, None] == key_seg[None, :])
    return jnp.where(allowed[None], raw_scores * scaling, masked_score)


def key_window(keys_all, values_all, row_seg, begin_at, span):
    key_block = lax.dynamic_slice_in_dim(keys_all, begin_at, span)
    value_block = lax.dynamic_slice_in_dim(values_all, begin_at, span)
    key_pos = begin_at + lax.iota(jnp.int32, span)
    key_seg = lax.dynamic_slice_in_dim(row_seg, begin_at, span)
    return (key_block, value_block, key_pos, key_seg)


def project_front(hidden, layer_full, positions):
    tokens, model_width = hidden.shape
    normed = normalize(hidden, layer_full[5].astype(jnp.float32)).astype(jnp.bfloat16)
    query = jnp.dot(normed, layer_full[0], preferred_element_type=jnp.float32)
    key_proj = jnp.dot(normed, layer_full[1], preferred_element_type=jnp.float32)
    value_proj = jnp.dot(normed, layer_full[2], preferred_element_type=jnp.float32)
    query_rot = rotate_normed(query, layer_full[6].astype(jnp.float32), positions).astype(
        jnp.bfloat16
    )
    key_rot = rotate_normed(key_proj, layer_full[7].astype(jnp.float32), positions).astype(
        jnp.bfloat16
    )
    value_in = value_proj.astype(jnp.bfloat16).reshape(tokens, model_width // HEAD, HEAD)
    return (normed, query, key_proj, query_rot, key_rot, value_in)


def attend_local(query_rot, keys_all, values_all, row_seg, offset, span):
    tokens, head_count, head_dim = query_rot.shape
    scaling = head_dim ** (-0.5)
    query_pos = offset + lax.iota(jnp.int32, tokens)
    query_seg = lax.dynamic_slice_in_dim(row_seg, offset, tokens)
    reach_blocks = (offset + tokens + span - 1) // span

    def block_scores(block_index):
        begin_at = block_index * span
        key_block, value_block, key_pos, key_seg = key_window(
            keys_all, values_all, row_seg, begin_at, span
        )
        return (
            masked_scores(query_rot, key_block, query_pos, query_seg, key_pos, key_seg, scaling),
            value_block,
        )

    def first_pass(block_index, state_pair):
        peak_value, denominator = state_pair
        scores, unused_values = block_scores(block_index)
        new_peak = jnp.maximum(peak_value, jnp.max(scores, axis=-1))
        denominator = denominator * jnp.exp(peak_value - new_peak) + jnp.sum(
            jnp.exp(scores - new_peak[..., None]), axis=-1
        )
        return (new_peak, denominator)

    start_state = (
        jnp.full((head_count, tokens), masked_score, jnp.float32),
        jnp.zeros((head_count, tokens), jnp.float32),
    )
    peak_value, denominator = lax.fori_loop(0, reach_blocks, first_pass, start_state)
    log_total = peak_value + jnp.log(denominator)

    def second_pass(block_index, running):
        scores, value_block = block_scores(block_index)
        weights = jnp.exp(scores - log_total[..., None]).astype(jnp.bfloat16)
        return running + jnp.einsum(
            "hqk,khd->qhd", weights, value_block, preferred_element_type=jnp.float32
        )

    attention = lax.fori_loop(
        0, reach_blocks, second_pass, jnp.zeros((tokens, head_count, head_dim), jnp.float32)
    )
    return (attention, log_total)


def query_grads(query_rot, keys_all, values_all, row_seg, offset, span, log_total, grad_attended):
    tokens, head_count, head_dim = query_rot.shape
    scaling = head_dim ** (-0.5)
    query_pos = offset + lax.iota(jnp.int32, tokens)
    query_seg = lax.dynamic_slice_in_dim(row_seg, offset, tokens)
    reach_blocks = (offset + tokens + span - 1) // span

    def block_terms(block_index):
        begin_at = block_index * span
        key_block, value_block, key_pos, key_seg = key_window(
            keys_all, values_all, row_seg, begin_at, span
        )
        scores = masked_scores(
            query_rot, key_block, query_pos, query_seg, key_pos, key_seg, scaling
        )
        weights = jnp.exp(scores - log_total[..., None])
        grad_weights = jnp.einsum(
            "qhd,khd->hqk", grad_attended, value_block, preferred_element_type=jnp.float32
        )
        return (key_block, weights, grad_weights)

    def delta_pass(block_index, running):
        unused_keys, weights, grad_weights = block_terms(block_index)
        return running + jnp.sum(weights * grad_weights, axis=-1)

    delta = lax.fori_loop(0, reach_blocks, delta_pass, jnp.zeros((head_count, tokens), jnp.float32))

    def query_pass(block_index, running):
        key_block, weights, grad_weights = block_terms(block_index)
        grad_scores = (weights * (grad_weights - delta[..., None]) * scaling).astype(jnp.bfloat16)
        return running + jnp.einsum(
            "hqk,khd->qhd", grad_scores, key_block, preferred_element_type=jnp.float32
        )

    grad_query_rot = lax.fori_loop(
        0, reach_blocks, query_pass, jnp.zeros((tokens, head_count, head_dim), jnp.float32)
    )
    return (delta, grad_query_rot)


def route_tokens(hidden_mid, layer_full, choice_rows):
    tokens, pick_count = choice_rows.shape
    normed_ffn = normalize(hidden_mid, layer_full[8].astype(jnp.float32)).astype(jnp.bfloat16)
    logits = jnp.dot(normed_ffn, layer_full[4], preferred_element_type=jnp.float32)
    expert_count = logits.shape[1]
    capacity = 3 * tokens * pick_count // (2 * expert_count)
    chances = softmax_rows(logits)
    picks = choice_rows[:, :, None] == lax.iota(jnp.int32, expert_count)[None, None, :]
    gate_values = jnp.sum(jnp.where(picks, chances[:, None, :], 0.0), axis=-1)
    flat_hits = picks.reshape(tokens * pick_count, expert_count).astype(jnp.int32)
    earlier = jnp.cumsum(flat_hits, axis=0) - flat_hits
    slot_ids = choice_rows.reshape(-1) * capacity + jnp.sum(earlier * flat_hits, axis=1)
    pair_table = lax.iota(jnp.int32, expert_count * capacity)[:, None] == slot_ids[None, :]
    spread = jnp.sum(
        pair_table.reshape(expert_count * capacity, tokens, pick_count).astype(jnp.int32), axis=2
    ).astype(jnp.bfloat16)
    send_rows = jnp.dot(spread, normed_ffn, preferred_element_type=jnp.float32).astype(jnp.bfloat16)
    send_rows = send_rows.reshape(expert_count, capacity, hidden_mid.shape[1])
    return (normed_ffn, chances, picks, gate_values, slot_ids, pair_table, spread, send_rows)


def group_rows(row_block, held_experts):
    sources = row_block.shape[0] // held_experts
    grouped = row_block.reshape(
        sources, held_experts, row_block.shape[1], row_block.shape[2]
    ).transpose(1, 0, 2, 3)
    return grouped.reshape(held_experts, sources * row_block.shape[1], row_block.shape[2])


def ungroup_rows(grouped, whole_shape):
    held_experts = grouped.shape[0]
    sources = whole_shape[0] // held_experts
    spread_out = grouped.reshape(held_experts, sources, whole_shape[1], whole_shape[2]).transpose(
        1, 0, 2, 3
    )
    return spread_out.reshape(whole_shape)


def expert_forward(row_block, gate_full, up_full, down_full):
    inputs = group_rows(row_block, gate_full.shape[0])
    gate_pre = jnp.einsum("erd,edf->erf", inputs, gate_full, preferred_element_type=jnp.float32)
    up_pre = jnp.einsum("erd,edf->erf", inputs, up_full, preferred_element_type=jnp.float32)
    activated = (gate_pre * lax.logistic(gate_pre) * up_pre).astype(jnp.bfloat16)
    result = jnp.einsum(
        "erf,efd->erd", activated, down_full, preferred_element_type=jnp.float32
    ).astype(jnp.bfloat16)
    return ungroup_rows(result, row_block.shape)


def expert_backward(row_block, grad_block, gate_full, up_full, down_full):
    inputs = group_rows(row_block, gate_full.shape[0])
    grad_outputs = group_rows(grad_block, gate_full.shape[0])
    gate_pre = jnp.einsum("erd,edf->erf", inputs, gate_full, preferred_element_type=jnp.float32)
    up_pre = jnp.einsum("erd,edf->erf", inputs, up_full, preferred_element_type=jnp.float32)
    sigmoid_gate = lax.logistic(gate_pre)
    activated = (gate_pre * sigmoid_gate * up_pre).astype(jnp.bfloat16)
    grad_act = jnp.einsum(
        "erd,efd->erf", grad_outputs, down_full, preferred_element_type=jnp.float32
    )
    grad_down = jnp.einsum(
        "erf,erd->efd", activated, grad_outputs, preferred_element_type=jnp.float32
    )
    grad_gate_pre = (
        grad_act * up_pre * sigmoid_gate * (1.0 + gate_pre * (1.0 - sigmoid_gate))
    ).astype(jnp.bfloat16)
    grad_up_pre = (grad_act * gate_pre * sigmoid_gate).astype(jnp.bfloat16)
    grad_gate_w = jnp.einsum(
        "erd,erf->edf", inputs, grad_gate_pre, preferred_element_type=jnp.float32
    )
    grad_up_w = jnp.einsum("erd,erf->edf", inputs, grad_up_pre, preferred_element_type=jnp.float32)
    grad_inputs = jnp.einsum(
        "erf,edf->erd", grad_gate_pre, gate_full, preferred_element_type=jnp.float32
    )
    grad_inputs = grad_inputs + jnp.einsum(
        "erf,edf->erd", grad_up_pre, up_full, preferred_element_type=jnp.float32
    )
    return (
        ungroup_rows(grad_inputs.astype(jnp.bfloat16), row_block.shape),
        grad_gate_w,
        grad_up_w,
        grad_down,
    )


def contract_rows(left, right):
    return lax.dot_general(
        left, right, (((0,), (0,)), ((), ())), preferred_element_type=jnp.float32
    )


def contract_cols(left, right):
    return lax.dot_general(
        left, right, (((1,), (1,)), ((), ())), preferred_element_type=jnp.float32
    )


def on_device(
    hidden_in,
    segment_ids,
    routes,
    w_query,
    w_key,
    w_value,
    w_out,
    gain_attn,
    gain_query,
    gain_key,
    gain_ffn,
    w_router,
    w_gate,
    w_up,
    w_down,
    cotangent,
):
    hidden = hidden_in[0].astype(jnp.float32)
    tokens, model_width = hidden.shape
    head_count = model_width // HEAD
    row_seg = segment_ids[0]
    choice_rows = routes[0]
    offset = lax.axis_index("seq") * tokens
    positions = offset + lax.iota(jnp.int32, tokens)
    span = min(512, row_seg.shape[0])
    layer_full = (
        lax.all_gather(w_query, ("dp", "seq"), axis=0, tiled=True),
        lax.all_gather(w_key, ("dp", "seq"), axis=0, tiled=True),
        lax.all_gather(w_value, ("dp", "seq"), axis=0, tiled=True),
        lax.all_gather(w_out, ("dp", "seq"), axis=0, tiled=True),
        lax.all_gather(w_router, ("dp", "seq"), axis=0, tiled=True),
        lax.all_gather(gain_attn, ("dp", "seq"), axis=0, tiled=True),
        lax.all_gather(gain_query, ("dp", "seq"), axis=0, tiled=True),
        lax.all_gather(gain_key, ("dp", "seq"), axis=0, tiled=True),
        lax.all_gather(gain_ffn, ("dp", "seq"), axis=0, tiled=True),
    )
    expert_full = (
        lax.all_gather(w_gate, "dp", axis=1, tiled=True),
        lax.all_gather(w_up, "dp", axis=1, tiled=True),
        lax.all_gather(w_down, "dp", axis=2, tiled=True),
    )
    projected = project_front(hidden, layer_full, positions)
    keys_all, values_all = (
        lax.all_gather(projected[4], "seq", axis=0, tiled=True),
        lax.all_gather(projected[5], "seq", axis=0, tiled=True),
    )
    attention, log_total = attend_local(projected[3], keys_all, values_all, row_seg, offset, span)
    attended = attention.reshape(tokens, model_width).astype(jnp.bfloat16)
    hidden_mid = hidden + jnp.dot(attended, layer_full[3], preferred_element_type=jnp.float32)
    routing = route_tokens(hidden_mid, layer_full, choice_rows)
    expert_count, capacity = (routing[7].shape[0], routing[7].shape[1])
    expert_out = expert_forward(
        lax.all_to_all(routing[7], "seq", split_axis=0, concat_axis=0, tiled=True),
        expert_full[0],
        expert_full[1],
        expert_full[2],
    )
    returned = lax.all_to_all(expert_out, "seq", split_axis=0, concat_axis=0, tiled=True)
    picked = jnp.take(returned.reshape(expert_count * capacity, model_width), routing[4], axis=0)
    picked = picked.reshape(tokens, choice_rows.shape[1], model_width)
    mixture = jnp.sum(routing[3][:, :, None] * picked.astype(jnp.float32), axis=1)
    block_out = (hidden_mid + mixture).astype(jnp.bfloat16)
    layer_full = (
        lax.all_gather(w_query, ("dp", "seq"), axis=0, tiled=True),
        lax.all_gather(w_key, ("dp", "seq"), axis=0, tiled=True),
        lax.all_gather(w_value, ("dp", "seq"), axis=0, tiled=True),
        lax.all_gather(w_out, ("dp", "seq"), axis=0, tiled=True),
        lax.all_gather(w_router, ("dp", "seq"), axis=0, tiled=True),
        lax.all_gather(gain_attn, ("dp", "seq"), axis=0, tiled=True),
        lax.all_gather(gain_query, ("dp", "seq"), axis=0, tiled=True),
        lax.all_gather(gain_key, ("dp", "seq"), axis=0, tiled=True),
        lax.all_gather(gain_ffn, ("dp", "seq"), axis=0, tiled=True),
    )
    expert_full = (
        lax.all_gather(w_gate, "dp", axis=1, tiled=True),
        lax.all_gather(w_up, "dp", axis=1, tiled=True),
        lax.all_gather(w_down, "dp", axis=2, tiled=True),
    )
    projected = project_front(hidden, layer_full, positions)
    keys_all, values_all = (
        lax.all_gather(projected[4], "seq", axis=0, tiled=True),
        lax.all_gather(projected[5], "seq", axis=0, tiled=True),
    )
    attention, log_total = attend_local(projected[3], keys_all, values_all, row_seg, offset, span)
    attended = attention.reshape(tokens, model_width).astype(jnp.bfloat16)
    hidden_mid = hidden + jnp.dot(attended, layer_full[3], preferred_element_type=jnp.float32)
    routing = route_tokens(hidden_mid, layer_full, choice_rows)
    normed_ffn, chances, picks, gate_values, slot_ids, pair_table, spread, send_rows = routing
    grad_out = cotangent[0].astype(jnp.float32)
    grad_gates = jnp.sum(grad_out[:, None, :] * picked.astype(jnp.float32), axis=-1)
    slot_gates = jnp.sum(jnp.where(pair_table, gate_values.reshape(-1)[None, :], 0.0), axis=1)
    grad_rows_in = jnp.dot(spread, cotangent[0], preferred_element_type=jnp.float32)
    grad_slots = (
        (slot_gates[:, None] * grad_rows_in)
        .astype(jnp.bfloat16)
        .reshape(expert_count, capacity, model_width)
    )
    arrived_rows, arrived_grads = (
        lax.all_to_all(send_rows, "seq", split_axis=0, concat_axis=0, tiled=True),
        lax.all_to_all(grad_slots, "seq", split_axis=0, concat_axis=0, tiled=True),
    )
    grad_inputs, grad_gate_w, grad_up_w, grad_down_w = expert_backward(
        arrived_rows, arrived_grads, expert_full[0], expert_full[1], expert_full[2]
    )
    grad_back = lax.all_to_all(grad_inputs, "seq", split_axis=0, concat_axis=0, tiled=True)
    grad_normed_ffn = contract_rows(spread, grad_back.reshape(expert_count * capacity, model_width))
    grad_chances = jnp.sum(jnp.where(picks, grad_gates[:, :, None], 0.0), axis=1)
    grad_logits = (
        chances * (grad_chances - jnp.sum(chances * grad_chances, axis=-1, keepdims=True))
    ).astype(jnp.bfloat16)
    grad_router_w = contract_rows(normed_ffn, grad_logits)
    grad_normed_ffn = grad_normed_ffn + contract_cols(grad_logits, layer_full[4])
    unused_ffn, pull_ffn = jax.vjp(normalize, hidden_mid, layer_full[8].astype(jnp.float32))
    grad_mid_norm, grad_gain_ffn_w = pull_ffn(grad_normed_ffn)
    grad_mid = grad_out + grad_mid_norm
    grad_mid_low = grad_mid.astype(jnp.bfloat16)
    grad_w_out = contract_rows(attended, grad_mid_low)
    grad_attended = (
        contract_cols(grad_mid_low, layer_full[3])
        .astype(jnp.bfloat16)
        .reshape(tokens, head_count, HEAD)
    )
    query_rot = projected[3]
    delta, grad_query_rot = query_grads(
        query_rot, keys_all, values_all, row_seg, offset, span, log_total, grad_attended
    )
    scaling = HEAD ** (-0.5)
    query_seg = lax.dynamic_slice_in_dim(row_seg, offset, tokens)
    row_count = lax.axis_size("seq") * tokens
    step_rows = math.gcd(row_count, 512)

    def one_window(window_index, running):
        window_start = window_index * step_rows
        key_block, value_block, key_pos, key_seg = key_window(
            keys_all, values_all, row_seg, window_start, step_rows
        )
        scores = masked_scores(
            query_rot, key_block, positions, query_seg, key_pos, key_seg, scaling
        )
        weights = jnp.exp(scores - log_total[..., None])
        grad_weights = jnp.einsum(
            "qhd,khd->hqk", grad_attended, value_block, preferred_element_type=jnp.float32
        )
        grad_scores = (weights * (grad_weights - delta[..., None]) * scaling).astype(jnp.bfloat16)
        grad_key_part = jnp.einsum(
            "hqk,qhd->khd", grad_scores, query_rot, preferred_element_type=jnp.float32
        )
        grad_value_part = jnp.einsum(
            "hqk,qhd->khd",
            weights.astype(jnp.bfloat16),
            grad_attended,
            preferred_element_type=jnp.float32,
        )
        term = jnp.concatenate(
            [
                grad_key_part.reshape(step_rows, model_width),
                grad_value_part.reshape(step_rows, model_width),
            ],
            axis=1,
        )
        return lax.dynamic_update_slice_in_dim(running, term, window_index * step_rows, 0)

    key_sums = lax.psum_scatter(
        lax.fori_loop(
            0,
            row_count // step_rows,
            one_window,
            jnp.zeros((row_count, 2 * model_width), jnp.float32),
        ).astype(jnp.bfloat16),
        "seq",
        scatter_dimension=0,
        tiled=True,
    ).astype(jnp.float32)
    grad_key_rot = key_sums[:, :model_width].reshape(tokens, head_count, HEAD)
    grad_v_low = key_sums[:, model_width:].astype(jnp.bfloat16)

    def query_chain(projection, gain_vec):
        return rotate_normed(projection, gain_vec, positions)

    unused_query, pull_query = jax.vjp(query_chain, projected[1], layer_full[6].astype(jnp.float32))
    grad_query_pre, grad_gain_query_w = pull_query(grad_query_rot)
    unused_key, pull_key = jax.vjp(query_chain, projected[2], layer_full[7].astype(jnp.float32))
    grad_key_pre, grad_gain_key_w = pull_key(grad_key_rot)
    grad_q_low = grad_query_pre.astype(jnp.bfloat16)
    grad_k_low = grad_key_pre.astype(jnp.bfloat16)
    normed = projected[0]
    grad_w_query = contract_rows(normed, grad_q_low)
    grad_w_key = contract_rows(normed, grad_k_low)
    grad_w_value = contract_rows(normed, grad_v_low)
    grad_normed = (
        contract_cols(grad_q_low, layer_full[0])
        + contract_cols(grad_k_low, layer_full[1])
        + contract_cols(grad_v_low, layer_full[2])
    )
    unused_attn, pull_attn = jax.vjp(normalize, hidden, layer_full[5].astype(jnp.float32))
    grad_hidden_norm, grad_gain_attn_w = pull_attn(grad_normed)
    grad_hidden = grad_mid + grad_hidden_norm
    shares = (
        lax.psum_scatter(grad_w_query, ("dp", "seq"), scatter_dimension=0, tiled=True),
        lax.psum_scatter(grad_w_key, ("dp", "seq"), scatter_dimension=0, tiled=True),
        lax.psum_scatter(grad_w_value, ("dp", "seq"), scatter_dimension=0, tiled=True),
        lax.psum_scatter(grad_w_out, ("dp", "seq"), scatter_dimension=0, tiled=True),
        lax.psum_scatter(grad_router_w, ("dp", "seq"), scatter_dimension=0, tiled=True),
        lax.psum_scatter(grad_gain_attn_w, ("dp", "seq"), scatter_dimension=0, tiled=True),
        lax.psum_scatter(grad_gain_query_w, ("dp", "seq"), scatter_dimension=0, tiled=True),
        lax.psum_scatter(grad_gain_key_w, ("dp", "seq"), scatter_dimension=0, tiled=True),
        lax.psum_scatter(grad_gain_ffn_w, ("dp", "seq"), scatter_dimension=0, tiled=True),
    )
    expert_shares = (
        lax.psum_scatter(
            grad_gate_w.astype(jnp.bfloat16), "dp", scatter_dimension=1, tiled=True
        ).astype(jnp.float32),
        lax.psum_scatter(
            grad_up_w.astype(jnp.bfloat16), "dp", scatter_dimension=1, tiled=True
        ).astype(jnp.float32),
        lax.psum_scatter(
            grad_down_w.astype(jnp.bfloat16), "dp", scatter_dimension=2, tiled=True
        ).astype(jnp.float32),
    )
    return (
        block_out[None],
        grad_hidden[None],
        shares[0],
        shares[1],
        shares[2],
        shares[3],
        shares[5],
        shares[6],
        shares[7],
        shares[8],
        shares[4],
        expert_shares[0],
        expert_shares[1],
        expert_shares[2],
    )


VMEM_GRANT = 56 * 1024 * 1024


def mm(left, right, dims):
    return lax.dot_general(left, right, (dims, ((), ())), preferred_element_type=jnp.float32)


def cost(flops, transcendentals, *arrays):
    moved = sum(math.prod(a.shape) * a.dtype.itemsize for a in arrays)
    return pl.CostEstimate(
        flops=flops // 4, transcendentals=transcendentals // 4, bytes_accessed=moved // 4
    )


def grid_call(body, grid, in_specs, out_specs, outs, flops, transcendentals, *args):
    return pl.pallas_call(
        body,
        grid=grid,
        in_specs=in_specs,
        out_specs=out_specs,
        out_shape=outs,
        compiler_params=pltpu.CompilerParams(vmem_limit_bytes=VMEM_GRANT),
        cost_estimate=cost(flops, transcendentals, *args, *jax.tree.leaves(outs)),
    )(*args)


def row_tiles(rows):
    return math.gcd(rows, 512)


def finish_attention(order, attended, out_pieces, x_row, gain, router, chosen, own, expert_count):
    shards, rows, cols = attended.shape
    width = x_row.shape[1]
    held = own.shape[0]
    chunk = width // 4
    per_chunk = chunk // cols
    tm = math.gcd(rows, 256)

    def body(order_ref, att_ref, p0, p1, p2, p3, x_ref, gain_ref, router_ref, chosen_ref, own_ref, *outs):
        mid_ref, normed_ref, r_ref, chance_ref, gate_ref, att_all = outs
        for h in range(shards):
            source = order_ref[h // per_chunk] * per_chunk + h % per_chunk
            att_all[:, h * cols : (h + 1) * cols] = att_ref[source]
        squares = jnp.zeros((tm, 1), jnp.float32)
        for n in range(4):
            at = slice(n * chunk, (n + 1) * chunk)
            total = x_ref[:, at].astype(jnp.float32)
            for j, piece in enumerate((p0, p1, p2, p3)):
                k = n ^ j
                total = total + mm(
                    att_all[:, j * chunk : (j + 1) * chunk],
                    piece[:, k * chunk : (k + 1) * chunk],
                    ((1,), (0,)),
                )
            mid_ref[:, at] = total
            squares = squares + jnp.sum(total * total, axis=-1, keepdims=True)
        r = lax.rsqrt(squares / width + epsilon)
        r_ref[...] = r
        logits = jnp.zeros((tm, 128), jnp.float32)
        for n in range(4):
            at = slice(n * chunk, (n + 1) * chunk)
            normed = (mid_ref[:, at] * r * gain_ref[:, at]).astype(jnp.bfloat16)
            normed_ref[:, at] = normed
            logits = logits + mm(normed, router_ref[at, :], ((1,), (0,)))
        lane = lax.broadcasted_iota(jnp.int32, (tm, 128), 1)
        logits = jnp.where(lane < expert_count, logits, masked_score)
        raised = jnp.exp(logits - jnp.max(logits, axis=-1, keepdims=True))
        chances = raised / jnp.sum(raised, axis=-1, keepdims=True)
        chance_ref[...] = chances
        taken = chances * chosen_ref[...]
        for e in range(held):
            gate_ref[e] = jnp.sum(taken * own_ref[e : e + 1, :], axis=-1, keepdims=True)

    full = jnp.float32
    piece_spec = pl.BlockSpec((chunk, width), lambda i, o: (0, 0))
    wide = pl.BlockSpec((tm, width), lambda i, o: (i, 0))
    lanes = pl.BlockSpec((tm, 128), lambda i, o: (i, 0))
    outs = [
        jax.ShapeDtypeStruct((rows, width), full),
        jax.ShapeDtypeStruct((rows, width), jnp.bfloat16),
        jax.ShapeDtypeStruct((rows, 1), full),
        jax.ShapeDtypeStruct((rows, 128), full),
        jax.ShapeDtypeStruct((held, rows, 1), full),
    ]
    return pl.pallas_call(
        body,
        grid_spec=pltpu.PrefetchScalarGridSpec(
            num_scalar_prefetch=1,
            grid=(rows // tm,),
            in_specs=[
                pl.BlockSpec((shards, tm, cols), lambda i, o: (0, i, 0)),
                piece_spec,
                piece_spec,
                piece_spec,
                piece_spec,
                wide,
                pl.BlockSpec((1, width), lambda i, o: (0, 0)),
                pl.BlockSpec((width, 128), lambda i, o: (0, 0)),
                lanes,
                pl.BlockSpec((held, 128), lambda i, o: (0, 0)),
            ],
            out_specs=[
                wide,
                wide,
                pl.BlockSpec((tm, 1), lambda i, o: (i, 0)),
                lanes,
                pl.BlockSpec((held, tm, 1), lambda i, o: (0, i, 0)),
            ],
            scratch_shapes=[pltpu.VMEM((tm, width), jnp.bfloat16)],
        ),
        out_shape=outs,
        compiler_params=pltpu.CompilerParams(vmem_limit_bytes=VMEM_GRANT),
        cost_estimate=cost(2 * rows * width * width, rows * 128, attended, *out_pieces, *outs),
    )(order, attended, *out_pieces, x_row, gain, router, chosen, own)


def expert_activations(normed, gate, up):
    held, width, ff = gate.shape
    rows = normed.shape[0]
    tile, tm = (math.gcd(ff, 512), row_tiles(rows))

    def body(x_ref, gate_ref, up_ref, act_ref, dgate_ref, dup_ref):
        @pl.loop(0, rows // tm)
        def _(i):
            at = pl.ds(pl.multiple_of(i * tm, tm), tm)
            gate_pre = mm(x_ref[at, :], gate_ref[0], ((1,), (0,)))
            up_pre = mm(x_ref[at, :], up_ref[0], ((1,), (0,)))
            sig = lax.logistic(gate_pre)
            silu = gate_pre * sig
            act_ref[0, at, :] = (silu * up_pre).astype(jnp.bfloat16)
            dgate_ref[0, at, :] = (up_pre * (sig + silu * (1.0 - sig))).astype(jnp.bfloat16)
            dup_ref[0, at, :] = silu.astype(jnp.bfloat16)

    tiled = pl.BlockSpec((1, rows, tile), lambda e, f: (e, 0, f))
    low = jax.ShapeDtypeStruct((held, rows, ff), jnp.bfloat16)
    return grid_call(
        body,
        (held, ff // tile),
        [
            pl.BlockSpec((rows, width), lambda e, f: (0, 0)),
            pl.BlockSpec((1, width, tile), lambda e, f: (e, 0, f)),
            pl.BlockSpec((1, width, tile), lambda e, f: (e, 0, f)),
        ],
        [tiled, tiled, tiled],
        [low, low, low],
        4 * held * rows * ff * width,
        held * rows * ff,
        normed,
        gate,
        up,
    )


def expert_gradients(dy, down, act, dgate_factor, dup_factor, weight):
    held, ff, width = down.shape
    rows = dy.shape[0]
    tile, tm = (math.gcd(ff, 512), row_tiles(rows))

    def body(dy_ref, down_ref, act_ref, a_ref, b_ref, weight_ref, out_ref, dgate_ref, dup_ref, sum_ref):
        first = pl.program_id(1) == 0

        @pl.loop(0, rows // tm)
        def _(i):
            at = pl.ds(pl.multiple_of(i * tm, tm), tm)
            grad = mm(dy_ref[at, :], down_ref[0], ((1,), (1,)))
            scale = weight_ref[0, at, :]
            act = act_ref[0, at, :].astype(jnp.float32)
            product = act * grad
            partial = product[:, :128]
            for j in range(1, tile // 128):
                partial = partial + product[:, j * 128 : (j + 1) * 128]

            @pl.when(first)
            def _():
                sum_ref[0, at, :] = partial

            @pl.when(jnp.logical_not(first))
            def _():
                sum_ref[0, at, :] = sum_ref[0, at, :] + partial

            out_ref[0, at, :] = (scale * act).astype(jnp.bfloat16)
            grad = scale * grad
            dgate_ref[0, at, :] = (grad * a_ref[0, at, :].astype(jnp.float32)).astype(jnp.bfloat16)
            dup_ref[0, at, :] = (grad * b_ref[0, at, :].astype(jnp.float32)).astype(jnp.bfloat16)

    tiled = pl.BlockSpec((1, rows, tile), lambda e, f: (e, 0, f))
    low = jax.ShapeDtypeStruct((held, rows, ff), jnp.bfloat16)
    return grid_call(
        body,
        (held, ff // tile),
        [
            pl.BlockSpec((rows, width), lambda e, f: (0, 0)),
            pl.BlockSpec((1, tile, width), lambda e, f: (e, f, 0)),
            tiled,
            tiled,
            tiled,
            pl.BlockSpec((1, rows, 1), lambda e, f: (e, 0, 0)),
        ],
        [tiled, tiled, tiled, pl.BlockSpec((1, rows, 128), lambda e, f: (e, 0, 0))],
        [low, low, low, jax.ShapeDtypeStruct((held, rows, 128), jnp.float32)],
        2 * held * rows * ff * width,
        0,
        dy,
        down,
        act,
        dgate_factor,
        dup_factor,
        weight,
    )


def input_gradient(dgate, dup, gate, up, gate_sums, chances, chosen, own, router):
    held, width, ff = gate.shape
    rows = dgate.shape[1]
    tile, tm = (math.gcd(width, 512), row_tiles(rows))

    def body(dgate_ref, dup_ref, gate_ref, up_ref, sum_ref, chance_ref, chosen_ref, own_ref, router_ref, out_ref, logits_ref):
        @pl.loop(0, rows // tm)
        def _(i):
            at = pl.ds(pl.multiple_of(i * tm, tm), tm)
            chances = chance_ref[at, :]
            placed = jnp.zeros((tm, 128), jnp.float32)
            for e in range(held):
                got = jnp.sum(sum_ref[e, at, :], axis=-1, keepdims=True)
                placed = placed + own_ref[e : e + 1, :] * got
            placed = placed * chosen_ref[at, :]
            inner = jnp.sum(chances * placed, axis=-1, keepdims=True)
            logits = (chances * (placed - inner)).astype(jnp.bfloat16)
            logits_ref[at, :] = logits
            total = mm(logits, router_ref[...], ((1,), (1,)))
            for e in range(held):
                total = total + mm(dgate_ref[e, at, :], gate_ref[e], ((1,), (1,)))
                total = total + mm(dup_ref[e, at, :], up_ref[e], ((1,), (1,)))
            out_ref[at, :] = total.astype(jnp.bfloat16)

    whole = pl.BlockSpec((held, rows, ff), lambda n: (0, 0, 0))
    weights = pl.BlockSpec((held, tile, ff), lambda n: (0, n, 0))
    lanes = pl.BlockSpec((rows, 128), lambda n: (0, 0))
    return grid_call(
        body,
        (width // tile,),
        [
            whole,
            whole,
            weights,
            weights,
            pl.BlockSpec((held, rows, 128), lambda n: (0, 0, 0)),
            lanes,
            lanes,
            pl.BlockSpec((held, 128), lambda n: (0, 0)),
            pl.BlockSpec((tile, 128), lambda n: (n, 0)),
        ],
        [pl.BlockSpec((rows, tile), lambda n: (0, n)), lanes],
        [jax.ShapeDtypeStruct((rows, width), jnp.bfloat16), jax.ShapeDtypeStruct((rows, 128), jnp.bfloat16)],
        4 * held * rows * ff * width,
        0,
        dgate,
        dup,
        gate,
        up,
        gate_sums,
        chances,
        chosen,
        own,
        router,
    )


def combine_experts(y_at, act, down, weight):
    held, ff, width = down.shape
    rows = act.shape[1]
    block = rows // 8
    tile, tm = (math.gcd(width, 512), 4 * block)

    def body(y_ref, act_ref, down_ref, weight_ref, near_ref, far_ref):
        for i in range(2):
            at = slice(i * tm, (i + 1) * tm)
            total = weight_ref[0, at, :] * mm(act_ref[0, at, :], down_ref[0], ((1,), (0,)))
            for e in range(1, held):
                term = mm(act_ref[e, at, :], down_ref[e], ((1,), (0,)))
                total = total + weight_ref[e, at, :] * term
            total = total.astype(jnp.bfloat16)
            for y, outs in ((0, (near_ref, far_ref)), (1, (far_ref, near_ref))):

                @pl.when(y_ref[0] == y)
                def _(outs=outs):
                    for j in range(4):
                        to = (2 * i + j // 2) * block
                        outs[j % 2][to : to + block, :] = total[j * block : (j + 1) * block]

    half = jax.ShapeDtypeStruct((rows // 2, width), jnp.bfloat16)
    tiled = pl.BlockSpec((rows // 2, tile), lambda n, y: (0, n))
    return pl.pallas_call(
        body,
        grid_spec=pltpu.PrefetchScalarGridSpec(
            num_scalar_prefetch=1,
            grid=(width // tile,),
            in_specs=[
                pl.BlockSpec((held, rows, ff), lambda n, y: (0, 0, 0)),
                pl.BlockSpec((held, ff, tile), lambda n, y: (0, 0, n)),
                pl.BlockSpec((held, rows, 1), lambda n, y: (0, 0, 0)),
            ],
            out_specs=[tiled, tiled],
        ),
        out_shape=[half, half],
        compiler_params=pltpu.CompilerParams(vmem_limit_bytes=VMEM_GRANT),
        cost_estimate=cost(2 * held * rows * ff * width, 0, act, down, half, half),
    )(y_at, act, down, weight)


def weight_pieces(left, right, parts, split_left):
    flat, stacked = (left, right) if split_left else (right, left)
    held, rows, ff = stacked.shape
    piece = flat.shape[1] // parts
    shape = (held, piece, ff) if split_left else (held, ff, piece)
    tm = math.gcd(shape[1], 512)

    def body(flat_ref, stacked_ref, *outs):
        step = pl.program_id(0)
        for j in range(parts):

            @pl.when(step == j)
            def _(j=j):
                @pl.loop(0, shape[1] // tm)
                def _(i):
                    at = pl.ds(pl.multiple_of(i * tm, tm), tm)
                    if split_left:
                        value = mm(flat_ref[:, at], stacked_ref[0], ((0,), (0,)))
                    else:
                        value = mm(stacked_ref[0, :, at], flat_ref[...], ((0,), (0,)))
                    outs[j][0, at, :] = value.astype(jnp.bfloat16)

    def place(j):
        return lambda k, e: (jnp.where(k < j, 0, jnp.where(k > j, held - 1, e)), 0, 0)

    return grid_call(
        body,
        (parts, held),
        [
            pl.BlockSpec((rows, piece), lambda k, e: (0, k)),
            pl.BlockSpec((1, rows, ff), lambda k, e: (e, 0, 0)),
        ],
        [pl.BlockSpec((1,) + shape[1:], place(j)) for j in range(parts)],
        [jax.ShapeDtypeStruct(shape, jnp.bfloat16)] * parts,
        2 * held * rows * ff * flat.shape[1],
        0,
        flat,
        stacked,
    )


def rope_tables(row_count, head_dim):
    half_dim = head_dim // 2
    frequency = jnp.exp(
        jnp.arange(half_dim, dtype=jnp.float32) * (-2.0 * math.log(rope_base) / head_dim)
    )
    angles = jnp.arange(row_count, dtype=jnp.float32)[:, None] * frequency[None, :]
    cosine, sine = (jnp.cos(angles), jnp.sin(angles))
    return (
        jnp.concatenate([cosine, cosine], axis=1),
        jnp.concatenate([-sine, sine], axis=1),
    )


def seen(first, count, keys, seg_col, seg_row):
    position = first + lax.broadcasted_iota(jnp.int32, (count, keys), 0)
    other = lax.broadcasted_iota(jnp.int32, (count, keys), 1)
    return (position >= other) & (seg_col == seg_row)


def pair_rows(first, second):
    lane = lax.broadcasted_iota(jnp.int32, (first.shape[0], 128), 1)
    both = jnp.where(lane == 0, first, jnp.where(lane == 1, second, 0.0))
    return both.T[:8]


def pair_columns(sums):
    total = sum(sums[1:], sums[0])
    total = jnp.concatenate([total] * 16, axis=0).T
    return (total[:, 0:1], total[:, 1:2])


def project(x_row, gain, w_qkv):
    rows, width = x_row.shape
    held_cols = w_qkv.shape[1]
    cols = held_cols // 3
    tm = math.gcd(rows, 256)

    def body(x_ref, gain_ref, w_ref, normed_ref, qkv_ref, r_ref, stat_ref):
        x = x_ref[...].astype(jnp.float32)
        r = lax.rsqrt(jnp.mean(x * x, axis=-1, keepdims=True) + epsilon)
        r_ref[...] = r
        normed = (x * r * gain_ref[...]).astype(jnp.bfloat16)
        normed_ref[...] = normed
        qkv = mm(normed, w_ref[...], ((1,), (0,)))
        qkv_ref[...] = qkv
        squares = qkv[:, : 2 * cols] * qkv[:, : 2 * cols]
        stat_ref[...] = pair_rows(
            jnp.sum(squares[:, :cols], axis=-1, keepdims=True),
            jnp.sum(squares[:, cols:], axis=-1, keepdims=True),
        )

    full = jnp.float32
    return grid_call(
        body,
        (rows // tm,),
        [
            pl.BlockSpec((tm, width), lambda i: (i, 0)),
            pl.BlockSpec((1, width), lambda i: (0, 0)),
            pl.BlockSpec((width, held_cols), lambda i: (0, 0)),
        ],
        [
            pl.BlockSpec((tm, width), lambda i: (i, 0)),
            pl.BlockSpec((tm, held_cols), lambda i: (i, 0)),
            pl.BlockSpec((tm, 1), lambda i: (i, 0)),
            pl.BlockSpec((8, tm), lambda i: (0, i)),
        ],
        [
            jax.ShapeDtypeStruct((rows, width), jnp.bfloat16),
            jax.ShapeDtypeStruct((rows, held_cols), full),
            jax.ShapeDtypeStruct((rows, 1), full),
            jax.ShapeDtypeStruct((8, rows), full),
        ],
        2 * rows * width * held_cols,
        0,
        x_row,
        gain,
        w_qkv,
    )


def attend(qkv, sums, width, g_query, g_key, cosine, sine, seg_col, seg_row):
    rows, held_cols = qkv.shape
    cols = held_cols // 3
    heads = cols // HEAD
    tq = math.gcd(rows, 256)
    scaling = HEAD ** (-0.5)
    shards = sums.shape[0]

    def body(q, k, v, sums_ref, gq, gk, cos, sin, sc, sr, q_out, k_out, v_out, att_out, log_out, rq, rk):
        @pl.when(pl.program_id(0) == 0)
        def _():
            for i in range(rows // tq):
                at = slice(i * tq, (i + 1) * tq)
                first, second = pair_columns([sums_ref[d, :, at] for d in range(shards)])
                rq[at, :] = lax.rsqrt(first / width + epsilon)
                rk[at, :] = lax.rsqrt(second / width + epsilon)

        def rotated(ref, r, g):
            values = ref[...] * r[...] * g[...]
            swapped = pltpu.roll(values, HEAD // 2, 1)
            return (values * cos[...] + swapped * sin[...]).astype(jnp.bfloat16)

        q_out[...] = rotated(q, rq, gq)
        k_out[...] = rotated(k, rk, gk)
        v_out[...] = v[...].astype(jnp.bfloat16)
        for i in range(rows // tq):
            at, keys = (slice(i * tq, (i + 1) * tq), (i + 1) * tq)
            scores = mm(q_out[at, :], k_out[:keys, :], ((1,), (1,))) * scaling
            allowed = seen(i * tq, tq, keys, sc[at, :], sr[:, :keys])
            scores = jnp.where(allowed, scores, masked_score)
            peak = jnp.max(scores, axis=-1, keepdims=True)
            raised = jnp.exp(scores - peak)
            total = jnp.sum(raised, axis=-1, keepdims=True)
            log_out[0, at, :] = peak + jnp.log(total)
            weights = (raised * (1.0 / total)).astype(jnp.bfloat16)
            att_out[at, :] = mm(weights, v_out[:keys, :], ((1,), (0,))).astype(jnp.bfloat16)

    def col(offset):
        return pl.BlockSpec((rows, HEAD), lambda h: (0, offset + h))

    row = pl.BlockSpec((1, HEAD), lambda h: (0, h))
    one = pl.BlockSpec((rows, 1), lambda h: (0, 0))
    table = pl.BlockSpec((rows, HEAD), lambda h: (0, 0))
    low = jax.ShapeDtypeStruct((rows, cols), jnp.bfloat16)
    column = jax.ShapeDtypeStruct((rows, 1), jnp.float32)
    return grid_call(
        body,
        (heads,),
        [
            col(0),
            col(heads),
            col(2 * heads),
            pl.BlockSpec((shards, 8, rows), lambda h: (0, 0, 0)),
            row,
            row,
            table,
            table,
            one,
            pl.BlockSpec((1, rows), lambda h: (0, 0)),
        ],
        [col(0)] * 4 + [pl.BlockSpec((1, rows, 1), lambda h: (h, 0, 0)), one, one],
        [low] * 4 + [jax.ShapeDtypeStruct((heads, rows, 1), jnp.float32), column, column],
        4 * heads * rows * rows * HEAD,
        heads * rows * rows,
        qkv,
        qkv,
        qkv,
        sums,
        g_query,
        g_key,
        cosine,
        sine,
        seg_col,
        seg_row,
    )


def attend_back(qkv, q_rot, k_rot, value_in, grad, log_total, r_query, r_key, g_query, g_key, cosine, sine, seg_col, seg_row):
    rows, cols = q_rot.shape
    heads = cols // HEAD
    tq = math.gcd(rows, 256)
    scaling = HEAD ** (-0.5)

    def body(q, k, qr, kr, v, ga, lt, rq, rk, gq, gk, cos, sin, sc, sr, q_out, k_out, v_out, stat_out, gq_out, gk_out, q_sum, k_sum, v_sum, stats):
        k_sum[...] = jnp.zeros_like(k_sum)
        v_sum[...] = jnp.zeros_like(v_sum)
        for i in range(rows // tq):
            at, keys = (slice(i * tq, (i + 1) * tq), (i + 1) * tq)
            scores = mm(qr[at, :], kr[:keys, :], ((1,), (1,))) * scaling
            allowed = seen(i * tq, tq, keys, sc[at, :], sr[:, :keys])
            p = jnp.exp(jnp.where(allowed, scores, masked_score) - lt[0, at, :])
            grad_weights = mm(ga[at, :], v[:keys, :], ((1,), (1,)))
            delta = jnp.sum(p * grad_weights, axis=-1, keepdims=True)
            grad_scores = (scaling * p * (grad_weights - delta)).astype(jnp.bfloat16)
            q_sum[at, :] = mm(grad_scores, kr[:keys, :], ((1,), (0,)))
            k_sum[:keys, :] += mm(grad_scores, qr[at, :], ((0,), (0,)))
            v_sum[:keys, :] += mm(p.astype(jnp.bfloat16), ga[at, :], ((0,), (0,)))

        first = pl.program_id(0) == 0

        def back(total, ref, r, g, out, place, gain):
            values = total[...]
            values = values * cos[...] - pltpu.roll(values, HEAD // 2, 1) * sin[...]
            gain[...] = jnp.sum(values * ref[...] * r[...], axis=0, keepdims=True)
            values = values * g[...]
            stat = jnp.sum(values * ref[...], axis=-1, keepdims=True)
            stats[place] += stat
            out[...] = values

        @pl.when(first)
        def _():
            stats[...] = jnp.zeros_like(stats)

        back(q_sum, q, rq, gq, q_out, 0, gq_out)
        back(k_sum, k, rk, gk, k_out, 1, gk_out)

        @pl.when(pl.program_id(0) == heads - 1)
        def _():
            for i in range(rows // tq):
                at = slice(i * tq, (i + 1) * tq)
                stat_out[:, at] = pair_rows(stats[0, at, :], stats[1, at, :])

        v_out[...] = v_sum[...].astype(jnp.bfloat16)

    def col(offset):
        return pl.BlockSpec((rows, HEAD), lambda h: (0, offset + h))

    row = pl.BlockSpec((1, HEAD), lambda h: (0, h))
    one = pl.BlockSpec((rows, 1), lambda h: (0, 0))
    stat = pl.BlockSpec((1, rows, 1), lambda h: (h, 0, 0))
    table = pl.BlockSpec((rows, HEAD), lambda h: (0, 0))
    full = jnp.float32
    outs = (
        [jax.ShapeDtypeStruct((rows, cols), full)] * 2
        + [jax.ShapeDtypeStruct((rows, cols), jnp.bfloat16)]
        + [jax.ShapeDtypeStruct((8, rows), full)]
        + [jax.ShapeDtypeStruct((1, cols), full)] * 2
    )
    args = (qkv, qkv, q_rot, k_rot, value_in, grad, log_total, r_query, r_key, g_query, g_key, cosine, sine, seg_col, seg_row)
    return pl.pallas_call(
        body,
        grid=(heads,),
        in_specs=[col(0), col(heads), col(0), col(0), col(0), col(0), stat, one, one, row, row, table, table, one,
                  pl.BlockSpec((1, rows), lambda h: (0, 0))],
        out_specs=[col(0), col(0), col(0), pl.BlockSpec((8, rows), lambda h: (0, 0)), row, row],
        out_shape=outs,
        scratch_shapes=[pltpu.VMEM((rows, HEAD), full)] * 3 + [pltpu.VMEM((2, rows, 1), full)],
        compiler_params=pltpu.CompilerParams(vmem_limit_bytes=VMEM_GRANT),
        cost_estimate=cost(10 * heads * rows * rows * HEAD, heads * rows * rows, *args, *outs),
    )(*args)


def normed_gradient(q_grad, k_grad, v_low, qkv, sums, r_query, r_key, w_qkv, x_row, r_attn):
    rows, cols = q_grad.shape
    width = x_row.shape[1]
    shards = sums.shape[0]
    tm = math.gcd(rows, 256)

    def body(qg, kg, v, q, k, sums_ref, rq, rk, w, x, ra, low_ref, out_ref, gain_ref):
        means = pair_columns([sums_ref[d] for d in range(shards)])
        parts = []
        for grad, ref, r_ref, mean in ((qg, q, rq, means[0]), (kg, k, rk, means[1])):
            r = r_ref[...]
            part = r * grad[...] - ref[...] * (r * r * r) * (mean / width)
            parts.append(part.astype(jnp.bfloat16))
        parts.append(v[...])
        for i in range(3):
            low_ref[:, i * cols : (i + 1) * cols] = parts[i]
        total = mm(low_ref[...], w[...], ((1,), (1,)))
        out_ref[...] = total.astype(jnp.bfloat16)
        gain = jnp.sum(total * x[...].astype(jnp.float32) * ra[...], axis=0, keepdims=True)
        first = pl.program_id(0) == 0

        @pl.when(first)
        def _():
            gain_ref[...] = gain

        @pl.when(jnp.logical_not(first))
        def _():
            gain_ref[...] += gain

    def tiled(count, at=0):
        return pl.BlockSpec((tm, count), lambda i: (i, at))

    return grid_call(
        body,
        (rows // tm,),
        [
            tiled(cols),
            tiled(cols),
            tiled(cols),
            tiled(cols),
            tiled(cols, 1),
            pl.BlockSpec((shards, 8, tm), lambda i: (0, 0, i)),
            tiled(1),
            tiled(1),
            pl.BlockSpec((width, 3 * cols), lambda i: (0, 0)),
            tiled(width),
            tiled(1),
        ],
        [tiled(3 * cols), tiled(width), pl.BlockSpec((1, width), lambda i: (0, 0))],
        [
            jax.ShapeDtypeStruct((rows, 3 * cols), jnp.bfloat16),
            jax.ShapeDtypeStruct((rows, width), jnp.bfloat16),
            jax.ShapeDtypeStruct((1, width), jnp.float32),
        ],
        6 * rows * width * cols,
        0,
        q_grad,
        k_grad,
        v_low,
        qkv,
        qkv,
        sums,
        r_query,
        r_key,
        w_qkv,
        x_row,
        r_attn,
    )


def middle(order, nf_own, mid, r_ffn, gain, dy, out_pieces):
    tokens, width = nf_own.shape
    chunk = width // 4

    def body(order_ref, nf, mid_ref, r_ref, gain_ref, dy_ref, p0, p1, p2, p3, grad_ref, low_ref, att_ref, gain_out):
        r = r_ref[...]
        own = mid_ref[...]
        grad = nf[...].astype(jnp.float32)
        gain_out[...] = jnp.sum(grad * own * r, axis=0, keepdims=True)
        grad = grad * gain_ref[...]
        mean = jnp.mean(grad * own, axis=-1, keepdims=True)
        total = dy_ref[...].astype(jnp.float32) + r * grad - own * (r * r * r) * mean
        grad_ref[...] = total
        low_ref[...] = total.astype(jnp.bfloat16)
        for j, piece in enumerate((p0, p1, p2, p3)):
            back = jnp.zeros((tokens, chunk), jnp.float32)
            for k in range(4):
                n = k ^ j
                back = back + mm(
                    low_ref[:, n * chunk : (n + 1) * chunk],
                    piece[:, k * chunk : (k + 1) * chunk],
                    ((1,), (1,)),
                )
            att_ref[order_ref[j]] = back.astype(jnp.bfloat16)

    def whole(*shape):
        return pl.BlockSpec(shape, lambda i, o: (0,) * len(shape))

    outs = [
        jax.ShapeDtypeStruct((tokens, width), jnp.float32),
        jax.ShapeDtypeStruct((tokens, width), jnp.bfloat16),
        jax.ShapeDtypeStruct((4, tokens, chunk), jnp.bfloat16),
        jax.ShapeDtypeStruct((1, width), jnp.float32),
    ]
    return pl.pallas_call(
        body,
        grid_spec=pltpu.PrefetchScalarGridSpec(
            num_scalar_prefetch=1,
            grid=(1,),
            in_specs=[
                whole(tokens, width),
                pl.BlockSpec((tokens, width), lambda i, o: (o[4], 0)),
                pl.BlockSpec((tokens, 1), lambda i, o: (o[4], 0)),
                whole(1, width),
                whole(tokens, width),
                *[whole(chunk, width)] * 4,
            ],
            out_specs=[whole(*o.shape) for o in outs],
        ),
        out_shape=outs,
        compiler_params=pltpu.CompilerParams(vmem_limit_bytes=VMEM_GRANT),
        cost_estimate=cost(2 * tokens * width * width, 0, *out_pieces, *outs),
    )(order, nf_own, mid, r_ffn, gain, dy, *out_pieces)


def out_grad_pieces(order, attended, columns):
    shards, rows, cols = attended.shape
    per_chunk = shards // 4
    count = columns.shape[1]
    tm = math.gcd(cols, 256)

    def body(order_ref, att_ref, col_ref, *outs):
        step = pl.program_id(0)
        for j in range(4):

            @pl.when(step == j)
            def _(j=j):
                outs[j][...] = mm(att_ref[0], col_ref[...], ((0,), (0,))).astype(jnp.bfloat16)

    def place(j):
        return lambda k, i, o: (jnp.where(k < j, 0, jnp.where(k > j, per_chunk - 1, i)), 0)

    outs = [jax.ShapeDtypeStruct((per_chunk * cols, count), jnp.bfloat16)] * 4
    return pl.pallas_call(
        body,
        grid_spec=pltpu.PrefetchScalarGridSpec(
            num_scalar_prefetch=1,
            grid=(4, per_chunk),
            in_specs=[
                pl.BlockSpec((1, rows, cols), lambda k, i, o: (o[k] * per_chunk + i, 0, 0)),
                pl.BlockSpec((rows, count), lambda k, i, o: (0, 0)),
            ],
            out_specs=[pl.BlockSpec((cols, count), place(j)) for j in range(4)],
        ),
        out_shape=outs,
        compiler_params=pltpu.CompilerParams(vmem_limit_bytes=VMEM_GRANT),
        cost_estimate=cost(2 * rows * shards * cols * count, 0, attended, columns, *outs),
    )(order, attended, columns)


def over_y(values):
    return lax.ppermute(values, "seq", [(i, i ^ 1) for i in range(8)])


def along_z(values):
    lines = [[0, 2, 4, 6], [1, 3, 5, 7]]
    return lax.all_gather(values, "seq", axis=0, tiled=False, axis_index_groups=lines)


def both_y(line, other):
    y = lax.axis_index("seq") % 2
    row = jnp.zeros((4, 2) + line.shape[1:], line.dtype)
    for blocks, at in ((line, y), (other, 1 - y)):
        row = lax.dynamic_update_slice(row, blocks[:, None], (0, at) + (0,) * (line.ndim - 1))
    return row.reshape((8,) + line.shape[1:])


def sum_along_z(values):
    lines = [[0, 2, 4, 6], [1, 3, 5, 7]]
    return lax.psum_scatter(
        values, "seq", scatter_dimension=0, tiled=True, axis_index_groups=lines
    )


def swap(values, bits):
    return lax.ppermute(values, "dp", [(i, i ^ bits) for i in range(4)])


def sum_in_chip(pieces, sent):
    wide = jnp.float32
    kept = pieces[0].astype(wide) + swap(pieces[1], 1).astype(wide)
    return (kept.astype(sent), (pieces[2].astype(wide) + swap(pieces[3], 1).astype(wide)).astype(sent))


def across_by_expert(passed):
    return [swap(passed[e], 2) for e in range(passed.shape[0])]


def add_arrived(kept, arrived):
    return jnp.stack(
        [kept[e].astype(jnp.float32) + a.astype(jnp.float32) for e, a in enumerate(arrived)]
    )


def sum_pieces(pieces, sent):
    kept, passed = sum_in_chip(pieces, sent)
    return kept.astype(jnp.float32) + swap(passed, 2).astype(jnp.float32)


def reorder(values, dp_index, axis):
    size = values.shape[axis] // 4
    return jnp.concatenate(
        [
            lax.dynamic_slice_in_dim(values, (dp_index ^ k) * size, size, axis=axis)
            for k in range(4)
        ],
        axis=axis,
    )


def on_device_heads(
    hidden_in,
    segment_ids,
    routes,
    w_query,
    w_key,
    w_value,
    w_out,
    gain_attn,
    gain_query,
    gain_key,
    gain_ffn,
    w_router,
    w_gate,
    w_up,
    w_down,
    cotangent,
):
    low, full = (jnp.bfloat16, jnp.float32)
    shards = lax.axis_size("seq")
    seq_index, dp_index = (lax.axis_index("seq"), lax.axis_index("dp"))
    tokens, width = hidden_in.shape[1:]
    rows = shards * tokens
    cols = width // shards
    heads = cols // HEAD
    held = w_gate.shape[0]
    expert_count = held * shards
    block_rows = w_query.shape[0]
    chunk = shards * block_rows
    row_seg = segment_ids[0]
    first_row = seq_index * tokens
    barrier = lax.optimization_barrier

    def own_cols(values, count):
        return lax.dynamic_slice_in_dim(values, seq_index * count, count, axis=values.ndim - 1)

    cosine, sine = rope_tables(rows, HEAD)
    seg_col, seg_row = (row_seg[:, None], row_seg[None, :])

    x_shard = reorder(hidden_in[0], dp_index, 1)
    x_row = lax.all_gather(x_shard, "seq", axis=0, tiled=True)
    blocks = jnp.stack(
        [w.reshape(block_rows, shards, cols).transpose(1, 0, 2) for w in (w_query, w_key, w_value)],
        axis=1,
    )
    blocks = blocks.reshape(shards, 3 * block_rows, cols)
    place_at = (dp_index * shards + seq_index) * block_rows
    gain_rows = lax.dynamic_update_slice(
        jnp.zeros((shards, 16, cols), low),
        jnp.stack([gain_query, gain_key])[None],
        (place_at // cols, 0, place_at % cols),
    )
    gain_rows = lax.dynamic_update_slice(
        gain_rows, jnp.broadcast_to(gain_attn[None, None], (shards, 1, block_rows)), (0, 2, 0)
    )
    blocks = lax.all_to_all(jnp.concatenate([blocks, gain_rows], axis=1), "seq", 0, 0, tiled=True)
    across = swap(blocks, 2)
    qkv_pieces = (blocks, swap(blocks, 1), across, swap(across, 1))
    gate_across = swap(w_gate, 2)
    w_qkv = jnp.concatenate(
        [
            p[:, : 3 * block_rows]
            .reshape(shards, 3, block_rows, cols)
            .transpose(0, 2, 1, 3)
            .reshape(chunk, 3 * cols)
            for p in qkv_pieces
        ],
        axis=0,
    )
    gain_rows = jnp.concatenate([p[:, 3 * block_rows :] for p in qkv_pieces], axis=0)
    gain_pair = jnp.sum(gain_rows[:, :2].astype(full), axis=0)
    g_query, g_key = (gain_pair[0:1], gain_pair[1:2])
    g_attn = gain_rows[:, 2, :block_rows].reshape(1, width).astype(full)
    gate_pieces = (w_gate, swap(w_gate, 1), gate_across, swap(gate_across, 1))
    x_row, w_qkv, g_query, g_key, g_attn, gate_pieces = barrier(
        (x_row, w_qkv, g_query, g_key, g_attn, gate_pieces)
    )

    picks = routes.shape[2]
    packed = tokens // block_rows
    extra = jnp.concatenate(
        [routes[0].astype(low).reshape(block_rows, packed * picks), w_router, gain_ffn[:, None]],
        axis=1,
    )
    extra = jnp.pad(extra, ((0, 0), (0, 128 - extra.shape[1])))
    out_line = along_z(jnp.concatenate([reorder(w_out, dp_index, 1), extra], axis=1))
    up_across = swap(w_up, 2)

    def share(sums):
        spread = jnp.broadcast_to(sums[None], (shards,) + sums.shape)
        return lax.all_to_all(spread, "seq", 0, 0, tiled=True)

    normed, qkv, r_attn, sums = project(x_row, g_attn, w_qkv)
    q_rot, k_rot, value_in, attended, log_total, r_query, r_key = attend(
        qkv, share(sums), width, g_query, g_key, cosine, sine, seg_col, seg_row
    )
    attended, out_line, up_across = barrier((attended, out_line, up_across))

    attended_row = lax.all_gather(attended, "seq", axis=0)
    out_other, line_across = (over_y(out_line), swap(out_line, 2))
    gate_full = jnp.concatenate(gate_pieces, axis=1)
    up_full = jnp.concatenate([w_up, swap(w_up, 1), up_across, swap(up_across, 1)], axis=1)
    out_other, line_across, gate_full = barrier((out_other, line_across, gate_full))
    other_across = swap(out_other, 2)
    out_own = both_y(out_line, out_other).reshape(chunk, width + 128)
    other_across, up_full, out_own = barrier((other_across, up_full, out_own))
    out_across = both_y(line_across, other_across).reshape(chunk, width + 128)
    out_pieces = (out_own, swap(out_own, 1), out_across, swap(out_across, 1))
    extras = [p[:, width:] for p in out_pieces]
    routes_row = extras[0][:, : packed * picks].reshape(rows, picks).astype(jnp.int32)
    extras = jnp.concatenate([p[:, packed * picks :] for p in extras], axis=0)
    router = jnp.pad(extras[:, :expert_count], ((0, 0), (0, 128 - expert_count)))
    g_ffn = extras[:, expert_count].astype(full)[None]
    lane_ids = lax.iota(jnp.int32, 128)
    chosen = jnp.any(routes_row[:, :, None] == lane_ids[None, None, :], axis=1).astype(full)
    own = (
        lane_ids[None, :] == seq_index * held + lax.iota(jnp.int32, held)[:, None]
    ).astype(full)
    attended_row, out_pieces, up_full, router, g_ffn, chosen = barrier(
        (attended_row, out_pieces, up_full, router, g_ffn, chosen)
    )

    dy_shard, attended_row = barrier((reorder(cotangent[0], dp_index, 1), attended_row))
    dy_row = lax.all_gather(dy_shard, "seq", axis=0, tiled=True)
    order = jnp.stack([dp_index ^ k for k in range(4)] + [seq_index]).astype(jnp.int32)
    hidden_mid, normed_ffn, r_ffn, chances, gates = finish_attention(
        order, attended_row, out_pieces, x_row, g_ffn, router, chosen, own, expert_count
    )
    act, dgate_factor, dup_factor = expert_activations(normed_ffn, gate_full, up_full)
    act, down_across = barrier((act, swap(w_down, 2)))
    down_full = jnp.concatenate([w_down, swap(w_down, 1), down_across, swap(down_across, 1)], axis=2)
    y_at = (seq_index % 2).astype(jnp.int32)[None]
    mixture, mixture_far = combine_experts(y_at, act, down_full, gates)
    dy_row, mixture_far, act = barrier((dy_row, mixture_far, act))
    mixture_far = over_y(mixture_far)

    scaled, dgate, dup, gate_sums = expert_gradients(
        dy_row, down_full, act, dgate_factor, dup_factor, gates
    )
    nf_grad, grad_logits = input_gradient(
        dgate, dup, gate_full, up_full, gate_sums, chances, chosen, own, router
    )
    nf_grad, mixture_far = barrier((nf_grad, mixture_far))
    nf_sum = lax.psum_scatter(nf_grad, "seq", scatter_dimension=0, tiled=True)
    mixture = (mixture.astype(full) + mixture_far.astype(full)).astype(low)

    down_kept, down_passed = sum_in_chip(weight_pieces(scaled, dy_row, 4, False), low)
    gate_pieces = weight_pieces(normed_ffn, dgate, 4, True)
    dup, down_passed = barrier((dup, down_passed))
    down_arrived = across_by_expert(down_passed)
    gate_kept, gate_passed = sum_in_chip(gate_pieces, low)
    up_pieces = weight_pieces(normed_ffn, dup, 4, True)
    up_pieces, down_arrived[0] = barrier((up_pieces, down_arrived[0]))
    up_kept, up_passed = sum_in_chip(up_pieces, low)
    router_grad = mm(grad_logits[:, :expert_count], normed_ffn, ((0,), (0,)))
    nf_sum, mixture, down_arrived[1], gate_passed, up_passed, router_grad, down_kept, gate_kept, up_kept = barrier(
        (nf_sum, mixture, down_arrived[1], gate_passed, up_passed, router_grad, down_kept, gate_kept, up_kept)
    )
    gate_arrived, up_arrived = (across_by_expert(gate_passed), [swap(up_passed[0], 2)])

    grad_mid, mid_low, grad_attended, gain_ffn_grad = middle(
        order, nf_sum, hidden_mid, r_ffn, g_ffn, dy_shard, out_pieces
    )
    def to_columns(values):
        return lax.all_to_all(values, "seq", 0, 0, tiled=True).reshape(rows, cols)

    grad_attended = grad_attended.reshape(4, tokens, shards // 4, cols).transpose(0, 2, 1, 3)
    grad_attended = to_columns(grad_attended.reshape(shards, tokens, cols))
    grad_attended, gate_arrived[0], mixture = barrier((grad_attended, gate_arrived[0], mixture))
    mixture_own = sum_along_z(mixture)
    mid_cols = to_columns(
        reorder(mid_low, dp_index, 1).reshape(tokens, shards, cols).transpose(1, 0, 2)
    )
    q_grad, k_grad, v_low, sums, gain_query_grad, gain_key_grad = attend_back(
        qkv, q_rot, k_rot, value_in, grad_attended, log_total,
        r_query, r_key, g_query, g_key, cosine, sine, seg_col, seg_row,
    )
    sums, gate_arrived[1] = barrier((sums, gate_arrived[1]))
    sums, mid_cols = barrier((share(sums), mid_cols))
    qkv_low, normed_grad, gain_attn_grad = normed_gradient(
        q_grad, k_grad, v_low, qkv, sums, r_query, r_key, w_qkv, x_row, r_attn
    )
    normed_grad, up_arrived[0], mixture_own = barrier((normed_grad, up_arrived[0], mixture_own))
    normed_sum = lax.psum_scatter(normed_grad, "seq", scatter_dimension=0, tiled=True).astype(full)

    def to_owners(kept, passed, count):
        total = kept.astype(full) + swap(passed, 2).astype(full)
        total = lax.all_to_all(
            total.astype(low).reshape(shards, block_rows, count * cols), "seq", 0, 0, tiled=True
        )
        total = total.reshape(shards, block_rows, count, cols).transpose(2, 1, 0, 3)
        return total.reshape(count, block_rows, width).astype(full)

    qkv_parts = [p[0] for p in weight_pieces(normed, qkv_low[None], 4, True)]
    qkv_parts, mid_cols, gain_attn_grad, gain_ffn_grad = barrier(
        (qkv_parts, mid_cols, gain_attn_grad, gain_ffn_grad)
    )
    qkv_kept, qkv_passed = sum_in_chip(qkv_parts, low)
    out_parts = out_grad_pieces(order, attended_row, mid_cols)
    out_kept, out_passed = sum_in_chip(out_parts, low)
    qkv_passed, out_passed, up_last = barrier((qkv_passed, out_passed, up_passed[1]))
    proj_grad = to_owners(qkv_kept, qkv_passed, 3)
    out_grad = to_owners(out_kept, out_passed, 1)
    up_arrived.append(swap(up_last, 2))
    grad_w_down = add_arrived(down_kept, down_arrived)
    grad_w_gate = add_arrived(gate_kept, gate_arrived)
    grad_w_up = add_arrived(up_kept, up_arrived)
    mid_own = lax.dynamic_slice_in_dim(hidden_mid, first_row, tokens)
    block_out = (mid_own + mixture_own.astype(full)).astype(low)
    normed_sum, grad_w_down, grad_w_gate, grad_w_up, out_grad, block_out = barrier(
        (normed_sum, grad_w_down, grad_w_gate, grad_w_up, out_grad, block_out)
    )

    x_own = x_shard.astype(full)
    r_here = lax.rsqrt(jnp.mean(x_own * x_own, axis=-1, keepdims=True) + epsilon)
    scaled_grad = normed_sum * g_attn
    grad_hidden = (
        grad_mid
        + r_here * scaled_grad
        - x_own * (r_here**3) * jnp.mean(scaled_grad * x_own, axis=-1, keepdims=True)
    )

    def place(values):
        whole = lax.dynamic_update_slice_in_dim(
            jnp.zeros((1, width), full), values[None], seq_index * cols, 1
        )
        return reorder(whole, dp_index, 1)

    vectors = jnp.concatenate(
        [
            router_grad,
            gain_attn_grad,
            place(gain_query_grad[0]),
            place(gain_key_grad[0]),
            gain_ffn_grad,
        ]
    )
    count = vectors.shape[0]
    vectors = sum_pieces([vectors[:, k * chunk : (k + 1) * chunk] for k in range(4)], full)
    vectors = vectors.reshape(count, shards, block_rows).transpose(1, 0, 2)
    vectors = jnp.sum(lax.all_to_all(vectors, "seq", 0, 0, tiled=True), axis=0)
    return (
        reorder(block_out, dp_index, 1)[None],
        reorder(grad_hidden, dp_index, 1)[None],
        proj_grad[0],
        proj_grad[1],
        proj_grad[2],
        out_grad[0],
        vectors[expert_count],
        vectors[expert_count + 1],
        vectors[expert_count + 2],
        vectors[expert_count + 3],
        vectors[:expert_count].T,
        grad_w_gate,
        grad_w_up,
        grad_w_down,
    )


def solution(mesh):
    def layer(*arrays):
        whole_heads = (arrays[0].shape[2] // HEAD) % mesh.shape["seq"] == 0
        if whole_heads and mesh.shape["dp"] == 4 and mesh.shape["seq"] == 8:
            return on_device_heads(*arrays)
        return on_device(*arrays)

    return jax.shard_map(
        layer,
        mesh=mesh,
        in_specs=(
            P("dp", "seq", None),
            P("dp", None),
            P("dp", "seq", None),
            P(("dp", "seq"), None),
            P(("dp", "seq"), None),
            P(("dp", "seq"), None),
            P(("dp", "seq"), None),
            P(("dp", "seq")),
            P(("dp", "seq")),
            P(("dp", "seq")),
            P(("dp", "seq")),
            P(("dp", "seq"), None),
            P("seq", "dp", None),
            P("seq", "dp", None),
            P("seq", None, "dp"),
            P("dp", "seq", None),
        ),
        out_specs=(
            P("dp", "seq", None),
            P("dp", "seq", None),
            P(("dp", "seq"), None),
            P(("dp", "seq"), None),
            P(("dp", "seq"), None),
            P(("dp", "seq"), None),
            P(("dp", "seq")),
            P(("dp", "seq")),
            P(("dp", "seq")),
            P(("dp", "seq")),
            P(("dp", "seq"), None),
            P("seq", "dp", None),
            P("seq", "dp", None),
            P("seq", None, "dp"),
        ),
        check_vma=False,
    )
```

```python
import math

import jax
import jax.numpy as jnp
from jax import lax
from jax.experimental import pallas as pl
from jax.experimental.pallas import tpu as pltpu
from jax.sharding import PartitionSpec as P

HEAD = 128


epsilon = 1e-05
masked_score = -1e30
rope_base = 10000.0


def normalize(values, gain_vec):
    return (
        values * lax.rsqrt(jnp.mean(values * values, axis=-1, keepdims=True) + epsilon) * gain_vec
    )


def rotary(values, positions):
    half_dim = values.shape[-1] // 2
    frequency = jnp.exp(
        jnp.arange(half_dim, dtype=jnp.float32) * (-2.0 * math.log(rope_base) / values.shape[-1])
    )
    angles = positions.astype(jnp.float32)[:, None] * frequency[None, :]
    cosine = jnp.cos(angles)[:, None, :]
    sine_table = jnp.sin(angles)[:, None, :]
    first_half = values[..., :half_dim]
    second = values[..., half_dim:]
    return jnp.concatenate(
        [first_half * cosine - second * sine_table, second * cosine + first_half * sine_table],
        axis=-1,
    )


def softmax_rows(values):
    peak_value = jnp.max(values, axis=-1, keepdims=True)
    raised = jnp.exp(values - peak_value)
    return raised / jnp.sum(raised, axis=-1, keepdims=True)


def rotate_normed(projection, gain_vec, positions):
    tokens, model_width = projection.shape
    return rotary(
        normalize(projection, gain_vec).reshape(tokens, model_width // HEAD, HEAD), positions
    )


def masked_scores(queries, key_block, query_pos, query_seg, key_pos, key_seg, scaling):
    raw_scores = jnp.einsum("qhd,khd->hqk", queries, key_block, preferred_element_type=jnp.float32)
    allowed = (query_pos[:, None] >= key_pos[None, :]) & (query_seg[:, None] == key_seg[None, :])
    return jnp.where(allowed[None], raw_scores * scaling, masked_score)


def key_window(keys_all, values_all, row_seg, begin_at, span):
    key_block = lax.dynamic_slice_in_dim(keys_all, begin_at, span)
    value_block = lax.dynamic_slice_in_dim(values_all, begin_at, span)
    key_pos = begin_at + lax.iota(jnp.int32, span)
    key_seg = lax.dynamic_slice_in_dim(row_seg, begin_at, span)
    return (key_block, value_block, key_pos, key_seg)


def project_front(hidden, layer_full, positions):
    tokens, model_width = hidden.shape
    normed = normalize(hidden, layer_full[5].astype(jnp.float32)).astype(jnp.bfloat16)
    query = jnp.dot(normed, layer_full[0], preferred_element_type=jnp.float32)
    key_proj = jnp.dot(normed, layer_full[1], preferred_element_type=jnp.float32)
    value_proj = jnp.dot(normed, layer_full[2], preferred_element_type=jnp.float32)
    query_rot = rotate_normed(query, layer_full[6].astype(jnp.float32), positions).astype(
        jnp.bfloat16
    )
    key_rot = rotate_normed(key_proj, layer_full[7].astype(jnp.float32), positions).astype(
        jnp.bfloat16
    )
    value_in = value_proj.astype(jnp.bfloat16).reshape(tokens, model_width // HEAD, HEAD)
    return (normed, query, key_proj, query_rot, key_rot, value_in)


def attend_local(query_rot, keys_all, values_all, row_seg, offset, span):
    tokens, head_count, head_dim = query_rot.shape
    scaling = head_dim ** (-0.5)
    query_pos = offset + lax.iota(jnp.int32, tokens)
    query_seg = lax.dynamic_slice_in_dim(row_seg, offset, tokens)
    reach_blocks = (offset + tokens + span - 1) // span

    def block_scores(block_index):
        begin_at = block_index * span
        key_block, value_block, key_pos, key_seg = key_window(
            keys_all, values_all, row_seg, begin_at, span
        )
        return (
            masked_scores(query_rot, key_block, query_pos, query_seg, key_pos, key_seg, scaling),
            value_block,
        )

    def first_pass(block_index, state_pair):
        peak_value, denominator = state_pair
        scores, unused_values = block_scores(block_index)
        new_peak = jnp.maximum(peak_value, jnp.max(scores, axis=-1))
        denominator = denominator * jnp.exp(peak_value - new_peak) + jnp.sum(
            jnp.exp(scores - new_peak[..., None]), axis=-1
        )
        return (new_peak, denominator)

    start_state = (
        jnp.full((head_count, tokens), masked_score, jnp.float32),
        jnp.zeros((head_count, tokens), jnp.float32),
    )
    peak_value, denominator = lax.fori_loop(0, reach_blocks, first_pass, start_state)
    log_total = peak_value + jnp.log(denominator)

    def second_pass(block_index, running):
        scores, value_block = block_scores(block_index)
        weights = jnp.exp(scores - log_total[..., None]).astype(jnp.bfloat16)
        return running + jnp.einsum(
            "hqk,khd->qhd", weights, value_block, preferred_element_type=jnp.float32
        )

    attention = lax.fori_loop(
        0, reach_blocks, second_pass, jnp.zeros((tokens, head_count, head_dim), jnp.float32)
    )
    return (attention, log_total)


def query_grads(query_rot, keys_all, values_all, row_seg, offset, span, log_total, grad_attended):
    tokens, head_count, head_dim = query_rot.shape
    scaling = head_dim ** (-0.5)
    query_pos = offset + lax.iota(jnp.int32, tokens)
    query_seg = lax.dynamic_slice_in_dim(row_seg, offset, tokens)
    reach_blocks = (offset + tokens + span - 1) // span

    def block_terms(block_index):
        begin_at = block_index * span
        key_block, value_block, key_pos, key_seg = key_window(
            keys_all, values_all, row_seg, begin_at, span
        )
        scores = masked_scores(
            query_rot, key_block, query_pos, query_seg, key_pos, key_seg, scaling
        )
        weights = jnp.exp(scores - log_total[..., None])
        grad_weights = jnp.einsum(
            "qhd,khd->hqk", grad_attended, value_block, preferred_element_type=jnp.float32
        )
        return (key_block, weights, grad_weights)

    def delta_pass(block_index, running):
        unused_keys, weights, grad_weights = block_terms(block_index)
        return running + jnp.sum(weights * grad_weights, axis=-1)

    delta = lax.fori_loop(0, reach_blocks, delta_pass, jnp.zeros((head_count, tokens), jnp.float32))

    def query_pass(block_index, running):
        key_block, weights, grad_weights = block_terms(block_index)
        grad_scores = (weights * (grad_weights - delta[..., None]) * scaling).astype(jnp.bfloat16)
        return running + jnp.einsum(
            "hqk,khd->qhd", grad_scores, key_block, preferred_element_type=jnp.float32
        )

    grad_query_rot = lax.fori_loop(
        0, reach_blocks, query_pass, jnp.zeros((tokens, head_count, head_dim), jnp.float32)
    )
    return (delta, grad_query_rot)


def route_tokens(hidden_mid, layer_full, choice_rows):
    tokens, pick_count = choice_rows.shape
    normed_ffn = normalize(hidden_mid, layer_full[8].astype(jnp.float32)).astype(jnp.bfloat16)
    logits = jnp.dot(normed_ffn, layer_full[4], preferred_element_type=jnp.float32)
    expert_count = logits.shape[1]
    capacity = 3 * tokens * pick_count // (2 * expert_count)
    chances = softmax_rows(logits)
    picks = choice_rows[:, :, None] == lax.iota(jnp.int32, expert_count)[None, None, :]
    gate_values = jnp.sum(jnp.where(picks, chances[:, None, :], 0.0), axis=-1)
    flat_hits = picks.reshape(tokens * pick_count, expert_count).astype(jnp.int32)
    earlier = jnp.cumsum(flat_hits, axis=0) - flat_hits
    slot_ids = choice_rows.reshape(-1) * capacity + jnp.sum(earlier * flat_hits, axis=1)
    pair_table = lax.iota(jnp.int32, expert_count * capacity)[:, None] == slot_ids[None, :]
    spread = jnp.sum(
        pair_table.reshape(expert_count * capacity, tokens, pick_count).astype(jnp.int32), axis=2
    ).astype(jnp.bfloat16)
    send_rows = jnp.dot(spread, normed_ffn, preferred_element_type=jnp.float32).astype(jnp.bfloat16)
    send_rows = send_rows.reshape(expert_count, capacity, hidden_mid.shape[1])
    return (normed_ffn, chances, picks, gate_values, slot_ids, pair_table, spread, send_rows)


def group_rows(row_block, held_experts):
    sources = row_block.shape[0] // held_experts
    grouped = row_block.reshape(
        sources, held_experts, row_block.shape[1], row_block.shape[2]
    ).transpose(1, 0, 2, 3)
    return grouped.reshape(held_experts, sources * row_block.shape[1], row_block.shape[2])


def ungroup_rows(grouped, whole_shape):
    held_experts = grouped.shape[0]
    sources = whole_shape[0] // held_experts
    spread_out = grouped.reshape(held_experts, sources, whole_shape[1], whole_shape[2]).transpose(
        1, 0, 2, 3
    )
    return spread_out.reshape(whole_shape)


def expert_forward(row_block, gate_full, up_full, down_full):
    inputs = group_rows(row_block, gate_full.shape[0])
    gate_pre = jnp.einsum("erd,edf->erf", inputs, gate_full, preferred_element_type=jnp.float32)
    up_pre = jnp.einsum("erd,edf->erf", inputs, up_full, preferred_element_type=jnp.float32)
    activated = (gate_pre * lax.logistic(gate_pre) * up_pre).astype(jnp.bfloat16)
    result = jnp.einsum(
        "erf,efd->erd", activated, down_full, preferred_element_type=jnp.float32
    ).astype(jnp.bfloat16)
    return ungroup_rows(result, row_block.shape)


def expert_backward(row_block, grad_block, gate_full, up_full, down_full):
    inputs = group_rows(row_block, gate_full.shape[0])
    grad_outputs = group_rows(grad_block, gate_full.shape[0])
    gate_pre = jnp.einsum("erd,edf->erf", inputs, gate_full, preferred_element_type=jnp.float32)
    up_pre = jnp.einsum("erd,edf->erf", inputs, up_full, preferred_element_type=jnp.float32)
    sigmoid_gate = lax.logistic(gate_pre)
    activated = (gate_pre * sigmoid_gate * up_pre).astype(jnp.bfloat16)
    grad_act = jnp.einsum(
        "erd,efd->erf", grad_outputs, down_full, preferred_element_type=jnp.float32
    )
    grad_down = jnp.einsum(
        "erf,erd->efd", activated, grad_outputs, preferred_element_type=jnp.float32
    )
    grad_gate_pre = (
        grad_act * up_pre * sigmoid_gate * (1.0 + gate_pre * (1.0 - sigmoid_gate))
    ).astype(jnp.bfloat16)
    grad_up_pre = (grad_act * gate_pre * sigmoid_gate).astype(jnp.bfloat16)
    grad_gate_w = jnp.einsum(
        "erd,erf->edf", inputs, grad_gate_pre, preferred_element_type=jnp.float32
    )
    grad_up_w = jnp.einsum("erd,erf->edf", inputs, grad_up_pre, preferred_element_type=jnp.float32)
    grad_inputs = jnp.einsum(
        "erf,edf->erd", grad_gate_pre, gate_full, preferred_element_type=jnp.float32
    )
    grad_inputs = grad_inputs + jnp.einsum(
        "erf,edf->erd", grad_up_pre, up_full, preferred_element_type=jnp.float32
    )
    return (
        ungroup_rows(grad_inputs.astype(jnp.bfloat16), row_block.shape),
        grad_gate_w,
        grad_up_w,
        grad_down,
    )


def contract_rows(left, right):
    return lax.dot_general(
        left, right, (((0,), (0,)), ((), ())), preferred_element_type=jnp.float32
    )


def contract_cols(left, right):
    return lax.dot_general(
        left, right, (((1,), (1,)), ((), ())), preferred_element_type=jnp.float32
    )


def on_device(
    hidden_in,
    segment_ids,
    routes,
    w_query,
    w_key,
    w_value,
    w_out,
    gain_attn,
    gain_query,
    gain_key,
    gain_ffn,
    w_router,
    w_gate,
    w_up,
    w_down,
    cotangent,
):
    hidden = hidden_in[0].astype(jnp.float32)
    tokens, model_width = hidden.shape
    head_count = model_width // HEAD
    row_seg = segment_ids[0]
    choice_rows = routes[0]
    offset = lax.axis_index("seq") * tokens
    positions = offset + lax.iota(jnp.int32, tokens)
    span = min(512, row_seg.shape[0])
    layer_full = (
        lax.all_gather(w_query, ("dp", "seq"), axis=0, tiled=True),
        lax.all_gather(w_key, ("dp", "seq"), axis=0, tiled=True),
        lax.all_gather(w_value, ("dp", "seq"), axis=0, tiled=True),
        lax.all_gather(w_out, ("dp", "seq"), axis=0, tiled=True),
        lax.all_gather(w_router, ("dp", "seq"), axis=0, tiled=True),
        lax.all_gather(gain_attn, ("dp", "seq"), axis=0, tiled=True),
        lax.all_gather(gain_query, ("dp", "seq"), axis=0, tiled=True),
        lax.all_gather(gain_key, ("dp", "seq"), axis=0, tiled=True),
        lax.all_gather(gain_ffn, ("dp", "seq"), axis=0, tiled=True),
    )
    expert_full = (
        lax.all_gather(w_gate, "dp", axis=1, tiled=True),
        lax.all_gather(w_up, "dp", axis=1, tiled=True),
        lax.all_gather(w_down, "dp", axis=2, tiled=True),
    )
    projected = project_front(hidden, layer_full, positions)
    keys_all, values_all = (
        lax.all_gather(projected[4], "seq", axis=0, tiled=True),
        lax.all_gather(projected[5], "seq", axis=0, tiled=True),
    )
    attention, log_total = attend_local(projected[3], keys_all, values_all, row_seg, offset, span)
    attended = attention.reshape(tokens, model_width).astype(jnp.bfloat16)
    hidden_mid = hidden + jnp.dot(attended, layer_full[3], preferred_element_type=jnp.float32)
    routing = route_tokens(hidden_mid, layer_full, choice_rows)
    expert_count, capacity = (routing[7].shape[0], routing[7].shape[1])
    expert_out = expert_forward(
        lax.all_to_all(routing[7], "seq", split_axis=0, concat_axis=0, tiled=True),
        expert_full[0],
        expert_full[1],
        expert_full[2],
    )
    returned = lax.all_to_all(expert_out, "seq", split_axis=0, concat_axis=0, tiled=True)
    picked = jnp.take(returned.reshape(expert_count * capacity, model_width), routing[4], axis=0)
    picked = picked.reshape(tokens, choice_rows.shape[1], model_width)
    mixture = jnp.sum(routing[3][:, :, None] * picked.astype(jnp.float32), axis=1)
    block_out = (hidden_mid + mixture).astype(jnp.bfloat16)
    layer_full = (
        lax.all_gather(w_query, ("dp", "seq"), axis=0, tiled=True),
        lax.all_gather(w_key, ("dp", "seq"), axis=0, tiled=True),
        lax.all_gather(w_value, ("dp", "seq"), axis=0, tiled=True),
        lax.all_gather(w_out, ("dp", "seq"), axis=0, tiled=True),
        lax.all_gather(w_router, ("dp", "seq"), axis=0, tiled=True),
        lax.all_gather(gain_attn, ("dp", "seq"), axis=0, tiled=True),
        lax.all_gather(gain_query, ("dp", "seq"), axis=0, tiled=True),
        lax.all_gather(gain_key, ("dp", "seq"), axis=0, tiled=True),
        lax.all_gather(gain_ffn, ("dp", "seq"), axis=0, tiled=True),
    )
    expert_full = (
        lax.all_gather(w_gate, "dp", axis=1, tiled=True),
        lax.all_gather(w_up, "dp", axis=1, tiled=True),
        lax.all_gather(w_down, "dp", axis=2, tiled=True),
    )
    projected = project_front(hidden, layer_full, positions)
    keys_all, values_all = (
        lax.all_gather(projected[4], "seq", axis=0, tiled=True),
        lax.all_gather(projected[5], "seq", axis=0, tiled=True),
    )
    attention, log_total = attend_local(projected[3], keys_all, values_all, row_seg, offset, span)
    attended = attention.reshape(tokens, model_width).astype(jnp.bfloat16)
    hidden_mid = hidden + jnp.dot(attended, layer_full[3], preferred_element_type=jnp.float32)
    routing = route_tokens(hidden_mid, layer_full, choice_rows)
    normed_ffn, chances, picks, gate_values, slot_ids, pair_table, spread, send_rows = routing
    grad_out = cotangent[0].astype(jnp.float32)
    grad_gates = jnp.sum(grad_out[:, None, :] * picked.astype(jnp.float32), axis=-1)
    slot_gates = jnp.sum(jnp.where(pair_table, gate_values.reshape(-1)[None, :], 0.0), axis=1)
    grad_rows_in = jnp.dot(spread, cotangent[0], preferred_element_type=jnp.float32)
    grad_slots = (
        (slot_gates[:, None] * grad_rows_in)
        .astype(jnp.bfloat16)
        .reshape(expert_count, capacity, model_width)
    )
    arrived_rows, arrived_grads = (
        lax.all_to_all(send_rows, "seq", split_axis=0, concat_axis=0, tiled=True),
        lax.all_to_all(grad_slots, "seq", split_axis=0, concat_axis=0, tiled=True),
    )
    grad_inputs, grad_gate_w, grad_up_w, grad_down_w = expert_backward(
        arrived_rows, arrived_grads, expert_full[0], expert_full[1], expert_full[2]
    )
    grad_back = lax.all_to_all(grad_inputs, "seq", split_axis=0, concat_axis=0, tiled=True)
    grad_normed_ffn = contract_rows(spread, grad_back.reshape(expert_count * capacity, model_width))
    grad_chances = jnp.sum(jnp.where(picks, grad_gates[:, :, None], 0.0), axis=1)
    grad_logits = (
        chances * (grad_chances - jnp.sum(chances * grad_chances, axis=-1, keepdims=True))
    ).astype(jnp.bfloat16)
    grad_router_w = contract_rows(normed_ffn, grad_logits)
    grad_normed_ffn = grad_normed_ffn + contract_cols(grad_logits, layer_full[4])
    unused_ffn, pull_ffn = jax.vjp(normalize, hidden_mid, layer_full[8].astype(jnp.float32))
    grad_mid_norm, grad_gain_ffn_w = pull_ffn(grad_normed_ffn)
    grad_mid = grad_out + grad_mid_norm
    grad_mid_low = grad_mid.astype(jnp.bfloat16)
    grad_w_out = contract_rows(attended, grad_mid_low)
    grad_attended = (
        contract_cols(grad_mid_low, layer_full[3])
        .astype(jnp.bfloat16)
        .reshape(tokens, head_count, HEAD)
    )
    query_rot = projected[3]
    delta, grad_query_rot = query_grads(
        query_rot, keys_all, values_all, row_seg, offset, span, log_total, grad_attended
    )
    scaling = HEAD ** (-0.5)
    query_seg = lax.dynamic_slice_in_dim(row_seg, offset, tokens)
    row_count = lax.axis_size("seq") * tokens
    step_rows = math.gcd(row_count, 512)

    def one_window(window_index, running):
        window_start = window_index * step_rows
        key_block, value_block, key_pos, key_seg = key_window(
            keys_all, values_all, row_seg, window_start, step_rows
        )
        scores = masked_scores(
            query_rot, key_block, positions, query_seg, key_pos, key_seg, scaling
        )
        weights = jnp.exp(scores - log_total[..., None])
        grad_weights = jnp.einsum(
            "qhd,khd->hqk", grad_attended, value_block, preferred_element_type=jnp.float32
        )
        grad_scores = (weights * (grad_weights - delta[..., None]) * scaling).astype(jnp.bfloat16)
        grad_key_part = jnp.einsum(
            "hqk,qhd->khd", grad_scores, query_rot, preferred_element_type=jnp.float32
        )
        grad_value_part = jnp.einsum(
            "hqk,qhd->khd",
            weights.astype(jnp.bfloat16),
            grad_attended,
            preferred_element_type=jnp.float32,
        )
        term = jnp.concatenate(
            [
                grad_key_part.reshape(step_rows, model_width),
                grad_value_part.reshape(step_rows, model_width),
            ],
            axis=1,
        )
        return lax.dynamic_update_slice_in_dim(running, term, window_index * step_rows, 0)

    key_sums = lax.psum_scatter(
        lax.fori_loop(
            0,
            row_count // step_rows,
            one_window,
            jnp.zeros((row_count, 2 * model_width), jnp.float32),
        ).astype(jnp.bfloat16),
        "seq",
        scatter_dimension=0,
        tiled=True,
    ).astype(jnp.float32)
    grad_key_rot = key_sums[:, :model_width].reshape(tokens, head_count, HEAD)
    grad_v_low = key_sums[:, model_width:].astype(jnp.bfloat16)

    def query_chain(projection, gain_vec):
        return rotate_normed(projection, gain_vec, positions)

    unused_query, pull_query = jax.vjp(query_chain, projected[1], layer_full[6].astype(jnp.float32))
    grad_query_pre, grad_gain_query_w = pull_query(grad_query_rot)
    unused_key, pull_key = jax.vjp(query_chain, projected[2], layer_full[7].astype(jnp.float32))
    grad_key_pre, grad_gain_key_w = pull_key(grad_key_rot)
    grad_q_low = grad_query_pre.astype(jnp.bfloat16)
    grad_k_low = grad_key_pre.astype(jnp.bfloat16)
    normed = projected[0]
    grad_w_query = contract_rows(normed, grad_q_low)
    grad_w_key = contract_rows(normed, grad_k_low)
    grad_w_value = contract_rows(normed, grad_v_low)
    grad_normed = (
        contract_cols(grad_q_low, layer_full[0])
        + contract_cols(grad_k_low, layer_full[1])
        + contract_cols(grad_v_low, layer_full[2])
    )
    unused_attn, pull_attn = jax.vjp(normalize, hidden, layer_full[5].astype(jnp.float32))
    grad_hidden_norm, grad_gain_attn_w = pull_attn(grad_normed)
    grad_hidden = grad_mid + grad_hidden_norm
    shares = (
        lax.psum_scatter(grad_w_query, ("dp", "seq"), scatter_dimension=0, tiled=True),
        lax.psum_scatter(grad_w_key, ("dp", "seq"), scatter_dimension=0, tiled=True),
        lax.psum_scatter(grad_w_value, ("dp", "seq"), scatter_dimension=0, tiled=True),
        lax.psum_scatter(grad_w_out, ("dp", "seq"), scatter_dimension=0, tiled=True),
        lax.psum_scatter(grad_router_w, ("dp", "seq"), scatter_dimension=0, tiled=True),
        lax.psum_scatter(grad_gain_attn_w, ("dp", "seq"), scatter_dimension=0, tiled=True),
        lax.psum_scatter(grad_gain_query_w, ("dp", "seq"), scatter_dimension=0, tiled=True),
        lax.psum_scatter(grad_gain_key_w, ("dp", "seq"), scatter_dimension=0, tiled=True),
        lax.psum_scatter(grad_gain_ffn_w, ("dp", "seq"), scatter_dimension=0, tiled=True),
    )
    expert_shares = (
        lax.psum_scatter(
            grad_gate_w.astype(jnp.bfloat16), "dp", scatter_dimension=1, tiled=True
        ).astype(jnp.float32),
        lax.psum_scatter(
            grad_up_w.astype(jnp.bfloat16), "dp", scatter_dimension=1, tiled=True
        ).astype(jnp.float32),
        lax.psum_scatter(
            grad_down_w.astype(jnp.bfloat16), "dp", scatter_dimension=2, tiled=True
        ).astype(jnp.float32),
    )
    return (
        block_out[None],
        grad_hidden[None],
        shares[0],
        shares[1],
        shares[2],
        shares[3],
        shares[5],
        shares[6],
        shares[7],
        shares[8],
        shares[4],
        expert_shares[0],
        expert_shares[1],
        expert_shares[2],
    )


VMEM_GRANT = 56 * 1024 * 1024


def mm(left, right, dims):
    return lax.dot_general(left, right, (dims, ((), ())), preferred_element_type=jnp.float32)


def cost(flops, transcendentals, *arrays):
    moved = sum(math.prod(a.shape) * a.dtype.itemsize for a in arrays)
    return pl.CostEstimate(
        flops=flops // 4, transcendentals=transcendentals // 4, bytes_accessed=moved // 4
    )


def grid_call(body, grid, in_specs, out_specs, outs, flops, transcendentals, *args):
    return pl.pallas_call(
        body,
        grid=grid,
        in_specs=in_specs,
        out_specs=out_specs,
        out_shape=outs,
        compiler_params=pltpu.CompilerParams(vmem_limit_bytes=VMEM_GRANT),
        cost_estimate=cost(flops, transcendentals, *args, *jax.tree.leaves(outs)),
    )(*args)


def row_tiles(rows):
    return math.gcd(rows, 512)


def finish_attention(order, attended, out_pieces, x_row, gain, router, chosen, own, expert_count):
    shards, rows, cols = attended.shape
    width = x_row.shape[1]
    held = own.shape[0]
    chunk = width // 4
    per_chunk = chunk // cols
    tm = math.gcd(rows, 256)

    def body(order_ref, att_ref, p0, p1, p2, p3, x_ref, gain_ref, router_ref, chosen_ref, own_ref, *outs):
        mid_ref, normed_ref, r_ref, chance_ref, gate_ref, att_all = outs
        for h in range(shards):
            source = order_ref[h // per_chunk] * per_chunk + h % per_chunk
            att_all[:, h * cols : (h + 1) * cols] = att_ref[source]
        squares = jnp.zeros((tm, 1), jnp.float32)
        for n in range(4):
            at = slice(n * chunk, (n + 1) * chunk)
            total = x_ref[:, at].astype(jnp.float32)
            for j, piece in enumerate((p0, p1, p2, p3)):
                k = n ^ j
                total = total + mm(
                    att_all[:, j * chunk : (j + 1) * chunk],
                    piece[:, k * chunk : (k + 1) * chunk],
                    ((1,), (0,)),
                )
            mid_ref[:, at] = total
            squares = squares + jnp.sum(total * total, axis=-1, keepdims=True)
        r = lax.rsqrt(squares / width + epsilon)
        r_ref[...] = r
        logits = jnp.zeros((tm, 128), jnp.float32)
        for n in range(4):
            at = slice(n * chunk, (n + 1) * chunk)
            normed = (mid_ref[:, at] * r * gain_ref[:, at]).astype(jnp.bfloat16)
            normed_ref[:, at] = normed
            logits = logits + mm(normed, router_ref[at, :], ((1,), (0,)))
        lane = lax.broadcasted_iota(jnp.int32, (tm, 128), 1)
        logits = jnp.where(lane < expert_count, logits, masked_score)
        raised = jnp.exp(logits - jnp.max(logits, axis=-1, keepdims=True))
        chances = raised / jnp.sum(raised, axis=-1, keepdims=True)
        chance_ref[...] = chances
        taken = chances * chosen_ref[...]
        for e in range(held):
            gate_ref[e] = jnp.sum(taken * own_ref[e : e + 1, :], axis=-1, keepdims=True)

    full = jnp.float32
    piece_spec = pl.BlockSpec((chunk, width), lambda i, o: (0, 0))
    wide = pl.BlockSpec((tm, width), lambda i, o: (i, 0))
    lanes = pl.BlockSpec((tm, 128), lambda i, o: (i, 0))
    outs = [
        jax.ShapeDtypeStruct((rows, width), full),
        jax.ShapeDtypeStruct((rows, width), jnp.bfloat16),
        jax.ShapeDtypeStruct((rows, 1), full),
        jax.ShapeDtypeStruct((rows, 128), full),
        jax.ShapeDtypeStruct((held, rows, 1), full),
    ]
    return pl.pallas_call(
        body,
        grid_spec=pltpu.PrefetchScalarGridSpec(
            num_scalar_prefetch=1,
            grid=(rows // tm,),
            in_specs=[
                pl.BlockSpec((shards, tm, cols), lambda i, o: (0, i, 0)),
                piece_spec,
                piece_spec,
                piece_spec,
                piece_spec,
                wide,
                pl.BlockSpec((1, width), lambda i, o: (0, 0)),
                pl.BlockSpec((width, 128), lambda i, o: (0, 0)),
                lanes,
                pl.BlockSpec((held, 128), lambda i, o: (0, 0)),
            ],
            out_specs=[
                wide,
                wide,
                pl.BlockSpec((tm, 1), lambda i, o: (i, 0)),
                lanes,
                pl.BlockSpec((held, tm, 1), lambda i, o: (0, i, 0)),
            ],
            scratch_shapes=[pltpu.VMEM((tm, width), jnp.bfloat16)],
        ),
        out_shape=outs,
        compiler_params=pltpu.CompilerParams(vmem_limit_bytes=VMEM_GRANT),
        cost_estimate=cost(2 * rows * width * width, rows * 128, attended, *out_pieces, *outs),
    )(order, attended, *out_pieces, x_row, gain, router, chosen, own)


def expert_activations(normed, gate, up):
    held, width, ff = gate.shape
    rows = normed.shape[0]
    tile, tm = (math.gcd(ff, 512), row_tiles(rows))

    def body(x_ref, gate_ref, up_ref, act_ref, dgate_ref, dup_ref):
        @pl.loop(0, rows // tm)
        def _(i):
            at = pl.ds(pl.multiple_of(i * tm, tm), tm)
            gate_pre = mm(x_ref[at, :], gate_ref[0], ((1,), (0,)))
            up_pre = mm(x_ref[at, :], up_ref[0], ((1,), (0,)))
            sig = lax.logistic(gate_pre)
            silu = gate_pre * sig
            act_ref[0, at, :] = (silu * up_pre).astype(jnp.bfloat16)
            dgate_ref[0, at, :] = (up_pre * (sig + silu * (1.0 - sig))).astype(jnp.bfloat16)
            dup_ref[0, at, :] = silu.astype(jnp.bfloat16)

    tiled = pl.BlockSpec((1, rows, tile), lambda e, f: (e, 0, f))
    low = jax.ShapeDtypeStruct((held, rows, ff), jnp.bfloat16)
    return grid_call(
        body,
        (held, ff // tile),
        [
            pl.BlockSpec((rows, width), lambda e, f: (0, 0)),
            pl.BlockSpec((1, width, tile), lambda e, f: (e, 0, f)),
            pl.BlockSpec((1, width, tile), lambda e, f: (e, 0, f)),
        ],
        [tiled, tiled, tiled],
        [low, low, low],
        4 * held * rows * ff * width,
        held * rows * ff,
        normed,
        gate,
        up,
    )


def expert_gradients(dy, down, act, dgate_factor, dup_factor, weight):
    held, ff, width = down.shape
    rows = dy.shape[0]
    tile, tm = (math.gcd(ff, 512), row_tiles(rows))

    def body(dy_ref, down_ref, act_ref, a_ref, b_ref, weight_ref, out_ref, dgate_ref, dup_ref, sum_ref):
        first = pl.program_id(1) == 0

        @pl.loop(0, rows // tm, unroll=True)
        def _(i):
            at = pl.ds(pl.multiple_of(i * tm, tm), tm)
            grad = mm(dy_ref[at, :], down_ref[0], ((1,), (1,)))
            scale = weight_ref[0, at, :]
            act = act_ref[0, at, :].astype(jnp.float32)
            product = act * grad
            partial = product[:, :128]
            for j in range(1, tile // 128):
                partial = partial + product[:, j * 128 : (j + 1) * 128]

            @pl.when(first)
            def _():
                sum_ref[0, at, :] = partial

            @pl.when(jnp.logical_not(first))
            def _():
                sum_ref[0, at, :] = sum_ref[0, at, :] + partial

            out_ref[0, at, :] = (scale * act).astype(jnp.bfloat16)
            grad = scale * grad
            dgate_ref[0, at, :] = (grad * a_ref[0, at, :].astype(jnp.float32)).astype(jnp.bfloat16)
            dup_ref[0, at, :] = (grad * b_ref[0, at, :].astype(jnp.float32)).astype(jnp.bfloat16)

    tiled = pl.BlockSpec((1, rows, tile), lambda e, f: (e, 0, f))
    low = jax.ShapeDtypeStruct((held, rows, ff), jnp.bfloat16)
    return grid_call(
        body,
        (held, ff // tile),
        [
            pl.BlockSpec((rows, width), lambda e, f: (0, 0)),
            pl.BlockSpec((1, tile, width), lambda e, f: (e, f, 0)),
            tiled,
            tiled,
            tiled,
            pl.BlockSpec((1, rows, 1), lambda e, f: (e, 0, 0)),
        ],
        [tiled, tiled, tiled, pl.BlockSpec((1, rows, 128), lambda e, f: (e, 0, 0))],
        [low, low, low, jax.ShapeDtypeStruct((held, rows, 128), jnp.float32)],
        2 * held * rows * ff * width,
        0,
        dy,
        down,
        act,
        dgate_factor,
        dup_factor,
        weight,
    )


def input_gradient(dgate, dup, gate, up, gate_sums, chances, chosen, own, router):
    held, width, ff = gate.shape
    rows = dgate.shape[1]
    tile, tm = (math.gcd(width, 512), row_tiles(rows))

    def body(dgate_ref, dup_ref, gate_ref, up_ref, sum_ref, chance_ref, chosen_ref, own_ref, router_ref, out_ref, logits_ref):
        @pl.loop(0, rows // tm, unroll=True)
        def _(i):
            at = pl.ds(pl.multiple_of(i * tm, tm), tm)
            chances = chance_ref[at, :]
            placed = jnp.zeros((tm, 128), jnp.float32)
            for e in range(held):
                got = jnp.sum(sum_ref[e, at, :], axis=-1, keepdims=True)
                placed = placed + own_ref[e : e + 1, :] * got
            placed = placed * chosen_ref[at, :]
            inner = jnp.sum(chances * placed, axis=-1, keepdims=True)
            logits = (chances * (placed - inner)).astype(jnp.bfloat16)
            logits_ref[at, :] = logits
            total = mm(logits, router_ref[...], ((1,), (1,)))
            for e in range(held):
                total = total + mm(dgate_ref[e, at, :], gate_ref[e], ((1,), (1,)))
                total = total + mm(dup_ref[e, at, :], up_ref[e], ((1,), (1,)))
            out_ref[at, :] = total.astype(jnp.bfloat16)

    whole = pl.BlockSpec((held, rows, ff), lambda n: (0, 0, 0))
    weights = pl.BlockSpec((held, tile, ff), lambda n: (0, n, 0))
    lanes = pl.BlockSpec((rows, 128), lambda n: (0, 0))
    return grid_call(
        body,
        (width // tile,),
        [
            whole,
            whole,
            weights,
            weights,
            pl.BlockSpec((held, rows, 128), lambda n: (0, 0, 0)),
            lanes,
            lanes,
            pl.BlockSpec((held, 128), lambda n: (0, 0)),
            pl.BlockSpec((tile, 128), lambda n: (n, 0)),
        ],
        [pl.BlockSpec((rows, tile), lambda n: (0, n)), lanes],
        [jax.ShapeDtypeStruct((rows, width), jnp.bfloat16), jax.ShapeDtypeStruct((rows, 128), jnp.bfloat16)],
        4 * held * rows * ff * width,
        0,
        dgate,
        dup,
        gate,
        up,
        gate_sums,
        chances,
        chosen,
        own,
        router,
    )


def combine_experts(y_at, act, down, weight):
    held, ff, width = down.shape
    rows = act.shape[1]
    block = rows // 8
    tile, tm = (math.gcd(width, 512), 4 * block)

    def body(y_ref, act_ref, down_ref, weight_ref, near_ref, far_ref):
        for i in range(2):
            at = slice(i * tm, (i + 1) * tm)
            total = weight_ref[0, at, :] * mm(act_ref[0, at, :], down_ref[0], ((1,), (0,)))
            for e in range(1, held):
                term = mm(act_ref[e, at, :], down_ref[e], ((1,), (0,)))
                total = total + weight_ref[e, at, :] * term
            total = total.astype(jnp.bfloat16)
            for y, outs in ((0, (near_ref, far_ref)), (1, (far_ref, near_ref))):

                @pl.when(y_ref[0] == y)
                def _(outs=outs):
                    for j in range(4):
                        to = (2 * i + j // 2) * block
                        outs[j % 2][to : to + block, :] = total[j * block : (j + 1) * block]

    half = jax.ShapeDtypeStruct((rows // 2, width), jnp.bfloat16)
    tiled = pl.BlockSpec((rows // 2, tile), lambda n, y: (0, n))
    return pl.pallas_call(
        body,
        grid_spec=pltpu.PrefetchScalarGridSpec(
            num_scalar_prefetch=1,
            grid=(width // tile,),
            in_specs=[
                pl.BlockSpec((held, rows, ff), lambda n, y: (0, 0, 0)),
                pl.BlockSpec((held, ff, tile), lambda n, y: (0, 0, n)),
                pl.BlockSpec((held, rows, 1), lambda n, y: (0, 0, 0)),
            ],
            out_specs=[tiled, tiled],
        ),
        out_shape=[half, half],
        compiler_params=pltpu.CompilerParams(vmem_limit_bytes=VMEM_GRANT),
        cost_estimate=cost(2 * held * rows * ff * width, 0, act, down, half, half),
    )(y_at, act, down, weight)


def weight_pieces(left, right, parts, split_left):
    flat, stacked = (left, right) if split_left else (right, left)
    held, rows, ff = stacked.shape
    piece = flat.shape[1] // parts
    shape = (held, piece, ff) if split_left else (held, ff, piece)
    tm = math.gcd(shape[1], 512)

    def body(flat_ref, stacked_ref, *outs):
        step = pl.program_id(0)
        for j in range(parts):

            @pl.when(step == j)
            def _(j=j):
                @pl.loop(0, shape[1] // tm)
                def _(i):
                    at = pl.ds(pl.multiple_of(i * tm, tm), tm)
                    if split_left:
                        value = mm(flat_ref[:, at], stacked_ref[0], ((0,), (0,)))
                    else:
                        value = mm(stacked_ref[0, :, at], flat_ref[...], ((0,), (0,)))
                    outs[j][0, at, :] = value.astype(jnp.bfloat16)

    def place(j):
        return lambda k, e: (jnp.where(k < j, 0, jnp.where(k > j, held - 1, e)), 0, 0)

    return grid_call(
        body,
        (parts, held),
        [
            pl.BlockSpec((rows, piece), lambda k, e: (0, k)),
            pl.BlockSpec((1, rows, ff), lambda k, e: (e, 0, 0)),
        ],
        [pl.BlockSpec((1,) + shape[1:], place(j)) for j in range(parts)],
        [jax.ShapeDtypeStruct(shape, jnp.bfloat16)] * parts,
        2 * held * rows * ff * flat.shape[1],
        0,
        flat,
        stacked,
    )


def rope_tables(row_count, head_dim):
    half_dim = head_dim // 2
    frequency = jnp.exp(
        jnp.arange(half_dim, dtype=jnp.float32) * (-2.0 * math.log(rope_base) / head_dim)
    )
    angles = jnp.arange(row_count, dtype=jnp.float32)[:, None] * frequency[None, :]
    cosine, sine = (jnp.cos(angles), jnp.sin(angles))
    return (
        jnp.concatenate([cosine, cosine], axis=1),
        jnp.concatenate([-sine, sine], axis=1),
    )


def seen(first, count, keys, seg_col, seg_row):
    position = first + lax.broadcasted_iota(jnp.int32, (count, keys), 0)
    other = lax.broadcasted_iota(jnp.int32, (count, keys), 1)
    return (position >= other) & (seg_col == seg_row)


def pair_rows(first, second):
    lane = lax.broadcasted_iota(jnp.int32, (first.shape[0], 128), 1)
    both = jnp.where(lane == 0, first, jnp.where(lane == 1, second, 0.0))
    return both.T[:8]


def pair_columns(sums):
    rows = [sum((s[i : i + 1] for s in sums[1:]), sums[0][i : i + 1]) for i in range(2)]
    wide = (128, rows[0].shape[1])
    first = lax.broadcasted_iota(jnp.int32, wide, 0) == 0
    both = jnp.where(first, jnp.broadcast_to(rows[0], wide), jnp.broadcast_to(rows[1], wide)).T
    return (both[:, 0:1], both[:, 1:2])


def project(x_row, gain, w_qkv):
    rows, width = x_row.shape
    held_cols = w_qkv.shape[1]
    cols = held_cols // 3
    tm = math.gcd(rows, 256)

    def body(x_ref, gain_ref, w_ref, normed_ref, qkv_ref, r_ref, stat_ref):
        x = x_ref[...].astype(jnp.float32)
        r = lax.rsqrt(jnp.mean(x * x, axis=-1, keepdims=True) + epsilon)
        r_ref[...] = r
        normed = (x * r * gain_ref[...]).astype(jnp.bfloat16)
        normed_ref[...] = normed
        qkv = mm(normed, w_ref[...], ((1,), (0,)))
        qkv_ref[...] = qkv
        squares = qkv[:, : 2 * cols] * qkv[:, : 2 * cols]
        stat_ref[...] = pair_rows(
            jnp.sum(squares[:, :cols], axis=-1, keepdims=True),
            jnp.sum(squares[:, cols:], axis=-1, keepdims=True),
        )

    full = jnp.float32
    return grid_call(
        body,
        (rows // tm,),
        [
            pl.BlockSpec((tm, width), lambda i: (i, 0)),
            pl.BlockSpec((1, width), lambda i: (0, 0)),
            pl.BlockSpec((width, held_cols), lambda i: (0, 0)),
        ],
        [
            pl.BlockSpec((tm, width), lambda i: (i, 0)),
            pl.BlockSpec((tm, held_cols), lambda i: (i, 0)),
            pl.BlockSpec((tm, 1), lambda i: (i, 0)),
            pl.BlockSpec((8, tm), lambda i: (0, i)),
        ],
        [
            jax.ShapeDtypeStruct((rows, width), jnp.bfloat16),
            jax.ShapeDtypeStruct((rows, held_cols), full),
            jax.ShapeDtypeStruct((rows, 1), full),
            jax.ShapeDtypeStruct((8, rows), full),
        ],
        2 * rows * width * held_cols,
        0,
        x_row,
        gain,
        w_qkv,
    )


def attend(qkv, sums, width, g_query, g_key, cosine, sine, seg_col, seg_row):
    rows, held_cols = qkv.shape
    cols = held_cols // 3
    heads = cols // HEAD
    tq = math.gcd(rows, 256)
    scaling = HEAD ** (-0.5)
    shards = sums.shape[0]

    def body(q, k, v, sums_ref, gq, gk, cos, sin, sc, sr, q_out, k_out, v_out, att_out, log_out, rq, rk):
        @pl.when(pl.program_id(0) == 0)
        def _():
            for i in range(rows // tq):
                at = slice(i * tq, (i + 1) * tq)
                first, second = pair_columns([sums_ref[d, :, at] for d in range(shards)])
                rq[at, :] = lax.rsqrt(first / width + epsilon)
                rk[at, :] = lax.rsqrt(second / width + epsilon)

        def rotated(ref, r, g):
            values = ref[...] * r[...] * g[...]
            swapped = pltpu.roll(values, HEAD // 2, 1)
            return (values * cos[...] + swapped * sin[...]).astype(jnp.bfloat16)

        q_out[...] = rotated(q, rq, gq)
        k_out[...] = rotated(k, rk, gk)
        v_out[...] = v[...].astype(jnp.bfloat16)
        for i in range(rows // tq):
            at, keys = (slice(i * tq, (i + 1) * tq), (i + 1) * tq)
            scores = mm(q_out[at, :], k_out[:keys, :], ((1,), (1,))) * scaling
            allowed = seen(i * tq, tq, keys, sc[at, :], sr[:, :keys])
            scores = jnp.where(allowed, scores, masked_score)
            peak = jnp.max(scores, axis=-1, keepdims=True)
            raised = jnp.exp(scores - peak)
            total = jnp.sum(raised, axis=-1, keepdims=True)
            log_out[0, at, :] = peak + jnp.log(total)
            weights = (raised * (1.0 / total)).astype(jnp.bfloat16)
            att_out[at, :] = mm(weights, v_out[:keys, :], ((1,), (0,))).astype(jnp.bfloat16)

    def col(offset):
        return pl.BlockSpec((rows, HEAD), lambda h: (0, offset + h))

    row = pl.BlockSpec((1, HEAD), lambda h: (0, h))
    one = pl.BlockSpec((rows, 1), lambda h: (0, 0))
    table = pl.BlockSpec((rows, HEAD), lambda h: (0, 0))
    low = jax.ShapeDtypeStruct((rows, cols), jnp.bfloat16)
    column = jax.ShapeDtypeStruct((rows, 1), jnp.float32)
    return grid_call(
        body,
        (heads,),
        [
            col(0),
            col(heads),
            col(2 * heads),
            pl.BlockSpec((shards, 2, rows), lambda h: (0, 0, 0)),
            row,
            row,
            table,
            table,
            one,
            pl.BlockSpec((1, rows), lambda h: (0, 0)),
        ],
        [col(0)] * 4 + [pl.BlockSpec((1, rows, 1), lambda h: (h, 0, 0)), one, one],
        [low] * 4 + [jax.ShapeDtypeStruct((heads, rows, 1), jnp.float32), column, column],
        4 * heads * rows * rows * HEAD,
        heads * rows * rows,
        qkv,
        qkv,
        qkv,
        sums,
        g_query,
        g_key,
        cosine,
        sine,
        seg_col,
        seg_row,
    )


def attend_back(qkv, q_rot, k_rot, value_in, grad, log_total, r_query, r_key, g_query, g_key, cosine, sine, seg_col, seg_row):
    rows, cols = q_rot.shape
    heads = cols // HEAD
    tq = math.gcd(rows, 256)
    scaling = HEAD ** (-0.5)

    def body(q, k, qr, kr, v, ga, lt, rq, rk, gq, gk, cos, sin, sc, sr, q_out, k_out, v_out, stat_out, gq_out, gk_out, q_sum, k_sum, v_sum, stats):
        k_sum[...] = jnp.zeros_like(k_sum)
        v_sum[...] = jnp.zeros_like(v_sum)
        for i in range(rows // tq):
            at, keys = (slice(i * tq, (i + 1) * tq), (i + 1) * tq)
            scores = mm(qr[at, :], kr[:keys, :], ((1,), (1,))) * scaling
            allowed = seen(i * tq, tq, keys, sc[at, :], sr[:, :keys])
            p = jnp.exp(jnp.where(allowed, scores, masked_score) - lt[0, at, :])
            grad_weights = mm(ga[at, :], v[:keys, :], ((1,), (1,)))
            delta = jnp.sum(p * grad_weights, axis=-1, keepdims=True)
            grad_scores = (scaling * p * (grad_weights - delta)).astype(jnp.bfloat16)
            q_sum[at, :] = mm(grad_scores, kr[:keys, :], ((1,), (0,)))
            k_sum[:keys, :] += mm(grad_scores, qr[at, :], ((0,), (0,)))
            v_sum[:keys, :] += mm(p.astype(jnp.bfloat16), ga[at, :], ((0,), (0,)))

        first = pl.program_id(0) == 0

        def back(total, ref, r, g, out, place, gain):
            values = total[...]
            values = values * cos[...] - pltpu.roll(values, HEAD // 2, 1) * sin[...]
            gain[...] = jnp.sum(values * ref[...] * r[...], axis=0, keepdims=True)
            values = values * g[...]
            stat = jnp.sum(values * ref[...], axis=-1, keepdims=True)
            stats[place] += stat
            out[...] = values

        @pl.when(first)
        def _():
            stats[...] = jnp.zeros_like(stats)

        back(q_sum, q, rq, gq, q_out, 0, gq_out)
        back(k_sum, k, rk, gk, k_out, 1, gk_out)

        @pl.when(pl.program_id(0) == heads - 1)
        def _():
            for i in range(rows // tq):
                at = slice(i * tq, (i + 1) * tq)
                stat_out[:, at] = pair_rows(stats[0, at, :], stats[1, at, :])

        v_out[...] = v_sum[...].astype(jnp.bfloat16)

    def col(offset):
        return pl.BlockSpec((rows, HEAD), lambda h: (0, offset + h))

    row = pl.BlockSpec((1, HEAD), lambda h: (0, h))
    one = pl.BlockSpec((rows, 1), lambda h: (0, 0))
    stat = pl.BlockSpec((1, rows, 1), lambda h: (h, 0, 0))
    table = pl.BlockSpec((rows, HEAD), lambda h: (0, 0))
    full = jnp.float32
    outs = (
        [jax.ShapeDtypeStruct((rows, cols), full)] * 2
        + [jax.ShapeDtypeStruct((rows, cols), jnp.bfloat16)]
        + [jax.ShapeDtypeStruct((8, rows), full)]
        + [jax.ShapeDtypeStruct((1, cols), full)] * 2
    )
    args = (qkv, qkv, q_rot, k_rot, value_in, grad, log_total, r_query, r_key, g_query, g_key, cosine, sine, seg_col, seg_row)
    return pl.pallas_call(
        body,
        grid=(heads,),
        in_specs=[col(0), col(heads), col(0), col(0), col(0), col(0), stat, one, one, row, row, table, table, one,
                  pl.BlockSpec((1, rows), lambda h: (0, 0))],
        out_specs=[col(0), col(0), col(0), pl.BlockSpec((8, rows), lambda h: (0, 0)), row, row],
        out_shape=outs,
        scratch_shapes=[pltpu.VMEM((rows, HEAD), full)] * 3 + [pltpu.VMEM((2, rows, 1), full)],
        compiler_params=pltpu.CompilerParams(vmem_limit_bytes=VMEM_GRANT),
        cost_estimate=cost(10 * heads * rows * rows * HEAD, heads * rows * rows, *args, *outs),
    )(*args)


def normed_gradient(q_grad, k_grad, v_low, qkv, sums, r_query, r_key, w_qkv, x_row, r_attn):
    rows, cols = q_grad.shape
    width = x_row.shape[1]
    shards = sums.shape[0]
    tm = math.gcd(rows, 256)

    def body(qg, kg, v, q, k, sums_ref, rq, rk, w, x, ra, low_ref, out_ref, gain_ref):
        means = pair_columns([sums_ref[d] for d in range(shards)])
        parts = []
        for grad, ref, r_ref, mean in ((qg, q, rq, means[0]), (kg, k, rk, means[1])):
            r = r_ref[...]
            part = r * grad[...] - ref[...] * (r * r * r) * (mean / width)
            parts.append(part.astype(jnp.bfloat16))
        parts.append(v[...])
        for i in range(3):
            low_ref[:, i * cols : (i + 1) * cols] = parts[i]
        total = mm(low_ref[...], w[...], ((1,), (1,)))
        out_ref[...] = total.astype(jnp.bfloat16)
        gain = jnp.sum(total * x[...].astype(jnp.float32) * ra[...], axis=0, keepdims=True)
        first = pl.program_id(0) == 0

        @pl.when(first)
        def _():
            gain_ref[...] = gain

        @pl.when(jnp.logical_not(first))
        def _():
            gain_ref[...] += gain

    def tiled(count, at=0):
        return pl.BlockSpec((tm, count), lambda i: (i, at))

    return grid_call(
        body,
        (rows // tm,),
        [
            tiled(cols),
            tiled(cols),
            tiled(cols),
            tiled(cols),
            tiled(cols, 1),
            pl.BlockSpec((shards, 2, tm), lambda i: (0, 0, i)),
            tiled(1),
            tiled(1),
            pl.BlockSpec((width, 3 * cols), lambda i: (0, 0)),
            tiled(width),
            tiled(1),
        ],
        [tiled(3 * cols), tiled(width), pl.BlockSpec((1, width), lambda i: (0, 0))],
        [
            jax.ShapeDtypeStruct((rows, 3 * cols), jnp.bfloat16),
            jax.ShapeDtypeStruct((rows, width), jnp.bfloat16),
            jax.ShapeDtypeStruct((1, width), jnp.float32),
        ],
        6 * rows * width * cols,
        0,
        q_grad,
        k_grad,
        v_low,
        qkv,
        qkv,
        sums,
        r_query,
        r_key,
        w_qkv,
        x_row,
        r_attn,
    )


def middle(order, nf_own, mid, r_ffn, gain, dy, out_pieces):
    tokens, width = nf_own.shape
    chunk = width // 4

    def body(order_ref, nf, mid_ref, r_ref, gain_ref, dy_ref, p0, p1, p2, p3, grad_ref, low_ref, att_ref, gain_out):
        r = r_ref[...]
        own = mid_ref[...]
        grad = nf[...].astype(jnp.float32)
        gain_out[...] = jnp.sum(grad * own * r, axis=0, keepdims=True)
        grad = grad * gain_ref[...]
        mean = jnp.mean(grad * own, axis=-1, keepdims=True)
        total = dy_ref[...].astype(jnp.float32) + r * grad - own * (r * r * r) * mean
        grad_ref[...] = total
        low_ref[...] = total.astype(jnp.bfloat16)
        for j, piece in enumerate((p0, p1, p2, p3)):
            back = jnp.zeros((tokens, chunk), jnp.float32)
            for k in range(4):
                n = k ^ j
                back = back + mm(
                    low_ref[:, n * chunk : (n + 1) * chunk],
                    piece[:, k * chunk : (k + 1) * chunk],
                    ((1,), (1,)),
                )
            att_ref[order_ref[j]] = back.astype(jnp.bfloat16)

    def whole(*shape):
        return pl.BlockSpec(shape, lambda i, o: (0,) * len(shape))

    outs = [
        jax.ShapeDtypeStruct((tokens, width), jnp.float32),
        jax.ShapeDtypeStruct((tokens, width), jnp.bfloat16),
        jax.ShapeDtypeStruct((4, tokens, chunk), jnp.bfloat16),
        jax.ShapeDtypeStruct((1, width), jnp.float32),
    ]
    return pl.pallas_call(
        body,
        grid_spec=pltpu.PrefetchScalarGridSpec(
            num_scalar_prefetch=1,
            grid=(1,),
            in_specs=[
                whole(tokens, width),
                pl.BlockSpec((tokens, width), lambda i, o: (o[4], 0)),
                pl.BlockSpec((tokens, 1), lambda i, o: (o[4], 0)),
                whole(1, width),
                whole(tokens, width),
                *[whole(chunk, width)] * 4,
            ],
            out_specs=[whole(*o.shape) for o in outs],
        ),
        out_shape=outs,
        compiler_params=pltpu.CompilerParams(vmem_limit_bytes=VMEM_GRANT),
        cost_estimate=cost(2 * tokens * width * width, 0, *out_pieces, *outs),
    )(order, nf_own, mid, r_ffn, gain, dy, *out_pieces)


def out_grad_pieces(order, attended, columns):
    shards, rows, cols = attended.shape
    per_chunk = shards // 4
    count = columns.shape[1]
    tm = math.gcd(cols, 256)

    def body(order_ref, att_ref, col_ref, *outs):
        step = pl.program_id(0)
        for j in range(4):

            @pl.when(step == j)
            def _(j=j):
                outs[j][...] = mm(att_ref[0], col_ref[...], ((0,), (0,))).astype(jnp.bfloat16)

    def place(j):
        return lambda k, i, o: (jnp.where(k < j, 0, jnp.where(k > j, per_chunk - 1, i)), 0)

    outs = [jax.ShapeDtypeStruct((per_chunk * cols, count), jnp.bfloat16)] * 4
    return pl.pallas_call(
        body,
        grid_spec=pltpu.PrefetchScalarGridSpec(
            num_scalar_prefetch=1,
            grid=(4, per_chunk),
            in_specs=[
                pl.BlockSpec((1, rows, cols), lambda k, i, o: (o[k] * per_chunk + i, 0, 0)),
                pl.BlockSpec((rows, count), lambda k, i, o: (0, 0)),
            ],
            out_specs=[pl.BlockSpec((cols, count), place(j)) for j in range(4)],
        ),
        out_shape=outs,
        compiler_params=pltpu.CompilerParams(vmem_limit_bytes=VMEM_GRANT),
        cost_estimate=cost(2 * rows * shards * cols * count, 0, attended, columns, *outs),
    )(order, attended, columns)


def over_y(values):
    return lax.ppermute(values, "seq", [(i, i ^ 1) for i in range(8)])


def along_z(values):
    lines = [[0, 2, 4, 6], [1, 3, 5, 7]]
    return lax.all_gather(values, "seq", axis=0, tiled=False, axis_index_groups=lines)


def both_y(line, other):
    y = lax.axis_index("seq") % 2
    row = jnp.zeros((4, 2) + line.shape[1:], line.dtype)
    for blocks, at in ((line, y), (other, 1 - y)):
        row = lax.dynamic_update_slice(row, blocks[:, None], (0, at) + (0,) * (line.ndim - 1))
    return row.reshape((8,) + line.shape[1:])


def sum_along_z(values):
    lines = [[0, 2, 4, 6], [1, 3, 5, 7]]
    return lax.psum_scatter(
        values, "seq", scatter_dimension=0, tiled=True, axis_index_groups=lines
    )


def swap(values, bits):
    return lax.ppermute(values, "dp", [(i, i ^ bits) for i in range(4)])


def sum_in_chip(pieces, sent):
    wide = jnp.float32
    kept = pieces[0].astype(wide) + swap(pieces[1], 1).astype(wide)
    return (kept.astype(sent), (pieces[2].astype(wide) + swap(pieces[3], 1).astype(wide)).astype(sent))


def sum_experts_in_chip(pieces):
    wide, low = (jnp.float32, jnp.bfloat16)
    arrived = swap(pieces[3], 1)
    kept = pieces[0].astype(wide) + swap(pieces[1], 1).astype(wide)
    passed = [
        (pieces[2][e].astype(wide) + arrived[e].astype(wide)).astype(low)
        for e in range(arrived.shape[0])
    ]
    return (kept.astype(low), passed)


def across_by_expert(passed):
    return [swap(p, 2) for p in passed]


def add_arrived(kept, arrived):
    return jnp.stack(
        [kept[e].astype(jnp.float32) + a.astype(jnp.float32) for e, a in enumerate(arrived)]
    )


def sum_pieces(pieces, sent):
    kept, passed = sum_in_chip(pieces, sent)
    return kept.astype(jnp.float32) + swap(passed, 2).astype(jnp.float32)


def reorder(values, dp_index, axis):
    size = values.shape[axis] // 4
    return jnp.concatenate(
        [
            lax.dynamic_slice_in_dim(values, (dp_index ^ k) * size, size, axis=axis)
            for k in range(4)
        ],
        axis=axis,
    )


def on_device_heads(
    hidden_in,
    segment_ids,
    routes,
    w_query,
    w_key,
    w_value,
    w_out,
    gain_attn,
    gain_query,
    gain_key,
    gain_ffn,
    w_router,
    w_gate,
    w_up,
    w_down,
    cotangent,
):
    low, full = (jnp.bfloat16, jnp.float32)
    shards = lax.axis_size("seq")
    seq_index, dp_index = (lax.axis_index("seq"), lax.axis_index("dp"))
    tokens, width = hidden_in.shape[1:]
    rows = shards * tokens
    cols = width // shards
    heads = cols // HEAD
    held = w_gate.shape[0]
    expert_count = held * shards
    block_rows = w_query.shape[0]
    chunk = shards * block_rows
    row_seg = segment_ids[0]
    first_row = seq_index * tokens
    barrier = lax.optimization_barrier

    def own_cols(values, count):
        return lax.dynamic_slice_in_dim(values, seq_index * count, count, axis=values.ndim - 1)

    cosine, sine = rope_tables(rows, HEAD)
    seg_col, seg_row = (row_seg[:, None], row_seg[None, :])

    x_shard = reorder(hidden_in[0], dp_index, 1)
    x_row = lax.all_gather(x_shard, "seq", axis=0, tiled=True)
    blocks = jnp.stack(
        [w.reshape(block_rows, shards, cols).transpose(1, 0, 2) for w in (w_query, w_key, w_value)],
        axis=1,
    )
    blocks = blocks.reshape(shards, 3 * block_rows, cols)
    place_at = (dp_index * shards + seq_index) * block_rows
    gain_rows = lax.dynamic_update_slice(
        jnp.zeros((shards, 16, cols), low),
        jnp.stack([gain_query, gain_key])[None],
        (place_at // cols, 0, place_at % cols),
    )
    gain_rows = lax.dynamic_update_slice(
        gain_rows, jnp.broadcast_to(gain_attn[None, None], (shards, 1, block_rows)), (0, 2, 0)
    )
    blocks = lax.all_to_all(jnp.concatenate([blocks, gain_rows], axis=1), "seq", 0, 0, tiled=True)
    across = swap(blocks, 2)
    qkv_pieces = (blocks, swap(blocks, 1), across, swap(across, 1))
    gate_across = swap(w_gate, 2)
    w_qkv = jnp.concatenate(
        [
            p[:, : 3 * block_rows]
            .reshape(shards, 3, block_rows, cols)
            .transpose(0, 2, 1, 3)
            .reshape(chunk, 3 * cols)
            for p in qkv_pieces
        ],
        axis=0,
    )
    gain_rows = jnp.concatenate([p[:, 3 * block_rows :] for p in qkv_pieces], axis=0)
    gain_pair = jnp.sum(gain_rows[:, :2].astype(full), axis=0)
    g_query, g_key = (gain_pair[0:1], gain_pair[1:2])
    g_attn = gain_rows[:, 2, :block_rows].reshape(1, width).astype(full)
    gate_pieces = (w_gate, swap(w_gate, 1), gate_across, swap(gate_across, 1))
    x_row, w_qkv, g_query, g_key, g_attn, gate_pieces = barrier(
        (x_row, w_qkv, g_query, g_key, g_attn, gate_pieces)
    )

    picks = routes.shape[2]
    packed = tokens // block_rows
    extra = jnp.concatenate(
        [routes[0].astype(low).reshape(block_rows, packed * picks), w_router, gain_ffn[:, None]],
        axis=1,
    )
    extra = jnp.pad(extra, ((0, 0), (0, 128 - extra.shape[1])))
    out_line = along_z(jnp.concatenate([reorder(w_out, dp_index, 1), extra], axis=1))
    up_across = swap(w_up, 2)

    def share(sums):
        spread = jnp.broadcast_to(sums[None, :2], (shards, 2, rows))
        return lax.all_to_all(spread, "seq", 0, 0, tiled=True)

    normed, qkv, r_attn, sums = project(x_row, g_attn, w_qkv)
    q_rot, k_rot, value_in, attended, log_total, r_query, r_key = attend(
        qkv, share(sums), width, g_query, g_key, cosine, sine, seg_col, seg_row
    )
    attended, out_line, up_across = barrier((attended, out_line, up_across))

    attended_row = lax.all_gather(attended, "seq", axis=0)
    out_other, line_across = (over_y(out_line), swap(out_line, 2))
    gate_full = jnp.concatenate(gate_pieces, axis=1)
    up_full = jnp.concatenate([w_up, swap(w_up, 1), up_across, swap(up_across, 1)], axis=1)
    out_other, line_across, gate_full = barrier((out_other, line_across, gate_full))
    other_across = swap(out_other, 2)
    out_own = both_y(out_line, out_other).reshape(chunk, width + 128)
    other_across, up_full, out_own = barrier((other_across, up_full, out_own))
    out_across = both_y(line_across, other_across).reshape(chunk, width + 128)
    out_pieces = (out_own, swap(out_own, 1), out_across, swap(out_across, 1))
    extras = [p[:, width:] for p in out_pieces]
    routes_row = extras[0][:, : packed * picks].reshape(rows, picks).astype(jnp.int32)
    extras = jnp.concatenate([p[:, packed * picks :] for p in extras], axis=0)
    router = jnp.pad(extras[:, :expert_count], ((0, 0), (0, 128 - expert_count)))
    g_ffn = extras[:, expert_count].astype(full)[None]
    lane_ids = lax.iota(jnp.int32, 128)
    chosen = jnp.any(routes_row[:, :, None] == lane_ids[None, None, :], axis=1).astype(full)
    own = (
        lane_ids[None, :] == seq_index * held + lax.iota(jnp.int32, held)[:, None]
    ).astype(full)
    attended_row, out_pieces, up_full, router, g_ffn, chosen = barrier(
        (attended_row, out_pieces, up_full, router, g_ffn, chosen)
    )

    dy_shard, attended_row = barrier((reorder(cotangent[0], dp_index, 1), attended_row))
    dy_row = lax.all_gather(dy_shard, "seq", axis=0, tiled=True)
    order = jnp.stack([dp_index ^ k for k in range(4)] + [seq_index]).astype(jnp.int32)
    hidden_mid, normed_ffn, r_ffn, chances, gates = finish_attention(
        order, attended_row, out_pieces, x_row, g_ffn, router, chosen, own, expert_count
    )
    act, dgate_factor, dup_factor = expert_activations(normed_ffn, gate_full, up_full)
    act, down_across = barrier((act, swap(w_down, 2)))
    down_full = jnp.concatenate([w_down, swap(w_down, 1), down_across, swap(down_across, 1)], axis=2)
    y_at = (seq_index % 2).astype(jnp.int32)[None]
    mixture, mixture_far = combine_experts(y_at, act, down_full, gates)
    dy_row, mixture_far, act = barrier((dy_row, mixture_far, act))
    mixture_far = over_y(mixture_far)

    scaled, dgate, dup, gate_sums = expert_gradients(
        dy_row, down_full, act, dgate_factor, dup_factor, gates
    )
    nf_grad, grad_logits = input_gradient(
        dgate, dup, gate_full, up_full, gate_sums, chances, chosen, own, router
    )
    nf_grad, mixture_far = barrier((nf_grad, mixture_far))
    nf_sum = lax.psum_scatter(nf_grad, "seq", scatter_dimension=0, tiled=True)
    mixture = (mixture.astype(full) + mixture_far.astype(full)).astype(low)

    down_kept, down_passed = sum_experts_in_chip(weight_pieces(scaled, dy_row, 4, False))
    gate_pieces = weight_pieces(normed_ffn, dgate, 4, True)
    dup, down_passed = barrier((dup, down_passed))
    down_arrived = across_by_expert(down_passed)
    gate_kept, gate_passed = sum_experts_in_chip(gate_pieces)
    up_pieces = weight_pieces(normed_ffn, dup, 4, True)
    up_kept, up_passed = sum_experts_in_chip(up_pieces)
    router_grad = mm(grad_logits[:, :expert_count], normed_ffn, ((0,), (0,)))
    nf_sum, mixture, down_arrived[0], gate_passed, up_passed, router_grad, down_kept, gate_kept, up_kept = barrier(
        (nf_sum, mixture, down_arrived[0], gate_passed, up_passed, router_grad, down_kept, gate_kept, up_kept)
    )
    gate_arrived, up_arrived = (across_by_expert(gate_passed), [swap(up_passed[0], 2)])

    grad_mid, mid_low, grad_attended, gain_ffn_grad = middle(
        order, nf_sum, hidden_mid, r_ffn, g_ffn, dy_shard, out_pieces
    )
    def to_columns(values):
        return lax.all_to_all(values, "seq", 0, 0, tiled=True).reshape(rows, cols)

    grad_attended = grad_attended.reshape(4, tokens, shards // 4, cols).transpose(0, 2, 1, 3)
    grad_attended = to_columns(grad_attended.reshape(shards, tokens, cols))
    grad_attended, down_arrived[1], gate_arrived[0], mixture = barrier(
        (grad_attended, down_arrived[1], gate_arrived[0], mixture)
    )
    mixture_own = sum_along_z(mixture)
    mid_cols = to_columns(
        reorder(mid_low, dp_index, 1).reshape(tokens, shards, cols).transpose(1, 0, 2)
    )
    q_grad, k_grad, v_low, sums, gain_query_grad, gain_key_grad = attend_back(
        qkv, q_rot, k_rot, value_in, grad_attended, log_total,
        r_query, r_key, g_query, g_key, cosine, sine, seg_col, seg_row,
    )
    sums, gate_arrived[1] = barrier((sums, gate_arrived[1]))
    sums, mid_cols = barrier((share(sums), mid_cols))
    qkv_low, normed_grad, gain_attn_grad = normed_gradient(
        q_grad, k_grad, v_low, qkv, sums, r_query, r_key, w_qkv, x_row, r_attn
    )
    normed_grad, up_arrived[0], mixture_own = barrier((normed_grad, up_arrived[0], mixture_own))
    normed_sum = lax.psum_scatter(normed_grad, "seq", scatter_dimension=0, tiled=True).astype(full)

    def to_owners(kept, passed, count):
        total = kept.astype(full) + swap(passed, 2).astype(full)
        total = lax.all_to_all(
            total.astype(low).reshape(shards, block_rows, count * cols), "seq", 0, 0, tiled=True
        )
        total = total.reshape(shards, block_rows, count, cols).transpose(2, 1, 0, 3)
        return total.reshape(count, block_rows, width).astype(full)

    qkv_parts = [p[0] for p in weight_pieces(normed, qkv_low[None], 4, True)]
    qkv_parts, mid_cols, gain_attn_grad, gain_ffn_grad = barrier(
        (qkv_parts, mid_cols, gain_attn_grad, gain_ffn_grad)
    )
    qkv_kept, qkv_passed = sum_in_chip(qkv_parts, low)
    out_parts = out_grad_pieces(order, attended_row, mid_cols)
    out_kept, out_passed = sum_in_chip(out_parts, low)
    qkv_passed, out_passed, up_last = barrier((qkv_passed, out_passed, up_passed[1]))
    proj_grad = to_owners(qkv_kept, qkv_passed, 3)
    out_grad = to_owners(out_kept, out_passed, 1)
    up_arrived.append(swap(up_last, 2))
    grad_w_down = add_arrived(down_kept, down_arrived)
    grad_w_gate = add_arrived(gate_kept, gate_arrived)
    grad_w_up = add_arrived(up_kept, up_arrived)
    mid_own = lax.dynamic_slice_in_dim(hidden_mid, first_row, tokens)
    block_out = (mid_own + mixture_own.astype(full)).astype(low)
    normed_sum, grad_w_down, grad_w_gate, grad_w_up, out_grad, block_out = barrier(
        (normed_sum, grad_w_down, grad_w_gate, grad_w_up, out_grad, block_out)
    )

    x_own = x_shard.astype(full)
    r_here = lax.rsqrt(jnp.mean(x_own * x_own, axis=-1, keepdims=True) + epsilon)
    scaled_grad = normed_sum * g_attn
    grad_hidden = (
        grad_mid
        + r_here * scaled_grad
        - x_own * (r_here**3) * jnp.mean(scaled_grad * x_own, axis=-1, keepdims=True)
    )

    def place(values):
        whole = lax.dynamic_update_slice_in_dim(
            jnp.zeros((1, width), full), values[None], seq_index * cols, 1
        )
        return reorder(whole, dp_index, 1)

    vectors = jnp.concatenate(
        [
            router_grad,
            gain_attn_grad,
            place(gain_query_grad[0]),
            place(gain_key_grad[0]),
            gain_ffn_grad,
        ]
    )
    count = vectors.shape[0]
    vectors = sum_pieces([vectors[:, k * chunk : (k + 1) * chunk] for k in range(4)], full)
    vectors = vectors.reshape(count, shards, block_rows).transpose(1, 0, 2)
    vectors = jnp.sum(lax.all_to_all(vectors, "seq", 0, 0, tiled=True), axis=0)
    return (
        reorder(block_out, dp_index, 1)[None],
        reorder(grad_hidden, dp_index, 1)[None],
        proj_grad[0],
        proj_grad[1],
        proj_grad[2],
        out_grad[0],
        vectors[expert_count],
        vectors[expert_count + 1],
        vectors[expert_count + 2],
        vectors[expert_count + 3],
        vectors[:expert_count].T,
        grad_w_gate,
        grad_w_up,
        grad_w_down,
    )


def solution(mesh):
    def layer(*arrays):
        whole_heads = (arrays[0].shape[2] // HEAD) % mesh.shape["seq"] == 0
        if whole_heads and mesh.shape["dp"] == 4 and mesh.shape["seq"] == 8:
            return on_device_heads(*arrays)
        return on_device(*arrays)

    return jax.shard_map(
        layer,
        mesh=mesh,
        in_specs=(
            P("dp", "seq", None),
            P("dp", None),
            P("dp", "seq", None),
            P(("dp", "seq"), None),
            P(("dp", "seq"), None),
            P(("dp", "seq"), None),
            P(("dp", "seq"), None),
            P(("dp", "seq")),
            P(("dp", "seq")),
            P(("dp", "seq")),
            P(("dp", "seq")),
            P(("dp", "seq"), None),
            P("seq", "dp", None),
            P("seq", "dp", None),
            P("seq", None, "dp"),
            P("dp", "seq", None),
        ),
        out_specs=(
            P("dp", "seq", None),
            P("dp", "seq", None),
            P(("dp", "seq"), None),
            P(("dp", "seq"), None),
            P(("dp", "seq"), None),
            P(("dp", "seq"), None),
            P(("dp", "seq")),
            P(("dp", "seq")),
            P(("dp", "seq")),
            P(("dp", "seq")),
            P(("dp", "seq"), None),
            P("seq", "dp", None),
            P("seq", "dp", None),
            P("seq", None, "dp"),
        ),
        check_vma=False,
    )
```

```python
import math

import jax
import jax.numpy as jnp
from jax import lax
from jax.experimental import pallas as pl
from jax.experimental.pallas import tpu as pltpu
from jax.sharding import PartitionSpec as P

HEAD = 128


epsilon = 1e-05
masked_score = -1e30
rope_base = 10000.0


def normalize(values, gain_vec):
    return (
        values * lax.rsqrt(jnp.mean(values * values, axis=-1, keepdims=True) + epsilon) * gain_vec
    )


def rotary(values, positions):
    half_dim = values.shape[-1] // 2
    frequency = jnp.exp(
        jnp.arange(half_dim, dtype=jnp.float32) * (-2.0 * math.log(rope_base) / values.shape[-1])
    )
    angles = positions.astype(jnp.float32)[:, None] * frequency[None, :]
    cosine = jnp.cos(angles)[:, None, :]
    sine_table = jnp.sin(angles)[:, None, :]
    first_half = values[..., :half_dim]
    second = values[..., half_dim:]
    return jnp.concatenate(
        [first_half * cosine - second * sine_table, second * cosine + first_half * sine_table],
        axis=-1,
    )


def softmax_rows(values):
    peak_value = jnp.max(values, axis=-1, keepdims=True)
    raised = jnp.exp(values - peak_value)
    return raised / jnp.sum(raised, axis=-1, keepdims=True)


def rotate_normed(projection, gain_vec, positions):
    tokens, model_width = projection.shape
    return rotary(
        normalize(projection, gain_vec).reshape(tokens, model_width // HEAD, HEAD), positions
    )


def masked_scores(queries, key_block, query_pos, query_seg, key_pos, key_seg, scaling):
    raw_scores = jnp.einsum("qhd,khd->hqk", queries, key_block, preferred_element_type=jnp.float32)
    allowed = (query_pos[:, None] >= key_pos[None, :]) & (query_seg[:, None] == key_seg[None, :])
    return jnp.where(allowed[None], raw_scores * scaling, masked_score)


def key_window(keys_all, values_all, row_seg, begin_at, span):
    key_block = lax.dynamic_slice_in_dim(keys_all, begin_at, span)
    value_block = lax.dynamic_slice_in_dim(values_all, begin_at, span)
    key_pos = begin_at + lax.iota(jnp.int32, span)
    key_seg = lax.dynamic_slice_in_dim(row_seg, begin_at, span)
    return (key_block, value_block, key_pos, key_seg)


def project_front(hidden, layer_full, positions):
    tokens, model_width = hidden.shape
    normed = normalize(hidden, layer_full[5].astype(jnp.float32)).astype(jnp.bfloat16)
    query = jnp.dot(normed, layer_full[0], preferred_element_type=jnp.float32)
    key_proj = jnp.dot(normed, layer_full[1], preferred_element_type=jnp.float32)
    value_proj = jnp.dot(normed, layer_full[2], preferred_element_type=jnp.float32)
    query_rot = rotate_normed(query, layer_full[6].astype(jnp.float32), positions).astype(
        jnp.bfloat16
    )
    key_rot = rotate_normed(key_proj, layer_full[7].astype(jnp.float32), positions).astype(
        jnp.bfloat16
    )
    value_in = value_proj.astype(jnp.bfloat16).reshape(tokens, model_width // HEAD, HEAD)
    return (normed, query, key_proj, query_rot, key_rot, value_in)


def attend_local(query_rot, keys_all, values_all, row_seg, offset, span):
    tokens, head_count, head_dim = query_rot.shape
    scaling = head_dim ** (-0.5)
    query_pos = offset + lax.iota(jnp.int32, tokens)
    query_seg = lax.dynamic_slice_in_dim(row_seg, offset, tokens)
    reach_blocks = (offset + tokens + span - 1) // span

    def block_scores(block_index):
        begin_at = block_index * span
        key_block, value_block, key_pos, key_seg = key_window(
            keys_all, values_all, row_seg, begin_at, span
        )
        return (
            masked_scores(query_rot, key_block, query_pos, query_seg, key_pos, key_seg, scaling),
            value_block,
        )

    def first_pass(block_index, state_pair):
        peak_value, denominator = state_pair
        scores, unused_values = block_scores(block_index)
        new_peak = jnp.maximum(peak_value, jnp.max(scores, axis=-1))
        denominator = denominator * jnp.exp(peak_value - new_peak) + jnp.sum(
            jnp.exp(scores - new_peak[..., None]), axis=-1
        )
        return (new_peak, denominator)

    start_state = (
        jnp.full((head_count, tokens), masked_score, jnp.float32),
        jnp.zeros((head_count, tokens), jnp.float32),
    )
    peak_value, denominator = lax.fori_loop(0, reach_blocks, first_pass, start_state)
    log_total = peak_value + jnp.log(denominator)

    def second_pass(block_index, running):
        scores, value_block = block_scores(block_index)
        weights = jnp.exp(scores - log_total[..., None]).astype(jnp.bfloat16)
        return running + jnp.einsum(
            "hqk,khd->qhd", weights, value_block, preferred_element_type=jnp.float32
        )

    attention = lax.fori_loop(
        0, reach_blocks, second_pass, jnp.zeros((tokens, head_count, head_dim), jnp.float32)
    )
    return (attention, log_total)


def query_grads(query_rot, keys_all, values_all, row_seg, offset, span, log_total, grad_attended):
    tokens, head_count, head_dim = query_rot.shape
    scaling = head_dim ** (-0.5)
    query_pos = offset + lax.iota(jnp.int32, tokens)
    query_seg = lax.dynamic_slice_in_dim(row_seg, offset, tokens)
    reach_blocks = (offset + tokens + span - 1) // span

    def block_terms(block_index):
        begin_at = block_index * span
        key_block, value_block, key_pos, key_seg = key_window(
            keys_all, values_all, row_seg, begin_at, span
        )
        scores = masked_scores(
            query_rot, key_block, query_pos, query_seg, key_pos, key_seg, scaling
        )
        weights = jnp.exp(scores - log_total[..., None])
        grad_weights = jnp.einsum(
            "qhd,khd->hqk", grad_attended, value_block, preferred_element_type=jnp.float32
        )
        return (key_block, weights, grad_weights)

    def delta_pass(block_index, running):
        unused_keys, weights, grad_weights = block_terms(block_index)
        return running + jnp.sum(weights * grad_weights, axis=-1)

    delta = lax.fori_loop(0, reach_blocks, delta_pass, jnp.zeros((head_count, tokens), jnp.float32))

    def query_pass(block_index, running):
        key_block, weights, grad_weights = block_terms(block_index)
        grad_scores = (weights * (grad_weights - delta[..., None]) * scaling).astype(jnp.bfloat16)
        return running + jnp.einsum(
            "hqk,khd->qhd", grad_scores, key_block, preferred_element_type=jnp.float32
        )

    grad_query_rot = lax.fori_loop(
        0, reach_blocks, query_pass, jnp.zeros((tokens, head_count, head_dim), jnp.float32)
    )
    return (delta, grad_query_rot)


def route_tokens(hidden_mid, layer_full, choice_rows):
    tokens, pick_count = choice_rows.shape
    normed_ffn = normalize(hidden_mid, layer_full[8].astype(jnp.float32)).astype(jnp.bfloat16)
    logits = jnp.dot(normed_ffn, layer_full[4], preferred_element_type=jnp.float32)
    expert_count = logits.shape[1]
    capacity = 3 * tokens * pick_count // (2 * expert_count)
    chances = softmax_rows(logits)
    picks = choice_rows[:, :, None] == lax.iota(jnp.int32, expert_count)[None, None, :]
    gate_values = jnp.sum(jnp.where(picks, chances[:, None, :], 0.0), axis=-1)
    flat_hits = picks.reshape(tokens * pick_count, expert_count).astype(jnp.int32)
    earlier = jnp.cumsum(flat_hits, axis=0) - flat_hits
    slot_ids = choice_rows.reshape(-1) * capacity + jnp.sum(earlier * flat_hits, axis=1)
    pair_table = lax.iota(jnp.int32, expert_count * capacity)[:, None] == slot_ids[None, :]
    spread = jnp.sum(
        pair_table.reshape(expert_count * capacity, tokens, pick_count).astype(jnp.int32), axis=2
    ).astype(jnp.bfloat16)
    send_rows = jnp.dot(spread, normed_ffn, preferred_element_type=jnp.float32).astype(jnp.bfloat16)
    send_rows = send_rows.reshape(expert_count, capacity, hidden_mid.shape[1])
    return (normed_ffn, chances, picks, gate_values, slot_ids, pair_table, spread, send_rows)


def group_rows(row_block, held_experts):
    sources = row_block.shape[0] // held_experts
    grouped = row_block.reshape(
        sources, held_experts, row_block.shape[1], row_block.shape[2]
    ).transpose(1, 0, 2, 3)
    return grouped.reshape(held_experts, sources * row_block.shape[1], row_block.shape[2])


def ungroup_rows(grouped, whole_shape):
    held_experts = grouped.shape[0]
    sources = whole_shape[0] // held_experts
    spread_out = grouped.reshape(held_experts, sources, whole_shape[1], whole_shape[2]).transpose(
        1, 0, 2, 3
    )
    return spread_out.reshape(whole_shape)


def expert_forward(row_block, gate_full, up_full, down_full):
    inputs = group_rows(row_block, gate_full.shape[0])
    gate_pre = jnp.einsum("erd,edf->erf", inputs, gate_full, preferred_element_type=jnp.float32)
    up_pre = jnp.einsum("erd,edf->erf", inputs, up_full, preferred_element_type=jnp.float32)
    activated = (gate_pre * lax.logistic(gate_pre) * up_pre).astype(jnp.bfloat16)
    result = jnp.einsum(
        "erf,efd->erd", activated, down_full, preferred_element_type=jnp.float32
    ).astype(jnp.bfloat16)
    return ungroup_rows(result, row_block.shape)


def expert_backward(row_block, grad_block, gate_full, up_full, down_full):
    inputs = group_rows(row_block, gate_full.shape[0])
    grad_outputs = group_rows(grad_block, gate_full.shape[0])
    gate_pre = jnp.einsum("erd,edf->erf", inputs, gate_full, preferred_element_type=jnp.float32)
    up_pre = jnp.einsum("erd,edf->erf", inputs, up_full, preferred_element_type=jnp.float32)
    sigmoid_gate = lax.logistic(gate_pre)
    activated = (gate_pre * sigmoid_gate * up_pre).astype(jnp.bfloat16)
    grad_act = jnp.einsum(
        "erd,efd->erf", grad_outputs, down_full, preferred_element_type=jnp.float32
    )
    grad_down = jnp.einsum(
        "erf,erd->efd", activated, grad_outputs, preferred_element_type=jnp.float32
    )
    grad_gate_pre = (
        grad_act * up_pre * sigmoid_gate * (1.0 + gate_pre * (1.0 - sigmoid_gate))
    ).astype(jnp.bfloat16)
    grad_up_pre = (grad_act * gate_pre * sigmoid_gate).astype(jnp.bfloat16)
    grad_gate_w = jnp.einsum(
        "erd,erf->edf", inputs, grad_gate_pre, preferred_element_type=jnp.float32
    )
    grad_up_w = jnp.einsum("erd,erf->edf", inputs, grad_up_pre, preferred_element_type=jnp.float32)
    grad_inputs = jnp.einsum(
        "erf,edf->erd", grad_gate_pre, gate_full, preferred_element_type=jnp.float32
    )
    grad_inputs = grad_inputs + jnp.einsum(
        "erf,edf->erd", grad_up_pre, up_full, preferred_element_type=jnp.float32
    )
    return (
        ungroup_rows(grad_inputs.astype(jnp.bfloat16), row_block.shape),
        grad_gate_w,
        grad_up_w,
        grad_down,
    )


def contract_rows(left, right):
    return lax.dot_general(
        left, right, (((0,), (0,)), ((), ())), preferred_element_type=jnp.float32
    )


def contract_cols(left, right):
    return lax.dot_general(
        left, right, (((1,), (1,)), ((), ())), preferred_element_type=jnp.float32
    )


def on_device(
    hidden_in,
    segment_ids,
    routes,
    w_query,
    w_key,
    w_value,
    w_out,
    gain_attn,
    gain_query,
    gain_key,
    gain_ffn,
    w_router,
    w_gate,
    w_up,
    w_down,
    cotangent,
):
    hidden = hidden_in[0].astype(jnp.float32)
    tokens, model_width = hidden.shape
    head_count = model_width // HEAD
    row_seg = segment_ids[0]
    choice_rows = routes[0]
    offset = lax.axis_index("seq") * tokens
    positions = offset + lax.iota(jnp.int32, tokens)
    span = min(512, row_seg.shape[0])
    layer_full = (
        lax.all_gather(w_query, ("dp", "seq"), axis=0, tiled=True),
        lax.all_gather(w_key, ("dp", "seq"), axis=0, tiled=True),
        lax.all_gather(w_value, ("dp", "seq"), axis=0, tiled=True),
        lax.all_gather(w_out, ("dp", "seq"), axis=0, tiled=True),
        lax.all_gather(w_router, ("dp", "seq"), axis=0, tiled=True),
        lax.all_gather(gain_attn, ("dp", "seq"), axis=0, tiled=True),
        lax.all_gather(gain_query, ("dp", "seq"), axis=0, tiled=True),
        lax.all_gather(gain_key, ("dp", "seq"), axis=0, tiled=True),
        lax.all_gather(gain_ffn, ("dp", "seq"), axis=0, tiled=True),
    )
    expert_full = (
        lax.all_gather(w_gate, "dp", axis=1, tiled=True),
        lax.all_gather(w_up, "dp", axis=1, tiled=True),
        lax.all_gather(w_down, "dp", axis=2, tiled=True),
    )
    projected = project_front(hidden, layer_full, positions)
    keys_all, values_all = (
        lax.all_gather(projected[4], "seq", axis=0, tiled=True),
        lax.all_gather(projected[5], "seq", axis=0, tiled=True),
    )
    attention, log_total = attend_local(projected[3], keys_all, values_all, row_seg, offset, span)
    attended = attention.reshape(tokens, model_width).astype(jnp.bfloat16)
    hidden_mid = hidden + jnp.dot(attended, layer_full[3], preferred_element_type=jnp.float32)
    routing = route_tokens(hidden_mid, layer_full, choice_rows)
    expert_count, capacity = (routing[7].shape[0], routing[7].shape[1])
    expert_out = expert_forward(
        lax.all_to_all(routing[7], "seq", split_axis=0, concat_axis=0, tiled=True),
        expert_full[0],
        expert_full[1],
        expert_full[2],
    )
    returned = lax.all_to_all(expert_out, "seq", split_axis=0, concat_axis=0, tiled=True)
    picked = jnp.take(returned.reshape(expert_count * capacity, model_width), routing[4], axis=0)
    picked = picked.reshape(tokens, choice_rows.shape[1], model_width)
    mixture = jnp.sum(routing[3][:, :, None] * picked.astype(jnp.float32), axis=1)
    block_out = (hidden_mid + mixture).astype(jnp.bfloat16)
    layer_full = (
        lax.all_gather(w_query, ("dp", "seq"), axis=0, tiled=True),
        lax.all_gather(w_key, ("dp", "seq"), axis=0, tiled=True),
        lax.all_gather(w_value, ("dp", "seq"), axis=0, tiled=True),
        lax.all_gather(w_out, ("dp", "seq"), axis=0, tiled=True),
        lax.all_gather(w_router, ("dp", "seq"), axis=0, tiled=True),
        lax.all_gather(gain_attn, ("dp", "seq"), axis=0, tiled=True),
        lax.all_gather(gain_query, ("dp", "seq"), axis=0, tiled=True),
        lax.all_gather(gain_key, ("dp", "seq"), axis=0, tiled=True),
        lax.all_gather(gain_ffn, ("dp", "seq"), axis=0, tiled=True),
    )
    expert_full = (
        lax.all_gather(w_gate, "dp", axis=1, tiled=True),
        lax.all_gather(w_up, "dp", axis=1, tiled=True),
        lax.all_gather(w_down, "dp", axis=2, tiled=True),
    )
    projected = project_front(hidden, layer_full, positions)
    keys_all, values_all = (
        lax.all_gather(projected[4], "seq", axis=0, tiled=True),
        lax.all_gather(projected[5], "seq", axis=0, tiled=True),
    )
    attention, log_total = attend_local(projected[3], keys_all, values_all, row_seg, offset, span)
    attended = attention.reshape(tokens, model_width).astype(jnp.bfloat16)
    hidden_mid = hidden + jnp.dot(attended, layer_full[3], preferred_element_type=jnp.float32)
    routing = route_tokens(hidden_mid, layer_full, choice_rows)
    normed_ffn, chances, picks, gate_values, slot_ids, pair_table, spread, send_rows = routing
    grad_out = cotangent[0].astype(jnp.float32)
    grad_gates = jnp.sum(grad_out[:, None, :] * picked.astype(jnp.float32), axis=-1)
    slot_gates = jnp.sum(jnp.where(pair_table, gate_values.reshape(-1)[None, :], 0.0), axis=1)
    grad_rows_in = jnp.dot(spread, cotangent[0], preferred_element_type=jnp.float32)
    grad_slots = (
        (slot_gates[:, None] * grad_rows_in)
        .astype(jnp.bfloat16)
        .reshape(expert_count, capacity, model_width)
    )
    arrived_rows, arrived_grads = (
        lax.all_to_all(send_rows, "seq", split_axis=0, concat_axis=0, tiled=True),
        lax.all_to_all(grad_slots, "seq", split_axis=0, concat_axis=0, tiled=True),
    )
    grad_inputs, grad_gate_w, grad_up_w, grad_down_w = expert_backward(
        arrived_rows, arrived_grads, expert_full[0], expert_full[1], expert_full[2]
    )
    grad_back = lax.all_to_all(grad_inputs, "seq", split_axis=0, concat_axis=0, tiled=True)
    grad_normed_ffn = contract_rows(spread, grad_back.reshape(expert_count * capacity, model_width))
    grad_chances = jnp.sum(jnp.where(picks, grad_gates[:, :, None], 0.0), axis=1)
    grad_logits = (
        chances * (grad_chances - jnp.sum(chances * grad_chances, axis=-1, keepdims=True))
    ).astype(jnp.bfloat16)
    grad_router_w = contract_rows(normed_ffn, grad_logits)
    grad_normed_ffn = grad_normed_ffn + contract_cols(grad_logits, layer_full[4])
    unused_ffn, pull_ffn = jax.vjp(normalize, hidden_mid, layer_full[8].astype(jnp.float32))
    grad_mid_norm, grad_gain_ffn_w = pull_ffn(grad_normed_ffn)
    grad_mid = grad_out + grad_mid_norm
    grad_mid_low = grad_mid.astype(jnp.bfloat16)
    grad_w_out = contract_rows(attended, grad_mid_low)
    grad_attended = (
        contract_cols(grad_mid_low, layer_full[3])
        .astype(jnp.bfloat16)
        .reshape(tokens, head_count, HEAD)
    )
    query_rot = projected[3]
    delta, grad_query_rot = query_grads(
        query_rot, keys_all, values_all, row_seg, offset, span, log_total, grad_attended
    )
    scaling = HEAD ** (-0.5)
    query_seg = lax.dynamic_slice_in_dim(row_seg, offset, tokens)
    row_count = lax.axis_size("seq") * tokens
    step_rows = math.gcd(row_count, 512)

    def one_window(window_index, running):
        window_start = window_index * step_rows
        key_block, value_block, key_pos, key_seg = key_window(
            keys_all, values_all, row_seg, window_start, step_rows
        )
        scores = masked_scores(
            query_rot, key_block, positions, query_seg, key_pos, key_seg, scaling
        )
        weights = jnp.exp(scores - log_total[..., None])
        grad_weights = jnp.einsum(
            "qhd,khd->hqk", grad_attended, value_block, preferred_element_type=jnp.float32
        )
        grad_scores = (weights * (grad_weights - delta[..., None]) * scaling).astype(jnp.bfloat16)
        grad_key_part = jnp.einsum(
            "hqk,qhd->khd", grad_scores, query_rot, preferred_element_type=jnp.float32
        )
        grad_value_part = jnp.einsum(
            "hqk,qhd->khd",
            weights.astype(jnp.bfloat16),
            grad_attended,
            preferred_element_type=jnp.float32,
        )
        term = jnp.concatenate(
            [
                grad_key_part.reshape(step_rows, model_width),
                grad_value_part.reshape(step_rows, model_width),
            ],
            axis=1,
        )
        return lax.dynamic_update_slice_in_dim(running, term, window_index * step_rows, 0)

    key_sums = lax.psum_scatter(
        lax.fori_loop(
            0,
            row_count // step_rows,
            one_window,
            jnp.zeros((row_count, 2 * model_width), jnp.float32),
        ).astype(jnp.bfloat16),
        "seq",
        scatter_dimension=0,
        tiled=True,
    ).astype(jnp.float32)
    grad_key_rot = key_sums[:, :model_width].reshape(tokens, head_count, HEAD)
    grad_v_low = key_sums[:, model_width:].astype(jnp.bfloat16)

    def query_chain(projection, gain_vec):
        return rotate_normed(projection, gain_vec, positions)

    unused_query, pull_query = jax.vjp(query_chain, projected[1], layer_full[6].astype(jnp.float32))
    grad_query_pre, grad_gain_query_w = pull_query(grad_query_rot)
    unused_key, pull_key = jax.vjp(query_chain, projected[2], layer_full[7].astype(jnp.float32))
    grad_key_pre, grad_gain_key_w = pull_key(grad_key_rot)
    grad_q_low = grad_query_pre.astype(jnp.bfloat16)
    grad_k_low = grad_key_pre.astype(jnp.bfloat16)
    normed = projected[0]
    grad_w_query = contract_rows(normed, grad_q_low)
    grad_w_key = contract_rows(normed, grad_k_low)
    grad_w_value = contract_rows(normed, grad_v_low)
    grad_normed = (
        contract_cols(grad_q_low, layer_full[0])
        + contract_cols(grad_k_low, layer_full[1])
        + contract_cols(grad_v_low, layer_full[2])
    )
    unused_attn, pull_attn = jax.vjp(normalize, hidden, layer_full[5].astype(jnp.float32))
    grad_hidden_norm, grad_gain_attn_w = pull_attn(grad_normed)
    grad_hidden = grad_mid + grad_hidden_norm
    shares = (
        lax.psum_scatter(grad_w_query, ("dp", "seq"), scatter_dimension=0, tiled=True),
        lax.psum_scatter(grad_w_key, ("dp", "seq"), scatter_dimension=0, tiled=True),
        lax.psum_scatter(grad_w_value, ("dp", "seq"), scatter_dimension=0, tiled=True),
        lax.psum_scatter(grad_w_out, ("dp", "seq"), scatter_dimension=0, tiled=True),
        lax.psum_scatter(grad_router_w, ("dp", "seq"), scatter_dimension=0, tiled=True),
        lax.psum_scatter(grad_gain_attn_w, ("dp", "seq"), scatter_dimension=0, tiled=True),
        lax.psum_scatter(grad_gain_query_w, ("dp", "seq"), scatter_dimension=0, tiled=True),
        lax.psum_scatter(grad_gain_key_w, ("dp", "seq"), scatter_dimension=0, tiled=True),
        lax.psum_scatter(grad_gain_ffn_w, ("dp", "seq"), scatter_dimension=0, tiled=True),
    )
    expert_shares = (
        lax.psum_scatter(
            grad_gate_w.astype(jnp.bfloat16), "dp", scatter_dimension=1, tiled=True
        ).astype(jnp.float32),
        lax.psum_scatter(
            grad_up_w.astype(jnp.bfloat16), "dp", scatter_dimension=1, tiled=True
        ).astype(jnp.float32),
        lax.psum_scatter(
            grad_down_w.astype(jnp.bfloat16), "dp", scatter_dimension=2, tiled=True
        ).astype(jnp.float32),
    )
    return (
        block_out[None],
        grad_hidden[None],
        shares[0],
        shares[1],
        shares[2],
        shares[3],
        shares[5],
        shares[6],
        shares[7],
        shares[8],
        shares[4],
        expert_shares[0],
        expert_shares[1],
        expert_shares[2],
    )


VMEM_GRANT = 56 * 1024 * 1024


def mm(left, right, dims):
    return lax.dot_general(left, right, (dims, ((), ())), preferred_element_type=jnp.float32)


def cost(flops, transcendentals, *arrays):
    moved = sum(math.prod(a.shape) * a.dtype.itemsize for a in arrays)
    return pl.CostEstimate(
        flops=flops // 4, transcendentals=transcendentals // 4, bytes_accessed=moved // 4
    )


def grid_call(body, grid, in_specs, out_specs, outs, flops, transcendentals, *args):
    return pl.pallas_call(
        body,
        grid=grid,
        in_specs=in_specs,
        out_specs=out_specs,
        out_shape=outs,
        compiler_params=pltpu.CompilerParams(vmem_limit_bytes=VMEM_GRANT),
        cost_estimate=cost(flops, transcendentals, *args, *jax.tree.leaves(outs)),
    )(*args)


def row_tiles(rows):
    return math.gcd(rows, 512)


def finish_attention(order, attended, out_pieces, x_row, gain, router, chosen, own, expert_count):
    shards, rows, cols = attended.shape
    width = x_row.shape[1]
    held = own.shape[0]
    chunk = width // 4
    per_chunk = chunk // cols
    tm = math.gcd(rows, 256)

    def body(order_ref, att_ref, p0, p1, p2, p3, x_ref, gain_ref, router_ref, chosen_ref, own_ref, *outs):
        mid_ref, normed_ref, r_ref, chance_ref, gate_ref, att_all = outs
        for h in range(shards):
            source = order_ref[h // per_chunk] * per_chunk + h % per_chunk
            att_all[:, h * cols : (h + 1) * cols] = att_ref[source]
        squares = jnp.zeros((tm, 1), jnp.float32)
        for n in range(4):
            at = slice(n * chunk, (n + 1) * chunk)
            total = x_ref[:, at].astype(jnp.float32)
            for j, piece in enumerate((p0, p1, p2, p3)):
                k = n ^ j
                total = total + mm(
                    att_all[:, j * chunk : (j + 1) * chunk],
                    piece[:, k * chunk : (k + 1) * chunk],
                    ((1,), (0,)),
                )
            mid_ref[:, at] = total
            squares = squares + jnp.sum(total * total, axis=-1, keepdims=True)
        r = lax.rsqrt(squares / width + epsilon)
        r_ref[...] = r
        logits = jnp.zeros((tm, 128), jnp.float32)
        for n in range(4):
            at = slice(n * chunk, (n + 1) * chunk)
            normed = (mid_ref[:, at] * r * gain_ref[:, at]).astype(jnp.bfloat16)
            normed_ref[:, at] = normed
            logits = logits + mm(normed, router_ref[at, :], ((1,), (0,)))
        lane = lax.broadcasted_iota(jnp.int32, (tm, 128), 1)
        logits = jnp.where(lane < expert_count, logits, masked_score)
        raised = jnp.exp(logits - jnp.max(logits, axis=-1, keepdims=True))
        chances = raised / jnp.sum(raised, axis=-1, keepdims=True)
        chance_ref[...] = chances
        taken = chances * chosen_ref[...]
        for e in range(held):
            gate_ref[e] = jnp.sum(taken * own_ref[e : e + 1, :], axis=-1, keepdims=True)

    full = jnp.float32
    piece_spec = pl.BlockSpec((chunk, width), lambda i, o: (0, 0))
    wide = pl.BlockSpec((tm, width), lambda i, o: (i, 0))
    lanes = pl.BlockSpec((tm, 128), lambda i, o: (i, 0))
    outs = [
        jax.ShapeDtypeStruct((rows, width), full),
        jax.ShapeDtypeStruct((rows, width), jnp.bfloat16),
        jax.ShapeDtypeStruct((rows, 1), full),
        jax.ShapeDtypeStruct((rows, 128), full),
        jax.ShapeDtypeStruct((held, rows, 1), full),
    ]
    return pl.pallas_call(
        body,
        grid_spec=pltpu.PrefetchScalarGridSpec(
            num_scalar_prefetch=1,
            grid=(rows // tm,),
            in_specs=[
                pl.BlockSpec((shards, tm, cols), lambda i, o: (0, i, 0)),
                piece_spec,
                piece_spec,
                piece_spec,
                piece_spec,
                wide,
                pl.BlockSpec((1, width), lambda i, o: (0, 0)),
                pl.BlockSpec((width, 128), lambda i, o: (0, 0)),
                lanes,
                pl.BlockSpec((held, 128), lambda i, o: (0, 0)),
            ],
            out_specs=[
                wide,
                wide,
                pl.BlockSpec((tm, 1), lambda i, o: (i, 0)),
                lanes,
                pl.BlockSpec((held, tm, 1), lambda i, o: (0, i, 0)),
            ],
            scratch_shapes=[pltpu.VMEM((tm, width), jnp.bfloat16)],
        ),
        out_shape=outs,
        compiler_params=pltpu.CompilerParams(vmem_limit_bytes=VMEM_GRANT),
        cost_estimate=cost(2 * rows * width * width, rows * 128, attended, *out_pieces, *outs),
    )(order, attended, *out_pieces, x_row, gain, router, chosen, own)


def expert_activations(normed, gate, up):
    held, width, ff = gate.shape
    rows = normed.shape[0]
    tile, tm = (math.gcd(ff, 512), row_tiles(rows))

    def body(x_ref, gate_ref, up_ref, act_ref, dgate_ref, dup_ref):
        @pl.loop(0, rows // tm)
        def _(i):
            at = pl.ds(pl.multiple_of(i * tm, tm), tm)
            gate_pre = mm(x_ref[at, :], gate_ref[0], ((1,), (0,)))
            up_pre = mm(x_ref[at, :], up_ref[0], ((1,), (0,)))
            sig = lax.logistic(gate_pre)
            silu = gate_pre * sig
            act_ref[0, at, :] = (silu * up_pre).astype(jnp.bfloat16)
            dgate_ref[0, at, :] = (up_pre * (sig + silu * (1.0 - sig))).astype(jnp.bfloat16)
            dup_ref[0, at, :] = silu.astype(jnp.bfloat16)

    tiled = pl.BlockSpec((1, rows, tile), lambda e, f: (e, 0, f))
    low = jax.ShapeDtypeStruct((held, rows, ff), jnp.bfloat16)
    return grid_call(
        body,
        (held, ff // tile),
        [
            pl.BlockSpec((rows, width), lambda e, f: (0, 0)),
            pl.BlockSpec((1, width, tile), lambda e, f: (e, 0, f)),
            pl.BlockSpec((1, width, tile), lambda e, f: (e, 0, f)),
        ],
        [tiled, tiled, tiled],
        [low, low, low],
        4 * held * rows * ff * width,
        held * rows * ff,
        normed,
        gate,
        up,
    )


def expert_gradients(dy, down, act, dgate_factor, dup_factor, weight):
    held, ff, width = down.shape
    rows = dy.shape[0]
    tile, tm = (math.gcd(ff, 512), row_tiles(rows))

    def body(dy_ref, down_ref, act_ref, a_ref, b_ref, weight_ref, out_ref, dgate_ref, dup_ref, sum_ref):
        first = pl.program_id(1) == 0

        @pl.loop(0, rows // tm, unroll=True)
        def _(i):
            at = pl.ds(pl.multiple_of(i * tm, tm), tm)
            grad = mm(dy_ref[at, :], down_ref[0], ((1,), (1,)))
            scale = weight_ref[0, at, :]
            act = act_ref[0, at, :].astype(jnp.float32)
            product = act * grad
            partial = product[:, :128]
            for j in range(1, tile // 128):
                partial = partial + product[:, j * 128 : (j + 1) * 128]

            @pl.when(first)
            def _():
                sum_ref[0, at, :] = partial

            @pl.when(jnp.logical_not(first))
            def _():
                sum_ref[0, at, :] = sum_ref[0, at, :] + partial

            out_ref[0, at, :] = (scale * act).astype(jnp.bfloat16)
            grad = scale * grad
            dgate_ref[0, at, :] = (grad * a_ref[0, at, :].astype(jnp.float32)).astype(jnp.bfloat16)
            dup_ref[0, at, :] = (grad * b_ref[0, at, :].astype(jnp.float32)).astype(jnp.bfloat16)

    tiled = pl.BlockSpec((1, rows, tile), lambda e, f: (e, 0, f))
    low = jax.ShapeDtypeStruct((held, rows, ff), jnp.bfloat16)
    return grid_call(
        body,
        (held, ff // tile),
        [
            pl.BlockSpec((rows, width), lambda e, f: (0, 0)),
            pl.BlockSpec((1, tile, width), lambda e, f: (e, f, 0)),
            tiled,
            tiled,
            tiled,
            pl.BlockSpec((1, rows, 1), lambda e, f: (e, 0, 0)),
        ],
        [tiled, tiled, tiled, pl.BlockSpec((1, rows, 128), lambda e, f: (e, 0, 0))],
        [low, low, low, jax.ShapeDtypeStruct((held, rows, 128), jnp.float32)],
        2 * held * rows * ff * width,
        0,
        dy,
        down,
        act,
        dgate_factor,
        dup_factor,
        weight,
    )


def input_gradient(dgate, dup, gate, up, gate_sums, chances, chosen, own, router):
    held, width, ff = gate.shape
    rows = dgate.shape[1]
    tile, tm = (math.gcd(width, 512), row_tiles(rows))

    def body(dgate_ref, dup_ref, gate_ref, up_ref, sum_ref, chance_ref, chosen_ref, own_ref, router_ref, out_ref, logits_ref):
        @pl.loop(0, rows // tm, unroll=True)
        def _(i):
            at = pl.ds(pl.multiple_of(i * tm, tm), tm)
            chances = chance_ref[at, :]
            placed = jnp.zeros((tm, 128), jnp.float32)
            for e in range(held):
                got = jnp.sum(sum_ref[e, at, :], axis=-1, keepdims=True)
                placed = placed + own_ref[e : e + 1, :] * got
            placed = placed * chosen_ref[at, :]
            inner = jnp.sum(chances * placed, axis=-1, keepdims=True)
            logits = (chances * (placed - inner)).astype(jnp.bfloat16)
            logits_ref[at, :] = logits
            total = mm(logits, router_ref[...], ((1,), (1,)))
            for e in range(held):
                total = total + mm(dgate_ref[e, at, :], gate_ref[e], ((1,), (1,)))
                total = total + mm(dup_ref[e, at, :], up_ref[e], ((1,), (1,)))
            out_ref[at, :] = total.astype(jnp.bfloat16)

    whole = pl.BlockSpec((held, rows, ff), lambda n: (0, 0, 0))
    weights = pl.BlockSpec((held, tile, ff), lambda n: (0, n, 0))
    lanes = pl.BlockSpec((rows, 128), lambda n: (0, 0))
    return grid_call(
        body,
        (width // tile,),
        [
            whole,
            whole,
            weights,
            weights,
            pl.BlockSpec((held, rows, 128), lambda n: (0, 0, 0)),
            lanes,
            lanes,
            pl.BlockSpec((held, 128), lambda n: (0, 0)),
            pl.BlockSpec((tile, 128), lambda n: (n, 0)),
        ],
        [pl.BlockSpec((rows, tile), lambda n: (0, n)), lanes],
        [jax.ShapeDtypeStruct((rows, width), jnp.bfloat16), jax.ShapeDtypeStruct((rows, 128), jnp.bfloat16)],
        4 * held * rows * ff * width,
        0,
        dgate,
        dup,
        gate,
        up,
        gate_sums,
        chances,
        chosen,
        own,
        router,
    )


def combine_experts(y_at, act, down, weight):
    held, ff, width = down.shape
    rows = act.shape[1]
    block = rows // 8
    tile, tm = (math.gcd(width, 512), 4 * block)

    def body(y_ref, act_ref, down_ref, weight_ref, near_ref, far_ref):
        for i in range(2):
            at = slice(i * tm, (i + 1) * tm)
            total = weight_ref[0, at, :] * mm(act_ref[0, at, :], down_ref[0], ((1,), (0,)))
            for e in range(1, held):
                term = mm(act_ref[e, at, :], down_ref[e], ((1,), (0,)))
                total = total + weight_ref[e, at, :] * term
            total = total.astype(jnp.bfloat16)
            for y, outs in ((0, (near_ref, far_ref)), (1, (far_ref, near_ref))):

                @pl.when(y_ref[0] == y)
                def _(outs=outs):
                    for j in range(4):
                        to = (2 * i + j // 2) * block
                        outs[j % 2][to : to + block, :] = total[j * block : (j + 1) * block]

    half = jax.ShapeDtypeStruct((rows // 2, width), jnp.bfloat16)
    tiled = pl.BlockSpec((rows // 2, tile), lambda n, y: (0, n))
    return pl.pallas_call(
        body,
        grid_spec=pltpu.PrefetchScalarGridSpec(
            num_scalar_prefetch=1,
            grid=(width // tile,),
            in_specs=[
                pl.BlockSpec((held, rows, ff), lambda n, y: (0, 0, 0)),
                pl.BlockSpec((held, ff, tile), lambda n, y: (0, 0, n)),
                pl.BlockSpec((held, rows, 1), lambda n, y: (0, 0, 0)),
            ],
            out_specs=[tiled, tiled],
        ),
        out_shape=[half, half],
        compiler_params=pltpu.CompilerParams(vmem_limit_bytes=VMEM_GRANT),
        cost_estimate=cost(2 * held * rows * ff * width, 0, act, down, half, half),
    )(y_at, act, down, weight)


def weight_pieces(left, right, parts, split_left):
    flat, stacked = (left, right) if split_left else (right, left)
    held, rows, ff = stacked.shape
    piece = flat.shape[1] // parts
    shape = (held, piece, ff) if split_left else (held, ff, piece)
    tm = math.gcd(shape[1], 512)

    def body(flat_ref, stacked_ref, *outs):
        step = pl.program_id(0)
        for j in range(parts):

            @pl.when(step == j)
            def _(j=j):
                @pl.loop(0, shape[1] // tm)
                def _(i):
                    at = pl.ds(pl.multiple_of(i * tm, tm), tm)
                    if split_left:
                        value = mm(flat_ref[:, at], stacked_ref[0], ((0,), (0,)))
                    else:
                        value = mm(stacked_ref[0, :, at], flat_ref[...], ((0,), (0,)))
                    outs[j][0, at, :] = value.astype(jnp.bfloat16)

    def place(j):
        return lambda k, e: (jnp.where(k < j, 0, jnp.where(k > j, held - 1, e)), 0, 0)

    return grid_call(
        body,
        (parts, held),
        [
            pl.BlockSpec((rows, piece), lambda k, e: (0, k)),
            pl.BlockSpec((1, rows, ff), lambda k, e: (e, 0, 0)),
        ],
        [pl.BlockSpec((1,) + shape[1:], place(j)) for j in range(parts)],
        [jax.ShapeDtypeStruct(shape, jnp.bfloat16)] * parts,
        2 * held * rows * ff * flat.shape[1],
        0,
        flat,
        stacked,
    )


def rope_tables(row_count, head_dim):
    half_dim = head_dim // 2
    frequency = jnp.exp(
        jnp.arange(half_dim, dtype=jnp.float32) * (-2.0 * math.log(rope_base) / head_dim)
    )
    angles = jnp.arange(row_count, dtype=jnp.float32)[:, None] * frequency[None, :]
    cosine, sine = (jnp.cos(angles), jnp.sin(angles))
    return (
        jnp.concatenate([cosine, cosine], axis=1),
        jnp.concatenate([-sine, sine], axis=1),
    )


def seen(first, count, keys, seg_col, seg_row):
    position = first + lax.broadcasted_iota(jnp.int32, (count, keys), 0)
    other = lax.broadcasted_iota(jnp.int32, (count, keys), 1)
    return (position >= other) & (seg_col == seg_row)


def pair_rows(first, second):
    lane = lax.broadcasted_iota(jnp.int32, (first.shape[0], 128), 1)
    both = jnp.where(lane == 0, first, jnp.where(lane == 1, second, 0.0))
    return both.T[:8]


def pair_columns(sums):
    rows = [sum((s[i : i + 1] for s in sums[1:]), sums[0][i : i + 1]) for i in range(2)]
    wide = (128, rows[0].shape[1])
    first = lax.broadcasted_iota(jnp.int32, wide, 0) == 0
    both = jnp.where(first, jnp.broadcast_to(rows[0], wide), jnp.broadcast_to(rows[1], wide)).T
    return (both[:, 0:1], both[:, 1:2])


def project(x_row, gain, w_qkv):
    rows, width = x_row.shape
    held_cols = w_qkv.shape[1]
    cols = held_cols // 3
    tm = math.gcd(rows, 256)

    def body(x_ref, gain_ref, w_ref, normed_ref, qkv_ref, r_ref, stat_ref):
        x = x_ref[...].astype(jnp.float32)
        r = lax.rsqrt(jnp.mean(x * x, axis=-1, keepdims=True) + epsilon)
        r_ref[...] = r
        normed = (x * r * gain_ref[...]).astype(jnp.bfloat16)
        normed_ref[...] = normed
        qkv = mm(normed, w_ref[...], ((1,), (0,)))
        qkv_ref[...] = qkv
        squares = qkv[:, : 2 * cols] * qkv[:, : 2 * cols]
        stat_ref[...] = pair_rows(
            jnp.sum(squares[:, :cols], axis=-1, keepdims=True),
            jnp.sum(squares[:, cols:], axis=-1, keepdims=True),
        )

    full = jnp.float32
    return grid_call(
        body,
        (rows // tm,),
        [
            pl.BlockSpec((tm, width), lambda i: (i, 0)),
            pl.BlockSpec((1, width), lambda i: (0, 0)),
            pl.BlockSpec((width, held_cols), lambda i: (0, 0)),
        ],
        [
            pl.BlockSpec((tm, width), lambda i: (i, 0)),
            pl.BlockSpec((tm, held_cols), lambda i: (i, 0)),
            pl.BlockSpec((tm, 1), lambda i: (i, 0)),
            pl.BlockSpec((8, tm), lambda i: (0, i)),
        ],
        [
            jax.ShapeDtypeStruct((rows, width), jnp.bfloat16),
            jax.ShapeDtypeStruct((rows, held_cols), full),
            jax.ShapeDtypeStruct((rows, 1), full),
            jax.ShapeDtypeStruct((8, rows), full),
        ],
        2 * rows * width * held_cols,
        0,
        x_row,
        gain,
        w_qkv,
    )


def attend(qkv, sums, width, g_query, g_key, cosine, sine, seg_col, seg_row):
    rows, held_cols = qkv.shape
    cols = held_cols // 3
    heads = cols // HEAD
    tq = math.gcd(rows, 256)
    scaling = HEAD ** (-0.5)
    shards = sums.shape[0]

    def body(q, k, v, sums_ref, gq, gk, cos, sin, sc, sr, q_out, k_out, v_out, att_out, log_out, rq, rk):
        @pl.when(pl.program_id(0) == 0)
        def _():
            for i in range(rows // tq):
                at = slice(i * tq, (i + 1) * tq)
                first, second = pair_columns([sums_ref[d, :, at] for d in range(shards)])
                rq[at, :] = lax.rsqrt(first / width + epsilon)
                rk[at, :] = lax.rsqrt(second / width + epsilon)

        def rotated(ref, r, g):
            values = ref[...] * r[...] * g[...]
            swapped = pltpu.roll(values, HEAD // 2, 1)
            return (values * cos[...] + swapped * sin[...]).astype(jnp.bfloat16)

        q_out[...] = rotated(q, rq, gq)
        k_out[...] = rotated(k, rk, gk)
        v_out[...] = v[...].astype(jnp.bfloat16)
        for i in range(rows // tq):
            at, keys = (slice(i * tq, (i + 1) * tq), (i + 1) * tq)
            scores = mm(q_out[at, :], k_out[:keys, :], ((1,), (1,))) * scaling
            allowed = seen(i * tq, tq, keys, sc[at, :], sr[:, :keys])
            scores = jnp.where(allowed, scores, masked_score)
            peak = jnp.max(scores, axis=-1, keepdims=True)
            raised = jnp.exp(scores - peak)
            total = jnp.sum(raised, axis=-1, keepdims=True)
            log_out[0, at, :] = peak + jnp.log(total)
            weights = (raised * (1.0 / total)).astype(jnp.bfloat16)
            att_out[at, :] = mm(weights, v_out[:keys, :], ((1,), (0,))).astype(jnp.bfloat16)

    def col(offset):
        return pl.BlockSpec((rows, HEAD), lambda h: (0, offset + h))

    row = pl.BlockSpec((1, HEAD), lambda h: (0, h))
    one = pl.BlockSpec((rows, 1), lambda h: (0, 0))
    table = pl.BlockSpec((rows, HEAD), lambda h: (0, 0))
    low = jax.ShapeDtypeStruct((rows, cols), jnp.bfloat16)
    column = jax.ShapeDtypeStruct((rows, 1), jnp.float32)
    return grid_call(
        body,
        (heads,),
        [
            col(0),
            col(heads),
            col(2 * heads),
            pl.BlockSpec((shards, 2, rows), lambda h: (0, 0, 0)),
            row,
            row,
            table,
            table,
            one,
            pl.BlockSpec((1, rows), lambda h: (0, 0)),
        ],
        [col(0)] * 4 + [pl.BlockSpec((1, rows, 1), lambda h: (h, 0, 0)), one, one],
        [low] * 4 + [jax.ShapeDtypeStruct((heads, rows, 1), jnp.float32), column, column],
        4 * heads * rows * rows * HEAD,
        heads * rows * rows,
        qkv,
        qkv,
        qkv,
        sums,
        g_query,
        g_key,
        cosine,
        sine,
        seg_col,
        seg_row,
    )


def attend_back(qkv, q_rot, k_rot, value_in, grad, log_total, r_query, r_key, g_query, g_key, cosine, sine, seg_col, seg_row):
    rows, cols = q_rot.shape
    heads = cols // HEAD
    tq = math.gcd(rows, 256)
    scaling = HEAD ** (-0.5)

    def body(q, k, qr, kr, v, ga, lt, rq, rk, gq, gk, cos, sin, sc, sr, q_out, k_out, v_out, stat_out, gq_out, gk_out, q_sum, k_sum, v_sum, stats):
        k_sum[...] = jnp.zeros_like(k_sum)
        v_sum[...] = jnp.zeros_like(v_sum)
        for i in range(rows // tq):
            at, keys = (slice(i * tq, (i + 1) * tq), (i + 1) * tq)
            scores = mm(qr[at, :], kr[:keys, :], ((1,), (1,))) * scaling
            allowed = seen(i * tq, tq, keys, sc[at, :], sr[:, :keys])
            p = jnp.exp(jnp.where(allowed, scores, masked_score) - lt[0, at, :])
            grad_weights = mm(ga[at, :], v[:keys, :], ((1,), (1,)))
            delta = jnp.sum(p * grad_weights, axis=-1, keepdims=True)
            grad_scores = (scaling * p * (grad_weights - delta)).astype(jnp.bfloat16)
            q_sum[at, :] = mm(grad_scores, kr[:keys, :], ((1,), (0,)))
            k_sum[:keys, :] += mm(grad_scores, qr[at, :], ((0,), (0,)))
            v_sum[:keys, :] += mm(p.astype(jnp.bfloat16), ga[at, :], ((0,), (0,)))

        first = pl.program_id(0) == 0

        def back(total, ref, r, g, out, place, gain):
            values = total[...]
            values = values * cos[...] - pltpu.roll(values, HEAD // 2, 1) * sin[...]
            gain[...] = jnp.sum(values * ref[...] * r[...], axis=0, keepdims=True)
            values = values * g[...]
            stat = jnp.sum(values * ref[...], axis=-1, keepdims=True)
            stats[place] += stat
            out[...] = values

        @pl.when(first)
        def _():
            stats[...] = jnp.zeros_like(stats)

        back(q_sum, q, rq, gq, q_out, 0, gq_out)
        back(k_sum, k, rk, gk, k_out, 1, gk_out)

        @pl.when(pl.program_id(0) == heads - 1)
        def _():
            for i in range(rows // tq):
                at = slice(i * tq, (i + 1) * tq)
                stat_out[:, at] = pair_rows(stats[0, at, :], stats[1, at, :])

        v_out[...] = v_sum[...].astype(jnp.bfloat16)

    def col(offset):
        return pl.BlockSpec((rows, HEAD), lambda h: (0, offset + h))

    row = pl.BlockSpec((1, HEAD), lambda h: (0, h))
    one = pl.BlockSpec((rows, 1), lambda h: (0, 0))
    stat = pl.BlockSpec((1, rows, 1), lambda h: (h, 0, 0))
    table = pl.BlockSpec((rows, HEAD), lambda h: (0, 0))
    full = jnp.float32
    outs = (
        [jax.ShapeDtypeStruct((rows, cols), full)] * 2
        + [jax.ShapeDtypeStruct((rows, cols), jnp.bfloat16)]
        + [jax.ShapeDtypeStruct((8, rows), full)]
        + [jax.ShapeDtypeStruct((1, cols), full)] * 2
    )
    args = (qkv, qkv, q_rot, k_rot, value_in, grad, log_total, r_query, r_key, g_query, g_key, cosine, sine, seg_col, seg_row)
    return pl.pallas_call(
        body,
        grid=(heads,),
        in_specs=[col(0), col(heads), col(0), col(0), col(0), col(0), stat, one, one, row, row, table, table, one,
                  pl.BlockSpec((1, rows), lambda h: (0, 0))],
        out_specs=[col(0), col(0), col(0), pl.BlockSpec((8, rows), lambda h: (0, 0)), row, row],
        out_shape=outs,
        scratch_shapes=[pltpu.VMEM((rows, HEAD), full)] * 3 + [pltpu.VMEM((2, rows, 1), full)],
        compiler_params=pltpu.CompilerParams(vmem_limit_bytes=VMEM_GRANT),
        cost_estimate=cost(10 * heads * rows * rows * HEAD, heads * rows * rows, *args, *outs),
    )(*args)


def normed_gradient(q_grad, k_grad, v_low, qkv, sums, r_query, r_key, w_qkv, x_row, r_attn):
    rows, cols = q_grad.shape
    width = x_row.shape[1]
    shards = sums.shape[0]
    tm = math.gcd(rows, 256)

    def body(qg, kg, v, q, k, sums_ref, rq, rk, w, x, ra, low_ref, out_ref, gain_ref):
        means = pair_columns([sums_ref[d] for d in range(shards)])
        parts = []
        for grad, ref, r_ref, mean in ((qg, q, rq, means[0]), (kg, k, rk, means[1])):
            r = r_ref[...]
            part = r * grad[...] - ref[...] * (r * r * r) * (mean / width)
            parts.append(part.astype(jnp.bfloat16))
        parts.append(v[...])
        for i in range(3):
            low_ref[:, i * cols : (i + 1) * cols] = parts[i]
        total = mm(low_ref[...], w[...], ((1,), (1,)))
        out_ref[...] = total.astype(jnp.bfloat16)
        gain = jnp.sum(total * x[...].astype(jnp.float32) * ra[...], axis=0, keepdims=True)
        first = pl.program_id(0) == 0

        @pl.when(first)
        def _():
            gain_ref[...] = gain

        @pl.when(jnp.logical_not(first))
        def _():
            gain_ref[...] += gain

    def tiled(count, at=0):
        return pl.BlockSpec((tm, count), lambda i: (i, at))

    return grid_call(
        body,
        (rows // tm,),
        [
            tiled(cols),
            tiled(cols),
            tiled(cols),
            tiled(cols),
            tiled(cols, 1),
            pl.BlockSpec((shards, 2, tm), lambda i: (0, 0, i)),
            tiled(1),
            tiled(1),
            pl.BlockSpec((width, 3 * cols), lambda i: (0, 0)),
            tiled(width),
            tiled(1),
        ],
        [tiled(3 * cols), tiled(width), pl.BlockSpec((1, width), lambda i: (0, 0))],
        [
            jax.ShapeDtypeStruct((rows, 3 * cols), jnp.bfloat16),
            jax.ShapeDtypeStruct((rows, width), jnp.bfloat16),
            jax.ShapeDtypeStruct((1, width), jnp.float32),
        ],
        6 * rows * width * cols,
        0,
        q_grad,
        k_grad,
        v_low,
        qkv,
        qkv,
        sums,
        r_query,
        r_key,
        w_qkv,
        x_row,
        r_attn,
    )


def middle(order, nf_own, mid, r_ffn, gain, dy, out_pieces):
    tokens, width = nf_own.shape
    chunk = width // 4

    def body(order_ref, nf, mid_ref, r_ref, gain_ref, dy_ref, p0, p1, p2, p3, grad_ref, low_ref, att_ref, gain_out):
        r = r_ref[...]
        own = mid_ref[...]
        grad = nf[...].astype(jnp.float32)
        gain_out[...] = jnp.sum(grad * own * r, axis=0, keepdims=True)
        grad = grad * gain_ref[...]
        mean = jnp.mean(grad * own, axis=-1, keepdims=True)
        total = dy_ref[...].astype(jnp.float32) + r * grad - own * (r * r * r) * mean
        grad_ref[...] = total
        low_ref[...] = total.astype(jnp.bfloat16)
        for j, piece in enumerate((p0, p1, p2, p3)):
            back = jnp.zeros((tokens, chunk), jnp.float32)
            for k in range(4):
                n = k ^ j
                back = back + mm(
                    low_ref[:, n * chunk : (n + 1) * chunk],
                    piece[:, k * chunk : (k + 1) * chunk],
                    ((1,), (1,)),
                )
            att_ref[order_ref[j]] = back.astype(jnp.bfloat16)

    def whole(*shape):
        return pl.BlockSpec(shape, lambda i, o: (0,) * len(shape))

    outs = [
        jax.ShapeDtypeStruct((tokens, width), jnp.float32),
        jax.ShapeDtypeStruct((tokens, width), jnp.bfloat16),
        jax.ShapeDtypeStruct((4, tokens, chunk), jnp.bfloat16),
        jax.ShapeDtypeStruct((1, width), jnp.float32),
    ]
    return pl.pallas_call(
        body,
        grid_spec=pltpu.PrefetchScalarGridSpec(
            num_scalar_prefetch=1,
            grid=(1,),
            in_specs=[
                whole(tokens, width),
                pl.BlockSpec((tokens, width), lambda i, o: (o[4], 0)),
                pl.BlockSpec((tokens, 1), lambda i, o: (o[4], 0)),
                whole(1, width),
                whole(tokens, width),
                *[whole(chunk, width)] * 4,
            ],
            out_specs=[whole(*o.shape) for o in outs],
        ),
        out_shape=outs,
        compiler_params=pltpu.CompilerParams(vmem_limit_bytes=VMEM_GRANT),
        cost_estimate=cost(2 * tokens * width * width, 0, *out_pieces, *outs),
    )(order, nf_own, mid, r_ffn, gain, dy, *out_pieces)


def out_grad_pieces(order, attended, columns):
    shards, rows, cols = attended.shape
    per_chunk = shards // 4
    count = columns.shape[1]
    tm = math.gcd(cols, 256)

    def body(order_ref, att_ref, col_ref, *outs):
        step = pl.program_id(0)
        for j in range(4):

            @pl.when(step == j)
            def _(j=j):
                outs[j][...] = mm(att_ref[0], col_ref[...], ((0,), (0,))).astype(jnp.bfloat16)

    def place(j):
        return lambda k, i, o: (jnp.where(k < j, 0, jnp.where(k > j, per_chunk - 1, i)), 0)

    outs = [jax.ShapeDtypeStruct((per_chunk * cols, count), jnp.bfloat16)] * 4
    return pl.pallas_call(
        body,
        grid_spec=pltpu.PrefetchScalarGridSpec(
            num_scalar_prefetch=1,
            grid=(4, per_chunk),
            in_specs=[
                pl.BlockSpec((1, rows, cols), lambda k, i, o: (o[k] * per_chunk + i, 0, 0)),
                pl.BlockSpec((rows, count), lambda k, i, o: (0, 0)),
            ],
            out_specs=[pl.BlockSpec((cols, count), place(j)) for j in range(4)],
        ),
        out_shape=outs,
        compiler_params=pltpu.CompilerParams(vmem_limit_bytes=VMEM_GRANT),
        cost_estimate=cost(2 * rows * shards * cols * count, 0, attended, columns, *outs),
    )(order, attended, columns)


def over_y(values):
    return lax.ppermute(values, "seq", [(i, i ^ 1) for i in range(8)])


def along_z(values):
    lines = [[0, 2, 4, 6], [1, 3, 5, 7]]
    return lax.all_gather(values, "seq", axis=0, tiled=False, axis_index_groups=lines)


def both_y(line, other):
    y = lax.axis_index("seq") % 2
    row = jnp.zeros((4, 2) + line.shape[1:], line.dtype)
    for blocks, at in ((line, y), (other, 1 - y)):
        row = lax.dynamic_update_slice(row, blocks[:, None], (0, at) + (0,) * (line.ndim - 1))
    return row.reshape((8,) + line.shape[1:])


def sum_along_z(values):
    lines = [[0, 2, 4, 6], [1, 3, 5, 7]]
    return lax.psum_scatter(
        values, "seq", scatter_dimension=0, tiled=True, axis_index_groups=lines
    )


def swap(values, bits):
    return lax.ppermute(values, "dp", [(i, i ^ bits) for i in range(4)])


def sum_in_chip(pieces, sent):
    wide = jnp.float32
    kept = pieces[0].astype(wide) + swap(pieces[1], 1).astype(wide)
    return (kept.astype(sent), (pieces[2].astype(wide) + swap(pieces[3], 1).astype(wide)).astype(sent))


def sum_experts_in_chip(pieces):
    wide, low = (jnp.float32, jnp.bfloat16)
    arrived = swap(pieces[3], 1)
    kept = pieces[0].astype(wide) + swap(pieces[1], 1).astype(wide)
    passed = [
        (pieces[2][e].astype(wide) + arrived[e].astype(wide)).astype(low)
        for e in range(arrived.shape[0])
    ]
    return (kept.astype(low), passed)


def across_by_expert(passed):
    return [swap(p, 2) for p in passed]


def add_arrived(kept, arrived):
    return jnp.stack(
        [kept[e].astype(jnp.float32) + a.astype(jnp.float32) for e, a in enumerate(arrived)]
    )


def sum_pieces(pieces, sent):
    kept, passed = sum_in_chip(pieces, sent)
    return kept.astype(jnp.float32) + swap(passed, 2).astype(jnp.float32)


def reorder(values, dp_index, axis):
    size = values.shape[axis] // 4
    return jnp.concatenate(
        [
            lax.dynamic_slice_in_dim(values, (dp_index ^ k) * size, size, axis=axis)
            for k in range(4)
        ],
        axis=axis,
    )


def on_device_heads(
    hidden_in,
    segment_ids,
    routes,
    w_query,
    w_key,
    w_value,
    w_out,
    gain_attn,
    gain_query,
    gain_key,
    gain_ffn,
    w_router,
    w_gate,
    w_up,
    w_down,
    cotangent,
):
    low, full = (jnp.bfloat16, jnp.float32)
    shards = lax.axis_size("seq")
    seq_index, dp_index = (lax.axis_index("seq"), lax.axis_index("dp"))
    tokens, width = hidden_in.shape[1:]
    rows = shards * tokens
    cols = width // shards
    heads = cols // HEAD
    held = w_gate.shape[0]
    expert_count = held * shards
    block_rows = w_query.shape[0]
    chunk = shards * block_rows
    row_seg = segment_ids[0]
    first_row = seq_index * tokens
    barrier = lax.optimization_barrier

    def own_cols(values, count):
        return lax.dynamic_slice_in_dim(values, seq_index * count, count, axis=values.ndim - 1)

    cosine, sine = rope_tables(rows, HEAD)
    seg_col, seg_row = (row_seg[:, None], row_seg[None, :])

    x_shard = reorder(hidden_in[0], dp_index, 1)
    x_row = lax.all_gather(x_shard, "seq", axis=0, tiled=True)
    blocks = jnp.stack(
        [w.reshape(block_rows, shards, cols).transpose(1, 0, 2) for w in (w_query, w_key, w_value)],
        axis=1,
    )
    blocks = blocks.reshape(shards, 3 * block_rows, cols)
    place_at = (dp_index * shards + seq_index) * block_rows
    gain_rows = lax.dynamic_update_slice(
        jnp.zeros((shards, 16, cols), low),
        jnp.stack([gain_query, gain_key])[None],
        (place_at // cols, 0, place_at % cols),
    )
    gain_rows = lax.dynamic_update_slice(
        gain_rows, jnp.broadcast_to(gain_attn[None, None], (shards, 1, block_rows)), (0, 2, 0)
    )
    blocks = lax.all_to_all(jnp.concatenate([blocks, gain_rows], axis=1), "seq", 0, 0, tiled=True)
    across = swap(blocks, 2)
    qkv_pieces = (blocks, swap(blocks, 1), across, swap(across, 1))
    gate_across = swap(w_gate, 2)
    w_qkv = jnp.concatenate(
        [
            p[:, : 3 * block_rows]
            .reshape(shards, 3, block_rows, cols)
            .transpose(0, 2, 1, 3)
            .reshape(chunk, 3 * cols)
            for p in qkv_pieces
        ],
        axis=0,
    )
    gain_rows = jnp.concatenate([p[:, 3 * block_rows :] for p in qkv_pieces], axis=0)
    gain_pair = jnp.sum(gain_rows[:, :2].astype(full), axis=0)
    g_query, g_key = (gain_pair[0:1], gain_pair[1:2])
    g_attn = gain_rows[:, 2, :block_rows].reshape(1, width).astype(full)
    gate_pieces = (w_gate, swap(w_gate, 1), gate_across, swap(gate_across, 1))
    x_row, w_qkv, g_query, g_key, g_attn, gate_pieces = barrier(
        (x_row, w_qkv, g_query, g_key, g_attn, gate_pieces)
    )

    picks = routes.shape[2]
    packed = tokens // block_rows
    extra = jnp.concatenate(
        [routes[0].astype(low).reshape(block_rows, packed * picks), w_router, gain_ffn[:, None]],
        axis=1,
    )
    extra = jnp.pad(extra, ((0, 0), (0, 128 - extra.shape[1])))
    out_line = along_z(jnp.concatenate([reorder(w_out, dp_index, 1), extra], axis=1))
    up_across = swap(w_up, 2)

    def share(sums):
        spread = jnp.broadcast_to(sums[None, :2], (shards, 2, rows))
        return lax.all_to_all(spread, "seq", 0, 0, tiled=True)

    normed, qkv, r_attn, sums = project(x_row, g_attn, w_qkv)
    q_rot, k_rot, value_in, attended, log_total, r_query, r_key = attend(
        qkv, share(sums), width, g_query, g_key, cosine, sine, seg_col, seg_row
    )
    attended, out_line, up_across = barrier((attended, out_line, up_across))

    attended_row = lax.all_gather(attended, "seq", axis=0)
    out_other, line_across = (over_y(out_line), swap(out_line, 2))
    gate_full = jnp.concatenate(gate_pieces, axis=1)
    up_full = jnp.concatenate([w_up, swap(w_up, 1), up_across, swap(up_across, 1)], axis=1)
    out_other, line_across, gate_full = barrier((out_other, line_across, gate_full))
    other_across = swap(out_other, 2)
    out_own = both_y(out_line, out_other).reshape(chunk, width + 128)
    other_across, up_full, out_own = barrier((other_across, up_full, out_own))
    out_across = both_y(line_across, other_across).reshape(chunk, width + 128)
    out_pieces = (out_own, swap(out_own, 1), out_across, swap(out_across, 1))
    extras = [p[:, width:] for p in out_pieces]
    routes_row = extras[0][:, : packed * picks].reshape(rows, picks).astype(jnp.int32)
    extras = jnp.concatenate([p[:, packed * picks :] for p in extras], axis=0)
    router = jnp.pad(extras[:, :expert_count], ((0, 0), (0, 128 - expert_count)))
    g_ffn = extras[:, expert_count].astype(full)[None]
    lane_ids = lax.iota(jnp.int32, 128)
    chosen = jnp.any(routes_row[:, :, None] == lane_ids[None, None, :], axis=1).astype(full)
    own = (
        lane_ids[None, :] == seq_index * held + lax.iota(jnp.int32, held)[:, None]
    ).astype(full)
    attended_row, out_pieces, up_full, router, g_ffn, chosen = barrier(
        (attended_row, out_pieces, up_full, router, g_ffn, chosen)
    )

    dy_shard, attended_row = barrier((reorder(cotangent[0], dp_index, 1), attended_row))
    dy_row = lax.all_gather(dy_shard, "seq", axis=0, tiled=True)
    order = jnp.stack([dp_index ^ k for k in range(4)] + [seq_index]).astype(jnp.int32)
    hidden_mid, normed_ffn, r_ffn, chances, gates = finish_attention(
        order, attended_row, out_pieces, x_row, g_ffn, router, chosen, own, expert_count
    )
    act, dgate_factor, dup_factor = expert_activations(normed_ffn, gate_full, up_full)
    act, down_across = barrier((act, swap(w_down, 2)))
    down_full = jnp.concatenate([w_down, swap(w_down, 1), down_across, swap(down_across, 1)], axis=2)
    y_at = (seq_index % 2).astype(jnp.int32)[None]
    mixture, mixture_far = combine_experts(y_at, act, down_full, gates)
    dy_row, mixture_far, act = barrier((dy_row, mixture_far, act))
    mixture_far = over_y(mixture_far)

    scaled, dgate, dup, gate_sums = expert_gradients(
        dy_row, down_full, act, dgate_factor, dup_factor, gates
    )
    nf_grad, grad_logits = input_gradient(
        dgate, dup, gate_full, up_full, gate_sums, chances, chosen, own, router
    )
    nf_grad, mixture_far = barrier((nf_grad, mixture_far))
    nf_sum = lax.psum_scatter(nf_grad, "seq", scatter_dimension=0, tiled=True)
    mixture = (mixture.astype(full) + mixture_far.astype(full)).astype(low)

    down_kept, down_passed = sum_experts_in_chip(weight_pieces(scaled, dy_row, 4, False))
    gate_pieces = weight_pieces(normed_ffn, dgate, 4, True)
    dup, down_passed = barrier((dup, down_passed))
    down_arrived = across_by_expert(down_passed)
    gate_kept, gate_passed = sum_experts_in_chip(gate_pieces)
    up_pieces = weight_pieces(normed_ffn, dup, 4, True)
    up_pieces, down_arrived[0] = barrier((up_pieces, down_arrived[0]))
    up_kept, up_passed = sum_experts_in_chip(up_pieces)
    router_grad = mm(grad_logits[:, :expert_count], normed_ffn, ((0,), (0,)))
    nf_sum, mixture, down_arrived[0], gate_passed, up_passed, router_grad, down_kept, gate_kept, up_kept = barrier(
        (nf_sum, mixture, down_arrived[0], gate_passed, up_passed, router_grad, down_kept, gate_kept, up_kept)
    )
    gate_arrived, up_arrived = (across_by_expert(gate_passed), [swap(up_passed[0], 2)])

    grad_mid, mid_low, grad_attended, gain_ffn_grad = middle(
        order, nf_sum, hidden_mid, r_ffn, g_ffn, dy_shard, out_pieces
    )
    def to_columns(values):
        return lax.all_to_all(values, "seq", 0, 0, tiled=True).reshape(rows, cols)

    grad_attended = grad_attended.reshape(4, tokens, shards // 4, cols).transpose(0, 2, 1, 3)
    grad_attended = to_columns(grad_attended.reshape(shards, tokens, cols))
    grad_attended, down_arrived[1], gate_arrived[0], mixture = barrier(
        (grad_attended, down_arrived[1], gate_arrived[0], mixture)
    )
    mixture_own = sum_along_z(mixture)
    mid_cols = to_columns(
        reorder(mid_low, dp_index, 1).reshape(tokens, shards, cols).transpose(1, 0, 2)
    )
    q_grad, k_grad, v_low, sums, gain_query_grad, gain_key_grad = attend_back(
        qkv, q_rot, k_rot, value_in, grad_attended, log_total,
        r_query, r_key, g_query, g_key, cosine, sine, seg_col, seg_row,
    )
    sums, gate_arrived[1] = barrier((sums, gate_arrived[1]))
    sums, mid_cols = barrier((share(sums), mid_cols))
    qkv_low, normed_grad, gain_attn_grad = normed_gradient(
        q_grad, k_grad, v_low, qkv, sums, r_query, r_key, w_qkv, x_row, r_attn
    )
    normed_grad, up_arrived[0], mixture_own = barrier((normed_grad, up_arrived[0], mixture_own))
    normed_sum = lax.psum_scatter(normed_grad, "seq", scatter_dimension=0, tiled=True).astype(full)

    def to_owners(kept, passed, count):
        total = kept.astype(full) + swap(passed, 2).astype(full)
        total = lax.all_to_all(
            total.astype(low).reshape(shards, block_rows, count * cols), "seq", 0, 0, tiled=True
        )
        total = total.reshape(shards, block_rows, count, cols).transpose(2, 1, 0, 3)
        return total.reshape(count, block_rows, width).astype(full)

    qkv_parts = [p[0] for p in weight_pieces(normed, qkv_low[None], 4, True)]
    qkv_parts, mid_cols, gain_attn_grad, gain_ffn_grad = barrier(
        (qkv_parts, mid_cols, gain_attn_grad, gain_ffn_grad)
    )
    qkv_kept, qkv_passed = sum_in_chip(qkv_parts, low)
    out_parts = out_grad_pieces(order, attended_row, mid_cols)
    out_kept, out_passed = sum_in_chip(out_parts, low)
    qkv_passed, out_passed, up_last = barrier((qkv_passed, out_passed, up_passed[1]))
    proj_grad = to_owners(qkv_kept, qkv_passed, 3)
    out_grad = to_owners(out_kept, out_passed, 1)
    up_arrived.append(swap(up_last, 2))
    grad_w_down = add_arrived(down_kept, down_arrived)
    grad_w_gate = add_arrived(gate_kept, gate_arrived)
    grad_w_up = add_arrived(up_kept, up_arrived)
    mid_own = lax.dynamic_slice_in_dim(hidden_mid, first_row, tokens)
    block_out = (mid_own + mixture_own.astype(full)).astype(low)
    normed_sum, grad_w_down, grad_w_gate, grad_w_up, out_grad, block_out = barrier(
        (normed_sum, grad_w_down, grad_w_gate, grad_w_up, out_grad, block_out)
    )

    x_own = x_shard.astype(full)
    r_here = lax.rsqrt(jnp.mean(x_own * x_own, axis=-1, keepdims=True) + epsilon)
    scaled_grad = normed_sum * g_attn
    grad_hidden = (
        grad_mid
        + r_here * scaled_grad
        - x_own * (r_here**3) * jnp.mean(scaled_grad * x_own, axis=-1, keepdims=True)
    )

    def place(values):
        whole = lax.dynamic_update_slice_in_dim(
            jnp.zeros((1, width), full), values[None], seq_index * cols, 1
        )
        return reorder(whole, dp_index, 1)

    vectors = jnp.concatenate(
        [
            router_grad,
            gain_attn_grad,
            place(gain_query_grad[0]),
            place(gain_key_grad[0]),
            gain_ffn_grad,
        ]
    )
    count = vectors.shape[0]
    vectors = sum_pieces([vectors[:, k * chunk : (k + 1) * chunk] for k in range(4)], full)
    vectors = vectors.reshape(count, shards, block_rows).transpose(1, 0, 2)
    vectors = jnp.sum(lax.all_to_all(vectors, "seq", 0, 0, tiled=True), axis=0)
    return (
        reorder(block_out, dp_index, 1)[None],
        reorder(grad_hidden, dp_index, 1)[None],
        proj_grad[0],
        proj_grad[1],
        proj_grad[2],
        out_grad[0],
        vectors[expert_count],
        vectors[expert_count + 1],
        vectors[expert_count + 2],
        vectors[expert_count + 3],
        vectors[:expert_count].T,
        grad_w_gate,
        grad_w_up,
        grad_w_down,
    )


def solution(mesh):
    def layer(*arrays):
        whole_heads = (arrays[0].shape[2] // HEAD) % mesh.shape["seq"] == 0
        if whole_heads and mesh.shape["dp"] == 4 and mesh.shape["seq"] == 8:
            return on_device_heads(*arrays)
        return on_device(*arrays)

    return jax.shard_map(
        layer,
        mesh=mesh,
        in_specs=(
            P("dp", "seq", None),
            P("dp", None),
            P("dp", "seq", None),
            P(("dp", "seq"), None),
            P(("dp", "seq"), None),
            P(("dp", "seq"), None),
            P(("dp", "seq"), None),
            P(("dp", "seq")),
            P(("dp", "seq")),
            P(("dp", "seq")),
            P(("dp", "seq")),
            P(("dp", "seq"), None),
            P("seq", "dp", None),
            P("seq", "dp", None),
            P("seq", None, "dp"),
            P("dp", "seq", None),
        ),
        out_specs=(
            P("dp", "seq", None),
            P("dp", "seq", None),
            P(("dp", "seq"), None),
            P(("dp", "seq"), None),
            P(("dp", "seq"), None),
            P(("dp", "seq"), None),
            P(("dp", "seq")),
            P(("dp", "seq")),
            P(("dp", "seq")),
            P(("dp", "seq")),
            P(("dp", "seq"), None),
            P("seq", "dp", None),
            P("seq", "dp", None),
            P("seq", None, "dp"),
        ),
        check_vma=False,
    )
```
